32 devices in a mesh: dp: 16 (over z, y, core), seq: 2 (over x).
Axes of the slice: x: 2, y: 2, z: 4, core: 2. Of those that a mesh axis runs over, the one named last changes fastest.
Arguments:
- patches: bfloat16 [64, 448, 768], P(('dp', 'seq')), may hold values from -6 to 6
- masked_at: int32 [64, 448], P(('dp', 'seq')), may hold values from 0 to 1, as said below
- edge_w: float32 [768, 1536], P(('dp', 'seq')), may hold values from -0.21875 to 0.21875
- attn_w: float32 [768, 6144], P(('dp', 'seq')), may hold values from -0.21875 to 0.21875
- mlp_w: float32 [768, 12288], P(('dp', 'seq')), may hold values from -0.21875 to 0.21875
- posit_w: float32 [768, 448], P(('dp', 'seq')), may hold values from -1.2 to 1.2
- vecs_w: float32 [768, 6], P(('dp', 'seq')), may hold values from 0.5 to 1.5
- edge_m: float32 [768, 1536], P(('dp', 'seq')), may hold values from -6e-05 to 6e-05
- attn_m: float32 [768, 6144], P(('dp', 'seq')), may hold values from -6e-05 to 6e-05
- mlp_m: float32 [768, 12288], P(('dp', 'seq')), may hold values from -6e-05 to 6e-05
- posit_m: float32 [768, 448], P(('dp', 'seq')), may hold values from -6e-05 to 6e-05
- vecs_m: float32 [768, 6], P(('dp', 'seq')), may hold values from -6e-05 to 6e-05
- edge_v: float32 [768, 1536], P(('dp', 'seq')), may hold values from 1e-10 to 4e-10
- attn_v: float32 [768, 6144], P(('dp', 'seq')), may hold values from 1e-10 to 4e-10
- mlp_v: float32 [768, 12288], P(('dp', 'seq')), may hold values from 1e-10 to 4e-10
- posit_v: float32 [768, 448], P(('dp', 'seq')), may hold values from 1e-10 to 4e-10
- vecs_v: float32 [768, 6], P(('dp', 'seq')), may hold values from 1e-10 to 4e-10
- edge_t: float32 [768, 1536], P(('dp', 'seq')), may hold values from -0.21875 to 0.21875
- attn_t: float32 [768, 6144], P(('dp', 'seq')), may hold values from -0.21875 to 0.21875
- mlp_t: float32 [768, 12288], P(('dp', 'seq')), may hold values from -0.21875 to 0.21875
- posit_t: float32 [768, 448], P(('dp', 'seq')), may hold values from -1.2 to 1.2
- vecs_t: float32 [768, 6], P(('dp', 'seq')), may hold values from 0.5 to 1.5
Outputs:
- loss: float32 [], replicated
- new_edge_w: float32 [768, 1536], P(('dp', 'seq'))
- new_attn_w: float32 [768, 6144], P(('dp', 'seq'))
- new_mlp_w: float32 [768, 12288], P(('dp', 'seq'))
- new_posit_w: float32 [768, 448], P(('dp', 'seq'))
- new_vecs_w: float32 [768, 6], P(('dp', 'seq'))
- new_edge_m: float32 [768, 1536], P(('dp', 'seq'))
- new_attn_m: float32 [768, 6144], P(('dp', 'seq'))
- new_mlp_m: float32 [768, 12288], P(('dp', 'seq'))
- new_posit_m: float32 [768, 448], P(('dp', 'seq'))
- new_vecs_m: float32 [768, 6], P(('dp', 'seq'))
- new_edge_v: float32 [768, 1536], P(('dp', 'seq'))
- new_attn_v: float32 [768, 6144], P(('dp', 'seq'))
- new_mlp_v: float32 [768, 12288], P(('dp', 'seq'))
- new_posit_v: float32 [768, 448], P(('dp', 'seq'))
- new_vecs_v: float32 [768, 6], P(('dp', 'seq'))
- new_edge_t: float32 [768, 1536], P(('dp', 'seq'))
- new_attn_t: float32 [768, 6144], P(('dp', 'seq'))
- new_mlp_t: float32 [768, 12288], P(('dp', 'seq'))
- new_posit_t: float32 [768, 448], P(('dp', 'seq'))
- new_vecs_t: float32 [768, 6], P(('dp', 'seq'))
The draws below stay inside these ranges and needn't reach their ends.
Inputs may be any that keep to these rules, and one draw needn't show every extreme that they name: `masked_at`: sequence s (counted from 0) has exactly 112 + (448 // 2 * s) // 63 masked tokens.
All inputs are finite; a program needn't handle non-finite values.
Results may differ from the reference program's by a relative error of at most 0.002.
The reference program's roundings to bfloat16 on the way count: a program that leaves them out, or rounds other values in their place, can miss the bound.
Values may be sent and summed in bfloat16 or wider, within the bound.
No kernel may reach another device: no remote copies, remote signals or barrier semaphores. Data moves between devices by JAX's collectives and lax.ppermute only.
A program may use at most 448 MiB of HBM per device.

```python
import math
from functools import partial
import jax
import jax.numpy as jnp
from jax import lax

D = 768
HEADS = 12
HDIM = 64
FF = 3072
LAYERS = 2
LEN = 448
TOPK = 2
SEQS = 64
NORMER = 14336


def draw_masked_at(key, part):
    seq_keys = jax.random.split(key, SEQS)

    def one_order(seq_key):
        return jax.random.permutation(seq_key, LEN)
    orders = jax.vmap(one_order)(seq_keys)
    rank_table = jnp.argsort(orders, axis=1)
    seq_index = jnp.arange(SEQS, dtype=jnp.int32)
    counts = LEN // 4 + LEN // 2 * seq_index // (SEQS - 1)
    return (rank_table < counts[:, None]).astype(jnp.int32)


def block_levels(key, extent, cuts, least, top_value):
    level, own = 1.0, jax.random.fold_in(key, 6)
    for position, shards_of in cuts:
        draws = jnp.exp(jax.random.uniform(jax.random.fold_in(own, position), (shards_of,), jnp.float32, least / len(cuts), top_value / len(cuts)))
        level = level * jnp.repeat(draws, extent[position] // shards_of).reshape([-1 if axis == position else 1 for axis in range(len(extent))])
    return level


def bell_draw(stream_key, shape, spread, reach, shards=(), kind=jnp.bfloat16):
    factor_of = block_levels(stream_key, shape, shards, -0.22, 0.18) if shards else 1.0
    result = jax.random.normal(stream_key, shape, jnp.float32) * spread * factor_of
    return jnp.minimum(jnp.maximum(result, -reach), reach).astype(kind)


def setup_inputs(seed: int = 0) -> dict:
    key_of = jax.random.split(jax.random.key(seed), 23)
    return {
        "patches": bell_draw(key_of[0], (SEQS, LEN, D), 1.0, 6.0, ((0, 32),)),
        "masked_at": draw_masked_at(jax.random.fold_in(key_of[22], 71), 0),
        "edge_w": bell_draw(key_of[2], (D, 2 * D), D ** -0.5, 0.21875, ((0, 32),), jnp.float32),
        "attn_w": bell_draw(key_of[3], (D, LAYERS * 4 * D), D ** -0.5, 0.21875, ((0, 32),), jnp.float32),
        "mlp_w": bell_draw(key_of[4], (D, LAYERS * 2 * FF), D ** -0.5, 0.21875, ((0, 32),), jnp.float32),
        "posit_w": bell_draw(key_of[5], (D, LEN), 0.2, 1.2, ((0, 32),), jnp.float32),
        "vecs_w": jnp.clip(1.0 + 0.1 * jax.random.normal(key_of[6], (D, 2 * LAYERS + 2), jnp.float32), 0.5, 1.5),
        "edge_m": bell_draw(key_of[7], (D, 2 * D), (1e-5), 5.999999848427251e-05, ((0, 32),), jnp.float32),
        "attn_m": bell_draw(key_of[8], (D, LAYERS * 4 * D), (1e-5), 5.999999848427251e-05, ((0, 32),), jnp.float32),
        "mlp_m": bell_draw(key_of[9], (D, LAYERS * 2 * FF), (1e-5), 5.999999848427251e-05, ((0, 32),), jnp.float32),
        "posit_m": bell_draw(key_of[10], (D, LEN), (1e-5), 5.999999848427251e-05, ((0, 32),), jnp.float32),
        "vecs_m": bell_draw(key_of[11], (D, 2 * LAYERS + 2), (1e-5), 5.999999848427251e-05, ((0, 32),), jnp.float32),
        "edge_v": jnp.clip(jnp.exp(math.log(4.000000053405728e-10) - 1.3862944 * jax.random.uniform(key_of[12], (D, 2 * D), jnp.float32) ** block_levels(key_of[12], (D, 2 * D), ((0, 32),), -0.2, 0.2)), 1.000000013351432e-10, 4.000000053405728e-10),
        "attn_v": jnp.clip(jnp.exp(math.log(4.000000053405728e-10) - 1.3862944 * jax.random.uniform(key_of[13], (D, LAYERS * 4 * D), jnp.float32) ** block_levels(key_of[13], (D, LAYERS * 4 * D), ((0, 32),), -0.2, 0.2)), 1.000000013351432e-10, 4.000000053405728e-10),
        "mlp_v": jnp.clip(jnp.exp(math.log(4.000000053405728e-10) - 1.3862944 * jax.random.uniform(key_of[14], (D, LAYERS * 2 * FF), jnp.float32) ** block_levels(key_of[14], (D, LAYERS * 2 * FF), ((0, 32),), -0.2, 0.2)), 1.000000013351432e-10, 4.000000053405728e-10),
        "posit_v": jnp.clip(jnp.exp(math.log(4.000000053405728e-10) - 1.3862944 * jax.random.uniform(key_of[15], (D, LEN), jnp.float32) ** block_levels(key_of[15], (D, LEN), ((0, 32),), -0.2, 0.2)), 1.000000013351432e-10, 4.000000053405728e-10),
        "vecs_v": jnp.clip(jnp.exp(math.log(4.000000053405728e-10) - 1.3862944 * jax.random.uniform(key_of[16], (D, 2 * LAYERS + 2), jnp.float32) ** block_levels(key_of[16], (D, 2 * LAYERS + 2), ((0, 32),), -0.2, 0.2)), 1.000000013351432e-10, 4.000000053405728e-10),
        "edge_t": bell_draw(key_of[17], (D, 2 * D), D ** -0.5, 0.21875, ((0, 32),), jnp.float32),
        "attn_t": bell_draw(key_of[18], (D, LAYERS * 4 * D), D ** -0.5, 0.21875, ((0, 32),), jnp.float32),
        "mlp_t": bell_draw(key_of[19], (D, LAYERS * 2 * FF), D ** -0.5, 0.21875, ((0, 32),), jnp.float32),
        "posit_t": bell_draw(key_of[20], (D, LEN), 0.2, 1.2, ((0, 32),), jnp.float32),
        "vecs_t": jnp.clip(1.0 + 0.1 * jax.random.normal(key_of[21], (D, 2 * LAYERS + 2), jnp.float32), 0.5, 1.5),
    }


@jax.custom_vjp
def low(v):
    return lax.optimization_barrier(v.astype(jnp.bfloat16)).astype(jnp.float32)

@jax.custom_vjp
def low_back(v):
    return v

def low_keep(v):
    return (low(v), None)

def low_pass(kept, grad):
    return (grad,)

def back_keep(v):
    return (v, None)

def back_low(kept, grad):
    return (low(grad),)
low.defvjp(low_keep, low_pass)
low_back.defvjp(back_keep, back_low)
ln_eps = 1e-05
in_eps = 1e-05
learn_rate = 0.02
first_decay = 0.5
second_decay = 0.5
adam_eps = 1e-08
weight_decay = 0.1
teacher_keep = 0.5
huber_beta = 1.0
score_scale = 0.125
entry_clip = 1e-05

def matmul(left, right):
    return jnp.dot(left, right, precision=lax.Precision.HIGHEST, preferred_element_type=jnp.float32)

def normalize(values, gain_vec):
    centre = values - lax.optimization_barrier(jnp.mean(values, axis=-1, keepdims=True))
    return centre * lax.rsqrt(lax.optimization_barrier(jnp.mean(centre * centre, axis=-1, keepdims=True)) + ln_eps) * gain_vec

def layer_pass(current, attn_full, mlp_full, gain_one, gain_two):
    normed_one = low(normalize(current, gain_one))
    projected = low(low_back(matmul(normed_one, attn_full[:, :3 * D])))
    queries = projected[:, :D].reshape(LEN, HEADS, HDIM)
    key_part = projected[:, D:2 * D].reshape(LEN, HEADS, HDIM)
    value_part = projected[:, 2 * D:].reshape(LEN, HEADS, HDIM)
    scores = jnp.einsum('qhd,khd->hqk', queries, key_part, precision=lax.Precision.HIGHEST) * score_scale
    scores = low_back(scores)
    soft_probs = low(jax.nn.softmax(scores, axis=-1))
    mixed_out = jnp.einsum('hqk,khd->qhd', soft_probs, value_part, precision=lax.Precision.HIGHEST).reshape(LEN, D)
    mixed_out = low(low_back(mixed_out))
    middle = current + low_back(matmul(mixed_out, attn_full[:, 3 * D:]))
    normed_two = low(normalize(middle, gain_two))
    hidden_up = low_back(matmul(normed_two, mlp_full[:, :FF]))
    active = low(jax.nn.gelu(hidden_up, approximate=False))
    return middle + low_back(matmul(active, mlp_full[:, FF:].T))

def embed_tokens(weights, patch_seq, mask_seq):
    edge_part, attn_part, mlp_part, posit_part, vecs_part = weights
    embedded = low_back(matmul(patch_seq, edge_part[:, :D]))
    mask_col = mask_seq[:, None]
    return embedded * (1.0 - mask_col) + mask_col * vecs_part[:, 2 * LAYERS + 1][None, :] + posit_part.T

def layer_cols(weights, layer_idx):
    attn_part = weights[1][:, layer_idx * 4 * D:(layer_idx + 1) * 4 * D]
    mlp_part = weights[2][:, layer_idx * 2 * FF:(layer_idx + 1) * 2 * FF]
    return (attn_part, mlp_part)

def teacher_targets(weights, patch_seq):
    current = embed_tokens(weights, patch_seq, jnp.zeros((LEN,), jnp.float32))
    outputs = []
    for layer_idx in range(LAYERS):
        attn_part, mlp_part = layer_cols(weights, layer_idx)
        current = layer_pass(current, attn_part, mlp_part, weights[4][:, layer_idx], weights[4][:, LAYERS + layer_idx])
        outputs.append(current)
    normed_list = []
    for layer_out in outputs[LAYERS - TOPK:]:
        centre = layer_out - lax.optimization_barrier(jnp.mean(layer_out, axis=0, keepdims=True))
        variance = lax.optimization_barrier(jnp.mean(centre * centre, axis=0, keepdims=True))
        normed_list.append(centre * lax.rsqrt(variance + in_eps))
    return lax.optimization_barrier(jnp.mean(jnp.stack(normed_list), axis=0))

def student_loss(weights, patch_seq, mask_seq, target):
    current = embed_tokens(weights, patch_seq, mask_seq)
    for layer_idx in range(LAYERS):
        attn_part, mlp_part = layer_cols(weights, layer_idx)
        current = layer_pass(current, attn_part, mlp_part, weights[4][:, layer_idx], weights[4][:, LAYERS + layer_idx])
    final_norm = low(normalize(current, weights[4][:, 2 * LAYERS]))
    predicted = low_back(matmul(final_norm, weights[0][:, D:]))
    differ = predicted - target
    magnitude = jnp.abs(differ)
    huber_terms = jnp.where(magnitude < huber_beta, 0.5 * differ * differ / huber_beta, magnitude - 0.5 * huber_beta)
    return jnp.sum(huber_terms * mask_seq[:, None])

def clip_group(gradient):
    limit = entry_clip * jnp.sqrt(jnp.float32(gradient.size))
    norm_value = jnp.sqrt(jnp.sum(gradient * gradient))
    return gradient * (limit / jnp.maximum(norm_value, limit))

def adam_step(weight, first_mom, second_mom, teacher, gradient):
    first_new = first_decay * first_mom + (1.0 - first_decay) * gradient
    second_new = second_decay * second_mom + (1.0 - second_decay) * gradient * gradient
    weight_new = weight - learn_rate * (first_new / (jnp.sqrt(second_new) + adam_eps) + weight_decay * weight)
    teacher_new = teacher_keep * teacher + (1.0 - teacher_keep) * weight_new
    return (weight_new, first_new, second_new, teacher_new)

def reference(patches, masked_at, edge_w, attn_w, mlp_w, posit_w, vecs_w, edge_m, attn_m, mlp_m, posit_m, vecs_m, edge_v, attn_v, mlp_v, posit_v, vecs_v, edge_t, attn_t, mlp_t, posit_t, vecs_t):
    patches_full = patches.astype(jnp.float32)
    mask_full = masked_at.astype(jnp.float32)
    masters = (edge_w, attn_w, mlp_w, posit_w, vecs_w)
    teachers = (edge_t, attn_t, mlp_t, posit_t, vecs_t)
    teacher_low = tuple((low(weight_part) for weight_part in teachers))
    targets = lax.map(partial(teacher_targets, teacher_low), patches_full)

    def total_loss(master_parts):
        low_parts = tuple((low(weight_part) for weight_part in master_parts))

        def one_sequence(running, seq_items):
            patch_seq, mask_seq, target = seq_items
            return (running + student_loss(low_parts, patch_seq, mask_seq, target), None)
        summed, unused = lax.scan(jax.checkpoint(one_sequence), jnp.zeros((), jnp.float32), (patches_full, mask_full, targets))
        return summed / NORMER
    loss_value, pullback = jax.vjp(total_loss, masters)
    grad_parts = tuple((clip_group(part) for part in pullback(jnp.ones((), jnp.float32))[0]))
    edge_new = adam_step(edge_w, edge_m, edge_v, edge_t, grad_parts[0])
    attn_new = adam_step(attn_w, attn_m, attn_v, attn_t, grad_parts[1])
    mlp_new = adam_step(mlp_w, mlp_m, mlp_v, mlp_t, grad_parts[2])
    posit_new = adam_step(posit_w, posit_m, posit_v, posit_t, grad_parts[3])
    vecs_new = adam_step(vecs_w, vecs_m, vecs_v, vecs_t, grad_parts[4])
    return (loss_value, edge_new[0], attn_new[0], mlp_new[0], posit_new[0], vecs_new[0], edge_new[1], attn_new[1], mlp_new[1], posit_new[1], vecs_new[1], edge_new[2], attn_new[2], mlp_new[2], posit_new[2], vecs_new[2], edge_new[3], attn_new[3], mlp_new[3], posit_new[3], vecs_new[3])
```

```python
import jax
import jax.numpy as jnp
from jax import lax
from jax.experimental import pallas as pl
from jax.experimental.pallas import tpu as pltpu
from jax.sharding import PartitionSpec as P

HDIM = 64
LAYERS = 2
TOPK = 2
LANES = 128

ln_eps = 1e-05
in_eps = 1e-05
learn_rate = 0.02
first_decay = 0.5
second_decay = 0.5
adam_eps = 1e-08
weight_decay = 0.1
teacher_keep = 0.5
huber_beta = 1.0
score_scale = 0.125
entry_clip = 1e-05
half_type = jnp.bfloat16
full_type = jnp.float32
AXES = ("dp", "seq")


def contract(left, right, left_dim, right_dim):
    return lax.dot_general(
        left,
        right,
        (((left_dim,), (right_dim,)), ((), ())),
        preferred_element_type=full_type,
    )


def head_mask(which, width):
    lane = lax.broadcasted_iota(jnp.int32, (1, width), 1)
    return (lane // HDIM) == which


def attend_kernel(q_ref, k_ref, v_ref, o_ref):
    queries = q_ref[0] * jnp.asarray(score_scale, half_type)
    keys_all = k_ref[0]
    values_all = v_ref[0]
    width = queries.shape[1]
    mixed = None
    for which in range(width // HDIM):
        mask = head_mask(which, width)
        head_q = jnp.where(mask, queries, jnp.zeros_like(queries))
        scores = contract(head_q, keys_all, 1, 1)
        exps = jnp.exp(scores - jnp.max(scores, axis=1, keepdims=True))
        probs = (exps * (1.0 / jnp.sum(exps, axis=1, keepdims=True))).astype(half_type)
        head_out = contract(probs, values_all, 1, 0)
        mixed = head_out if mixed is None else jnp.where(mask, head_out, mixed)
    o_ref[0] = mixed.astype(half_type)


def attend_back_kernel(q_ref, k_ref, v_ref, do_ref, dq_ref, dk_ref, dv_ref):
    queries = q_ref[0] * jnp.asarray(score_scale, half_type)
    keys_all = k_ref[0]
    values_all = v_ref[0]
    grad_out = do_ref[0]
    width = queries.shape[1]
    grad_k = None
    grad_v = None
    grad_q_rows = []
    for which in range(width // HDIM):
        mask = head_mask(which, width)
        head_q = jnp.where(mask, queries, jnp.zeros_like(queries))
        head_do = jnp.where(mask, grad_out, jnp.zeros_like(grad_out))
        scores = contract(keys_all, head_q, 1, 1)
        exps = jnp.exp(scores - jnp.max(scores, axis=0, keepdims=True))
        probs = exps * (1.0 / jnp.sum(exps, axis=0, keepdims=True))
        grad_probs = contract(values_all, head_do, 1, 1)
        prods = probs * grad_probs
        grad_scores = (prods - probs * jnp.sum(prods, axis=0, keepdims=True)).astype(half_type)
        head_dv = contract(probs.astype(half_type), grad_out, 1, 0)
        head_dk = contract(grad_scores, queries, 1, 0)
        head_dq = contract(keys_all, grad_scores, 0, 0)
        grad_q_rows.append(head_dq[which * HDIM : (which + 1) * HDIM])
        grad_v = head_dv if grad_v is None else jnp.where(mask, head_dv, grad_v)
        grad_k = head_dk if grad_k is None else jnp.where(mask, head_dk, grad_k)
    grad_q = jnp.concatenate(grad_q_rows, axis=0).T * score_scale
    dq_ref[0] = grad_q.astype(half_type)
    dk_ref[0] = grad_k.astype(half_type)
    dv_ref[0] = grad_v.astype(half_type)


def qkv_specs(tokens, blocks):
    return [
        pl.BlockSpec((1, tokens, LANES), lambda s, j, off=off: (s, 0, off * blocks + j))
        for off in range(3)
    ]


def attend(projected):
    seqs, tokens, width3 = projected.shape
    width = width3 // 3
    blocks = width // LANES
    return pl.pallas_call(
        attend_kernel,
        grid=(seqs, blocks),
        in_specs=qkv_specs(tokens, blocks),
        out_specs=pl.BlockSpec((1, tokens, LANES), lambda s, j: (s, 0, j)),
        out_shape=jax.ShapeDtypeStruct((seqs, tokens, width), half_type),
        cost_estimate=pl.CostEstimate(
            flops=16 * seqs * tokens * tokens * width,
            transcendentals=seqs * tokens * tokens * width // HDIM,
            bytes_accessed=8 * seqs * tokens * width,
        ),
        name="attend",
    )(projected, projected, projected)


def attend_back(projected, grad_mixed):
    seqs, tokens, width3 = projected.shape
    width = width3 // 3
    blocks = width // LANES
    block = pl.BlockSpec((1, tokens, LANES), lambda s, j: (s, 0, j))
    shape = jax.ShapeDtypeStruct((seqs, tokens, width), half_type)
    return pl.pallas_call(
        attend_back_kernel,
        grid=(seqs, blocks),
        in_specs=qkv_specs(tokens, blocks) + [block],
        out_specs=[block, block, block],
        out_shape=[shape, shape, shape],
        cost_estimate=pl.CostEstimate(
            flops=32 * seqs * tokens * tokens * width,
            transcendentals=seqs * tokens * tokens * width // HDIM,
            bytes_accessed=14 * seqs * tokens * width,
        ),
        name="attend_back",
    )(projected, projected, projected, grad_mixed)


def normalize(values, gain_vec):
    centre = values - jnp.mean(values, axis=-1, keepdims=True)
    inv_scale = lax.rsqrt(jnp.mean(centre * centre, axis=-1, keepdims=True) + ln_eps)
    normed_unit = centre * inv_scale
    return (normed_unit * gain_vec).astype(half_type), normed_unit, inv_scale


def normalize_back(grad_out, gain_vec, normed_unit, inv_scale):
    grad_unit = grad_out * gain_vec
    inner_mean = jnp.mean(grad_unit, axis=-1, keepdims=True)
    along_mean = jnp.mean(grad_unit * normed_unit, axis=-1, keepdims=True)
    grad_in = (grad_unit - inner_mean - normed_unit * along_mean) * inv_scale
    return grad_in, jnp.sum(grad_out * normed_unit, axis=0)


def normal_cdf(values):
    return 0.5 + 0.5 * lax.erf(values * (0.5**0.5))


def gelu_exact(values):
    return values * normal_cdf(values)


def gelu_slope(values):
    density = jnp.exp(-0.5 * values * values) * (0.5 / jnp.pi) ** 0.5
    return normal_cdf(values) + values * density


class Plan:
    def __init__(self):
        self.seq_size = lax.axis_size("seq")
        self.count = lax.axis_size("dp") * self.seq_size
        self.bits = self.count.bit_length() - 1
        self.early = list(range(self.bits - 1, 2, -1))

        def flips(pick):
            return [(i, i ^ (1 << pick((i >> 1) & 1))) for i in range(self.count)]

        self.stages = [flips(lambda core, b=b: b) for b in self.early]
        self.stages.append(flips(lambda core: 0 if core else 2))
        self.stages.append(flips(lambda core: 2 if core else 0))
        self.core_stage = flips(lambda core: 1)
        self.index = lax.axis_index("dp") * self.seq_size + lax.axis_index("seq")

    def swap(self, value, perm):
        return lax.ppermute(value, AXES, perm)

    def row_table(self, width):
        rows = width // self.count
        place = lax.broadcasted_iota(jnp.int32, (1, width), 1)
        spot = place // rows
        early_count = len(self.early)
        other = (spot >> (self.bits - 1)) & 1
        holder_core = ((self.index >> 1) & 1) ^ other
        block = self.index ^ (other << 1)
        for step, bit in enumerate(self.early):
            block = block ^ (((spot >> step) & 1) << bit)
        first = (spot >> early_count) & 1
        second = (spot >> (early_count + 1)) & 1
        block = block ^ jnp.where(holder_core == 0, first << 2, first)
        block = block ^ jnp.where(holder_core == 0, second, second << 2)
        return block * rows + place % rows

    def mover(self, width):
        table = self.row_table(width)
        whole = lax.broadcasted_iota(jnp.int32, (width, width), 0)
        return (whole == table).astype(half_type)


def to_relative(values, mover):
    return contract(values, mover, 1, 0).astype(half_type)


def to_whole(values, mover):
    return contract(values, mover, 1, 1).astype(half_type)


def gather_chunks(plan, chunks):
    done = []
    last = [None] * len(plan.stages)
    for parts in chunks:
        value = jnp.concatenate(parts, axis=1)
        for step, perm in enumerate(plan.stages):
            if last[step] is not None:
                value, _ = lax.optimization_barrier((value, last[step]))
            got = plan.swap(value, perm)
            last[step] = got
            value = jnp.concatenate([value, got], axis=0)
        got = plan.swap(value, plan.core_stage)
        outs = []
        start = 0
        for part in parts:
            stop = start + part.shape[1]
            outs.append(jnp.concatenate([value[:, start:stop], got[:, start:stop]], axis=0))
            start = stop
        done.append(outs)
    return done


def scatter_chunk(plan, pieces):
    gots = [plan.swap(far, plan.core_stage) for _, far in pieces]
    quarter = pieces[0][0].shape[0] // 2
    send = jnp.concatenate(
        [near[quarter:] + got[quarter:] for (near, _), got in zip(pieces, gots)], axis=1
    )
    keep = jnp.concatenate(
        [near[:quarter] + got[:quarter] for (near, _), got in zip(pieces, gots)], axis=1
    )
    stages = plan.stages[::-1]
    for step, perm in enumerate(stages):
        got = plan.swap(send, perm)
        if step == len(stages) - 1:
            return keep + got
        half = keep.shape[0] // 2
        send = keep[half:] + got[half:]
        keep = keep[:half] + got[:half]


def halves(left, right):
    half = left.shape[1] // 2
    return contract(left[:, :half], right, 0, 0), contract(left[:, half:], right, 0, 0)


def row_halves(value):
    half = value.shape[0] // 2
    return value[:half], value[half:]


def layer_forward(flat_in, seqs, weights, gain_one, gain_two):
    w_qkv, w_out, w_up, w_down = weights
    tokens = flat_in.shape[0] // seqs
    normed_one, unit_one, scale_one = normalize(flat_in, gain_one)
    projected = contract(normed_one, w_qkv, 1, 0).astype(half_type)
    projected = projected.reshape(seqs, tokens, projected.shape[1])
    mixed = attend(projected).reshape(flat_in.shape)
    middle = flat_in + contract(mixed, w_out, 1, 0)
    normed_two, unit_two, scale_two = normalize(middle, gain_two)
    hidden_up = contract(normed_two, w_up, 1, 0)
    active = gelu_exact(hidden_up).astype(half_type)
    out = middle + contract(active, w_down, 1, 1)
    saved = (
        unit_one,
        scale_one,
        normed_one,
        projected,
        mixed,
        unit_two,
        scale_two,
        normed_two,
        hidden_up,
        active,
    )
    return out, saved


def layer_backward(grad_out, saved, weights, gain_one, gain_two, mover):
    (
        unit_one,
        scale_one,
        normed_one,
        projected,
        mixed,
        unit_two,
        scale_two,
        normed_two,
        hidden_up,
        active,
    ) = saved
    w_qkv, w_out, w_up, w_down = weights
    grad_down = grad_out.astype(half_type)
    grad_active = contract(grad_down, w_down, 1, 0)
    grad_hidden = (grad_active * gelu_slope(hidden_up)).astype(half_type)
    mlp_pieces = [halves(normed_two, grad_hidden), halves(grad_down, active)]
    grad_norm_two = contract(grad_hidden, w_up, 1, 1)
    grad_middle, grad_gain_two = normalize_back(grad_norm_two, gain_two, unit_two, scale_two)
    grad_middle = grad_out + grad_middle
    grad_branch = grad_middle.astype(half_type)
    out_piece = halves(to_relative(mixed, mover), to_whole(grad_branch, mover))
    grad_mixed = contract(grad_branch, w_out, 1, 1).astype(half_type)
    grad_q, grad_k, grad_v = attend_back(
        projected, grad_mixed.reshape(projected.shape[0], projected.shape[1], -1)
    )
    grad_proj = jnp.concatenate([grad_q, grad_k, grad_v], axis=2).reshape(
        grad_out.shape[0], projected.shape[2]
    )
    qkv_piece = halves(normed_one, grad_proj)
    grad_norm_one = contract(grad_proj, w_qkv, 1, 1)
    grad_in, grad_gain_one = normalize_back(grad_norm_one, gain_one, unit_one, scale_one)
    return (
        grad_middle + grad_in,
        [qkv_piece, out_piece],
        mlp_pieces,
        grad_gain_one,
        grad_gain_two,
    )


def adam_step(weight, first_mom, second_mom, teacher, gradient):
    first_new = first_decay * first_mom + (1.0 - first_decay) * gradient
    second_new = second_decay * second_mom + (1.0 - second_decay) * gradient * gradient
    weight_new = weight - learn_rate * (
        first_new / (jnp.sqrt(second_new) + adam_eps) + weight_decay * weight
    )
    teacher_new = teacher_keep * teacher + (1.0 - teacher_keep) * weight_new
    return (weight_new, first_new, second_new, teacher_new)


def pad_lanes(value):
    extra = -value.shape[1] % LANES
    return jnp.pad(value, ((0, 0), (0, extra)))


def local(
    patches,
    masked_at,
    edge_w,
    attn_w,
    mlp_w,
    posit_w,
    vecs_w,
    edge_m,
    attn_m,
    mlp_m,
    posit_m,
    vecs_m,
    edge_v,
    attn_v,
    mlp_v,
    posit_v,
    vecs_v,
    edge_t,
    attn_t,
    mlp_t,
    posit_t,
    vecs_t,
):
    seqs, tokens, width = patches.shape
    plan = Plan()
    total_masked = seqs * plan.count * tokens // 2
    ff_width = mlp_w.shape[1] // (2 * LAYERS)
    small_cols = tokens + vecs_w.shape[1]
    flat_patch = patches.reshape(-1, width)
    mask_flat = masked_at.astype(full_type).reshape(-1, 1)

    def shards(edge, attn, mlp, posit, vecs):
        edge, attn, mlp, posit, vecs = (
            part.astype(half_type) for part in (edge, attn, mlp, posit, vecs)
        )
        small = pad_lanes(jnp.concatenate([posit, vecs], axis=1))
        attn_parts = []
        mlp_parts = []
        for layer in range(LAYERS):
            base = layer * 4 * width
            attn_parts.append(
                [attn[:, base : base + 3 * width], attn[:, base + 3 * width : base + 4 * width]]
            )
            base = layer * 2 * ff_width
            mlp_parts.append(
                [mlp[:, base : base + ff_width], mlp[:, base + ff_width : base + 2 * ff_width]]
            )
        return edge[:, :width], edge[:, width:], small, attn_parts, mlp_parts

    t_patch, _, t_small, t_attn, t_mlp = shards(edge_t, attn_t, mlp_t, posit_t, vecs_t)
    s_patch, s_head, s_small, s_attn, s_mlp = shards(edge_w, attn_w, mlp_w, posit_w, vecs_w)
    chunks = [
        [t_patch, t_small] + t_attn[0],
        t_mlp[0],
        t_attn[1] + t_mlp[1],
        [s_patch, s_small] + s_attn[0],
        s_mlp[0],
        s_attn[1] + [s_head],
        s_mlp[1],
    ]
    gathered = gather_chunks(plan, chunks)
    t_first, t_mlp0, t_second, s_first, s_mlp0, s_second, s_mlp1 = gathered

    mover = plan.mover(width)
    patch_rel = to_relative(flat_patch, mover)

    def both_sides(w_out):
        return contract(mover, to_relative(w_out, mover), 1, 0).astype(half_type)

    def ready(first, mlp0, attn1, mlp1):
        patch, small, qkv0, out0 = first
        qkv1, out1 = attn1
        vec_table = small[:, tokens:small_cols].astype(full_type).T
        posit = small[:, :tokens].astype(full_type).T
        layers = [
            (qkv0, both_sides(out0), mlp0[0], mlp0[1]),
            (qkv1, both_sides(out1), mlp1[0], mlp1[1]),
        ]
        return to_relative(patch, mover), posit, vec_table, layers

    t_embed, t_posit, t_vecs, t_layers = ready(t_first, t_mlp0, t_second[:2], t_second[2:])
    s_embed, s_posit, s_vecs, s_layers = ready(s_first, s_mlp0, s_second[:2], s_mlp1)
    head_rel = to_relative(s_second[2], mover)

    def spread(table):
        return jnp.broadcast_to(table[None], (seqs, tokens, width)).reshape(-1, width)

    state = contract(patch_rel, t_embed, 1, 0) + spread(t_posit)
    target = None
    for layer in range(LAYERS):
        state, _ = layer_forward(
            state, seqs, t_layers[layer], t_vecs[layer], t_vecs[LAYERS + layer]
        )
        if layer >= LAYERS - TOPK:
            by_seq = state.reshape(seqs, tokens, width)
            centred = by_seq - jnp.mean(by_seq, axis=1, keepdims=True)
            variance = jnp.mean(centred * centred, axis=1, keepdims=True)
            term = centred * lax.rsqrt(variance + in_eps)
            target = term if target is None else target + term
    target = (target / TOPK).reshape(-1, width)

    embedded = contract(patch_rel, s_embed, 1, 0)
    current = (
        embedded * (1.0 - mask_flat) + mask_flat * s_vecs[2 * LAYERS + 1] + spread(s_posit)
    )
    kept = []
    for layer in range(LAYERS):
        current, saved = layer_forward(
            current, seqs, s_layers[layer], s_vecs[layer], s_vecs[LAYERS + layer]
        )
        kept.append(saved)
    final_normed, final_unit, final_scale = normalize(current, s_vecs[2 * LAYERS])
    predicted = contract(final_normed, head_rel, 1, 0)
    differ = predicted - target
    magnitude = jnp.abs(differ)
    huber_terms = jnp.where(
        magnitude < huber_beta, 0.5 * differ * differ / huber_beta, magnitude - 0.5 * huber_beta
    )
    loss_local = jnp.sum(huber_terms * mask_flat) / total_masked
    grad_pred = (mask_flat * jnp.clip(differ / huber_beta, -1.0, 1.0) / total_masked).astype(
        half_type
    )
    head_piece = halves(final_normed, to_whole(grad_pred, mover))
    grad_flow, grad_gain_final = normalize_back(
        contract(grad_pred, head_rel, 1, 1), s_vecs[2 * LAYERS], final_unit, final_scale
    )
    gain_ones = [None] * LAYERS
    gain_twos = [None] * LAYERS
    attn_shards = [None] * LAYERS
    mlp_shards = [None] * LAYERS
    head_shard = None
    for layer in reversed(range(LAYERS)):
        grad_flow, attn_pieces, mlp_pieces, gain_ones[layer], gain_twos[layer] = layer_backward(
            grad_flow,
            kept[layer],
            s_layers[layer],
            s_vecs[layer],
            s_vecs[LAYERS + layer],
            mover,
        )
        mlp_shards[layer] = scatter_chunk(plan, mlp_pieces)
        if head_shard is None:
            summed = scatter_chunk(plan, [head_piece] + attn_pieces)
            head_shard = summed[:, :width]
            attn_shards[layer] = summed[:, width:]
        else:
            attn_shards[layer] = scatter_chunk(plan, attn_pieces)
    grad_maskvec = jnp.sum(grad_flow * mask_flat, axis=0)
    grad_posit = jnp.sum(grad_flow.reshape(seqs, tokens, width), axis=0).T
    grad_embed = to_whole((grad_flow * (1.0 - mask_flat)).astype(half_type), mover)
    patch_piece = halves(patch_rel, grad_embed)
    vec_grads = jnp.stack(gain_ones + gain_twos + [grad_gain_final, grad_maskvec], axis=1)
    small_grads = pad_lanes(jnp.concatenate([grad_posit, vec_grads], axis=1))
    summed = scatter_chunk(plan, [patch_piece, row_halves(small_grads)])
    raw = (
        jnp.concatenate([summed[:, :width], head_shard], axis=1),
        jnp.concatenate(attn_shards, axis=1),
        jnp.concatenate(mlp_shards, axis=1),
        summed[:, width : width + tokens],
        summed[:, width + tokens : width + small_cols],
    )
    totals = jnp.stack([loss_local] + [jnp.sum(part * part) for part in raw])
    totals = jnp.broadcast_to(totals[:, None], (totals.shape[0], LANES))
    for perm in [plan.core_stage] + plan.stages:
        totals = totals + plan.swap(totals, perm)
    total_loss = totals[0, 0]
    clipped = []
    for group, part in enumerate(raw):
        limit = entry_clip * jnp.sqrt(jnp.float32(part.size * plan.count))
        norm_value = jnp.sqrt(totals[group + 1, 0])
        clipped.append(part * (limit / jnp.maximum(norm_value, limit)))
    edge_new = adam_step(edge_w, edge_m, edge_v, edge_t, clipped[0])
    attn_new = adam_step(attn_w, attn_m, attn_v, attn_t, clipped[1])
    mlp_new = adam_step(mlp_w, mlp_m, mlp_v, mlp_t, clipped[2])
    posit_new = adam_step(posit_w, posit_m, posit_v, posit_t, clipped[3])
    vecs_new = adam_step(vecs_w, vecs_m, vecs_v, vecs_t, clipped[4])
    news = (edge_new, attn_new, mlp_new, posit_new, vecs_new)
    return (total_loss,) + tuple(group[part] for part in range(4) for group in news)


def solution(mesh):
    rows = P(AXES, None)
    in_specs = (P(AXES, None, None),) + (rows,) * 21
    out_specs = (P(),) + (rows,) * 20
    return jax.shard_map(local, mesh=mesh, in_specs=in_specs, out_specs=out_specs, check_vma=False)
```

```python
import jax
import jax.numpy as jnp
from jax import lax
from jax.experimental import pallas as pl
from jax.experimental.pallas import tpu as pltpu
from jax.sharding import PartitionSpec as P

HDIM = 64
LAYERS = 2
TOPK = 2
LANES = 128

ln_eps = 1e-05
in_eps = 1e-05
learn_rate = 0.02
first_decay = 0.5
second_decay = 0.5
adam_eps = 1e-08
weight_decay = 0.1
teacher_keep = 0.5
huber_beta = 1.0
score_scale = 0.125
entry_clip = 1e-05
half_type = jnp.bfloat16
full_type = jnp.float32
AXES = ("dp", "seq")


def contract(left, right, left_dim, right_dim):
    return lax.dot_general(
        left,
        right,
        (((left_dim,), (right_dim,)), ((), ())),
        preferred_element_type=full_type,
    )


def head_mask(which, width):
    lane = lax.broadcasted_iota(jnp.int32, (1, width), 1)
    return (lane // HDIM) == which


def attend_kernel(q_ref, k_ref, v_ref, o_ref):
    queries = q_ref[0] * jnp.asarray(score_scale, half_type)
    keys_all = k_ref[0]
    values_all = v_ref[0]
    width = queries.shape[1]
    mixed = None
    for which in range(width // HDIM):
        mask = head_mask(which, width)
        head_q = jnp.where(mask, queries, jnp.zeros_like(queries))
        scores = contract(head_q, keys_all, 1, 1)
        exps = jnp.exp(scores - jnp.max(scores, axis=1, keepdims=True))
        probs = (exps * (1.0 / jnp.sum(exps, axis=1, keepdims=True))).astype(half_type)
        head_out = contract(probs, values_all, 1, 0)
        mixed = head_out if mixed is None else jnp.where(mask, head_out, mixed)
    o_ref[0] = mixed.astype(half_type)


def attend_back_kernel(q_ref, k_ref, v_ref, do_ref, dq_ref, dk_ref, dv_ref):
    queries = q_ref[0] * jnp.asarray(score_scale, half_type)
    keys_all = k_ref[0]
    values_all = v_ref[0]
    grad_out = do_ref[0]
    width = queries.shape[1]
    grad_k = None
    grad_v = None
    grad_q_rows = []
    for which in range(width // HDIM):
        mask = head_mask(which, width)
        head_q = jnp.where(mask, queries, jnp.zeros_like(queries))
        head_do = jnp.where(mask, grad_out, jnp.zeros_like(grad_out))
        scores = contract(keys_all, head_q, 1, 1)
        exps = jnp.exp(scores - jnp.max(scores, axis=0, keepdims=True))
        probs = exps * (1.0 / jnp.sum(exps, axis=0, keepdims=True))
        grad_probs = contract(values_all, head_do, 1, 1)
        prods = probs * grad_probs
        grad_scores = (prods - probs * jnp.sum(prods, axis=0, keepdims=True)).astype(half_type)
        head_dv = contract(probs.astype(half_type), grad_out, 1, 0)
        head_dk = contract(grad_scores, queries, 1, 0)
        head_dq = contract(keys_all, grad_scores, 0, 0)
        grad_q_rows.append(head_dq[which * HDIM : (which + 1) * HDIM])
        grad_v = head_dv if grad_v is None else jnp.where(mask, head_dv, grad_v)
        grad_k = head_dk if grad_k is None else jnp.where(mask, head_dk, grad_k)
    grad_q = jnp.concatenate(grad_q_rows, axis=0).T * score_scale
    dq_ref[0] = grad_q.astype(half_type)
    dk_ref[0] = grad_k.astype(half_type)
    dv_ref[0] = grad_v.astype(half_type)


def qkv_specs(tokens, blocks):
    return [
        pl.BlockSpec((1, tokens, LANES), lambda s, j, off=off: (s, 0, off * blocks + j))
        for off in range(3)
    ]


def attend(projected):
    seqs, tokens, width3 = projected.shape
    width = width3 // 3
    blocks = width // LANES
    return pl.pallas_call(
        attend_kernel,
        grid=(seqs, blocks),
        in_specs=qkv_specs(tokens, blocks),
        out_specs=pl.BlockSpec((1, tokens, LANES), lambda s, j: (s, 0, j)),
        out_shape=jax.ShapeDtypeStruct((seqs, tokens, width), half_type),
        cost_estimate=pl.CostEstimate(
            flops=16 * seqs * tokens * tokens * width,
            transcendentals=seqs * tokens * tokens * width // HDIM,
            bytes_accessed=8 * seqs * tokens * width,
        ),
        name="attend",
    )(projected, projected, projected)


def attend_back(projected, grad_mixed):
    seqs, tokens, width3 = projected.shape
    width = width3 // 3
    blocks = width // LANES
    block = pl.BlockSpec((1, tokens, LANES), lambda s, j: (s, 0, j))
    shape = jax.ShapeDtypeStruct((seqs, tokens, width), half_type)
    return pl.pallas_call(
        attend_back_kernel,
        grid=(seqs, blocks),
        in_specs=qkv_specs(tokens, blocks) + [block],
        out_specs=[block, block, block],
        out_shape=[shape, shape, shape],
        cost_estimate=pl.CostEstimate(
            flops=32 * seqs * tokens * tokens * width,
            transcendentals=seqs * tokens * tokens * width // HDIM,
            bytes_accessed=14 * seqs * tokens * width,
        ),
        name="attend_back",
    )(projected, projected, projected, grad_mixed)


def normalize(values, gain_vec):
    centre = values - jnp.mean(values, axis=-1, keepdims=True)
    inv_scale = lax.rsqrt(jnp.mean(centre * centre, axis=-1, keepdims=True) + ln_eps)
    normed_unit = centre * inv_scale
    return (normed_unit * gain_vec).astype(half_type), normed_unit, inv_scale


def normalize_back(grad_out, gain_vec, normed_unit, inv_scale):
    grad_unit = grad_out * gain_vec
    inner_mean = jnp.mean(grad_unit, axis=-1, keepdims=True)
    along_mean = jnp.mean(grad_unit * normed_unit, axis=-1, keepdims=True)
    grad_in = (grad_unit - inner_mean - normed_unit * along_mean) * inv_scale
    return grad_in, jnp.sum(grad_out * normed_unit, axis=0)


def normal_cdf(values):
    return 0.5 + 0.5 * lax.erf(values * (0.5**0.5))


def gelu_exact(values):
    return values * normal_cdf(values)


def gelu_slope(values):
    density = jnp.exp(-0.5 * values * values) * (0.5 / jnp.pi) ** 0.5
    return normal_cdf(values) + values * density


class Plan:
    def __init__(self):
        self.seq_size = lax.axis_size("seq")
        self.count = lax.axis_size("dp") * self.seq_size
        self.bits = self.count.bit_length() - 1
        self.early = list(range(self.bits - 1, 2, -1))

        def flips(pick):
            return [(i, i ^ (1 << pick((i >> 1) & 1))) for i in range(self.count)]

        self.stages = [flips(lambda core, b=b: b) for b in self.early]
        self.stages.append(flips(lambda core: 0 if core else 2))
        self.stages.append(flips(lambda core: 2 if core else 0))
        self.core_stage = flips(lambda core: 1)
        self.index = lax.axis_index("dp") * self.seq_size + lax.axis_index("seq")

    def swap(self, value, perm):
        return lax.ppermute(value, AXES, perm)

    def row_table(self, width):
        rows = width // self.count
        place = lax.broadcasted_iota(jnp.int32, (1, width), 1)
        spot = place // rows
        early_count = len(self.early)
        other = (spot >> (self.bits - 1)) & 1
        holder_core = ((self.index >> 1) & 1) ^ other
        block = self.index ^ (other << 1)
        for step, bit in enumerate(self.early):
            block = block ^ (((spot >> step) & 1) << bit)
        first = (spot >> early_count) & 1
        second = (spot >> (early_count + 1)) & 1
        block = block ^ jnp.where(holder_core == 0, first << 2, first)
        block = block ^ jnp.where(holder_core == 0, second, second << 2)
        return block * rows + place % rows

    def mover(self, width):
        table = self.row_table(width)
        whole = lax.broadcasted_iota(jnp.int32, (width, width), 0)
        return (whole == table).astype(half_type)


def to_relative(values, mover):
    return contract(values, mover, 1, 0).astype(half_type)


def to_whole(values, mover):
    return contract(values, mover, 1, 1).astype(half_type)


class Pump:
    def __init__(self, plan):
        self.plan = plan
        self.jobs = []
        self.flying = []

    def add(self, steps, done):
        self.jobs.append([steps, next(steps), done])

    def begin(self):
        self.flying = [
            [self.plan.swap(value, perm) for value, perm in sends] for _, sends, _ in self.jobs
        ]

    def end(self, values=()):
        flying, values = lax.optimization_barrier((self.flying, values))
        left = []
        for (steps, _, done), gots in zip(self.jobs, flying):
            try:
                left.append([steps, steps.send(gots), done])
            except StopIteration as stop:
                done(stop.value)
        self.jobs = left
        self.flying = []
        return values

    def drain(self):
        while self.jobs:
            self.begin()
            self.end()


def gather_steps(plan, parts):
    value = jnp.concatenate(parts, axis=1)
    for perm in plan.stages:
        (got,) = yield [(value, perm)]
        value = jnp.concatenate([value, got], axis=0)
    (got,) = yield [(value, plan.core_stage)]
    outs = []
    start = 0
    for part in parts:
        stop = start + part.shape[1]
        outs.append(jnp.concatenate([value[:, start:stop], got[:, start:stop]], axis=0))
        start = stop
    return outs


def scatter_steps(plan, pieces):
    gots = yield [(far, plan.core_stage) for _, far in pieces]
    quarter = pieces[0][0].shape[0] // 2
    send = jnp.concatenate(
        [
            (near[quarter:] + got[quarter:]).astype(half_type)
            for (near, _), got in zip(pieces, gots)
        ],
        axis=1,
    )
    keep = jnp.concatenate(
        [near[:quarter] + got[:quarter] for (near, _), got in zip(pieces, gots)], axis=1
    )
    stages = plan.stages[::-1]
    for step, perm in enumerate(stages):
        (got,) = yield [(send, perm)]
        got = got.astype(full_type)
        if step == len(stages) - 1:
            return keep + got
        half = keep.shape[0] // 2
        send = keep[half:] + got[half:]
        keep = keep[:half] + got[:half]


def halves(left, right):
    half = left.shape[1] // 2
    return contract(left[:, :half], right, 0, 0), contract(left[:, half:], right, 0, 0)


def row_halves(value):
    half = value.shape[0] // 2
    return value[:half], value[half:]


def attend_forward(flat_in, seqs, w_qkv, w_out, gain):
    tokens = flat_in.shape[0] // seqs
    normed, unit, scale = normalize(flat_in, gain)
    projected = contract(normed, w_qkv, 1, 0).astype(half_type)
    projected = projected.reshape(seqs, tokens, projected.shape[1])
    mixed = attend(projected).reshape(flat_in.shape)
    middle = flat_in + contract(mixed, w_out, 1, 0)
    return middle, (unit, scale, normed, projected, mixed)


def mlp_forward(middle, w_up, w_down, gain):
    normed, unit, scale = normalize(middle, gain)
    hidden_up = contract(normed, w_up, 1, 0)
    active = gelu_exact(hidden_up).astype(half_type)
    out = middle + contract(active, w_down, 1, 1)
    return out, (unit, scale, normed, hidden_up, active)


def adam_step(weight, first_mom, second_mom, teacher, gradient):
    first_new = first_decay * first_mom + (1.0 - first_decay) * gradient
    second_new = second_decay * second_mom + (1.0 - second_decay) * gradient * gradient
    weight_new = weight - learn_rate * (
        first_new / (jnp.sqrt(second_new) + adam_eps) + weight_decay * weight
    )
    teacher_new = teacher_keep * teacher + (1.0 - teacher_keep) * weight_new
    return (weight_new, first_new, second_new, teacher_new)


def pad_lanes(value):
    extra = -value.shape[1] % LANES
    return jnp.pad(value, ((0, 0), (0, extra)))


def local(
    patches,
    masked_at,
    edge_w,
    attn_w,
    mlp_w,
    posit_w,
    vecs_w,
    edge_m,
    attn_m,
    mlp_m,
    posit_m,
    vecs_m,
    edge_v,
    attn_v,
    mlp_v,
    posit_v,
    vecs_v,
    edge_t,
    attn_t,
    mlp_t,
    posit_t,
    vecs_t,
):
    seqs, tokens, width = patches.shape
    plan = Plan()
    total_masked = seqs * plan.count * tokens // 2
    ff_width = mlp_w.shape[1] // (2 * LAYERS)
    small_cols = tokens + vecs_w.shape[1]
    flat_patch = patches.reshape(-1, width)
    mask_flat = masked_at.astype(full_type).reshape(-1, 1)

    def shards(edge, attn, mlp, posit, vecs):
        edge, attn, mlp, posit, vecs = (
            part.astype(half_type) for part in (edge, attn, mlp, posit, vecs)
        )
        small = pad_lanes(jnp.concatenate([posit, vecs], axis=1))
        attn_parts = []
        mlp_parts = []
        for layer in range(LAYERS):
            base = layer * 4 * width
            attn_parts.append(
                [attn[:, base : base + 3 * width], attn[:, base + 3 * width : base + 4 * width]]
            )
            base = layer * 2 * ff_width
            mlp_parts.append(
                [mlp[:, base : base + ff_width], mlp[:, base + ff_width : base + 2 * ff_width]]
            )
        return edge[:, :width], edge[:, width:], small, attn_parts, mlp_parts

    t_patch, _, t_small, t_attn, t_mlp = shards(edge_t, attn_t, mlp_t, posit_t, vecs_t)
    s_patch, s_head, s_small, s_attn, s_mlp = shards(edge_w, attn_w, mlp_w, posit_w, vecs_w)
    chunks = [
        [t_patch, t_small] + t_attn[0],
        t_mlp[0],
        t_attn[1] + t_mlp[1],
        [s_patch, s_small] + s_attn[0],
        s_mlp[0],
        s_attn[1] + [s_head],
        s_mlp[1],
    ]
    mover = plan.mover(width)
    patch_rel = to_relative(flat_patch, mover)

    def both_sides(w_out):
        return contract(mover, to_relative(w_out, mover), 1, 0).astype(half_type)

    def spread(table):
        return jnp.broadcast_to(table[None], (seqs, tokens, width)).reshape(-1, width)

    def small_parts(small):
        vec_table = small[:, tokens:small_cols].astype(full_type).T
        posit = small[:, :tokens].astype(full_type).T
        return vec_table, spread(posit)

    def target_term(state):
        by_seq = state.reshape(seqs, tokens, width)
        centred = by_seq - jnp.mean(by_seq, axis=1, keepdims=True)
        variance = jnp.mean(centred * centred, axis=1, keepdims=True)
        return (centred * lax.rsqrt(variance + in_eps)).reshape(-1, width)

    pump = Pump(plan)
    arrived = []
    saved_attn = [None] * LAYERS
    saved_mlp = [None] * LAYERS
    s_layers = [None] * LAYERS

    def segment_t0(_, chunk):
        patch, small, w_qkv, w_out = chunk
        vec_table, posit = small_parts(small)
        state = contract(patch_rel, to_relative(patch, mover), 1, 0) + posit
        middle, _ = attend_forward(state, seqs, w_qkv, both_sides(w_out), vec_table[0])
        return middle, vec_table

    def segment_t1(values, chunk):
        middle, vec_table = values
        state, _ = mlp_forward(middle, chunk[0], chunk[1], vec_table[LAYERS])
        return state, vec_table

    def segment_t2(values, chunk):
        state, vec_table = values
        w_qkv, w_out, w_up, w_down = chunk
        target = target_term(state)
        middle, _ = attend_forward(state, seqs, w_qkv, both_sides(w_out), vec_table[1])
        state, _ = mlp_forward(middle, w_up, w_down, vec_table[LAYERS + 1])
        return (target + target_term(state)) / TOPK

    def segment_s0(target, chunk):
        patch, small, w_qkv, w_out = chunk
        vec_table, posit = small_parts(small)
        embedded = contract(patch_rel, to_relative(patch, mover), 1, 0)
        current = embedded * (1.0 - mask_flat) + mask_flat * vec_table[2 * LAYERS + 1] + posit
        w_out = both_sides(w_out)
        middle, saved = attend_forward(current, seqs, w_qkv, w_out, vec_table[0])
        return target, middle, vec_table, (w_qkv, w_out), saved

    def segment_s1(values, chunk):
        target, middle, vec_table, weights, saved = values
        saved_attn[0] = (weights, saved)
        current, saved = mlp_forward(middle, chunk[0], chunk[1], vec_table[LAYERS])
        return target, current, vec_table, tuple(chunk), saved

    def segment_s2(values, chunk):
        target, current, vec_table, weights, saved = values
        saved_mlp[0] = (weights, saved)
        w_qkv, w_out, head = chunk
        w_out = both_sides(w_out)
        middle, saved = attend_forward(current, seqs, w_qkv, w_out, vec_table[1])
        saved_attn[1] = ((w_qkv, w_out), saved)
        return target, middle, vec_table, to_relative(head, mover)

    segments = [segment_t0, segment_t1, segment_t2, segment_s0, segment_s1, segment_s2]
    values = ()
    for tick in range(len(chunks) + len(plan.stages)):
        if tick < len(chunks):
            pump.add(gather_steps(plan, chunks[tick]), arrived.append)
        pump.begin()
        place = tick - len(plan.stages) - 1
        if place >= 0:
            values = segments[place](values, arrived[place])
        values = pump.end(values)
    target, middle, s_vecs, head_rel = values
    current, saved = mlp_forward(middle, arrived[-1][0], arrived[-1][1], s_vecs[LAYERS + 1])
    saved_mlp[1] = (tuple(arrived[-1]), saved)

    final_normed, final_unit, final_scale = normalize(current, s_vecs[2 * LAYERS])
    predicted = contract(final_normed, head_rel, 1, 0)
    differ = predicted - target
    magnitude = jnp.abs(differ)
    huber_terms = jnp.where(
        magnitude < huber_beta, 0.5 * differ * differ / huber_beta, magnitude - 0.5 * huber_beta
    )
    loss_local = jnp.sum(huber_terms * mask_flat) / total_masked
    grad_pred = (mask_flat * jnp.clip(differ / huber_beta, -1.0, 1.0) / total_masked).astype(
        half_type
    )
    grad_flow, grad_gain_final = normalize_back(
        contract(grad_pred, head_rel, 1, 1), s_vecs[2 * LAYERS], final_unit, final_scale
    )
    head_piece = halves(final_normed, to_whole(grad_pred, mover))

    gain_ones = [None] * LAYERS
    gain_twos = [None] * LAYERS
    attn_shards = [None] * LAYERS
    mlp_shards = [None] * LAYERS
    extra_pieces = [head_piece]
    for layer in reversed(range(LAYERS)):
        (w_qkv, w_out), (unit_one, scale_one, normed_one, projected, mixed) = saved_attn[layer]
        (w_up, w_down), (unit_two, scale_two, normed_two, hidden_up, active) = saved_mlp[layer]
        pump.begin()
        grad_down = grad_flow.astype(half_type)
        grad_active = contract(grad_down, w_down, 1, 0)
        grad_hidden = (grad_active * gelu_slope(hidden_up)).astype(half_type)
        pieces = [halves(normed_two, grad_hidden), halves(grad_down, active)] + extra_pieces
        grad_flow, grad_hidden, pieces = pump.end((grad_flow, grad_hidden, pieces))
        pump.add(
            scatter_steps(plan, pieces), lambda out, layer=layer: mlp_shards.__setitem__(layer, out)
        )
        extra_pieces = []
        pump.begin()
        grad_norm_two = contract(grad_hidden, w_up, 1, 1)
        grad_middle, gain_twos[layer] = normalize_back(
            grad_norm_two, s_vecs[LAYERS + layer], unit_two, scale_two
        )
        grad_middle = grad_flow + grad_middle
        grad_branch = grad_middle.astype(half_type)
        grad_mixed = contract(grad_branch, w_out, 1, 1).astype(half_type)
        out_piece = halves(to_relative(mixed, mover), to_whole(grad_branch, mover))
        grad_middle, grad_mixed, out_piece = pump.end((grad_middle, grad_mixed, out_piece))
        pump.begin()
        grad_proj = attend_back(
            projected, grad_mixed.reshape(projected.shape[0], projected.shape[1], -1)
        )
        grad_proj = pump.end(tuple(grad_proj))
        pump.begin()
        grad_proj = jnp.concatenate(grad_proj, axis=2).reshape(
            grad_flow.shape[0], projected.shape[2]
        )
        grad_norm_one = contract(grad_proj, w_qkv, 1, 1)
        grad_in, gain_ones[layer] = normalize_back(
            grad_norm_one, s_vecs[layer], unit_one, scale_one
        )
        grad_flow = grad_middle + grad_in
        pieces = [halves(normed_one, grad_proj), out_piece]
        if layer:
            grad_flow, pieces = pump.end((grad_flow, pieces))
            pump.add(
                scatter_steps(plan, pieces),
                lambda out, layer=layer: attn_shards.__setitem__(layer, out),
            )
    grad_maskvec = jnp.sum(grad_flow * mask_flat, axis=0)
    grad_posit = jnp.sum(grad_flow.reshape(seqs, tokens, width), axis=0).T
    grad_embed = to_whole((grad_flow * (1.0 - mask_flat)).astype(half_type), mover)
    patch_piece = halves(patch_rel, grad_embed)
    vec_grads = jnp.stack(gain_ones + gain_twos + [grad_gain_final, grad_maskvec], axis=1)
    small_grads = pad_lanes(jnp.concatenate([grad_posit, vec_grads], axis=1))
    pieces = pump.end(pieces + [patch_piece, row_halves(small_grads)])
    last = []
    pump.add(scatter_steps(plan, pieces), last.append)
    pump.drain()
    attn_shards[0], patch_shard, small_shard = jnp.split(
        last[0], [4 * width, 5 * width], axis=1
    )
    mlp_shards[-1], head_shard = jnp.split(mlp_shards[-1], [2 * ff_width], axis=1)
    raw = (
        jnp.concatenate([patch_shard, head_shard], axis=1),
        jnp.concatenate(attn_shards, axis=1),
        jnp.concatenate(mlp_shards, axis=1),
        small_shard[:, :tokens],
        small_shard[:, tokens:small_cols],
    )
    totals = jnp.stack([loss_local] + [jnp.sum(part * part) for part in raw])
    totals = jnp.broadcast_to(totals[:, None], (totals.shape[0], LANES))
    for perm in [plan.core_stage] + plan.stages:
        totals = totals + plan.swap(totals, perm)
    total_loss = totals[0, 0]
    clipped = []
    for group, part in enumerate(raw):
        limit = entry_clip * jnp.sqrt(jnp.float32(part.size * plan.count))
        norm_value = jnp.sqrt(totals[group + 1, 0])
        clipped.append(part * (limit / jnp.maximum(norm_value, limit)))
    edge_new = adam_step(edge_w, edge_m, edge_v, edge_t, clipped[0])
    attn_new = adam_step(attn_w, attn_m, attn_v, attn_t, clipped[1])
    mlp_new = adam_step(mlp_w, mlp_m, mlp_v, mlp_t, clipped[2])
    posit_new = adam_step(posit_w, posit_m, posit_v, posit_t, clipped[3])
    vecs_new = adam_step(vecs_w, vecs_m, vecs_v, vecs_t, clipped[4])
    news = (edge_new, attn_new, mlp_new, posit_new, vecs_new)
    return (total_loss,) + tuple(group[part] for part in range(4) for group in news)


def solution(mesh):
    rows = P(AXES, None)
    in_specs = (P(AXES, None, None),) + (rows,) * 21
    out_specs = (P(),) + (rows,) * 20
    return jax.shard_map(local, mesh=mesh, in_specs=in_specs, out_specs=out_specs, check_vma=False)
```

```python
import jax
import jax.numpy as jnp
from jax import lax
from jax.experimental import pallas as pl
from jax.experimental.pallas import tpu as pltpu
from jax.sharding import PartitionSpec as P

HDIM = 64
LAYERS = 2
TOPK = 2
LANES = 128
FF_TILE = 512

ln_eps = 1e-05
in_eps = 1e-05
learn_rate = 0.02
first_decay = 0.5
second_decay = 0.5
adam_eps = 1e-08
weight_decay = 0.1
teacher_keep = 0.5
huber_beta = 1.0
score_scale = 0.125
entry_clip = 1e-05
half_type = jnp.bfloat16
full_type = jnp.float32
AXES = ("dp", "seq")


def contract(left, right, left_dim, right_dim):
    return lax.dot_general(
        left,
        right,
        (((left_dim,), (right_dim,)), ((), ())),
        preferred_element_type=full_type,
    )


def head_mask(which, width):
    lane = lax.broadcasted_iota(jnp.int32, (1, width), 1)
    return (lane // HDIM) == which


def attend_kernel(q_ref, k_ref, v_ref, o_ref):
    queries = q_ref[0] * jnp.asarray(score_scale, half_type)
    keys_all = k_ref[0]
    values_all = v_ref[0]
    width = queries.shape[1]
    mixed = None
    for which in range(width // HDIM):
        mask = head_mask(which, width)
        head_q = jnp.where(mask, queries, jnp.zeros_like(queries))
        scores = contract(head_q, keys_all, 1, 1)
        exps = jnp.exp(scores - jnp.max(scores, axis=1, keepdims=True))
        probs = (exps * (1.0 / jnp.sum(exps, axis=1, keepdims=True))).astype(half_type)
        head_out = contract(probs, values_all, 1, 0)
        mixed = head_out if mixed is None else jnp.where(mask, head_out, mixed)
    o_ref[0] = mixed.astype(half_type)


def attend_back_kernel(q_ref, k_ref, v_ref, do_ref, dq_ref, dk_ref, dv_ref):
    queries = q_ref[0] * jnp.asarray(score_scale, half_type)
    keys_all = k_ref[0]
    values_all = v_ref[0]
    grad_out = do_ref[0]
    width = queries.shape[1]
    grad_k = None
    grad_v = None
    grad_q_rows = []
    for which in range(width // HDIM):
        mask = head_mask(which, width)
        head_q = jnp.where(mask, queries, jnp.zeros_like(queries))
        head_do = jnp.where(mask, grad_out, jnp.zeros_like(grad_out))
        scores = contract(keys_all, head_q, 1, 1)
        exps = jnp.exp(scores - jnp.max(scores, axis=0, keepdims=True))
        probs = exps * (1.0 / jnp.sum(exps, axis=0, keepdims=True))
        grad_probs = contract(values_all, head_do, 1, 1)
        prods = probs * grad_probs
        grad_scores = (prods - probs * jnp.sum(prods, axis=0, keepdims=True)).astype(half_type)
        head_dv = contract(probs.astype(half_type), grad_out, 1, 0)
        head_dk = contract(grad_scores, queries, 1, 0)
        head_dq = contract(keys_all, grad_scores, 0, 0)
        grad_q_rows.append(head_dq[which * HDIM : (which + 1) * HDIM])
        grad_v = head_dv if grad_v is None else jnp.where(mask, head_dv, grad_v)
        grad_k = head_dk if grad_k is None else jnp.where(mask, head_dk, grad_k)
    grad_q = jnp.concatenate(grad_q_rows, axis=0).T * score_scale
    dq_ref[0] = grad_q.astype(half_type)
    dk_ref[0] = grad_k.astype(half_type)
    dv_ref[0] = grad_v.astype(half_type)


def qkv_specs(tokens, blocks):
    return [
        pl.BlockSpec((1, tokens, LANES), lambda s, j, off=off: (s, 0, off * blocks + j))
        for off in range(3)
    ]


def attend(projected):
    seqs, tokens, width3 = projected.shape
    width = width3 // 3
    blocks = width // LANES
    return pl.pallas_call(
        attend_kernel,
        grid=(seqs, blocks),
        in_specs=qkv_specs(tokens, blocks),
        out_specs=pl.BlockSpec((1, tokens, LANES), lambda s, j: (s, 0, j)),
        out_shape=jax.ShapeDtypeStruct((seqs, tokens, width), half_type),
        cost_estimate=pl.CostEstimate(
            flops=16 * seqs * tokens * tokens * width,
            transcendentals=seqs * tokens * tokens * width // HDIM,
            bytes_accessed=8 * seqs * tokens * width,
        ),
        name="attend",
    )(projected, projected, projected)


def attend_back(projected, grad_mixed):
    seqs, tokens, width3 = projected.shape
    width = width3 // 3
    blocks = width // LANES
    block = pl.BlockSpec((1, tokens, LANES), lambda s, j: (s, 0, j))
    shape = jax.ShapeDtypeStruct((seqs, tokens, width), half_type)
    return pl.pallas_call(
        attend_back_kernel,
        grid=(seqs, blocks),
        in_specs=qkv_specs(tokens, blocks) + [block],
        out_specs=[block, block, block],
        out_shape=[shape, shape, shape],
        cost_estimate=pl.CostEstimate(
            flops=32 * seqs * tokens * tokens * width,
            transcendentals=seqs * tokens * tokens * width // HDIM,
            bytes_accessed=14 * seqs * tokens * width,
        ),
        name="attend_back",
    )(projected, projected, projected, grad_mixed)


def normal_cdf(values):
    return 0.5 + 0.5 * lax.erf(values * (0.5**0.5))


def whole_block(shape):
    zeros = (0,) * len(shape)
    return pl.BlockSpec(shape, lambda *_: zeros)


def stacked(own_ref, got_ref):
    return jnp.concatenate([own_ref[...], got_ref[...]], axis=0)


def unit_of(values):
    centre = values - jnp.mean(values, axis=1, keepdims=True)
    inv_scale = lax.rsqrt(jnp.mean(centre * centre, axis=1, keepdims=True) + ln_eps)
    return centre * inv_scale, inv_scale


def norm_back(grad_out, gain, values):
    unit, inv_scale = unit_of(values)
    grad_unit = grad_out * gain
    inner_mean = jnp.mean(grad_unit, axis=1, keepdims=True)
    along_mean = jnp.mean(grad_unit * unit, axis=1, keepdims=True)
    grad_in = (grad_unit - inner_mean - unit * along_mean) * inv_scale
    return grad_in, jnp.sum(grad_out * unit, axis=0, keepdims=True)


def half(values):
    return values.astype(half_type)


def shape_of(shape, kind):
    return jax.ShapeDtypeStruct(shape, kind)


def cost(flops, moved):
    return pl.CostEstimate(flops=flops, transcendentals=0, bytes_accessed=moved)


class Weight:
    def __init__(self, own, got, start, cols):
        self.own, self.got, self.start, self.cols = own, got, start, cols

    def specs(self, width, index=lambda j: j):
        base = self.start // width
        spec = pl.BlockSpec(
            (self.own.shape[0], width), lambda j, base=base: (0, base + index(j))
        )
        return [spec, spec]

    def refs(self):
        return [self.own, self.got]


def embed(patches, mask, mover, weight, small, keep_patches):
    rows, width = patches.shape
    tokens = rows // 2
    masked = mask is not None

    def kernel(*refs):
        x_ref, mover_ref, own_ref, got_ref, sown_ref, sgot_ref = refs[:6]
        refs = refs[6:]
        if masked:
            mask_ref, refs = refs[0], refs[1:]
        h_ref, table_ref = refs[:2]
        x_rel = half(contract(x_ref[...], mover_ref[...], 1, 0))
        if keep_patches:
            refs[2][...] = x_rel
        w_rel = half(contract(stacked(own_ref, got_ref), mover_ref[...], 1, 0))
        small_t = stacked(sown_ref, sgot_ref).astype(full_type).T
        posit = small_t[:tokens]
        table = small_t[tokens : tokens + 8]
        table_ref[...] = table
        states = contract(x_rel, w_rel, 1, 0)
        for seq in range(rows // tokens):
            part = slice(seq * tokens, (seq + 1) * tokens)
            state = states[part]
            if masked:
                flag = mask_ref[part, :]
                state = state * (1.0 - flag) + flag * table[2 * LAYERS + 1 : 2 * LAYERS + 2]
            h_ref[part, :] = state + posit

    outs = [shape_of((rows, width), full_type), shape_of((8, width), full_type)]
    if keep_patches:
        outs.append(shape_of((rows, width), half_type))
    args = [patches, mover] + weight.refs() + list(small) + ([mask] if masked else [])
    specs = [whole_block(patches.shape), whole_block(mover.shape)] + weight.specs(width)
    specs += [whole_block(part.shape) for part in small]
    if masked:
        specs.append(whole_block(mask.shape))
    return pl.pallas_call(
        kernel,
        grid=(1,),
        in_specs=specs,
        out_specs=[whole_block(out.shape) for out in outs],
        out_shape=outs,
        cost_estimate=cost(6 * rows * width * width, 12 * rows * width),
        name="embed",
    )(*args)


def norm_project(states, table, row, weight, keep):
    rows, width = states.shape
    steps = weight.cols // width

    def kernel(h_ref, table_ref, own_ref, got_ref, out_ref, a_ref):
        @pl.when(pl.program_id(0) == 0)
        def _():
            unit, _ = unit_of(h_ref[...])
            a_ref[...] = half(unit * table_ref[row : row + 1, :])

        out_ref[...] = half(contract(a_ref[...], stacked(own_ref, got_ref), 1, 0))

    outs = [shape_of((rows, weight.cols), half_type)]
    out_specs = [pl.BlockSpec((rows, width), lambda j: (0, j))]
    scratch = []
    if keep:
        outs.append(shape_of((rows, width), half_type))
        out_specs.append(whole_block((rows, width)))
    else:
        scratch.append(pltpu.VMEM((rows, width), half_type))
    return pl.pallas_call(
        kernel,
        grid=(steps,),
        in_specs=[whole_block(states.shape), whole_block(table.shape)] + weight.specs(width),
        out_specs=out_specs,
        out_shape=outs,
        scratch_shapes=scratch,
        cost_estimate=cost(2 * rows * width * weight.cols, 12 * rows * width),
        name="norm_project",
    )(states, table, *weight.refs())


def mix_out(mixed, states, mover, table, row, weight, keep):
    rows, width = states.shape
    tile = rows // 2

    def kernel(o_ref, h_ref, mover_ref, table_ref, own_ref, got_ref, m_ref, b_ref, *rest):
        if keep:
            rel_ref, w_ref = rest
        else:
            (w_ref,) = rest

        @pl.when(pl.program_id(0) == 0)
        def _():
            w_ref[...] = half(contract(stacked(own_ref, got_ref), mover_ref[...], 1, 0))

        mixed_rel = half(contract(o_ref[...], mover_ref[...], 1, 0))
        if keep:
            rel_ref[...] = mixed_rel
        middle = h_ref[...] + contract(mixed_rel, w_ref[...], 1, 0)
        m_ref[...] = middle
        unit, _ = unit_of(middle)
        b_ref[...] = half(unit * table_ref[row : row + 1, :])

    part = pl.BlockSpec((tile, width), lambda j: (j, 0))
    outs = [shape_of((rows, width), full_type), shape_of((rows, width), half_type)]
    out_specs = [part, part]
    scratch = []
    if keep:
        outs += [shape_of((rows, width), half_type), shape_of((width, width), half_type)]
        out_specs += [part, whole_block((width, width))]
    else:
        scratch.append(pltpu.VMEM((width, width), half_type))
    return pl.pallas_call(
        kernel,
        grid=(2,),
        in_specs=[part, part, whole_block(mover.shape), whole_block(table.shape)]
        + weight.specs(width, lambda j: 0),
        out_specs=out_specs,
        out_shape=outs,
        scratch_shapes=scratch,
        cost_estimate=cost(6 * rows * width * width, 14 * rows * width),
        name="mix_out",
    )(mixed, states, mover, table, *weight.refs())


def feed_forward(normed, middle, w_up, w_down, keep):
    rows, width = middle.shape
    tile = FF_TILE
    steps = w_up.cols // tile

    def kernel(b_ref, m_ref, uown_ref, ugot_ref, down_ref, dgot_ref, out_ref, *rest):
        step = pl.program_id(0)
        hidden = contract(b_ref[...], stacked(uown_ref, ugot_ref), 1, 0)
        cdf = normal_cdf(hidden)
        active = half(hidden * cdf)
        if keep:
            rest[0][...] = active
            rest[1][...] = cdf + hidden * (
                jnp.exp(-0.5 * hidden * hidden) * ((0.5 / jnp.pi) ** 0.5)
            )
        part = contract(active, stacked(down_ref, dgot_ref), 1, 1)

        @pl.when(step == 0)
        def _():
            out_ref[...] = m_ref[...] + part

        @pl.when(step > 0)
        def _():
            out_ref[...] += part

    outs = [shape_of((rows, width), full_type)]
    out_specs = [whole_block((rows, width))]
    if keep:
        outs += [shape_of((rows, w_up.cols), half_type), shape_of((rows, w_up.cols), full_type)]
        out_specs += [pl.BlockSpec((rows, tile), lambda j: (0, j))] * 2
    return pl.pallas_call(
        kernel,
        grid=(steps,),
        in_specs=[whole_block(normed.shape), whole_block(middle.shape)]
        + w_up.specs(tile)
        + w_down.specs(tile),
        out_specs=out_specs,
        out_shape=outs,
        cost_estimate=cost(4 * rows * width * w_up.cols, 12 * rows * width + 16 * width * w_up.cols),
        name="feed_forward",
    )(normed, middle, *w_up.refs(), *w_down.refs())


def make_target(first, second, seqs):
    rows, width = first.shape
    tokens = rows // seqs
    cols = width // 2

    def kernel(one_ref, two_ref, out_ref):
        total = None
        for ref in (one_ref, two_ref):
            values = ref[...]
            centre = values - jnp.mean(values, axis=0, keepdims=True)
            variance = jnp.mean(centre * centre, axis=0, keepdims=True)
            term = centre * lax.rsqrt(variance + in_eps)
            total = term if total is None else total + term
        out_ref[...] = total * (1.0 / TOPK)

    block = pl.BlockSpec((tokens, cols), lambda s, j: (s, j))
    return pl.pallas_call(
        kernel,
        grid=(seqs, 2),
        in_specs=[block, block],
        out_specs=block,
        out_shape=shape_of((rows, width), full_type),
        cost_estimate=cost(20 * rows * width, 12 * rows * width),
        name="make_target",
    )(first, second)


def head_step(states, table, mover, weight, target, mask, total_masked):
    rows, width = states.shape
    tile = rows // 2
    final_row = 2 * LAYERS

    def kernel(
        h_ref, table_ref, mover_ref, own_ref, got_ref, t_ref, mask_ref,
        flow_ref, f_ref, pred_ref, gain_ref, loss_ref, w_ref,
    ):
        step = pl.program_id(0)

        @pl.when(step == 0)
        def _():
            w_ref[...] = half(contract(stacked(own_ref, got_ref), mover_ref[...], 1, 0))
            gain_ref[...] = jnp.zeros_like(gain_ref)
            loss_ref[...] = jnp.zeros_like(loss_ref)

        states_now = h_ref[...]
        gain = table_ref[final_row : final_row + 1, :]
        unit, _ = unit_of(states_now)
        final_normed = half(unit * gain)
        f_ref[...] = final_normed
        flag = mask_ref[...]
        differ = contract(final_normed, w_ref[...], 1, 0) - t_ref[...]
        magnitude = jnp.abs(differ)
        terms = jnp.where(
            magnitude < huber_beta,
            0.5 * differ * differ / huber_beta,
            magnitude - 0.5 * huber_beta,
        )
        loss_ref[...] += jnp.sum(terms * flag, axis=0, keepdims=True)
        grad_pred = half(flag * jnp.clip(differ / huber_beta, -1.0, 1.0) / total_masked)
        pred_ref[...] = half(contract(grad_pred, mover_ref[...], 1, 1))
        grad_in, grad_gain = norm_back(contract(grad_pred, w_ref[...], 1, 1), gain, states_now)
        flow_ref[...] = grad_in
        gain_ref[...] += grad_gain

    part = pl.BlockSpec((tile, width), lambda j: (j, 0))
    row = whole_block((1, width))
    return pl.pallas_call(
        kernel,
        grid=(2,),
        in_specs=[part, whole_block(table.shape), whole_block(mover.shape)]
        + weight.specs(width, lambda j: 0)
        + [part, pl.BlockSpec((tile, 1), lambda j: (j, 0))],
        out_specs=[part, part, part, row, row],
        out_shape=[
            shape_of((rows, width), full_type),
            shape_of((rows, width), half_type),
            shape_of((rows, width), half_type),
            shape_of((1, width), full_type),
            shape_of((1, width), full_type),
        ],
        scratch_shapes=[pltpu.VMEM((width, width), half_type)],
        cost_estimate=cost(8 * rows * width * width, 16 * rows * width),
        name="head_step",
    )(states, table, mover, *weight.refs(), target, mask)


def feed_back(flow, slope, middle, table, row, w_up, w_down):
    rows, width = flow.shape
    tile = FF_TILE
    steps = w_up.cols // tile

    def kernel(
        flow_ref, slope_ref, m_ref, table_ref, uown_ref, ugot_ref, down_ref, dgot_ref,
        du_ref, dy_ref, dm_ref, dz_ref, gain_ref, acc_ref,
    ):
        step = pl.program_id(0)

        @pl.when(step == 0)
        def _():
            dy_ref[...] = half(flow_ref[...])

        grad_active = contract(dy_ref[...], stacked(down_ref, dgot_ref), 1, 0)
        grad_hidden = half(grad_active * slope_ref[...])
        du_ref[...] = grad_hidden
        part = contract(grad_hidden, stacked(uown_ref, ugot_ref), 1, 1)

        @pl.when(step == 0)
        def _():
            acc_ref[...] = part

        @pl.when(step > 0)
        def _():
            acc_ref[...] += part

        @pl.when(step == steps - 1)
        def _():
            grad_in, grad_gain = norm_back(
                acc_ref[...], table_ref[row : row + 1, :], m_ref[...]
            )
            grad_middle = flow_ref[...] + grad_in
            dm_ref[...] = grad_middle
            dz_ref[...] = half(grad_middle)
            gain_ref[...] = grad_gain

    full = whole_block((rows, width))
    column = pl.BlockSpec((rows, tile), lambda j: (0, j))
    return pl.pallas_call(
        kernel,
        grid=(steps,),
        in_specs=[full, column, full, whole_block(table.shape)]
        + w_up.specs(tile)
        + w_down.specs(tile),
        out_specs=[column, full, full, full, whole_block((1, width))],
        out_shape=[
            shape_of((rows, w_up.cols), half_type),
            shape_of((rows, width), half_type),
            shape_of((rows, width), full_type),
            shape_of((rows, width), half_type),
            shape_of((1, width), full_type),
        ],
        scratch_shapes=[pltpu.VMEM((rows, width), full_type)],
        cost_estimate=cost(4 * rows * width * w_up.cols, 40 * rows * width + 8 * width * w_up.cols),
        name="feed_back",
    )(flow, slope, middle, table, *w_up.refs(), *w_down.refs())


def mix_back(grad_branch, w_rel, mover):
    rows, width = grad_branch.shape
    tile = rows // 2

    def kernel(dz_ref, w_ref, mover_ref, do_ref, nat_ref):
        branch = dz_ref[...]
        grad_rel = half(contract(branch, w_ref[...], 1, 1))
        do_ref[...] = half(contract(grad_rel, mover_ref[...], 1, 1))
        nat_ref[...] = half(contract(branch, mover_ref[...], 1, 1))

    part = pl.BlockSpec((tile, width), lambda j: (j, 0))
    square = whole_block((width, width))
    return pl.pallas_call(
        kernel,
        grid=(2,),
        in_specs=[part, square, square],
        out_specs=[part, part],
        out_shape=[shape_of((rows, width), half_type)] * 2,
        cost_estimate=cost(6 * rows * width * width, 10 * rows * width),
        name="mix_back",
    )(grad_branch, w_rel, mover)


def project_back(grads, grad_middle, states, table, row, weight, mover, mask):
    rows, width = states.shape
    tile = rows // 2
    count = len(grads)
    first = mask is not None

    def kernel(*refs):
        grad_refs, refs = refs[:count], refs[count:]
        w_refs, refs = refs[: 2 * count], refs[2 * count :]
        dm_ref, h_ref, table_ref = refs[:3]
        refs = refs[3:]
        if first:
            mover_ref, mask_ref = refs[:2]
            refs = refs[2:]
        dh_ref, gain_ref = refs[:2]
        step = pl.program_id(0)

        @pl.when(step == 0)
        def _():
            for ref in (gain_ref,) + ((refs[3],) if first else ()):
                ref[...] = jnp.zeros_like(ref)

        total = None
        for place in range(count):
            part = contract(
                grad_refs[place][...], stacked(w_refs[2 * place], w_refs[2 * place + 1]), 1, 1
            )
            total = part if total is None else total + part
        grad_in, grad_gain = norm_back(total, table_ref[row : row + 1, :], h_ref[...])
        flow = dm_ref[...] + grad_in
        dh_ref[...] = flow
        gain_ref[...] += grad_gain
        if first:
            flag = mask_ref[...]
            refs[2][...] = half(contract(half(flow * (1.0 - flag)), mover_ref[...], 1, 1))
            refs[3][...] += jnp.sum(flow * flag, axis=0, keepdims=True)

    part = pl.BlockSpec((tile, width), lambda j: (j, 0))
    vector = whole_block((1, width))
    specs = [part] * count
    args = list(grads)
    for place in range(count):
        specs += weight.specs(width, lambda j, place=place: place)
        args += weight.refs()
    specs += [part, part, whole_block(table.shape)]
    args += [grad_middle, states, table]
    outs = [shape_of((rows, width), full_type), shape_of((1, width), full_type)]
    out_specs = [part, vector]
    if first:
        specs += [whole_block(mover.shape), pl.BlockSpec((tile, 1), lambda j: (j, 0))]
        args += [mover, mask]
        outs += [shape_of((rows, width), half_type), shape_of((1, width), full_type)]
        out_specs += [part, vector]
    return pl.pallas_call(
        kernel,
        grid=(2,),
        in_specs=specs,
        out_specs=out_specs,
        out_shape=outs,
        cost_estimate=cost(2 * rows * width * weight.cols, 22 * rows * width),
        name="project_back",
    )(*args)


def weight_grads(pairs):
    rows, width = pairs[0][0].shape
    plan = []
    start = 0
    for place, (_, rights) in enumerate(pairs):
        first = start
        for right in rights:
            tiles = right.shape[1] // width
            plan.append((place, start, tiles, start == first))
            start += tiles
    total = start
    near_rows = width // 2

    def kernel(*refs):
        left_refs, refs = refs[: len(pairs)], refs[len(pairs) :]
        right_refs, refs = refs[: len(plan)], refs[len(plan) :]
        near_ref, far_ref, turned_ref = refs
        step = pl.program_id(0)
        for (place, begin, tiles, fresh), right_ref in zip(plan, right_refs):
            if fresh:

                @pl.when(step == begin)
                def _(place=place):
                    turned_ref[...] = left_refs[place][...].T

            @pl.when((step >= begin) & (step < begin + tiles))
            def _(right_ref=right_ref):
                out = contract(turned_ref[...], right_ref[...], 1, 0)
                near_ref[...] = out[:near_rows]
                far_ref[...] = out[near_rows:]

    specs = [whole_block((rows, width)) for _ in pairs]
    args = [left for left, _ in pairs]
    for (_, rights) in pairs:
        args += list(rights)
    for _, begin, tiles, _ in plan:
        specs.append(
            pl.BlockSpec(
                (rows, width),
                lambda j, begin=begin, tiles=tiles: (0, jnp.clip(j - begin, 0, tiles - 1)),
            )
        )
    block = pl.BlockSpec((near_rows, width), lambda j: (0, j))
    shape = shape_of((near_rows, total * width), full_type)
    return tuple(
        pl.pallas_call(
            kernel,
            grid=(total,),
            in_specs=specs,
            out_specs=[block, block],
            out_shape=[shape, shape],
            scratch_shapes=[pltpu.VMEM((width, rows), half_type)],
            cost_estimate=cost(
                2 * rows * width * width * total, width * total * (4 * width + 2 * rows)
            ),
            name="weight_grads",
        )(*args)
    )


def small_grads(flow, vectors, seqs):
    rows, width = flow.shape
    tokens = rows // seqs
    cols = tokens + 8
    cols += -cols % LANES

    def kernel(flow_ref, *refs):
        vector_refs, (near_ref, far_ref) = refs[:-2], refs[-2:]
        posit = flow_ref[:tokens]
        for seq in range(1, seqs):
            posit = posit + flow_ref[seq * tokens : (seq + 1) * tokens]
        fill = jnp.zeros((cols - tokens - len(vector_refs), width), full_type)
        table = jnp.concatenate([posit] + [ref[...] for ref in vector_refs] + [fill], axis=0).T
        near_ref[...] = table[: width // 2]
        far_ref[...] = table[width // 2 :]

    shape = shape_of((width // 2, cols), full_type)
    return tuple(
        pl.pallas_call(
            kernel,
            grid=(1,),
            in_specs=[whole_block(flow.shape)] + [whole_block((1, width)) for _ in vectors],
            out_specs=[whole_block(shape.shape)] * 2,
            out_shape=[shape, shape],
            cost_estimate=cost(2 * rows * width, 8 * rows * width),
            name="small_grads",
        )(flow, *vectors)
    )


class Plan:
    def __init__(self):
        self.seq_size = lax.axis_size("seq")
        self.count = lax.axis_size("dp") * self.seq_size
        self.bits = self.count.bit_length() - 1
        self.early = list(range(self.bits - 1, 2, -1))

        def flips(pick):
            return [(i, i ^ (1 << pick((i >> 1) & 1))) for i in range(self.count)]

        self.stages = [flips(lambda core, b=b: b) for b in self.early]
        self.stages.append(flips(lambda core: 0 if core else 2))
        self.stages.append(flips(lambda core: 2 if core else 0))
        self.core_stage = flips(lambda core: 1)
        self.index = lax.axis_index("dp") * self.seq_size + lax.axis_index("seq")

    def swap(self, value, perm):
        return lax.ppermute(value, AXES, perm)

    def row_table(self, width):
        rows = width // self.count
        place = lax.broadcasted_iota(jnp.int32, (1, width), 1)
        spot = place // rows
        early_count = len(self.early)
        other = (spot >> (self.bits - 1)) & 1
        holder_core = ((self.index >> 1) & 1) ^ other
        block = self.index ^ (other << 1)
        for step, bit in enumerate(self.early):
            block = block ^ (((spot >> step) & 1) << bit)
        first = (spot >> early_count) & 1
        second = (spot >> (early_count + 1)) & 1
        block = block ^ jnp.where(holder_core == 0, first << 2, first)
        block = block ^ jnp.where(holder_core == 0, second, second << 2)
        return block * rows + place % rows

    def mover(self, width):
        table = self.row_table(width)
        whole = lax.broadcasted_iota(jnp.int32, (width, width), 0)
        return (whole == table).astype(half_type)


class Pump:
    def __init__(self, plan):
        self.plan = plan
        self.jobs = []
        self.flying = []

    def add(self, steps, done):
        self.jobs.append([steps, next(steps), done])

    def begin(self):
        self.flying = [
            [self.plan.swap(value, perm) for value, perm in sends] for _, sends, _ in self.jobs
        ]

    def end(self, values=()):
        flying, values = lax.optimization_barrier((self.flying, values))
        left = []
        for (steps, _, done), gots in zip(self.jobs, flying):
            try:
                left.append([steps, steps.send(gots), done])
            except StopIteration as stop:
                done(stop.value)
        self.jobs = left
        self.flying = []
        return values

    def drain(self):
        while self.jobs:
            self.begin()
            self.end()


def gather_steps(plan, value):
    for perm in plan.stages:
        (got,) = yield [(value, perm)]
        value = jnp.concatenate([value, got], axis=0)
    return value


def scatter_steps(plan, pieces):
    gots = yield [(far, plan.core_stage) for _, far in pieces]
    quarter = pieces[0][0].shape[0] // 2
    sums = [
        (half(near[quarter:] + got[quarter:]), near[:quarter] + got[:quarter])
        for (near, _), got in zip(pieces, gots)
    ]
    send = jnp.concatenate([part for part, _ in sums], axis=1)
    keep = jnp.concatenate([part for _, part in sums], axis=1)
    stages = plan.stages[::-1]
    for step, perm in enumerate(stages):
        (got,) = yield [(send, perm)]
        got = got.astype(full_type)
        if step == len(stages) - 1:
            return keep + got
        middle = keep.shape[0] // 2
        send = keep[middle:] + got[middle:]
        keep = keep[:middle] + got[:middle]


def adam_step(weight, first_mom, second_mom, teacher, gradient):
    first_new = first_decay * first_mom + (1.0 - first_decay) * gradient
    second_new = second_decay * second_mom + (1.0 - second_decay) * gradient * gradient
    weight_new = weight - learn_rate * (
        first_new / (jnp.sqrt(second_new) + adam_eps) + weight_decay * weight
    )
    teacher_new = teacher_keep * teacher + (1.0 - teacher_keep) * weight_new
    return (weight_new, first_new, second_new, teacher_new)


def pad_lanes(value):
    extra = -value.shape[1] % LANES
    return jnp.pad(value, ((0, 0), (0, extra)))


def local(
    patches,
    masked_at,
    edge_w,
    attn_w,
    mlp_w,
    posit_w,
    vecs_w,
    edge_m,
    attn_m,
    mlp_m,
    posit_m,
    vecs_m,
    edge_v,
    attn_v,
    mlp_v,
    posit_v,
    vecs_v,
    edge_t,
    attn_t,
    mlp_t,
    posit_t,
    vecs_t,
):
    seqs, tokens, width = patches.shape
    plan = Plan()
    total_masked = seqs * plan.count * tokens // 2
    ff_width = mlp_w.shape[1] // (2 * LAYERS)
    small_cols = tokens + vecs_w.shape[1]
    flat_patch = patches.reshape(-1, width)
    mask_flat = masked_at.astype(full_type).reshape(-1, 1)
    mover = plan.mover(width)

    def shards(edge, attn, mlp, posit, vecs):
        small = pad_lanes(jnp.concatenate([posit, vecs], axis=1))
        return [edge[:, :width], edge[:, width:], small] + [
            [
                part[:, layer * part.shape[1] // LAYERS : (layer + 1) * part.shape[1] // LAYERS]
                for part in (attn, mlp)
            ]
            for layer in range(LAYERS)
        ]

    def joined(parts):
        return jnp.concatenate([half(part) for part in parts], axis=1)

    t_patch, _, t_small, t_one, t_two = shards(edge_t, attn_t, mlp_t, posit_t, vecs_t)
    s_patch, s_head, s_small, s_one, s_two = shards(edge_w, attn_w, mlp_w, posit_w, vecs_w)
    waiting = [
        joined([t_patch, t_one[0], t_small]),
        joined([t_one[1]]),
        joined(t_two),
        joined([s_patch, s_one[0], s_small]),
        joined([s_one[1]]),
        joined([s_two[0], s_head]),
        joined([s_two[1]]),
    ]

    def attn_weights(own, got, start):
        return Weight(own, got, start, 3 * width), Weight(own, got, start + 3 * width, width)

    def mlp_weights(own, got, start):
        return Weight(own, got, start, ff_width), Weight(own, got, start + ff_width, ff_width)

    def small_of(own, got):
        start = own.shape[1] - t_small.shape[1]
        return own[:, start:], got[:, start:]

    def attend_forward(states, table, layer, w_qkv, w_out, keep):
        outs = norm_project(states, table, layer, w_qkv, keep)
        projected = outs[0].reshape(seqs, tokens, w_qkv.cols)
        mixed = attend(projected).reshape(-1, width)
        results = mix_out(mixed, states, mover, table, LAYERS + layer, w_out, keep)
        if keep:
            return results[0], results[1], (states, outs[1], projected) + tuple(results[2:])
        return results[0], results[1], ()

    saved_attn = [None] * LAYERS
    saved_mlp = [None] * LAYERS

    def segment_t0(_, own, got):
        patch = Weight(own, got, 0, width)
        states, table, patch_rel = embed(
            flat_patch, None, mover, patch, small_of(own, got), True
        )
        middle, normed, _ = attend_forward(
            states, table, 0, *attn_weights(own, got, width), False
        )
        return middle, normed, table, patch_rel

    def segment_t1(values, own, got):
        middle, normed, table, patch_rel = values
        (states,) = feed_forward(normed, middle, *mlp_weights(own, got, 0), False)
        return states, table, patch_rel

    def segment_t2(values, own, got):
        first, table, patch_rel = values
        middle, normed, _ = attend_forward(first, table, 1, *attn_weights(own, got, 0), False)
        (second,) = feed_forward(normed, middle, *mlp_weights(own, got, 4 * width), False)
        return make_target(first, second, seqs), patch_rel

    def segment_s0(values, own, got):
        target, patch_rel = values
        patch = Weight(own, got, 0, width)
        states, table = embed(flat_patch, mask_flat, mover, patch, small_of(own, got), False)
        weights = attn_weights(own, got, width)
        middle, normed, saved = attend_forward(states, table, 0, *weights, True)
        saved_attn[0] = (weights[0], saved)
        return target, patch_rel, table, middle, normed

    def segment_s1(values, own, got):
        target, patch_rel, table, middle, normed = values
        weights = mlp_weights(own, got, 0)
        states, active, slope = feed_forward(normed, middle, *weights, True)
        saved_mlp[0] = (weights, middle, normed, active, slope)
        return target, patch_rel, table, states

    def segment_s2(values, own, got):
        target, patch_rel, table, states = values
        weights = attn_weights(own, got, 0)
        middle, normed, saved = attend_forward(states, table, 1, *weights, True)
        saved_attn[1] = (weights[0], saved)
        return target, patch_rel, table, middle, normed, own, got

    segments = [segment_t0, segment_t1, segment_t2, segment_s0, segment_s1, segment_s2]
    pump = Pump(plan)
    arrived = []
    values = ()
    total_chunks = len(waiting)
    for tick in range(total_chunks + len(plan.stages)):
        if waiting:
            pump.add(gather_steps(plan, waiting[0]), arrived.append)
            waiting = waiting[1:]
        pump.begin()
        place = tick - len(plan.stages)
        if 0 <= place < len(segments):
            own = arrived[place]
            values = segments[place](values, own, plan.swap(own, plan.core_stage))
        values, waiting = pump.end((values, waiting))
    target, patch_rel, table, middle, normed, head_own, head_got = values
    own = arrived[-1]
    weights = mlp_weights(own, plan.swap(own, plan.core_stage), 0)
    states, active, slope = feed_forward(normed, middle, *weights, True)
    saved_mlp[1] = (weights, middle, normed, active, slope)
    flow, final_normed, grad_pred, grad_gain_final, loss_row = head_step(
        states,
        table,
        mover,
        Weight(head_own, head_got, 4 * width, width),
        target,
        mask_flat,
        total_masked,
    )
    loss_local = jnp.sum(loss_row) / total_masked

    gain_ones = [None] * LAYERS
    gain_twos = [None] * LAYERS
    attn_shards = [None] * LAYERS
    mlp_shards = [None] * LAYERS
    extra_pairs = [(final_normed, [grad_pred])]
    for layer in reversed(range(LAYERS)):
        w_qkv, (states, normed_one, projected, mixed_rel, w_out_rel) = saved_attn[layer]
        (w_up, w_down), middle, normed_two, active, slope = saved_mlp[layer]
        grad_hidden, grad_down, grad_middle, grad_branch, gain_twos[layer] = feed_back(
            flow, slope, middle, table, LAYERS + layer, w_up, w_down
        )
        piece = weight_grads([(normed_two, [grad_hidden]), (grad_down, [active])])
        piece, grad_middle, grad_branch = pump.end((piece, grad_middle, grad_branch))
        pump.add(
            scatter_steps(plan, [piece]),
            lambda out, layer=layer: mlp_shards.__setitem__(layer, out),
        )
        pump.begin()
        grad_mixed, branch_whole = mix_back(grad_branch, w_out_rel, mover)
        grad_proj = attend_back(projected, grad_mixed.reshape(seqs, tokens, width))
        grad_proj, branch_whole = pump.end((tuple(grad_proj), branch_whole))
        grad_proj = [part.reshape(-1, width) for part in grad_proj]
        pump.begin()
        results = project_back(
            grad_proj,
            grad_middle,
            states,
            table,
            layer,
            w_qkv,
            mover,
            None if layer else mask_flat,
        )
        flow, gain_ones[layer] = results[:2]
        if layer == 0:
            grad_embed, grad_maskvec = results[2:]
            extra_pairs = [(patch_rel, [grad_embed])]
        pieces = [
            weight_grads([(normed_one, grad_proj), (mixed_rel, [branch_whole])] + extra_pairs)
        ]
        if layer == 0:
            vectors = gain_ones + gain_twos + [grad_gain_final, grad_maskvec]
            pieces.append(small_grads(flow, vectors, seqs))
        pieces, flow = pump.end((pieces, flow))
        pump.add(
            scatter_steps(plan, pieces),
            lambda out, layer=layer: attn_shards.__setitem__(layer, out),
        )
        if layer:
            pump.begin()
    pump.drain()
    last, first = attn_shards
    raw = (
        jnp.concatenate([last[:, 4 * width : 5 * width], first[:, 4 * width :]], axis=1),
        jnp.concatenate([last[:, : 4 * width], first[:, : 4 * width]], axis=1),
        jnp.concatenate(mlp_shards, axis=1),
        last[:, 5 * width : 5 * width + tokens],
        last[:, 5 * width + tokens : 5 * width + small_cols],
    )
    totals = jnp.stack([loss_local] + [jnp.sum(part * part) for part in raw])
    totals = jnp.broadcast_to(totals[:, None], (totals.shape[0], LANES))
    for perm in [plan.core_stage] + plan.stages:
        totals = totals + plan.swap(totals, perm)
    total_loss = totals[0, 0]
    clipped = []
    for group, part in enumerate(raw):
        limit = entry_clip * jnp.sqrt(jnp.float32(part.size * plan.count))
        norm_value = jnp.sqrt(totals[group + 1, 0])
        clipped.append(part * (limit / jnp.maximum(norm_value, limit)))
    edge_new = adam_step(edge_w, edge_m, edge_v, edge_t, clipped[0])
    attn_new = adam_step(attn_w, attn_m, attn_v, attn_t, clipped[1])
    mlp_new = adam_step(mlp_w, mlp_m, mlp_v, mlp_t, clipped[2])
    posit_new = adam_step(posit_w, posit_m, posit_v, posit_t, clipped[3])
    vecs_new = adam_step(vecs_w, vecs_m, vecs_v, vecs_t, clipped[4])
    news = (edge_new, attn_new, mlp_new, posit_new, vecs_new)
    return (total_loss,) + tuple(group[part] for part in range(4) for group in news)


def solution(mesh):
    rows = P(AXES, None)
    in_specs = (P(AXES, None, None),) + (rows,) * 21
    out_specs = (P(),) + (rows,) * 20
    return jax.shard_map(local, mesh=mesh, in_specs=in_specs, out_specs=out_specs, check_vma=False)
```

```python
import jax
import jax.numpy as jnp
from jax import lax
from jax.experimental import pallas as pl
from jax.experimental.pallas import tpu as pltpu
from jax.sharding import PartitionSpec as P

HDIM = 64
LAYERS = 2
TOPK = 2
LANES = 128
FF_TILE = 512
NARROW_STAGES = 1

ln_eps = 1e-05
in_eps = 1e-05
learn_rate = 0.02
first_decay = 0.5
second_decay = 0.5
adam_eps = 1e-08
weight_decay = 0.1
teacher_keep = 0.5
huber_beta = 1.0
score_scale = 0.125
entry_clip = 1e-05
half_type = jnp.bfloat16
full_type = jnp.float32
AXES = ("dp", "seq")


def contract(left, right, left_dim, right_dim):
    return lax.dot_general(
        left,
        right,
        (((left_dim,), (right_dim,)), ((), ())),
        preferred_element_type=full_type,
    )


def head_mask(which, width):
    lane = lax.broadcasted_iota(jnp.int32, (1, width), 1)
    return (lane // HDIM) == which


def attend_kernel(q_ref, k_ref, v_ref, o_ref):
    queries = q_ref[0] * jnp.asarray(score_scale, half_type)
    keys_all = k_ref[0]
    values_all = v_ref[0]
    width = queries.shape[1]
    mixed = None
    for which in range(width // HDIM):
        mask = head_mask(which, width)
        head_q = jnp.where(mask, queries, jnp.zeros_like(queries))
        scores = contract(head_q, keys_all, 1, 1)
        exps = jnp.exp(scores - jnp.max(scores, axis=1, keepdims=True))
        probs = (exps * (1.0 / jnp.sum(exps, axis=1, keepdims=True))).astype(half_type)
        head_out = contract(probs, values_all, 1, 0)
        mixed = head_out if mixed is None else jnp.where(mask, head_out, mixed)
    o_ref[0] = mixed.astype(half_type)


def attend_back_kernel(q_ref, k_ref, v_ref, do_ref, dq_ref, dk_ref, dv_ref):
    queries = q_ref[0] * jnp.asarray(score_scale, half_type)
    keys_all = k_ref[0]
    values_all = v_ref[0]
    grad_out = do_ref[0]
    width = queries.shape[1]
    grad_k = None
    grad_v = None
    grad_q_rows = []
    for which in range(width // HDIM):
        mask = head_mask(which, width)
        head_q = jnp.where(mask, queries, jnp.zeros_like(queries))
        head_do = jnp.where(mask, grad_out, jnp.zeros_like(grad_out))
        scores = contract(keys_all, head_q, 1, 1)
        exps = jnp.exp(scores - jnp.max(scores, axis=0, keepdims=True))
        probs = exps * (1.0 / jnp.sum(exps, axis=0, keepdims=True))
        grad_probs = contract(values_all, head_do, 1, 1)
        prods = probs * grad_probs
        grad_scores = (prods - probs * jnp.sum(prods, axis=0, keepdims=True)).astype(half_type)
        head_dv = contract(probs.astype(half_type), grad_out, 1, 0)
        head_dk = contract(grad_scores, queries, 1, 0)
        head_dq = contract(keys_all, grad_scores, 0, 0)
        grad_q_rows.append(head_dq[which * HDIM : (which + 1) * HDIM])
        grad_v = head_dv if grad_v is None else jnp.where(mask, head_dv, grad_v)
        grad_k = head_dk if grad_k is None else jnp.where(mask, head_dk, grad_k)
    grad_q = jnp.concatenate(grad_q_rows, axis=0).T * score_scale
    dq_ref[0] = grad_q.astype(half_type)
    dk_ref[0] = grad_k.astype(half_type)
    dv_ref[0] = grad_v.astype(half_type)


def qkv_specs(tokens, blocks):
    return [
        pl.BlockSpec((1, tokens, LANES), lambda s, j, off=off: (s, 0, off * blocks + j))
        for off in range(3)
    ]


def attend(projected):
    seqs, tokens, width3 = projected.shape
    width = width3 // 3
    blocks = width // LANES
    return pl.pallas_call(
        attend_kernel,
        grid=(seqs, blocks),
        in_specs=qkv_specs(tokens, blocks),
        out_specs=pl.BlockSpec((1, tokens, LANES), lambda s, j: (s, 0, j)),
        out_shape=jax.ShapeDtypeStruct((seqs, tokens, width), half_type),
        cost_estimate=pl.CostEstimate(
            flops=16 * seqs * tokens * tokens * width,
            transcendentals=seqs * tokens * tokens * width // HDIM,
            bytes_accessed=8 * seqs * tokens * width,
        ),
        compiler_params=grant(8),
        name="attend",
    )(projected, projected, projected)


def attend_back(projected, grad_mixed):
    seqs, tokens, width3 = projected.shape
    width = width3 // 3
    blocks = width // LANES
    block = pl.BlockSpec((1, tokens, LANES), lambda s, j: (s, 0, j))
    shape = jax.ShapeDtypeStruct((seqs, tokens, width), half_type)
    return pl.pallas_call(
        attend_back_kernel,
        grid=(seqs, blocks),
        in_specs=qkv_specs(tokens, blocks) + [block],
        out_specs=[block, block, block],
        out_shape=[shape, shape, shape],
        cost_estimate=pl.CostEstimate(
            flops=32 * seqs * tokens * tokens * width,
            transcendentals=seqs * tokens * tokens * width // HDIM,
            bytes_accessed=14 * seqs * tokens * width,
        ),
        compiler_params=grant(12),
        name="attend_back",
    )(projected, projected, projected, grad_mixed)


def normal_cdf(values):
    return 0.5 + 0.5 * lax.erf(values * (0.5**0.5))


def whole_block(shape):
    zeros = (0,) * len(shape)
    return pl.BlockSpec(shape, lambda *_: zeros, pipeline_mode=pl.Buffered(1))


def grant(mib):
    return pltpu.CompilerParams(vmem_limit_bytes=mib << 20)


def stacked(*refs):
    return jnp.concatenate([ref[...] for ref in refs], axis=0)


def unit_of(values):
    centre = values - jnp.mean(values, axis=1, keepdims=True)
    inv_scale = lax.rsqrt(jnp.mean(centre * centre, axis=1, keepdims=True) + ln_eps)
    return centre * inv_scale, inv_scale


def norm_back(grad_out, gain, values):
    unit, inv_scale = unit_of(values)
    grad_unit = grad_out * gain
    inner_mean = jnp.mean(grad_unit, axis=1, keepdims=True)
    along_mean = jnp.mean(grad_unit * unit, axis=1, keepdims=True)
    grad_in = (grad_unit - inner_mean - unit * along_mean) * inv_scale
    return grad_in, jnp.sum(grad_out * unit, axis=0, keepdims=True)


def half(values):
    return values.astype(half_type)


def shape_of(shape, kind):
    return jax.ShapeDtypeStruct(shape, kind)


def cost(flops, moved):
    return pl.CostEstimate(flops=flops, transcendentals=0, bytes_accessed=moved)


class Weight:
    def __init__(self, blocks, start, cols):
        self.blocks, self.start, self.cols = list(blocks), start, cols

    def specs(self, width, index=lambda j: j):
        base = self.start // width
        spec = pl.BlockSpec(
            (self.blocks[0].shape[0], width), lambda j, base=base: (0, base + index(j))
        )
        return [spec] * len(self.blocks)

    def refs(self):
        return self.blocks


def embed(patches, mask, mover, weight, small, keep_patches):
    rows, width = patches.shape
    tokens = rows // 2
    masked = mask is not None

    def kernel(*refs):
        x_ref, mover_ref = refs[:2]
        w_refs, small_refs, refs = refs[2:6], refs[6:10], refs[10:]
        if masked:
            mask_ref, refs = refs[0], refs[1:]
        h_ref, table_ref = refs[:2]
        x_rel = half(contract(x_ref[...], mover_ref[...], 1, 0))
        if keep_patches:
            refs[2][...] = x_rel
        w_rel = half(contract(stacked(*w_refs), mover_ref[...], 1, 0))
        small_t = stacked(*small_refs).astype(full_type).T
        posit = small_t[:tokens]
        table = small_t[tokens : tokens + 8]
        table_ref[...] = table
        states = contract(x_rel, w_rel, 1, 0)
        for seq in range(rows // tokens):
            part = slice(seq * tokens, (seq + 1) * tokens)
            state = states[part]
            if masked:
                flag = mask_ref[part, :]
                state = state * (1.0 - flag) + flag * table[2 * LAYERS + 1 : 2 * LAYERS + 2]
            h_ref[part, :] = state + posit

    outs = [shape_of((rows, width), full_type), shape_of((8, width), full_type)]
    if keep_patches:
        outs.append(shape_of((rows, width), half_type))
    args = [patches, mover] + weight.refs() + list(small) + ([mask] if masked else [])
    specs = [whole_block(patches.shape), whole_block(mover.shape)] + weight.specs(width)
    specs += [whole_block(part.shape) for part in small]
    if masked:
        specs.append(whole_block(mask.shape))
    return pl.pallas_call(
        kernel,
        grid=(1,),
        in_specs=specs,
        out_specs=[whole_block(out.shape) for out in outs],
        out_shape=outs,
        cost_estimate=cost(6 * rows * width * width, 12 * rows * width),
        compiler_params=grant(28),
        name="embed",
    )(*args)


def norm_project(states, table, row, weight, keep):
    rows, width = states.shape
    steps = weight.cols // width

    def kernel(h_ref, table_ref, own_ref, own2_ref, got_ref, got2_ref, out_ref, a_ref):
        @pl.when(pl.program_id(0) == 0)
        def _():
            unit, _ = unit_of(h_ref[...])
            a_ref[...] = half(unit * table_ref[row : row + 1, :])

        out_ref[...] = half(contract(a_ref[...], stacked(own_ref, own2_ref, got_ref, got2_ref), 1, 0))

    outs = [shape_of((rows, weight.cols), half_type)]
    out_specs = [pl.BlockSpec((rows, width), lambda j: (0, j))]
    scratch = []
    if keep:
        outs.append(shape_of((rows, width), half_type))
        out_specs.append(whole_block((rows, width)))
    else:
        scratch.append(pltpu.VMEM((rows, width), half_type))
    return pl.pallas_call(
        kernel,
        grid=(steps,),
        in_specs=[whole_block(states.shape), whole_block(table.shape)] + weight.specs(width),
        out_specs=out_specs,
        out_shape=outs,
        scratch_shapes=scratch,
        cost_estimate=cost(2 * rows * width * weight.cols, 12 * rows * width),
        compiler_params=grant(24),
        name="norm_project",
    )(states, table, *weight.refs())


def mix_out(mixed, states, mover, table, row, weight, keep):
    rows, width = states.shape
    tile = rows // 2

    def kernel(o_ref, h_ref, mover_ref, table_ref, own_ref, own2_ref, got_ref, got2_ref, m_ref, b_ref, *rest):
        if keep:
            rel_ref, w_ref = rest
        else:
            (w_ref,) = rest

        @pl.when(pl.program_id(0) == 0)
        def _():
            w_ref[...] = half(contract(stacked(own_ref, own2_ref, got_ref, got2_ref), mover_ref[...], 1, 0))

        mixed_rel = half(contract(o_ref[...], mover_ref[...], 1, 0))
        if keep:
            rel_ref[...] = mixed_rel
        middle = h_ref[...] + contract(mixed_rel, w_ref[...], 1, 0)
        m_ref[...] = middle
        unit, _ = unit_of(middle)
        b_ref[...] = half(unit * table_ref[row : row + 1, :])

    part = pl.BlockSpec((tile, width), lambda j: (j, 0))
    outs = [shape_of((rows, width), full_type), shape_of((rows, width), half_type)]
    out_specs = [part, part]
    scratch = []
    if keep:
        outs += [shape_of((rows, width), half_type), shape_of((width, width), half_type)]
        out_specs += [part, whole_block((width, width))]
    else:
        scratch.append(pltpu.VMEM((width, width), half_type))
    return pl.pallas_call(
        kernel,
        grid=(2,),
        in_specs=[part, part, whole_block(mover.shape), whole_block(table.shape)]
        + weight.specs(width, lambda j: 0),
        out_specs=out_specs,
        out_shape=outs,
        scratch_shapes=scratch,
        cost_estimate=cost(6 * rows * width * width, 14 * rows * width),
        compiler_params=grant(24),
        name="mix_out",
    )(mixed, states, mover, table, *weight.refs())


def feed_forward(normed, middle, w_up, w_down, keep):
    rows, width = middle.shape
    tile = FF_TILE
    steps = w_up.cols // tile

    def kernel(b_ref, m_ref, uown_ref, uown2_ref, ugot_ref, ugot2_ref, down_ref, down2_ref, dgot_ref, dgot2_ref, out_ref, *rest):
        step = pl.program_id(0)
        hidden = contract(b_ref[...], stacked(uown_ref, uown2_ref, ugot_ref, ugot2_ref), 1, 0)
        cdf = normal_cdf(hidden)
        active = half(hidden * cdf)
        if keep:
            rest[0][...] = active
            rest[1][...] = cdf + hidden * (
                jnp.exp(-0.5 * hidden * hidden) * ((0.5 / jnp.pi) ** 0.5)
            )
        part = contract(active, stacked(down_ref, down2_ref, dgot_ref, dgot2_ref), 1, 1)

        @pl.when(step == 0)
        def _():
            out_ref[...] = m_ref[...] + part

        @pl.when(step > 0)
        def _():
            out_ref[...] += part

    outs = [shape_of((rows, width), full_type)]
    out_specs = [whole_block((rows, width))]
    if keep:
        outs += [shape_of((rows, w_up.cols), half_type), shape_of((rows, w_up.cols), full_type)]
        out_specs += [pl.BlockSpec((rows, tile), lambda j: (0, j))] * 2
    return pl.pallas_call(
        kernel,
        grid=(steps,),
        in_specs=[whole_block(normed.shape), whole_block(middle.shape)]
        + w_up.specs(tile)
        + w_down.specs(tile),
        out_specs=out_specs,
        out_shape=outs,
        cost_estimate=cost(4 * rows * width * w_up.cols, 12 * rows * width + 16 * width * w_up.cols),
        compiler_params=grant(30),
        name="feed_forward",
    )(normed, middle, *w_up.refs(), *w_down.refs())


def make_target(first, second, seqs):
    rows, width = first.shape
    tokens = rows // seqs
    cols = width // 2

    def kernel(one_ref, two_ref, out_ref):
        total = None
        for ref in (one_ref, two_ref):
            values = ref[...]
            centre = values - jnp.mean(values, axis=0, keepdims=True)
            variance = jnp.mean(centre * centre, axis=0, keepdims=True)
            term = centre * lax.rsqrt(variance + in_eps)
            total = term if total is None else total + term
        out_ref[...] = total * (1.0 / TOPK)

    block = pl.BlockSpec((tokens, cols), lambda s, j: (s, j))
    return pl.pallas_call(
        kernel,
        grid=(seqs, 2),
        in_specs=[block, block],
        out_specs=block,
        out_shape=shape_of((rows, width), full_type),
        cost_estimate=cost(20 * rows * width, 12 * rows * width),
        compiler_params=grant(16),
        name="make_target",
    )(first, second)


def head_step(states, table, mover, weight, target, mask, total_masked):
    rows, width = states.shape
    tile = rows // 2
    final_row = 2 * LAYERS

    def kernel(
        h_ref, table_ref, mover_ref, own_ref, own2_ref, got_ref, got2_ref, t_ref, mask_ref,
        flow_ref, f_ref, pred_ref, gain_ref, loss_ref, w_ref,
    ):
        step = pl.program_id(0)

        @pl.when(step == 0)
        def _():
            w_ref[...] = half(contract(stacked(own_ref, own2_ref, got_ref, got2_ref), mover_ref[...], 1, 0))
            gain_ref[...] = jnp.zeros_like(gain_ref)
            loss_ref[...] = jnp.zeros_like(loss_ref)

        states_now = h_ref[...]
        gain = table_ref[final_row : final_row + 1, :]
        unit, _ = unit_of(states_now)
        final_normed = half(unit * gain)
        f_ref[...] = final_normed
        flag = mask_ref[...]
        differ = contract(final_normed, w_ref[...], 1, 0) - t_ref[...]
        magnitude = jnp.abs(differ)
        terms = jnp.where(
            magnitude < huber_beta,
            0.5 * differ * differ / huber_beta,
            magnitude - 0.5 * huber_beta,
        )
        loss_ref[...] += jnp.sum(terms * flag, axis=0, keepdims=True)
        grad_pred = half(flag * jnp.clip(differ / huber_beta, -1.0, 1.0) / total_masked)
        pred_ref[...] = half(contract(grad_pred, mover_ref[...], 1, 1))
        grad_in, grad_gain = norm_back(contract(grad_pred, w_ref[...], 1, 1), gain, states_now)
        flow_ref[...] = grad_in
        gain_ref[...] += grad_gain

    part = pl.BlockSpec((tile, width), lambda j: (j, 0))
    row = whole_block((1, width))
    return pl.pallas_call(
        kernel,
        grid=(2,),
        in_specs=[part, whole_block(table.shape), whole_block(mover.shape)]
        + weight.specs(width, lambda j: 0)
        + [part, pl.BlockSpec((tile, 1), lambda j: (j, 0))],
        out_specs=[part, part, part, row, row],
        out_shape=[
            shape_of((rows, width), full_type),
            shape_of((rows, width), half_type),
            shape_of((rows, width), half_type),
            shape_of((1, width), full_type),
            shape_of((1, width), full_type),
        ],
        scratch_shapes=[pltpu.VMEM((width, width), half_type)],
        cost_estimate=cost(8 * rows * width * width, 16 * rows * width),
        compiler_params=grant(30),
        name="head_step",
    )(states, table, mover, *weight.refs(), target, mask)


def feed_back(flow, slope, middle, table, row, w_up, w_down):
    rows, width = flow.shape
    tile = FF_TILE
    steps = w_up.cols // tile

    def kernel(
        flow_ref, slope_ref, m_ref, table_ref, uown_ref, uown2_ref, ugot_ref, ugot2_ref, down_ref, down2_ref, dgot_ref, dgot2_ref,
        du_ref, dy_ref, dm_ref, dz_ref, gain_ref, acc_ref,
    ):
        step = pl.program_id(0)

        @pl.when(step == 0)
        def _():
            dy_ref[...] = half(flow_ref[...])

        grad_active = contract(dy_ref[...], stacked(down_ref, down2_ref, dgot_ref, dgot2_ref), 1, 0)
        grad_hidden = half(grad_active * slope_ref[...])
        du_ref[...] = grad_hidden
        part = contract(grad_hidden, stacked(uown_ref, uown2_ref, ugot_ref, ugot2_ref), 1, 1)

        @pl.when(step == 0)
        def _():
            acc_ref[...] = part

        @pl.when(step > 0)
        def _():
            acc_ref[...] += part

        @pl.when(step == steps - 1)
        def _():
            grad_in, grad_gain = norm_back(
                acc_ref[...], table_ref[row : row + 1, :], m_ref[...]
            )
            grad_middle = flow_ref[...] + grad_in
            dm_ref[...] = grad_middle
            dz_ref[...] = half(grad_middle)
            gain_ref[...] = grad_gain

    full = whole_block((rows, width))
    column = pl.BlockSpec((rows, tile), lambda j: (0, j))
    return pl.pallas_call(
        kernel,
        grid=(steps,),
        in_specs=[full, column, full, whole_block(table.shape)]
        + w_up.specs(tile)
        + w_down.specs(tile),
        out_specs=[column, full, full, full, whole_block((1, width))],
        out_shape=[
            shape_of((rows, w_up.cols), half_type),
            shape_of((rows, width), half_type),
            shape_of((rows, width), full_type),
            shape_of((rows, width), half_type),
            shape_of((1, width), full_type),
        ],
        scratch_shapes=[pltpu.VMEM((rows, width), full_type)],
        cost_estimate=cost(4 * rows * width * w_up.cols, 40 * rows * width + 8 * width * w_up.cols),
        compiler_params=grant(32),
        name="feed_back",
    )(flow, slope, middle, table, *w_up.refs(), *w_down.refs())


def mix_back(grad_branch, w_rel, mover):
    rows, width = grad_branch.shape
    tile = rows // 2

    def kernel(dz_ref, w_ref, mover_ref, do_ref, nat_ref):
        branch = dz_ref[...]
        grad_rel = half(contract(branch, w_ref[...], 1, 1))
        do_ref[...] = half(contract(grad_rel, mover_ref[...], 1, 1))
        nat_ref[...] = half(contract(branch, mover_ref[...], 1, 1))

    part = pl.BlockSpec((tile, width), lambda j: (j, 0))
    square = whole_block((width, width))
    return pl.pallas_call(
        kernel,
        grid=(2,),
        in_specs=[part, square, square],
        out_specs=[part, part],
        out_shape=[shape_of((rows, width), half_type)] * 2,
        cost_estimate=cost(6 * rows * width * width, 10 * rows * width),
        compiler_params=grant(16),
        name="mix_back",
    )(grad_branch, w_rel, mover)


def project_back(grads, grad_middle, states, table, row, weight, mover, mask):
    rows, width = states.shape
    tile = rows // 2
    count = len(grads)
    first = mask is not None

    def kernel(*refs):
        grad_refs, refs = refs[:count], refs[count:]
        w_refs, refs = refs[: 4 * count], refs[4 * count :]
        dm_ref, h_ref, table_ref = refs[:3]
        refs = refs[3:]
        if first:
            mover_ref, mask_ref = refs[:2]
            refs = refs[2:]
        dh_ref, gain_ref = refs[:2]
        step = pl.program_id(0)

        @pl.when(step == 0)
        def _():
            for ref in (gain_ref,) + ((refs[3],) if first else ()):
                ref[...] = jnp.zeros_like(ref)

        total = None
        for place in range(count):
            part = contract(
                grad_refs[place][...], stacked(*w_refs[4 * place : 4 * place + 4]), 1, 1
            )
            total = part if total is None else total + part
        grad_in, grad_gain = norm_back(total, table_ref[row : row + 1, :], h_ref[...])
        flow = dm_ref[...] + grad_in
        dh_ref[...] = flow
        gain_ref[...] += grad_gain
        if first:
            flag = mask_ref[...]
            refs[2][...] = half(contract(half(flow * (1.0 - flag)), mover_ref[...], 1, 1))
            refs[3][...] += jnp.sum(flow * flag, axis=0, keepdims=True)

    part = pl.BlockSpec((tile, width), lambda j: (j, 0))
    vector = whole_block((1, width))
    specs = [part] * count
    args = list(grads)
    for place in range(count):
        specs += weight.specs(width, lambda j, place=place: place)
        args += weight.refs()
    specs += [part, part, whole_block(table.shape)]
    args += [grad_middle, states, table]
    outs = [shape_of((rows, width), full_type), shape_of((1, width), full_type)]
    out_specs = [part, vector]
    if first:
        specs += [whole_block(mover.shape), pl.BlockSpec((tile, 1), lambda j: (j, 0))]
        args += [mover, mask]
        outs += [shape_of((rows, width), half_type), shape_of((1, width), full_type)]
        out_specs += [part, vector]
    return pl.pallas_call(
        kernel,
        grid=(2,),
        in_specs=specs,
        out_specs=out_specs,
        out_shape=outs,
        cost_estimate=cost(2 * rows * width * weight.cols, 22 * rows * width),
        compiler_params=grant(30),
        name="project_back",
    )(*args)


def weight_grads(pairs):
    rows, width = pairs[0][0].shape
    plan = []
    start = 0
    for place, (_, rights) in enumerate(pairs):
        first = start
        for right in rights:
            tiles = right.shape[1] // width
            plan.append((place, start, tiles, start == first))
            start += tiles
    total = start
    near_rows = width // 2

    def kernel(*refs):
        left_refs, refs = refs[: len(pairs)], refs[len(pairs) :]
        right_refs, refs = refs[: len(plan)], refs[len(plan) :]
        near_ref, far_ref, turned_ref = refs
        step = pl.program_id(0)
        for (place, begin, tiles, fresh), right_ref in zip(plan, right_refs):
            if fresh:

                @pl.when(step == begin)
                def _(place=place):
                    turned_ref[...] = left_refs[place][...].T

            @pl.when((step >= begin) & (step < begin + tiles))
            def _(right_ref=right_ref):
                out = contract(turned_ref[...], right_ref[...], 1, 0)
                near_ref[...] = out[:near_rows]
                far_ref[...] = half(out[near_rows:])

    specs = [whole_block((rows, width)) for _ in pairs]
    args = [left for left, _ in pairs]
    for (_, rights) in pairs:
        args += list(rights)
    for _, begin, tiles, _ in plan:
        specs.append(
            pl.BlockSpec(
                (rows, width),
                lambda j, begin=begin, tiles=tiles: (0, jnp.clip(j - begin, 0, tiles - 1)),
            )
        )
    block = pl.BlockSpec((near_rows, width), lambda j: (0, j))
    shapes = [shape_of((near_rows, total * width), kind) for kind in (full_type, half_type)]
    return tuple(
        pl.pallas_call(
            kernel,
            grid=(total,),
            in_specs=specs,
            out_specs=[block, block],
            out_shape=shapes,
            scratch_shapes=[pltpu.VMEM((width, rows), half_type)],
            cost_estimate=cost(
                2 * rows * width * width * total, width * total * (4 * width + 2 * rows)
            ),
            compiler_params=grant(30),
        name="weight_grads",
        )(*args)
    )


def small_grads(flow, vectors, seqs):
    rows, width = flow.shape
    tokens = rows // seqs
    cols = tokens + 8
    cols += -cols % LANES

    def kernel(flow_ref, *refs):
        vector_refs, (near_ref, far_ref) = refs[:-2], refs[-2:]
        posit = flow_ref[:tokens]
        for seq in range(1, seqs):
            posit = posit + flow_ref[seq * tokens : (seq + 1) * tokens]
        fill = jnp.zeros((cols - tokens - len(vector_refs), width), full_type)
        table = jnp.concatenate([posit] + [ref[...] for ref in vector_refs] + [fill], axis=0).T
        near_ref[...] = table[: width // 2]
        far_ref[...] = half(table[width // 2 :])

    shapes = [shape_of((width // 2, cols), kind) for kind in (full_type, half_type)]
    return tuple(
        pl.pallas_call(
            kernel,
            grid=(1,),
            in_specs=[whole_block(flow.shape)] + [whole_block((1, width)) for _ in vectors],
            out_specs=[whole_block(shape.shape) for shape in shapes],
            out_shape=shapes,
            cost_estimate=cost(2 * rows * width, 8 * rows * width),
            compiler_params=grant(16),
        name="small_grads",
        )(flow, *vectors)
    )


class Plan:
    def __init__(self):
        self.seq_size = lax.axis_size("seq")
        self.count = lax.axis_size("dp") * self.seq_size
        self.bits = self.count.bit_length() - 1
        self.early = list(range(self.bits - 1, 2, -1))

        def flips(pick):
            return [(i, i ^ (1 << pick((i >> 1) & 1))) for i in range(self.count)]

        self.stages = [flips(lambda core, b=b: b) for b in self.early]
        self.stages.append(flips(lambda core: 0 if core else 2))
        self.stages.append(flips(lambda core: 2 if core else 0))
        self.core_stage = flips(lambda core: 1)
        self.index = lax.axis_index("dp") * self.seq_size + lax.axis_index("seq")

    def swap(self, value, perm):
        return lax.ppermute(value, AXES, perm)

    def row_table(self, width):
        rows = width // self.count
        place = lax.broadcasted_iota(jnp.int32, (1, width), 1)
        spot = place // rows
        early_count = len(self.early)
        other = (spot >> (self.bits - 1)) & 1
        holder_core = ((self.index >> 1) & 1) ^ other
        block = self.index ^ (other << 1)
        for step, bit in enumerate(self.early):
            block = block ^ (((spot >> step) & 1) << bit)
        first = (spot >> early_count) & 1
        second = (spot >> (early_count + 1)) & 1
        block = block ^ jnp.where(holder_core == 0, first << 2, first)
        block = block ^ jnp.where(holder_core == 0, second, second << 2)
        return block * rows + place % rows

    def mover(self, width):
        table = self.row_table(width)
        whole = lax.broadcasted_iota(jnp.int32, (width, width), 0)
        return (whole == table).astype(half_type)


class Pump:
    def __init__(self, plan):
        self.plan = plan
        self.jobs = []
        self.flying = []

    def add(self, steps, done):
        self.jobs.append([steps, next(steps), done])

    def begin(self):
        self.flying = [
            [self.plan.swap(value, perm) for value, perm in sends] for _, sends, _ in self.jobs
        ]

    def end(self, values=()):
        flying, values = lax.optimization_barrier((self.flying, values))
        left = []
        for (steps, _, done), gots in zip(self.jobs, flying):
            try:
                left.append([steps, steps.send(gots), done])
            except StopIteration as stop:
                done(stop.value)
        self.jobs = left
        self.flying = []
        return values

    def drain(self):
        while self.jobs:
            self.begin()
            self.end()


def gather_steps(plan, value):
    for perm in plan.stages[:-1]:
        (got,) = yield [(value, perm)]
        value = jnp.concatenate([value, got], axis=0)
    (got,) = yield [(value, plan.stages[-1])]
    return value, got


def scatter_steps(plan, pieces):
    gots = yield [(far, plan.core_stage) for _, far in pieces]
    quarter = pieces[0][0].shape[0] // 2
    sums = [
        (half(near[quarter:] + got[quarter:]), near[:quarter] + got[:quarter])
        for (near, _), got in zip(pieces, gots)
    ]
    send = jnp.concatenate([part for part, _ in sums], axis=1)
    keep = jnp.concatenate([part for _, part in sums], axis=1)
    stages = plan.stages[::-1]
    for step, perm in enumerate(stages):
        (got,) = yield [(send, perm)]
        if step == len(stages) - 1:
            return keep + got
        middle = keep.shape[0] // 2
        send = keep[middle:] + got[middle:]
        if step < NARROW_STAGES:
            send = half(send)
        keep = keep[:middle] + got[:middle]


def adam_step(weight, first_mom, second_mom, teacher, gradient):
    first_new = first_decay * first_mom + (1.0 - first_decay) * gradient
    second_new = second_decay * second_mom + (1.0 - second_decay) * gradient * gradient
    weight_new = weight - learn_rate * (
        first_new / (jnp.sqrt(second_new) + adam_eps) + weight_decay * weight
    )
    teacher_new = teacher_keep * teacher + (1.0 - teacher_keep) * weight_new
    return (weight_new, first_new, second_new, teacher_new)


def pad_lanes(value):
    extra = -value.shape[1] % LANES
    return jnp.pad(value, ((0, 0), (0, extra)))


def local(
    patches,
    masked_at,
    edge_w,
    attn_w,
    mlp_w,
    posit_w,
    vecs_w,
    edge_m,
    attn_m,
    mlp_m,
    posit_m,
    vecs_m,
    edge_v,
    attn_v,
    mlp_v,
    posit_v,
    vecs_v,
    edge_t,
    attn_t,
    mlp_t,
    posit_t,
    vecs_t,
):
    seqs, tokens, width = patches.shape
    plan = Plan()
    total_masked = seqs * plan.count * tokens // 2
    ff_width = mlp_w.shape[1] // (2 * LAYERS)
    small_cols = tokens + vecs_w.shape[1]
    flat_patch = patches.reshape(-1, width)
    mask_flat = masked_at.astype(full_type).reshape(-1, 1)
    mover = plan.mover(width)

    def shards(edge, attn, mlp, posit, vecs):
        small = pad_lanes(jnp.concatenate([posit, vecs], axis=1))
        return [edge[:, :width], edge[:, width:], small] + [
            [
                part[:, layer * part.shape[1] // LAYERS : (layer + 1) * part.shape[1] // LAYERS]
                for part in (attn, mlp)
            ]
            for layer in range(LAYERS)
        ]

    def joined(parts):
        return jnp.concatenate([half(part) for part in parts], axis=1)

    t_patch, _, t_small, t_one, t_two = shards(edge_t, attn_t, mlp_t, posit_t, vecs_t)
    s_patch, s_head, s_small, s_one, s_two = shards(edge_w, attn_w, mlp_w, posit_w, vecs_w)
    waiting = [
        joined([t_patch, t_one[0], t_small]),
        joined([t_one[1]]),
        joined(t_two),
        joined([s_patch, s_one[0], s_small]),
        joined([s_one[1]]),
        joined([s_two[0], s_head]),
        joined([s_two[1]]),
    ]

    def attn_weights(blocks, start):
        return Weight(blocks, start, 3 * width), Weight(blocks, start + 3 * width, width)

    def mlp_weights(blocks, start):
        return Weight(blocks, start, ff_width), Weight(blocks, start + ff_width, ff_width)

    def small_of(blocks):
        start = blocks[0].shape[1] - t_small.shape[1]
        return [block[:, start:] for block in blocks]

    def with_sibling(blocks):
        return list(blocks) + [plan.swap(block, plan.core_stage) for block in blocks]

    def attend_forward(states, table, layer, w_qkv, w_out, keep):
        outs = norm_project(states, table, layer, w_qkv, keep)
        projected = outs[0].reshape(seqs, tokens, w_qkv.cols)
        mixed = attend(projected).reshape(-1, width)
        results = mix_out(mixed, states, mover, table, LAYERS + layer, w_out, keep)
        if keep:
            return results[0], results[1], (states, outs[1], projected) + tuple(results[2:])
        return results[0], results[1], ()

    saved_attn = [None] * LAYERS
    saved_mlp = [None] * LAYERS

    def segment_t0(_, blocks):
        patch = Weight(blocks, 0, width)
        states, table, patch_rel = embed(
            flat_patch, None, mover, patch, small_of(blocks), True
        )
        middle, normed, _ = attend_forward(
            states, table, 0, *attn_weights(blocks, width), False
        )
        return middle, normed, table, patch_rel

    def segment_t1(values, blocks):
        middle, normed, table, patch_rel = values
        (states,) = feed_forward(normed, middle, *mlp_weights(blocks, 0), False)
        return states, table, patch_rel

    def segment_t2(values, blocks):
        first, table, patch_rel = values
        middle, normed, _ = attend_forward(first, table, 1, *attn_weights(blocks, 0), False)
        (second,) = feed_forward(normed, middle, *mlp_weights(blocks, 4 * width), False)
        return make_target(first, second, seqs), patch_rel

    def segment_s0(values, blocks):
        target, patch_rel = values
        patch = Weight(blocks, 0, width)
        states, table = embed(flat_patch, mask_flat, mover, patch, small_of(blocks), False)
        weights = attn_weights(blocks, width)
        middle, normed, saved = attend_forward(states, table, 0, *weights, True)
        saved_attn[0] = (weights[0], saved)
        return target, patch_rel, table, middle, normed

    def segment_s1(values, blocks):
        target, patch_rel, table, middle, normed = values
        weights = mlp_weights(blocks, 0)
        states, active, slope = feed_forward(normed, middle, *weights, True)
        saved_mlp[0] = (weights, middle, normed, active, slope)
        return target, patch_rel, table, states

    def segment_s2(values, blocks):
        target, patch_rel, table, states = values
        weights = attn_weights(blocks, 0)
        middle, normed, saved = attend_forward(states, table, 1, *weights, True)
        saved_attn[1] = (weights[0], saved)
        return target, patch_rel, table, middle, normed, blocks

    segments = [segment_t0, segment_t1, segment_t2, segment_s0, segment_s1, segment_s2]
    pump = Pump(plan)
    arrived = []
    values = ()
    total_chunks = len(waiting)
    for tick in range(total_chunks + len(plan.stages)):
        if waiting:
            pump.add(gather_steps(plan, waiting[0]), arrived.append)
            waiting = waiting[1:]
        pump.begin()
        place = tick - len(plan.stages)
        if 0 <= place < len(segments):
            values = segments[place](values, with_sibling(arrived[place]))
        values, waiting = pump.end((values, waiting))
    target, patch_rel, table, middle, normed, head_blocks = values
    weights = mlp_weights(with_sibling(arrived[-1]), 0)
    states, active, slope = feed_forward(normed, middle, *weights, True)
    saved_mlp[1] = (weights, middle, normed, active, slope)
    flow, final_normed, grad_pred, grad_gain_final, loss_row = head_step(
        states,
        table,
        mover,
        Weight(head_blocks, 4 * width, width),
        target,
        mask_flat,
        total_masked,
    )
    loss_local = jnp.sum(loss_row) / total_masked

    gain_ones = [None] * LAYERS
    gain_twos = [None] * LAYERS
    qkv_shards = [None] * LAYERS
    other_shards = [None] * LAYERS
    extra_pairs = [(final_normed, [grad_pred])]
    for layer in reversed(range(LAYERS)):
        w_qkv, (states, normed_one, projected, mixed_rel, w_out_rel) = saved_attn[layer]
        (w_up, w_down), middle, normed_two, active, slope = saved_mlp[layer]
        grad_hidden, grad_down, grad_middle, grad_branch, gain_twos[layer] = feed_back(
            flow, slope, middle, table, LAYERS + layer, w_up, w_down
        )
        if layer < LAYERS - 1:
            grad_hidden, grad_down, grad_middle, grad_branch, pieces = pump.end(
                (grad_hidden, grad_down, grad_middle, grad_branch, pieces)
            )
            pump.add(
                scatter_steps(plan, pieces),
                lambda out, layer=layer: qkv_shards.__setitem__(layer + 1, out),
            )
            pump.begin()
        grad_mixed, branch_whole = mix_back(grad_branch, w_out_rel, mover)
        piece = weight_grads(
            [
                (normed_two, [grad_hidden]),
                (grad_down, [active]),
                (mixed_rel, [branch_whole]),
            ]
            + extra_pairs
        )
        extra_pairs = []
        piece, grad_middle, grad_mixed = pump.end((piece, grad_middle, grad_mixed))
        pump.add(
            scatter_steps(plan, [piece]),
            lambda out, layer=layer: other_shards.__setitem__(layer, out),
        )
        pump.begin()
        grad_proj = attend_back(projected, grad_mixed.reshape(seqs, tokens, width))
        grad_proj = pump.end(tuple(grad_proj))
        grad_proj = [part.reshape(-1, width) for part in grad_proj]
        pump.begin()
        results = project_back(
            grad_proj,
            grad_middle,
            states,
            table,
            layer,
            w_qkv,
            mover,
            None if layer else mask_flat,
        )
        flow, gain_ones[layer] = results[:2]
        if layer == 0:
            grad_embed, grad_maskvec = results[2:]
            extra_pairs = [(patch_rel, [grad_embed])]
        pieces = [weight_grads([(normed_one, grad_proj)] + extra_pairs)]
        extra_pairs = []
    vectors = gain_ones + gain_twos + [grad_gain_final, grad_maskvec]
    pieces.append(small_grads(flow, vectors, seqs))
    pieces = pump.end(pieces)
    pump.add(scatter_steps(plan, pieces), lambda out: qkv_shards.__setitem__(0, out))
    pump.drain()
    last, qkv_one = qkv_shards
    other_zero, other_one = other_shards
    start = 2 * ff_width
    stop = start + width
    raw = (
        jnp.concatenate([last[:, 3 * width : 4 * width], other_one[:, stop:]], axis=1),
        jnp.concatenate(
            [last[:, : 3 * width], other_zero[:, start:stop], qkv_one, other_one[:, start:stop]],
            axis=1,
        ),
        jnp.concatenate([other_zero[:, :start], other_one[:, :start]], axis=1),
        last[:, 4 * width : 4 * width + tokens],
        last[:, 4 * width + tokens : 4 * width + small_cols],
    )
    totals = jnp.stack([loss_local] + [jnp.sum(part * part) for part in raw])
    totals = jnp.broadcast_to(totals[:, None], (totals.shape[0], LANES))
    for perm in [plan.core_stage] + plan.stages:
        totals = totals + plan.swap(totals, perm)
    total_loss = totals[0, 0]
    clipped = []
    for group, part in enumerate(raw):
        limit = entry_clip * jnp.sqrt(jnp.float32(part.size * plan.count))
        norm_value = jnp.sqrt(totals[group + 1, 0])
        clipped.append(part * (limit / jnp.maximum(norm_value, limit)))
    edge_new = adam_step(edge_w, edge_m, edge_v, edge_t, clipped[0])
    attn_new = adam_step(attn_w, attn_m, attn_v, attn_t, clipped[1])
    mlp_new = adam_step(mlp_w, mlp_m, mlp_v, mlp_t, clipped[2])
    posit_new = adam_step(posit_w, posit_m, posit_v, posit_t, clipped[3])
    vecs_new = [
        part.T for part in adam_step(vecs_w.T, vecs_m.T, vecs_v.T, vecs_t.T, clipped[4].T)
    ]
    news = (edge_new, attn_new, mlp_new, posit_new, vecs_new)
    return (total_loss,) + tuple(group[part] for part in range(4) for group in news)


def solution(mesh):
    rows = P(AXES, None)
    in_specs = (P(AXES, None, None),) + (rows,) * 21
    out_specs = (P(),) + (rows,) * 20
    return jax.shard_map(local, mesh=mesh, in_specs=in_specs, out_specs=out_specs, check_vma=False)
```

```python
import jax
import jax.numpy as jnp
from jax import lax
from jax.experimental import pallas as pl
from jax.experimental.pallas import tpu as pltpu
from jax.sharding import PartitionSpec as P

HDIM = 64
LAYERS = 2
TOPK = 2
LANES = 128
FF_TILE = 512
NARROW_STAGES = 1
FAST_LANE = True

ln_eps = 1e-05
in_eps = 1e-05
learn_rate = 0.02
first_decay = 0.5
second_decay = 0.5
adam_eps = 1e-08
weight_decay = 0.1
teacher_keep = 0.5
huber_beta = 1.0
score_scale = 0.125
entry_clip = 1e-05
half_type = jnp.bfloat16
full_type = jnp.float32
AXES = ("dp", "seq")


def contract(left, right, left_dim, right_dim):
    return lax.dot_general(
        left,
        right,
        (((left_dim,), (right_dim,)), ((), ())),
        preferred_element_type=full_type,
    )


def head_mask(which, width):
    lane = lax.broadcasted_iota(jnp.int32, (1, width), 1)
    return (lane // HDIM) == which


def attend_kernel(q_ref, k_ref, v_ref, o_ref):
    queries = q_ref[0] * jnp.asarray(score_scale, half_type)
    keys_all = k_ref[0]
    values_all = v_ref[0]
    width = queries.shape[1]
    mixed = None
    for which in range(width // HDIM):
        mask = head_mask(which, width)
        head_q = jnp.where(mask, queries, jnp.zeros_like(queries))
        scores = contract(head_q, keys_all, 1, 1)
        exps = jnp.exp(scores - jnp.max(scores, axis=1, keepdims=True))
        probs = (exps * (1.0 / jnp.sum(exps, axis=1, keepdims=True))).astype(half_type)
        head_out = contract(probs, values_all, 1, 0)
        mixed = head_out if mixed is None else jnp.where(mask, head_out, mixed)
    o_ref[0] = mixed.astype(half_type)


def attend_back_kernel(q_ref, k_ref, v_ref, do_ref, dq_ref, dk_ref, dv_ref):
    queries = q_ref[0] * jnp.asarray(score_scale, half_type)
    keys_all = k_ref[0]
    values_all = v_ref[0]
    grad_out = do_ref[0]
    width = queries.shape[1]
    grad_k = None
    grad_v = None
    grad_q_rows = []
    for which in range(width // HDIM):
        mask = head_mask(which, width)
        head_q = jnp.where(mask, queries, jnp.zeros_like(queries))
        head_do = jnp.where(mask, grad_out, jnp.zeros_like(grad_out))
        scores = contract(keys_all, head_q, 1, 1)
        exps = jnp.exp(scores - jnp.max(scores, axis=0, keepdims=True))
        probs = exps * (1.0 / jnp.sum(exps, axis=0, keepdims=True))
        grad_probs = contract(values_all, head_do, 1, 1)
        prods = probs * grad_probs
        grad_scores = (prods - probs * jnp.sum(prods, axis=0, keepdims=True)).astype(half_type)
        head_dv = contract(probs.astype(half_type), grad_out, 1, 0)
        head_dk = contract(grad_scores, queries, 1, 0)
        head_dq = contract(keys_all, grad_scores, 0, 0)
        grad_q_rows.append(head_dq[which * HDIM : (which + 1) * HDIM])
        grad_v = head_dv if grad_v is None else jnp.where(mask, head_dv, grad_v)
        grad_k = head_dk if grad_k is None else jnp.where(mask, head_dk, grad_k)
    grad_q = jnp.concatenate(grad_q_rows, axis=0).T * score_scale
    dq_ref[0] = grad_q.astype(half_type)
    dk_ref[0] = grad_k.astype(half_type)
    dv_ref[0] = grad_v.astype(half_type)


def qkv_specs(tokens, blocks):
    return [
        pl.BlockSpec((1, tokens, LANES), lambda s, j, off=off: (s, 0, off * blocks + j))
        for off in range(3)
    ]


def attend(projected):
    seqs, tokens, width3 = projected.shape
    width = width3 // 3
    blocks = width // LANES
    return pl.pallas_call(
        attend_kernel,
        grid=(seqs, blocks),
        in_specs=qkv_specs(tokens, blocks),
        out_specs=pl.BlockSpec((1, tokens, LANES), lambda s, j: (s, 0, j)),
        out_shape=jax.ShapeDtypeStruct((seqs, tokens, width), half_type),
        cost_estimate=pl.CostEstimate(
            flops=16 * seqs * tokens * tokens * width,
            transcendentals=seqs * tokens * tokens * width // HDIM,
            bytes_accessed=8 * seqs * tokens * width,
        ),
        compiler_params=grant(8),
        name="attend",
    )(projected, projected, projected)


def attend_back(projected, grad_mixed, seq, into=()):
    seqs, tokens, width3 = projected.shape
    width = width3 // 3
    blocks = width // LANES
    block = pl.BlockSpec((1, tokens, LANES), lambda j: (seq, 0, j))
    specs = [
        pl.BlockSpec((1, tokens, LANES), lambda j, off=off: (seq, 0, off * blocks + j))
        for off in range(3)
    ]

    def kernel(q_ref, k_ref, v_ref, do_ref, *refs):
        attend_back_kernel(q_ref, k_ref, v_ref, do_ref, *refs[-3:])

    shape = jax.ShapeDtypeStruct((seqs, tokens, width), half_type)
    return pl.pallas_call(
        kernel,
        grid=(blocks,),
        in_specs=specs + [block] + [pl.BlockSpec(memory_space=pl.ANY)] * len(into),
        out_specs=[block, block, block],
        out_shape=[shape, shape, shape],
        input_output_aliases={4 + place: place for place in range(len(into))},
        cost_estimate=pl.CostEstimate(
            flops=32 * tokens * tokens * width,
            transcendentals=tokens * tokens * width // HDIM,
            bytes_accessed=14 * tokens * width,
        ),
        compiler_params=grant(12),
        name="attend_back",
    )(projected, projected, projected, grad_mixed, *into)


def normal_cdf(values):
    return 0.5 + 0.5 * lax.erf(values * (0.5**0.5))


def whole_block(shape):
    zeros = (0,) * len(shape)
    return pl.BlockSpec(shape, lambda *_: zeros, pipeline_mode=pl.Buffered(1))


def grant(mib):
    return pltpu.CompilerParams(vmem_limit_bytes=mib << 20)


def stacked(*refs):
    return jnp.concatenate([ref[...] for ref in refs], axis=0)


def unit_of(values):
    centre = values - jnp.mean(values, axis=1, keepdims=True)
    inv_scale = lax.rsqrt(jnp.mean(centre * centre, axis=1, keepdims=True) + ln_eps)
    return centre * inv_scale, inv_scale


def norm_back(grad_out, gain, values):
    unit, inv_scale = unit_of(values)
    grad_unit = grad_out * gain
    inner_mean = jnp.mean(grad_unit, axis=1, keepdims=True)
    along_mean = jnp.mean(grad_unit * unit, axis=1, keepdims=True)
    grad_in = (grad_unit - inner_mean - unit * along_mean) * inv_scale
    return grad_in, jnp.sum(grad_out * unit, axis=0, keepdims=True)


def half(values):
    return values.astype(half_type)


def shape_of(shape, kind):
    return jax.ShapeDtypeStruct(shape, kind)


def kept_shape(shape, kind):
    return pltpu.HBM(shape, kind)


def cost(flops, moved):
    return pl.CostEstimate(flops=flops, transcendentals=0, bytes_accessed=moved)


class Weight:
    def __init__(self, blocks, start, cols):
        self.blocks, self.start, self.cols = list(blocks), start, cols

    def specs(self, width, index=lambda j: j):
        base = self.start // width
        spec = pl.BlockSpec(
            (self.blocks[0].shape[0], width), lambda j, base=base: (0, base + index(j))
        )
        return [spec] * len(self.blocks)

    def refs(self):
        return [pltpu.with_memory_space_constraint(block, pltpu.HBM) for block in self.blocks]


def embed(patches, mask, mover, weight, small, keep_patches):
    rows, width = patches.shape
    tokens = rows // 2
    masked = mask is not None

    def kernel(*refs):
        x_ref, mover_ref = refs[:2]
        w_refs, small_refs, refs = refs[2:6], refs[6:10], refs[10:]
        if masked:
            mask_ref, refs = refs[0], refs[1:]
        h_ref, table_ref = refs[:2]
        x_rel = half(contract(x_ref[...], mover_ref[...], 1, 0))
        if keep_patches:
            refs[2][...] = x_rel
        w_rel = half(contract(stacked(*w_refs), mover_ref[...], 1, 0))
        small_t = stacked(*small_refs).astype(full_type).T
        posit = small_t[:tokens]
        table = small_t[tokens : tokens + 8]
        table_ref[...] = table
        states = contract(x_rel, w_rel, 1, 0)
        for seq in range(rows // tokens):
            part = slice(seq * tokens, (seq + 1) * tokens)
            state = states[part]
            if masked:
                flag = mask_ref[part, :]
                state = state * (1.0 - flag) + flag * table[2 * LAYERS + 1 : 2 * LAYERS + 2]
            h_ref[part, :] = state + posit

    outs = [shape_of((rows, width), full_type), shape_of((8, width), full_type)]
    if keep_patches:
        outs.append(shape_of((rows, width), half_type))
    args = [patches, mover] + weight.refs() + list(small) + ([mask] if masked else [])
    specs = [whole_block(patches.shape), whole_block(mover.shape)] + weight.specs(width)
    specs += [whole_block(part.shape) for part in small]
    if masked:
        specs.append(whole_block(mask.shape))
    return pl.pallas_call(
        kernel,
        grid=(1,),
        in_specs=specs,
        out_specs=[whole_block(out.shape) for out in outs],
        out_shape=outs,
        cost_estimate=cost(6 * rows * width * width, 12 * rows * width),
        compiler_params=grant(28),
        name="embed",
    )(*args)


def norm_project(states, table, row, weight, keep):
    rows, width = states.shape
    steps = weight.cols // width

    def kernel(h_ref, table_ref, own_ref, own2_ref, got_ref, got2_ref, out_ref, a_ref):
        @pl.when(pl.program_id(0) == 0)
        def _():
            unit, _ = unit_of(h_ref[...])
            a_ref[...] = half(unit * table_ref[row : row + 1, :])

        out_ref[...] = half(contract(a_ref[...], stacked(own_ref, own2_ref, got_ref, got2_ref), 1, 0))

    outs = [shape_of((rows, weight.cols), half_type)]
    out_specs = [pl.BlockSpec((rows, width), lambda j: (0, j))]
    scratch = []
    if keep:
        outs.append(kept_shape((rows, width), half_type))
        out_specs.append(whole_block((rows, width)))
    else:
        scratch.append(pltpu.VMEM((rows, width), half_type))
    return pl.pallas_call(
        kernel,
        grid=(steps,),
        in_specs=[whole_block(states.shape), whole_block(table.shape)] + weight.specs(width),
        out_specs=out_specs,
        out_shape=outs,
        scratch_shapes=scratch,
        cost_estimate=cost(2 * rows * width * weight.cols, 12 * rows * width),
        compiler_params=grant(24),
        name="norm_project",
    )(states, table, *weight.refs())


def mix_out(mixed, states, mover, table, row, weight, keep):
    rows, width = states.shape
    tile = rows // 2

    def kernel(o_ref, h_ref, mover_ref, table_ref, own_ref, own2_ref, got_ref, got2_ref, m_ref, b_ref, *rest):
        if keep:
            rel_ref, w_ref = rest
        else:
            (w_ref,) = rest

        @pl.when(pl.program_id(0) == 0)
        def _():
            w_ref[...] = half(contract(stacked(own_ref, own2_ref, got_ref, got2_ref), mover_ref[...], 1, 0))

        mixed_rel = half(contract(o_ref[...], mover_ref[...], 1, 0))
        if keep:
            rel_ref[...] = mixed_rel
        middle = h_ref[...] + contract(mixed_rel, w_ref[...], 1, 0)
        m_ref[...] = middle
        unit, _ = unit_of(middle)
        b_ref[...] = half(unit * table_ref[row : row + 1, :])

    part = pl.BlockSpec((tile, width), lambda j: (j, 0))
    outs = [shape_of((rows, width), full_type), shape_of((rows, width), half_type)]
    out_specs = [part, part]
    scratch = []
    if keep:
        outs += [kept_shape((rows, width), half_type), kept_shape((width, width), half_type)]
        out_specs += [part, whole_block((width, width))]
    else:
        scratch.append(pltpu.VMEM((width, width), half_type))
    return pl.pallas_call(
        kernel,
        grid=(2,),
        in_specs=[part, part, whole_block(mover.shape), whole_block(table.shape)]
        + weight.specs(width, lambda j: 0),
        out_specs=out_specs,
        out_shape=outs,
        scratch_shapes=scratch,
        cost_estimate=cost(6 * rows * width * width, 14 * rows * width),
        compiler_params=grant(24),
        name="mix_out",
    )(mixed, states, mover, table, *weight.refs())


def feed_forward(normed, middle, w_up, w_down, keep):
    rows, width = middle.shape
    tile = FF_TILE
    steps = w_up.cols // tile

    def kernel(b_ref, m_ref, uown_ref, uown2_ref, ugot_ref, ugot2_ref, down_ref, down2_ref, dgot_ref, dgot2_ref, out_ref, *rest):
        step = pl.program_id(0)
        hidden = contract(b_ref[...], stacked(uown_ref, uown2_ref, ugot_ref, ugot2_ref), 1, 0)
        cdf = normal_cdf(hidden)
        active = half(hidden * cdf)
        if keep:
            rest[0][...] = active
            rest[1][...] = cdf + hidden * (
                jnp.exp(-0.5 * hidden * hidden) * ((0.5 / jnp.pi) ** 0.5)
            )
        part = contract(active, stacked(down_ref, down2_ref, dgot_ref, dgot2_ref), 1, 1)

        @pl.when(step == 0)
        def _():
            out_ref[...] = m_ref[...] + part

        @pl.when(step > 0)
        def _():
            out_ref[...] += part

    outs = [shape_of((rows, width), full_type)]
    out_specs = [whole_block((rows, width))]
    if keep:
        outs += [kept_shape((rows, w_up.cols), half_type), kept_shape((rows, w_up.cols), full_type)]
        out_specs += [pl.BlockSpec((rows, tile), lambda j: (0, j))] * 2
    return pl.pallas_call(
        kernel,
        grid=(steps,),
        in_specs=[whole_block(normed.shape), whole_block(middle.shape)]
        + w_up.specs(tile)
        + w_down.specs(tile),
        out_specs=out_specs,
        out_shape=outs,
        cost_estimate=cost(4 * rows * width * w_up.cols, 12 * rows * width + 16 * width * w_up.cols),
        compiler_params=grant(30),
        name="feed_forward",
    )(normed, middle, *w_up.refs(), *w_down.refs())


def make_target(first, second, seqs):
    rows, width = first.shape
    tokens = rows // seqs
    cols = width // 2

    def kernel(one_ref, two_ref, out_ref):
        total = None
        for ref in (one_ref, two_ref):
            values = ref[...]
            centre = values - jnp.mean(values, axis=0, keepdims=True)
            variance = jnp.mean(centre * centre, axis=0, keepdims=True)
            term = centre * lax.rsqrt(variance + in_eps)
            total = term if total is None else total + term
        out_ref[...] = total * (1.0 / TOPK)

    block = pl.BlockSpec((tokens, cols), lambda s, j: (s, j))
    return pl.pallas_call(
        kernel,
        grid=(seqs, 2),
        in_specs=[block, block],
        out_specs=block,
        out_shape=shape_of((rows, width), full_type),
        cost_estimate=cost(20 * rows * width, 12 * rows * width),
        compiler_params=grant(16),
        name="make_target",
    )(first, second)


def head_step(states, table, mover, weight, target, mask, total_masked):
    rows, width = states.shape
    tile = rows // 2
    final_row = 2 * LAYERS

    def kernel(
        h_ref, table_ref, mover_ref, own_ref, own2_ref, got_ref, got2_ref, t_ref, mask_ref,
        flow_ref, f_ref, pred_ref, gain_ref, loss_ref, w_ref,
    ):
        step = pl.program_id(0)

        @pl.when(step == 0)
        def _():
            w_ref[...] = half(contract(stacked(own_ref, own2_ref, got_ref, got2_ref), mover_ref[...], 1, 0))
            gain_ref[...] = jnp.zeros_like(gain_ref)
            loss_ref[...] = jnp.zeros_like(loss_ref)

        states_now = h_ref[...]
        gain = table_ref[final_row : final_row + 1, :]
        unit, _ = unit_of(states_now)
        final_normed = half(unit * gain)
        f_ref[...] = final_normed
        flag = mask_ref[...]
        differ = contract(final_normed, w_ref[...], 1, 0) - t_ref[...]
        magnitude = jnp.abs(differ)
        terms = jnp.where(
            magnitude < huber_beta,
            0.5 * differ * differ / huber_beta,
            magnitude - 0.5 * huber_beta,
        )
        loss_ref[...] += jnp.sum(terms * flag, axis=0, keepdims=True)
        grad_pred = half(flag * jnp.clip(differ / huber_beta, -1.0, 1.0) / total_masked)
        pred_ref[...] = half(contract(grad_pred, mover_ref[...], 1, 1))
        grad_in, grad_gain = norm_back(contract(grad_pred, w_ref[...], 1, 1), gain, states_now)
        flow_ref[...] = grad_in
        gain_ref[...] += grad_gain

    part = pl.BlockSpec((tile, width), lambda j: (j, 0))
    row = whole_block((1, width))
    return pl.pallas_call(
        kernel,
        grid=(2,),
        in_specs=[part, whole_block(table.shape), whole_block(mover.shape)]
        + weight.specs(width, lambda j: 0)
        + [part, pl.BlockSpec((tile, 1), lambda j: (j, 0))],
        out_specs=[part, part, part, row, row],
        out_shape=[
            shape_of((rows, width), full_type),
            shape_of((rows, width), half_type),
            shape_of((rows, width), half_type),
            shape_of((1, width), full_type),
            shape_of((1, width), full_type),
        ],
        scratch_shapes=[pltpu.VMEM((width, width), half_type)],
        cost_estimate=cost(8 * rows * width * width, 16 * rows * width),
        compiler_params=grant(30),
        name="head_step",
    )(states, table, mover, *weight.refs(), target, mask)


def feed_back(flow, slope, middle, table, row, w_up, w_down):
    rows, width = flow.shape
    tile = FF_TILE
    steps = w_up.cols // tile

    def kernel(
        flow_ref, slope_ref, m_ref, table_ref, uown_ref, uown2_ref, ugot_ref, ugot2_ref, down_ref, down2_ref, dgot_ref, dgot2_ref,
        du_ref, dy_ref, dm_ref, dz_ref, gain_ref, acc_ref,
    ):
        step = pl.program_id(0)

        @pl.when(step == 0)
        def _():
            dy_ref[...] = half(flow_ref[...])

        grad_active = contract(dy_ref[...], stacked(down_ref, down2_ref, dgot_ref, dgot2_ref), 1, 0)
        grad_hidden = half(grad_active * slope_ref[...])
        du_ref[...] = grad_hidden
        part = contract(grad_hidden, stacked(uown_ref, uown2_ref, ugot_ref, ugot2_ref), 1, 1)

        @pl.when(step == 0)
        def _():
            acc_ref[...] = part

        @pl.when(step > 0)
        def _():
            acc_ref[...] += part

        @pl.when(step == steps - 1)
        def _():
            grad_in, grad_gain = norm_back(
                acc_ref[...], table_ref[row : row + 1, :], m_ref[...]
            )
            grad_middle = flow_ref[...] + grad_in
            dm_ref[...] = grad_middle
            dz_ref[...] = half(grad_middle)
            gain_ref[...] = grad_gain

    full = whole_block((rows, width))
    column = pl.BlockSpec((rows, tile), lambda j: (0, j))
    return pl.pallas_call(
        kernel,
        grid=(steps,),
        in_specs=[full, column, full, whole_block(table.shape)]
        + w_up.specs(tile)
        + w_down.specs(tile),
        out_specs=[column, full, full, full, whole_block((1, width))],
        out_shape=[
            shape_of((rows, w_up.cols), half_type),
            shape_of((rows, width), half_type),
            shape_of((rows, width), full_type),
            shape_of((rows, width), half_type),
            shape_of((1, width), full_type),
        ],
        scratch_shapes=[pltpu.VMEM((rows, width), full_type)],
        cost_estimate=cost(4 * rows * width * w_up.cols, 40 * rows * width + 8 * width * w_up.cols),
        compiler_params=grant(32),
        name="feed_back",
    )(flow, slope, middle, table, *w_up.refs(), *w_down.refs())


def mix_back(grad_branch, w_rel, mover):
    rows, width = grad_branch.shape
    tile = rows // 2

    def kernel(dz_ref, w_ref, mover_ref, do_ref, nat_ref):
        branch = dz_ref[...]
        grad_rel = half(contract(branch, w_ref[...], 1, 1))
        do_ref[...] = half(contract(grad_rel, mover_ref[...], 1, 1))
        nat_ref[...] = half(contract(branch, mover_ref[...], 1, 1))

    part = pl.BlockSpec((tile, width), lambda j: (j, 0))
    square = whole_block((width, width))
    return pl.pallas_call(
        kernel,
        grid=(2,),
        in_specs=[part, square, square],
        out_specs=[part, part],
        out_shape=[shape_of((rows, width), half_type)] * 2,
        cost_estimate=cost(6 * rows * width * width, 10 * rows * width),
        compiler_params=grant(16),
        name="mix_back",
    )(grad_branch, w_rel, mover)


def project_back(grads, grad_middle, states, table, row, weight, mover, mask):
    rows, width = states.shape
    tile = rows // 2
    count = len(grads)
    first = mask is not None

    def kernel(*refs):
        grad_refs, refs = refs[:count], refs[count:]
        w_refs, refs = refs[: 4 * count], refs[4 * count :]
        dm_ref, h_ref, table_ref = refs[:3]
        refs = refs[3:]
        if first:
            mover_ref, mask_ref = refs[:2]
            refs = refs[2:]
        dh_ref, gain_ref = refs[:2]
        step = pl.program_id(0)

        @pl.when(step == 0)
        def _():
            for ref in (gain_ref,) + ((refs[3],) if first else ()):
                ref[...] = jnp.zeros_like(ref)

        total = None
        for place in range(count):
            part = contract(
                grad_refs[place][...], stacked(*w_refs[4 * place : 4 * place + 4]), 1, 1
            )
            total = part if total is None else total + part
        grad_in, grad_gain = norm_back(total, table_ref[row : row + 1, :], h_ref[...])
        flow = dm_ref[...] + grad_in
        dh_ref[...] = flow
        gain_ref[...] += grad_gain
        if first:
            flag = mask_ref[...]
            refs[2][...] = half(contract(half(flow * (1.0 - flag)), mover_ref[...], 1, 1))
            refs[3][...] += jnp.sum(flow * flag, axis=0, keepdims=True)

    part = pl.BlockSpec((tile, width), lambda j: (j, 0))
    vector = whole_block((1, width))
    specs = [part] * count
    args = list(grads)
    for place in range(count):
        specs += weight.specs(width, lambda j, place=place: place)
        args += weight.refs()
    specs += [part, part, whole_block(table.shape)]
    args += [grad_middle, states, table]
    outs = [shape_of((rows, width), full_type), shape_of((1, width), full_type)]
    out_specs = [part, vector]
    if first:
        specs += [whole_block(mover.shape), pl.BlockSpec((tile, 1), lambda j: (j, 0))]
        args += [mover, mask]
        outs += [shape_of((rows, width), half_type), shape_of((1, width), full_type)]
        out_specs += [part, vector]
    return pl.pallas_call(
        kernel,
        grid=(2,),
        in_specs=specs,
        out_specs=out_specs,
        out_shape=outs,
        cost_estimate=cost(2 * rows * width * weight.cols, 22 * rows * width),
        compiler_params=grant(30),
        name="project_back",
    )(*args)


def weight_grads(pairs):
    rows, width = pairs[0][0].shape
    plan = []
    start = 0
    for place, (_, rights) in enumerate(pairs):
        first = start
        for right in rights:
            tiles = right.shape[1] // width
            plan.append((place, start, tiles, start == first))
            start += tiles
    total = start
    near_rows = width // 2

    def kernel(*refs):
        left_refs, refs = refs[: len(pairs)], refs[len(pairs) :]
        right_refs, refs = refs[: len(plan)], refs[len(plan) :]
        near_ref, far_ref, turned_ref = refs
        step = pl.program_id(0)
        for (place, begin, tiles, fresh), right_ref in zip(plan, right_refs):
            if fresh:

                @pl.when(step == begin)
                def _(place=place):
                    turned_ref[...] = left_refs[place][...].T

            @pl.when((step >= begin) & (step < begin + tiles))
            def _(right_ref=right_ref):
                out = contract(turned_ref[...], right_ref[...], 1, 0)
                near_ref[...] = out[:near_rows]
                far_ref[...] = half(out[near_rows:])

    specs = [whole_block((rows, width)) for _ in pairs]
    args = [left for left, _ in pairs]
    for (_, rights) in pairs:
        args += list(rights)
    for _, begin, tiles, _ in plan:
        specs.append(
            pl.BlockSpec(
                (rows, width),
                lambda j, begin=begin, tiles=tiles: (0, jnp.clip(j - begin, 0, tiles - 1)),
            )
        )
    block = pl.BlockSpec((near_rows, width), lambda j: (0, j))
    shapes = [shape_of((near_rows, total * width), kind) for kind in (full_type, half_type)]
    return tuple(
        pl.pallas_call(
            kernel,
            grid=(total,),
            in_specs=specs,
            out_specs=[block, block],
            out_shape=shapes,
            scratch_shapes=[pltpu.VMEM((width, rows), half_type)],
            cost_estimate=cost(
                2 * rows * width * width * total, width * total * (4 * width + 2 * rows)
            ),
            compiler_params=grant(30),
        name="weight_grads",
        )(*args)
    )


def small_grads(flow, vectors, seqs):
    rows, width = flow.shape
    tokens = rows // seqs
    cols = tokens + 8
    cols += -cols % LANES

    def kernel(flow_ref, *refs):
        vector_refs, (near_ref, far_ref) = refs[:-2], refs[-2:]
        posit = flow_ref[:tokens]
        for seq in range(1, seqs):
            posit = posit + flow_ref[seq * tokens : (seq + 1) * tokens]
        fill = jnp.zeros((cols - tokens - len(vector_refs), width), full_type)
        table = jnp.concatenate([posit] + [ref[...] for ref in vector_refs] + [fill], axis=0).T
        near_ref[...] = table[: width // 2]
        far_ref[...] = half(table[width // 2 :])

    shapes = [shape_of((width // 2, cols), kind) for kind in (full_type, half_type)]
    return tuple(
        pl.pallas_call(
            kernel,
            grid=(1,),
            in_specs=[whole_block(flow.shape)] + [whole_block((1, width)) for _ in vectors],
            out_specs=[whole_block(shape.shape) for shape in shapes],
            out_shape=shapes,
            cost_estimate=cost(2 * rows * width, 8 * rows * width),
            compiler_params=grant(16),
        name="small_grads",
        )(flow, *vectors)
    )


class Plan:
    def __init__(self):
        self.seq_size = lax.axis_size("seq")
        self.count = lax.axis_size("dp") * self.seq_size
        self.bits = self.count.bit_length() - 1
        self.early = list(range(self.bits - 1, 2, -1))

        def flips(pick):
            return [(i, i ^ (1 << pick((i >> 1) & 1))) for i in range(self.count)]

        self.stages = [flips(lambda core, b=b: b) for b in self.early]
        self.stages.append(flips(lambda core: 0 if core else 2))
        self.stages.append(flips(lambda core: 2 if core else 0))
        self.core_stage = flips(lambda core: 1)
        self.index = lax.axis_index("dp") * self.seq_size + lax.axis_index("seq")

    def swap(self, value, perm):
        return lax.ppermute(value, AXES, perm)

    def row_table(self, width):
        rows = width // self.count
        place = lax.broadcasted_iota(jnp.int32, (1, width), 1)
        spot = place // rows
        early_count = len(self.early)
        other = (spot >> (self.bits - 1)) & 1
        holder_core = ((self.index >> 1) & 1) ^ other
        block = self.index ^ (other << 1)
        for step, bit in enumerate(self.early):
            block = block ^ (((spot >> step) & 1) << bit)
        first = (spot >> early_count) & 1
        second = (spot >> (early_count + 1)) & 1
        block = block ^ jnp.where(holder_core == 0, first << 2, first)
        block = block ^ jnp.where(holder_core == 0, second, second << 2)
        return block * rows + place % rows

    def mover(self, width):
        table = self.row_table(width)
        whole = lax.broadcasted_iota(jnp.int32, (width, width), 0)
        return (whole == table).astype(half_type)


class Pump:
    def __init__(self, plan):
        self.plan = plan
        self.jobs = []
        self.flying = []

    def add(self, steps, done):
        self.jobs.append([steps, next(steps), done])

    def begin(self):
        self.flying = [
            [self.plan.swap(value, perm) for value, perm in sends] for _, sends, _ in self.jobs
        ]

    def end(self, values=()):
        flying, values = lax.optimization_barrier((self.flying, values))
        left = []
        for (steps, _, done), gots in zip(self.jobs, flying):
            try:
                left.append([steps, steps.send(gots), done])
            except StopIteration as stop:
                done(stop.value)
        self.jobs = left
        self.flying = []
        return values

    def drain(self):
        for steps, sends, done in self.jobs:
            try:
                while True:
                    sends = steps.send([self.plan.swap(value, perm) for value, perm in sends])
            except StopIteration as stop:
                done(stop.value)
        self.jobs = []


def scatter_steps(plan, pieces):
    gots = yield [(far, plan.core_stage) for _, far in pieces]
    quarter = pieces[0][0].shape[0] // 2
    sums = [
        (half(near[quarter:] + got[quarter:]), near[:quarter] + got[:quarter])
        for (near, _), got in zip(pieces, gots)
    ]
    send = jnp.concatenate([part for part, _ in sums], axis=1)
    keep = jnp.concatenate([part for _, part in sums], axis=1)
    stages = plan.stages[::-1]
    for step, perm in enumerate(stages):
        (got,) = yield [(send, perm)]
        if step == len(stages) - 1:
            return keep + got
        middle = keep.shape[0] // 2
        send = keep[middle:] + got[middle:]
        if step < NARROW_STAGES:
            send = half(send)
        keep = keep[:middle] + got[:middle]


def adam_step(weight, first_mom, second_mom, teacher, gradient):
    first_new = first_decay * first_mom + (1.0 - first_decay) * gradient
    second_new = second_decay * second_mom + (1.0 - second_decay) * gradient * gradient
    weight_new = weight - learn_rate * (
        first_new / (jnp.sqrt(second_new) + adam_eps) + weight_decay * weight
    )
    teacher_new = teacher_keep * teacher + (1.0 - teacher_keep) * weight_new
    return (weight_new, first_new, second_new, teacher_new)


def norm_totals(last, attn_one, mlp_zero, mlp_one, loss_row, width, tokens):
    stop = mlp_zero.shape[1]

    def kernel(last_ref, attn_ref, zero_ref, one_ref, loss_ref, out_ref):
        def square(value):
            return jnp.sum(value * value)

        small = last_ref[:, 5 * width :]
        lane = lax.broadcasted_iota(jnp.int32, small.shape, 1)
        posit = jnp.where(lane < tokens, small, 0.0)
        vecs = jnp.where(lane >= tokens, small, 0.0)
        parts = [
            jnp.sum(loss_ref[...]),
            square(last_ref[:, 4 * width : 5 * width]) + square(one_ref[:, stop:]),
            square(last_ref[:, : 4 * width]) + square(attn_ref[...]),
            square(zero_ref[...]) + square(one_ref[:, :stop]),
            square(posit),
            square(vecs),
        ]
        row = lax.broadcasted_iota(jnp.int32, (8, LANES), 0)
        out = jnp.zeros((8, LANES), full_type)
        for place, part in enumerate(parts):
            out = jnp.where(row == place, part, out)
        out_ref[...] = out

    args = (last, attn_one, mlp_zero, mlp_one, loss_row)
    return pl.pallas_call(
        kernel,
        grid=(1,),
        in_specs=[whole_block(arg.shape) for arg in args],
        out_specs=whole_block((8, LANES)),
        out_shape=shape_of((8, LANES), full_type),
        compiler_params=grant(16),
        name="norm_totals",
    )(*args)


def update(totals, last, attn_one, mlp_zero, mlp_one, groups, sizes, width, tokens):
    stop = mlp_zero.shape[1]

    def kernel(total_ref, last_ref, attn_ref, zero_ref, one_ref, *refs):
        ins, outs = refs[:20], refs[20:]

        def step(group, gradient, cols=slice(None)):
            limit = entry_clip * sizes[group] ** 0.5
            norm_value = jnp.sqrt(total_ref[group + 1 : group + 2, 0:1])
            gradient = gradient * (limit / jnp.maximum(norm_value, limit))
            weight, first, second, teacher = (
                ref[:, cols] for ref in ins[4 * group : 4 * group + 4]
            )
            news = adam_step(weight, first, second, teacher, gradient)
            for ref, new in zip(outs[4 * group : 4 * group + 4], news):
                ref[:, cols] = new

        step(0, last_ref[:, 4 * width : 5 * width], slice(0, width))
        step(0, one_ref[:, stop:], slice(width, 2 * width))
        step(1, last_ref[:, : 4 * width], slice(0, 4 * width))
        step(1, attn_ref[...], slice(4 * width, 8 * width))
        step(2, zero_ref[...], slice(0, stop))
        step(2, one_ref[:, :stop], slice(stop, 2 * stop))
        step(3, last_ref[:, 5 * width : 5 * width + tokens])
        start = tokens // LANES * LANES
        turned = last_ref[:, 5 * width + start : 5 * width + start + LANES].T
        count = ins[16].shape[0]
        step(4, turned[tokens - start : tokens - start + count])

    args = [totals, last, attn_one, mlp_zero, mlp_one] + [part for group in groups for part in group]
    outs = [shape_of(part.shape, full_type) for group in groups for part in group]
    return pl.pallas_call(
        kernel,
        grid=(1,),
        in_specs=[whole_block(arg.shape) for arg in args],
        out_specs=[whole_block(out.shape) for out in outs],
        out_shape=outs,
        compiler_params=grant(40),
        name="update",
    )(*args)


def pad_lanes(value):
    extra = -value.shape[1] % LANES
    return jnp.pad(value, ((0, 0), (0, extra)))


def local(
    patches,
    masked_at,
    edge_w,
    attn_w,
    mlp_w,
    posit_w,
    vecs_w,
    edge_m,
    attn_m,
    mlp_m,
    posit_m,
    vecs_m,
    edge_v,
    attn_v,
    mlp_v,
    posit_v,
    vecs_v,
    edge_t,
    attn_t,
    mlp_t,
    posit_t,
    vecs_t,
):
    seqs, tokens, width = patches.shape
    plan = Plan()
    total_masked = seqs * plan.count * tokens // 2
    ff_width = mlp_w.shape[1] // (2 * LAYERS)
    small_cols = tokens + vecs_w.shape[1]
    flat_patch = patches.reshape(-1, width)
    mask_flat = masked_at.astype(full_type).reshape(-1, 1)
    mover = plan.mover(width)

    def shards(edge, attn, mlp, posit, vecs):
        small = pad_lanes(jnp.concatenate([posit, vecs], axis=1))
        return [edge[:, :width], edge[:, width:], small] + [
            [
                part[:, layer * part.shape[1] // LAYERS : (layer + 1) * part.shape[1] // LAYERS]
                for part in (attn, mlp)
            ]
            for layer in range(LAYERS)
        ]

    def joined(parts):
        return jnp.concatenate([half(part) for part in parts], axis=1)

    t_patch, _, t_small, t_one, t_two = shards(edge_t, attn_t, mlp_t, posit_t, vecs_t)
    s_patch, s_head, s_small, s_one, s_two = shards(edge_w, attn_w, mlp_w, posit_w, vecs_w)
    chunks = [
        [t_patch, t_one[0], t_small],
        [t_one[1]],
        t_two,
        [s_patch, s_one[0], s_small],
        [s_one[1]],
        [s_two[0], s_head],
        [s_two[1]],
    ]
    groups = [[0], [1], [2, 3], [4, 5, 6]]
    group_start = [0, 1, 2, 4]

    def attn_weights(blocks, start):
        return Weight(blocks, start, 3 * width), Weight(blocks, start + 3 * width, width)

    def mlp_weights(blocks, start):
        return Weight(blocks, start, ff_width), Weight(blocks, start + ff_width, ff_width)

    def small_of(blocks):
        start = blocks[0].shape[1] - t_small.shape[1]
        return [block[:, start:] for block in blocks]

    def finish(blocks):
        return list(blocks) + [plan.swap(blocks[1], plan.core_stage)]

    def attend_forward(states, table, layer, w_qkv, w_out, keep, outs=None):
        if outs is None:
            outs = norm_project(states, table, layer, w_qkv, keep)
        projected = outs[0].reshape(seqs, tokens, w_qkv.cols)
        mixed = attend(projected).reshape(-1, width)
        results = mix_out(mixed, states, mover, table, LAYERS + layer, w_out, keep)
        if keep:
            return results[0], results[1], (states, outs[1], projected) + tuple(results[2:])
        return results[0], results[1], ()

    saved_attn = [None] * LAYERS
    saved_mlp = [None] * LAYERS

    def segment_t0(_, blocks):
        patch = Weight(blocks, 0, width)
        states, table, patch_rel = embed(
            flat_patch, None, mover, patch, small_of(blocks), True
        )
        weights = attn_weights(blocks, width)
        return states, table, patch_rel, norm_project(states, table, 0, weights[0], False)

    def segment_t0_rest(values, blocks):
        states, table, patch_rel, outs = values
        weights = attn_weights(blocks, width)
        middle, normed, _ = attend_forward(states, table, 0, *weights, False, outs)
        return middle, normed, table, patch_rel

    def segment_t1(values, blocks):
        middle, normed, table, patch_rel = values
        (states,) = feed_forward(normed, middle, *mlp_weights(blocks, 0), False)
        return states, table, patch_rel

    def segment_t2(values, blocks):
        first, table, patch_rel = values
        middle, normed, _ = attend_forward(first, table, 1, *attn_weights(blocks, 0), False)
        (second,) = feed_forward(normed, middle, *mlp_weights(blocks, 4 * width), False)
        return make_target(first, second, seqs), patch_rel

    def segment_s0(values, blocks):
        target, patch_rel = values
        patch = Weight(blocks, 0, width)
        states, table = embed(flat_patch, mask_flat, mover, patch, small_of(blocks), False)
        weights = attn_weights(blocks, width)
        middle, normed, saved = attend_forward(states, table, 0, *weights, True)
        saved_attn[0] = (weights[0], saved)
        return target, patch_rel, table, middle, normed

    def segment_s1(values, blocks):
        target, patch_rel, table, middle, normed = values
        weights = mlp_weights(blocks, 0)
        states, active, slope = feed_forward(normed, middle, *weights, True)
        saved_mlp[0] = (weights, middle, normed, active, slope)
        return target, patch_rel, table, states

    def segment_s2(values, blocks):
        target, patch_rel, table, states = values
        weights = attn_weights(blocks, 0)
        middle, normed, saved = attend_forward(states, table, 1, *weights, True)
        saved_attn[1] = (weights[0], saved)
        return target, patch_rel, table, middle, normed, blocks

    segments = [segment_t0_rest, segment_t1, segment_t2, segment_s0, segment_s1, segment_s2]
    early = len(plan.early)
    group_values = [joined([part for c in group for part in chunks[c]]) for group in groups]
    own = [None] * len(chunks)
    blocks = [None] * len(chunks)
    values = ()
    for tick in range(len(chunks) + early + 1):
        sends = {}
        for group, start in enumerate(group_start):
            if 0 <= tick - start < early:
                sends["early", group] = (group_values[group], plan.stages[tick - start])
        for chunk in range(len(chunks)):
            if tick == chunk + early:
                sends["first", chunk] = (own[chunk], plan.stages[early])
            if tick == chunk + early + 1:
                sends["second", chunk] = (own[chunk], plan.stages[early + 1])
                sends["core", chunk] = (own[chunk], plan.core_stage)
        gots = {key: plan.swap(value, perm) for key, (value, perm) in sends.items()}
        place = tick - early - 2
        if 0 <= place < len(segments):
            values = segments[place](values, finish(blocks[place]))
        if tick == early + 1:
            first_blocks = (own[0], gots["second", 0], gots["core", 0])
            values = segment_t0(values, finish(first_blocks))
        apart = {key: got for key, got in gots.items() if FAST_LANE and key[1] == 0 and tick}
        gots = {key: got for key, got in gots.items() if key not in apart}
        later = [g for g in range(len(groups)) if group_start[g] > tick]
        idle = [c for c in range(1, len(chunks)) if own[c] is not None and c + early > tick]
        gots, values, held, held_own, _ = lax.optimization_barrier(
            (gots, values, [group_values[g] for g in later], [own[c] for c in idle], apart)
        )
        for g, value in zip(later, held):
            group_values[g] = value
        for c, value in zip(idle, held_own):
            own[c] = value
        gots.update(apart)
        for (kind, index), got in gots.items():
            if kind == "early":
                group_values[index] = jnp.concatenate([group_values[index], got], axis=0)
                if tick - group_start[index] == early - 1:
                    start = 0
                    for chunk in groups[index]:
                        stop = start + sum(part.shape[1] for part in chunks[chunk])
                        own[chunk] = group_values[index][:, start:stop]
                        start = stop
            elif kind == "first":
                own[index] = jnp.concatenate([own[index], got], axis=0)
        for chunk in range(len(chunks)):
            if ("second", chunk) in gots:
                blocks[chunk] = (own[chunk], gots["second", chunk], gots["core", chunk])
    pump = Pump(plan)
    target, patch_rel, table, middle, normed, head_blocks = values
    weights = mlp_weights(finish(blocks[-1]), 0)
    states, active, slope = feed_forward(normed, middle, *weights, True)
    saved_mlp[1] = (weights, middle, normed, active, slope)
    flow, final_normed, grad_pred, grad_gain_final, loss_row = head_step(
        states,
        table,
        mover,
        Weight(head_blocks, 4 * width, width),
        target,
        mask_flat,
        total_masked,
    )

    gain_ones = [None] * LAYERS
    gain_twos = [None] * LAYERS
    attn_shards = [None] * LAYERS
    mlp_shards = [None] * LAYERS
    extra_pairs = [(final_normed, [grad_pred])]
    for layer in reversed(range(LAYERS)):
        w_qkv, (states, normed_one, projected, mixed_rel, w_out_rel) = saved_attn[layer]
        (w_up, w_down), middle, normed_two, active, slope = saved_mlp[layer]
        grad_hidden, grad_down, grad_middle, grad_branch, gain_twos[layer] = feed_back(
            flow, slope, middle, table, LAYERS + layer, w_up, w_down
        )
        piece = weight_grads(
            [(normed_two, [grad_hidden]), (grad_down, [active])] + extra_pairs
        )
        extra_pairs = []
        piece, grad_middle, grad_branch = pump.end((piece, grad_middle, grad_branch))
        pump.add(
            scatter_steps(plan, [piece]),
            lambda out, layer=layer: mlp_shards.__setitem__(layer, out),
        )
        pump.begin()
        grad_mixed, branch_whole = mix_back(grad_branch, w_out_rel, mover)
        grad_mixed = grad_mixed.reshape(seqs, tokens, width)
        grad_proj = ()
        for seq in range(seqs):
            if seq == seqs - 1:
                grad_proj, grad_mixed, branch_whole = pump.end(
                    (grad_proj, grad_mixed, branch_whole)
                )
                pump.begin()
            grad_proj = attend_back(projected, grad_mixed, seq, tuple(grad_proj))
        if layer == 0:
            grad_proj = pump.end(tuple(grad_proj))
            pump.begin()
        grad_proj = [part.reshape(-1, width) for part in grad_proj]
        results = project_back(
            grad_proj,
            grad_middle,
            states,
            table,
            layer,
            w_qkv,
            mover,
            None if layer else mask_flat,
        )
        flow, gain_ones[layer] = results[:2]
        if layer == 0:
            grad_embed, grad_maskvec = results[2:]
            extra_pairs = [(patch_rel, [grad_embed])]
        pieces = [
            weight_grads([(normed_one, grad_proj), (mixed_rel, [branch_whole])] + extra_pairs)
        ]
        extra_pairs = []
        if layer == 0:
            vectors = gain_ones + gain_twos + [grad_gain_final, grad_maskvec]
            pieces.append(small_grads(flow, vectors, seqs))
        pieces, flow = pump.end((pieces, flow))
        pump.add(
            scatter_steps(plan, pieces),
            lambda out, layer=layer: attn_shards.__setitem__(layer, out),
        )
        if layer:
            pump.begin()
    pump.drain()
    last, attn_one = attn_shards
    pieces = (last, attn_one, mlp_shards[0], mlp_shards[1])
    totals = norm_totals(*pieces, loss_row, width, tokens)
    for perm in [plan.core_stage] + plan.stages:
        totals = totals + plan.swap(totals, perm)
    groups = [
        (edge_w, edge_m, edge_v, edge_t),
        (attn_w, attn_m, attn_v, attn_t),
        (mlp_w, mlp_m, mlp_v, mlp_t),
        (posit_w, posit_m, posit_v, posit_t),
        (vecs_w.T, vecs_m.T, vecs_v.T, vecs_t.T),
    ]
    sizes = [group[0].size * plan.count for group in groups]
    news = update(totals, *pieces, groups, sizes, width, tokens)
    news = [
        [news[4 * group + part] for group in range(4)] + [news[16 + part].T] for part in range(4)
    ]
    return (totals[0, 0] / total_masked,) + tuple(new for part in news for new in part)


def solution(mesh):
    rows = P(AXES, None)
    in_specs = (P(AXES, None, None),) + (rows,) * 21
    out_specs = (P(),) + (rows,) * 20
    return jax.shard_map(local, mesh=mesh, in_specs=in_specs, out_specs=out_specs, check_vma=False)
```

```python
import jax
import jax.numpy as jnp
from jax import lax
from jax.experimental import pallas as pl
from jax.experimental.pallas import tpu as pltpu
from jax.sharding import PartitionSpec as P

HDIM = 64
LAYERS = 2
TOPK = 2
LANES = 128
FF_TILE = 512
ROW_TILE = 64
PAIRS = 2
FAST_LANE = True

ln_eps = 1e-05
in_eps = 1e-05
learn_rate = 0.02
first_decay = 0.5
second_decay = 0.5
adam_eps = 1e-08
weight_decay = 0.1
teacher_keep = 0.5
huber_beta = 1.0
score_scale = 0.125
entry_clip = 1e-05
half_type = jnp.bfloat16
full_type = jnp.float32
AXES = ("dp", "seq")


def contract(left, right, left_dim, right_dim):
    return lax.dot_general(
        left,
        right,
        (((left_dim,), (right_dim,)), ((), ())),
        preferred_element_type=full_type,
    )


def head_mask(which, width):
    lane = lax.broadcasted_iota(jnp.int32, (1, width), 1)
    return (lane // HDIM) == which


def head_part(values, which):
    return jnp.where(head_mask(which, LANES), values, jnp.zeros_like(values))


def softmax_rows(scores):
    exps = jnp.exp(scores - jnp.max(scores, axis=1, keepdims=True))
    return exps * (1.0 / jnp.sum(exps, axis=1, keepdims=True))


def attend_kernel(q_ref, k_ref, v_ref, o_ref, score_ref, prob_ref):
    tokens = q_ref.shape[1]
    heads = LANES // HDIM
    for start in range(0, q_ref.shape[2], LANES):
        cols = slice(start, start + LANES)
        queries = q_ref[0, :, cols] * jnp.asarray(score_scale, half_type)
        for which in range(heads):
            score_ref[which] = contract(head_part(queries, which), k_ref[0, :, cols], 1, 1)
        for which in range(heads):
            for row in range(0, tokens, ROW_TILE):
                rows = slice(row, row + ROW_TILE)
                prob_ref[which, rows] = softmax_rows(score_ref[which, rows]).astype(half_type)
        mixed = None
        for which in range(heads):
            out = contract(prob_ref[which], v_ref[0, :, cols], 1, 0)
            mixed = out if mixed is None else jnp.where(head_mask(which, LANES), out, mixed)
        o_ref[0, :, cols] = mixed.astype(half_type)


def attend_back_kernel(q_ref, k_ref, v_ref, do_ref, dq_ref, dk_ref, dv_ref, *scratch):
    score_ref, grad_ref, prob_ref, back_ref = scratch
    tokens = q_ref.shape[1]
    heads = LANES // HDIM
    for start in range(0, q_ref.shape[2], LANES):
        cols = slice(start, start + LANES)
        queries = q_ref[0, :, cols] * jnp.asarray(score_scale, half_type)
        keys_now = k_ref[0, :, cols]
        grad_out = do_ref[0, :, cols]
        for which in range(heads):
            score_ref[which] = contract(head_part(queries, which), keys_now, 1, 1)
            grad_ref[which] = contract(head_part(grad_out, which), v_ref[0, :, cols], 1, 1)
        for which in range(heads):
            for row in range(0, tokens, ROW_TILE):
                rows = slice(row, row + ROW_TILE)
                probs = softmax_rows(score_ref[which, rows])
                prob_ref[which, rows] = probs.astype(half_type)
                prods = probs * grad_ref[which, rows]
                back_ref[which, rows] = (
                    prods - probs * jnp.sum(prods, axis=1, keepdims=True)
                ).astype(half_type)
        turned_k = []
        turned_v = []
        grad_q = None
        for which in range(heads):
            part = slice(which * HDIM, (which + 1) * HDIM)
            turned_v.append(contract(grad_out, prob_ref[which], 0, 0)[part])
            turned_k.append(contract(queries, back_ref[which], 0, 0)[part])
            out = contract(back_ref[which], keys_now, 1, 0)
            grad_q = out if grad_q is None else jnp.where(head_mask(which, LANES), out, grad_q)
        dq_ref[0, :, cols] = (grad_q * score_scale).astype(half_type)
        dk_ref[0, :, cols] = jnp.concatenate(turned_k, axis=0).T.astype(half_type)
        dv_ref[0, :, cols] = jnp.concatenate(turned_v, axis=0).T.astype(half_type)


def attend(projected):
    seqs, tokens, width3 = projected.shape
    width = width3 // 3
    wide = PAIRS * LANES
    blocks = width // wide
    specs = [
        pl.BlockSpec((1, tokens, wide), lambda s, j, off=off: (s, 0, off * blocks + j))
        for off in range(3)
    ]
    heads = LANES // HDIM
    return pl.pallas_call(
        attend_kernel,
        grid=(seqs, blocks),
        in_specs=specs,
        out_specs=pl.BlockSpec((1, tokens, wide), lambda s, j: (s, 0, j)),
        out_shape=jax.ShapeDtypeStruct((seqs, tokens, width), half_type),
        scratch_shapes=[
            pltpu.VMEM((heads, tokens, tokens), full_type),
            pltpu.VMEM((heads, tokens, tokens), half_type),
        ],
        cost_estimate=pl.CostEstimate(
            flops=16 * seqs * tokens * tokens * width,
            transcendentals=seqs * tokens * tokens * width // HDIM,
            bytes_accessed=8 * seqs * tokens * width,
        ),
        compiler_params=grant(16),
        name="attend",
    )(projected, projected, projected)


def attend_back(projected, grad_mixed, seq, into=()):
    seqs, tokens, width3 = projected.shape
    width = width3 // 3
    wide = PAIRS * LANES
    blocks = width // wide
    block = pl.BlockSpec((1, tokens, wide), lambda j: (seq, 0, j))
    specs = [
        pl.BlockSpec((1, tokens, wide), lambda j, off=off: (seq, 0, off * blocks + j))
        for off in range(3)
    ]
    heads = LANES // HDIM
    skip = len(into)

    def kernel(q_ref, k_ref, v_ref, do_ref, *refs):
        attend_back_kernel(q_ref, k_ref, v_ref, do_ref, *refs[skip:])

    shape = kept_shape((seqs, tokens, width), half_type)
    return pl.pallas_call(
        kernel,
        grid=(blocks,),
        in_specs=specs + [block] + [pl.BlockSpec(memory_space=pl.ANY)] * skip,
        out_specs=[block, block, block],
        out_shape=[shape, shape, shape],
        input_output_aliases={4 + place: place for place in range(skip)},
        scratch_shapes=[
            pltpu.VMEM((heads, tokens, tokens), kind)
            for kind in (full_type, full_type, half_type, half_type)
        ],
        cost_estimate=pl.CostEstimate(
            flops=32 * tokens * tokens * width,
            transcendentals=tokens * tokens * width // HDIM,
            bytes_accessed=14 * tokens * width,
        ),
        compiler_params=grant(20),
        name="attend_back",
    )(projected, projected, projected, grad_mixed, *into)


def normal_cdf(values):
    return 0.5 + 0.5 * lax.erf(values * (0.5**0.5))


def whole_block(shape):
    zeros = (0,) * len(shape)
    return pl.BlockSpec(shape, lambda *_: zeros, pipeline_mode=pl.Buffered(1))


def grant(mib):
    return pltpu.CompilerParams(vmem_limit_bytes=mib << 20)


def stacked(*refs):
    return jnp.concatenate([ref[...] for ref in refs], axis=0)


def unit_of(values):
    centre = values - jnp.mean(values, axis=1, keepdims=True)
    inv_scale = lax.rsqrt(jnp.mean(centre * centre, axis=1, keepdims=True) + ln_eps)
    return centre * inv_scale, inv_scale


def norm_back(grad_out, gain, values):
    unit, inv_scale = unit_of(values)
    grad_unit = grad_out * gain
    inner_mean = jnp.mean(grad_unit, axis=1, keepdims=True)
    along_mean = jnp.mean(grad_unit * unit, axis=1, keepdims=True)
    grad_in = (grad_unit - inner_mean - unit * along_mean) * inv_scale
    return grad_in, jnp.sum(grad_out * unit, axis=0, keepdims=True)


def half(values):
    return values.astype(half_type)


def shape_of(shape, kind):
    return jax.ShapeDtypeStruct(shape, kind)


def kept_shape(shape, kind):
    return pltpu.HBM(shape, kind)


def cost(flops, moved):
    return pl.CostEstimate(flops=flops, transcendentals=0, bytes_accessed=moved)


def in_hbm(value):
    return pltpu.with_memory_space_constraint(value, pltpu.HBM)


class Weight:
    def __init__(self, blocks, start, cols):
        self.blocks, self.start, self.cols = list(blocks), start, cols

    def specs(self, width, index=lambda j: j):
        base = self.start // width
        spec = pl.BlockSpec(
            (self.blocks[0].shape[0], width), lambda j, base=base: (0, base + index(j))
        )
        return [spec] * len(self.blocks)

    def refs(self):
        return [in_hbm(block) for block in self.blocks]


def embed(patches, mask, mover, weight, small, keep_patches):
    rows, width = patches.shape
    tokens = rows // 2
    masked = mask is not None

    def kernel(*refs):
        x_ref, mover_ref = refs[:2]
        w_refs, small_refs, refs = refs[2:6], refs[6:10], refs[10:]
        if masked:
            mask_ref, refs = refs[0], refs[1:]
        h_ref, table_ref = refs[:2]
        x_rel = half(contract(x_ref[...], mover_ref[...], 1, 0))
        if keep_patches:
            refs[2][...] = x_rel
        w_rel = half(contract(stacked(*w_refs), mover_ref[...], 1, 0))
        small_t = stacked(*small_refs).astype(full_type).T
        posit = small_t[:tokens]
        table = small_t[tokens : tokens + 8]
        table_ref[...] = table
        states = contract(x_rel, w_rel, 1, 0)
        for seq in range(rows // tokens):
            part = slice(seq * tokens, (seq + 1) * tokens)
            state = states[part]
            if masked:
                flag = mask_ref[part, :]
                state = state * (1.0 - flag) + flag * table[2 * LAYERS + 1 : 2 * LAYERS + 2]
            h_ref[part, :] = state + posit

    outs = [shape_of((rows, width), full_type), shape_of((8, width), full_type)]
    if keep_patches:
        outs.append(kept_shape((rows, width), half_type))
    args = [patches, mover] + weight.refs() + list(small) + ([mask] if masked else [])
    specs = [whole_block(patches.shape), whole_block(mover.shape)] + weight.specs(width)
    specs += [whole_block(part.shape) for part in small]
    if masked:
        specs.append(whole_block(mask.shape))
    return pl.pallas_call(
        kernel,
        grid=(1,),
        in_specs=specs,
        out_specs=[whole_block(out.shape) for out in outs],
        out_shape=outs,
        cost_estimate=cost(6 * rows * width * width, 12 * rows * width),
        compiler_params=grant(28),
        name="embed",
    )(*args)


def norm_project(states, table, row, weight, keep):
    rows, width = states.shape
    steps = weight.cols // width

    def kernel(h_ref, table_ref, own_ref, own2_ref, got_ref, got2_ref, out_ref, a_ref):
        @pl.when(pl.program_id(0) == 0)
        def _():
            unit, _ = unit_of(h_ref[...])
            a_ref[...] = half(unit * table_ref[row : row + 1, :])

        out_ref[...] = half(contract(a_ref[...], stacked(own_ref, own2_ref, got_ref, got2_ref), 1, 0))

    outs = [shape_of((rows, weight.cols), half_type)]
    out_specs = [pl.BlockSpec((rows, width), lambda j: (0, j))]
    scratch = []
    if keep:
        outs.append(kept_shape((rows, width), half_type))
        out_specs.append(whole_block((rows, width)))
    else:
        scratch.append(pltpu.VMEM((rows, width), half_type))
    return pl.pallas_call(
        kernel,
        grid=(steps,),
        in_specs=[whole_block(states.shape), whole_block(table.shape)] + weight.specs(width),
        out_specs=out_specs,
        out_shape=outs,
        scratch_shapes=scratch,
        cost_estimate=cost(2 * rows * width * weight.cols, 12 * rows * width),
        compiler_params=grant(24),
        name="norm_project",
    )(states, table, *weight.refs())


def mix_out(mixed, states, mover, table, row, weight, keep):
    rows, width = states.shape
    tile = rows // 2

    def kernel(o_ref, h_ref, mover_ref, table_ref, own_ref, own2_ref, got_ref, got2_ref, m_ref, b_ref, *rest):
        if keep:
            rel_ref, w_ref = rest
        else:
            (w_ref,) = rest

        @pl.when(pl.program_id(0) == 0)
        def _():
            w_ref[...] = half(contract(stacked(own_ref, own2_ref, got_ref, got2_ref), mover_ref[...], 1, 0))

        mixed_rel = half(contract(o_ref[...], mover_ref[...], 1, 0))
        if keep:
            rel_ref[...] = mixed_rel
        middle = h_ref[...] + contract(mixed_rel, w_ref[...], 1, 0)
        m_ref[...] = middle
        unit, _ = unit_of(middle)
        b_ref[...] = half(unit * table_ref[row : row + 1, :])

    part = pl.BlockSpec((tile, width), lambda j: (j, 0))
    outs = [shape_of((rows, width), full_type), shape_of((rows, width), half_type)]
    out_specs = [part, part]
    scratch = []
    if keep:
        outs += [kept_shape((rows, width), half_type), kept_shape((width, width), half_type)]
        out_specs += [part, whole_block((width, width))]
    else:
        scratch.append(pltpu.VMEM((width, width), half_type))
    return pl.pallas_call(
        kernel,
        grid=(2,),
        in_specs=[part, part, whole_block(mover.shape), whole_block(table.shape)]
        + weight.specs(width, lambda j: 0),
        out_specs=out_specs,
        out_shape=outs,
        scratch_shapes=scratch,
        cost_estimate=cost(6 * rows * width * width, 14 * rows * width),
        compiler_params=grant(24),
        name="mix_out",
    )(mixed, states, mover, table, *weight.refs())


def feed_forward(normed, middle, w_up, w_down, keep):
    rows, width = middle.shape
    tile = FF_TILE
    steps = w_up.cols // tile

    def kernel(b_ref, m_ref, uown_ref, uown2_ref, ugot_ref, ugot2_ref, down_ref, down2_ref, dgot_ref, dgot2_ref, out_ref, *rest):
        step = pl.program_id(0)
        hidden = contract(b_ref[...], stacked(uown_ref, uown2_ref, ugot_ref, ugot2_ref), 1, 0)
        cdf = normal_cdf(hidden)
        active = half(hidden * cdf)
        if keep:
            rest[0][...] = active
            rest[1][...] = cdf + hidden * (
                jnp.exp(-0.5 * hidden * hidden) * ((0.5 / jnp.pi) ** 0.5)
            )
        part = contract(active, stacked(down_ref, down2_ref, dgot_ref, dgot2_ref), 1, 1)

        @pl.when(step == 0)
        def _():
            out_ref[...] = m_ref[...] + part

        @pl.when(step > 0)
        def _():
            out_ref[...] += part

    outs = [shape_of((rows, width), full_type)]
    out_specs = [whole_block((rows, width))]
    if keep:
        outs += [kept_shape((rows, w_up.cols), half_type), kept_shape((rows, w_up.cols), full_type)]
        out_specs += [pl.BlockSpec((rows, tile), lambda j: (0, j))] * 2
    return pl.pallas_call(
        kernel,
        grid=(steps,),
        in_specs=[whole_block(normed.shape), whole_block(middle.shape)]
        + w_up.specs(tile)
        + w_down.specs(tile),
        out_specs=out_specs,
        out_shape=outs,
        cost_estimate=cost(4 * rows * width * w_up.cols, 12 * rows * width + 16 * width * w_up.cols),
        compiler_params=grant(30),
        name="feed_forward",
    )(normed, middle, *w_up.refs(), *w_down.refs())


def make_target(first, second, seqs):
    rows, width = first.shape
    tokens = rows // seqs
    cols = width // 2

    def kernel(one_ref, two_ref, out_ref):
        total = None
        for ref in (one_ref, two_ref):
            values = ref[...]
            centre = values - jnp.mean(values, axis=0, keepdims=True)
            variance = jnp.mean(centre * centre, axis=0, keepdims=True)
            term = centre * lax.rsqrt(variance + in_eps)
            total = term if total is None else total + term
        out_ref[...] = total * (1.0 / TOPK)

    block = pl.BlockSpec((tokens, cols), lambda s, j: (s, j))
    return pl.pallas_call(
        kernel,
        grid=(seqs, 2),
        in_specs=[block, block],
        out_specs=block,
        out_shape=shape_of((rows, width), full_type),
        cost_estimate=cost(20 * rows * width, 12 * rows * width),
        compiler_params=grant(16),
        name="make_target",
    )(first, second)


def head_step(states, table, mover, weight, target, mask, total_masked):
    rows, width = states.shape
    tile = rows // 2
    final_row = 2 * LAYERS

    def kernel(
        h_ref, table_ref, mover_ref, own_ref, own2_ref, got_ref, got2_ref, t_ref, mask_ref,
        flow_ref, f_ref, pred_ref, gain_ref, loss_ref, w_ref,
    ):
        step = pl.program_id(0)

        @pl.when(step == 0)
        def _():
            w_ref[...] = half(contract(stacked(own_ref, own2_ref, got_ref, got2_ref), mover_ref[...], 1, 0))
            gain_ref[...] = jnp.zeros_like(gain_ref)
            loss_ref[...] = jnp.zeros_like(loss_ref)

        states_now = h_ref[...]
        gain = table_ref[final_row : final_row + 1, :]
        unit, _ = unit_of(states_now)
        final_normed = half(unit * gain)
        f_ref[...] = final_normed
        flag = mask_ref[...]
        differ = contract(final_normed, w_ref[...], 1, 0) - t_ref[...]
        magnitude = jnp.abs(differ)
        terms = jnp.where(
            magnitude < huber_beta,
            0.5 * differ * differ / huber_beta,
            magnitude - 0.5 * huber_beta,
        )
        loss_ref[...] += jnp.sum(terms * flag, axis=0, keepdims=True)
        grad_pred = half(flag * jnp.clip(differ / huber_beta, -1.0, 1.0) / total_masked)
        pred_ref[...] = half(contract(grad_pred, mover_ref[...], 1, 1))
        grad_in, grad_gain = norm_back(contract(grad_pred, w_ref[...], 1, 1), gain, states_now)
        flow_ref[...] = grad_in
        gain_ref[...] += grad_gain

    part = pl.BlockSpec((tile, width), lambda j: (j, 0))
    row = whole_block((1, width))
    return pl.pallas_call(
        kernel,
        grid=(2,),
        in_specs=[part, whole_block(table.shape), whole_block(mover.shape)]
        + weight.specs(width, lambda j: 0)
        + [part, pl.BlockSpec((tile, 1), lambda j: (j, 0))],
        out_specs=[part, part, part, row, row],
        out_shape=[
            shape_of((rows, width), full_type),
            kept_shape((rows, width), half_type),
            kept_shape((rows, width), half_type),
            shape_of((1, width), full_type),
            shape_of((1, width), full_type),
        ],
        scratch_shapes=[pltpu.VMEM((width, width), half_type)],
        cost_estimate=cost(8 * rows * width * width, 16 * rows * width),
        compiler_params=grant(30),
        name="head_step",
    )(states, table, mover, *weight.refs(), target, mask)


def feed_back(flow, slope, middle, table, row, w_up, w_down):
    rows, width = flow.shape
    tile = FF_TILE
    steps = w_up.cols // tile

    def kernel(
        flow_ref, slope_ref, m_ref, table_ref, uown_ref, uown2_ref, ugot_ref, ugot2_ref, down_ref, down2_ref, dgot_ref, dgot2_ref,
        du_ref, dy_ref, dm_ref, dz_ref, gain_ref, acc_ref,
    ):
        step = pl.program_id(0)

        @pl.when(step == 0)
        def _():
            dy_ref[...] = half(flow_ref[...])

        grad_active = contract(dy_ref[...], stacked(down_ref, down2_ref, dgot_ref, dgot2_ref), 1, 0)
        grad_hidden = half(grad_active * slope_ref[...])
        du_ref[...] = grad_hidden
        part = contract(grad_hidden, stacked(uown_ref, uown2_ref, ugot_ref, ugot2_ref), 1, 1)

        @pl.when(step == 0)
        def _():
            acc_ref[...] = part

        @pl.when(step > 0)
        def _():
            acc_ref[...] += part

        @pl.when(step == steps - 1)
        def _():
            grad_in, grad_gain = norm_back(
                acc_ref[...], table_ref[row : row + 1, :], m_ref[...]
            )
            grad_middle = flow_ref[...] + grad_in
            dm_ref[...] = grad_middle
            dz_ref[...] = half(grad_middle)
            gain_ref[...] = grad_gain

    full = whole_block((rows, width))
    column = pl.BlockSpec((rows, tile), lambda j: (0, j))
    return pl.pallas_call(
        kernel,
        grid=(steps,),
        in_specs=[full, column, full, whole_block(table.shape)]
        + w_up.specs(tile)
        + w_down.specs(tile),
        out_specs=[column, full, full, full, whole_block((1, width))],
        out_shape=[
            kept_shape((rows, w_up.cols), half_type),
            kept_shape((rows, width), half_type),
            shape_of((rows, width), full_type),
            shape_of((rows, width), half_type),
            shape_of((1, width), full_type),
        ],
        scratch_shapes=[pltpu.VMEM((rows, width), full_type)],
        cost_estimate=cost(4 * rows * width * w_up.cols, 40 * rows * width + 8 * width * w_up.cols),
        compiler_params=grant(32),
        name="feed_back",
    )(flow, slope, middle, table, *w_up.refs(), *w_down.refs())


def mix_back(grad_branch, w_rel, mover):
    rows, width = grad_branch.shape
    tile = rows // 2

    def kernel(dz_ref, w_ref, mover_ref, do_ref, nat_ref):
        branch = dz_ref[...]
        grad_rel = half(contract(branch, w_ref[...], 1, 1))
        do_ref[...] = half(contract(grad_rel, mover_ref[...], 1, 1))
        nat_ref[...] = half(contract(branch, mover_ref[...], 1, 1))

    part = pl.BlockSpec((tile, width), lambda j: (j, 0))
    square = whole_block((width, width))
    return pl.pallas_call(
        kernel,
        grid=(2,),
        in_specs=[part, square, square],
        out_specs=[part, part],
        out_shape=[shape_of((rows, width), half_type), kept_shape((rows, width), half_type)],
        cost_estimate=cost(6 * rows * width * width, 10 * rows * width),
        compiler_params=grant(16),
        name="mix_back",
    )(grad_branch, w_rel, mover)


def project_back(grads, grad_middle, states, table, row, weight, mover, mask):
    rows, width = states.shape
    tile = rows // 2
    count = len(grads)
    first = mask is not None

    def kernel(*refs):
        grad_refs, refs = refs[:count], refs[count:]
        w_refs, refs = refs[: 4 * count], refs[4 * count :]
        dm_ref, h_ref, table_ref = refs[:3]
        refs = refs[3:]
        if first:
            mover_ref, mask_ref = refs[:2]
            refs = refs[2:]
        dh_ref, gain_ref = refs[:2]
        step = pl.program_id(0)

        @pl.when(step == 0)
        def _():
            for ref in (gain_ref,) + ((refs[3],) if first else ()):
                ref[...] = jnp.zeros_like(ref)

        total = None
        for place in range(count):
            part = contract(
                grad_refs[place][...], stacked(*w_refs[4 * place : 4 * place + 4]), 1, 1
            )
            total = part if total is None else total + part
        grad_in, grad_gain = norm_back(total, table_ref[row : row + 1, :], h_ref[...])
        flow = dm_ref[...] + grad_in
        dh_ref[...] = flow
        gain_ref[...] += grad_gain
        if first:
            flag = mask_ref[...]
            refs[2][...] = half(contract(half(flow * (1.0 - flag)), mover_ref[...], 1, 1))
            refs[3][...] += jnp.sum(flow * flag, axis=0, keepdims=True)

    part = pl.BlockSpec((tile, width), lambda j: (j, 0))
    vector = whole_block((1, width))
    specs = [part] * count
    args = list(grads)
    for place in range(count):
        specs += weight.specs(width, lambda j, place=place: place)
        args += weight.refs()
    specs += [part, part, whole_block(table.shape)]
    args += [grad_middle, states, table]
    outs = [shape_of((rows, width), full_type), shape_of((1, width), full_type)]
    out_specs = [part, vector]
    if first:
        specs += [whole_block(mover.shape), pl.BlockSpec((tile, 1), lambda j: (j, 0))]
        args += [mover, mask]
        outs += [kept_shape((rows, width), half_type), shape_of((1, width), full_type)]
        out_specs += [part, vector]
    return pl.pallas_call(
        kernel,
        grid=(2,),
        in_specs=specs,
        out_specs=out_specs,
        out_shape=outs,
        cost_estimate=cost(2 * rows * width * weight.cols, 22 * rows * width),
        compiler_params=grant(30),
        name="project_back",
    )(*args)


def weight_grads(pairs):
    rows, width = pairs[0][0].shape
    plan = []
    start = 0
    for place, (_, rights) in enumerate(pairs):
        first = start
        for right in rights:
            tiles = right.shape[1] // width
            plan.append((place, start, tiles, start == first))
            start += tiles
    total = start
    near_rows = width // 2

    def kernel(*refs):
        left_refs, refs = refs[: len(pairs)], refs[len(pairs) :]
        right_refs, refs = refs[: len(plan)], refs[len(plan) :]
        near_ref, far_ref, turned_ref = refs
        step = pl.program_id(0)
        for (place, begin, tiles, fresh), right_ref in zip(plan, right_refs):
            if fresh:

                @pl.when(step == begin)
                def _(place=place):
                    turned_ref[...] = left_refs[place][...].T

            @pl.when((step >= begin) & (step < begin + tiles))
            def _(right_ref=right_ref):
                out = contract(turned_ref[...], right_ref[...], 1, 0)
                near_ref[...] = out[:near_rows]
                far_ref[...] = half(out[near_rows:])

    specs = [whole_block((rows, width)) for _ in pairs]
    args = [left for left, _ in pairs]
    for (_, rights) in pairs:
        args += list(rights)
    for _, begin, tiles, _ in plan:
        specs.append(
            pl.BlockSpec(
                (rows, width),
                lambda j, begin=begin, tiles=tiles: (0, jnp.clip(j - begin, 0, tiles - 1)),
            )
        )
    block = pl.BlockSpec((near_rows, width), lambda j: (0, j))
    shapes = [shape_of((near_rows, total * width), kind) for kind in (full_type, half_type)]
    return tuple(
        pl.pallas_call(
            kernel,
            grid=(total,),
            in_specs=specs,
            out_specs=[block, block],
            out_shape=shapes,
            scratch_shapes=[pltpu.VMEM((width, rows), half_type)],
            cost_estimate=cost(
                2 * rows * width * width * total, width * total * (4 * width + 2 * rows)
            ),
            compiler_params=grant(30),
        name="weight_grads",
        )(*[in_hbm(arg) for arg in args])
    )


def small_grads(flow, vectors, seqs):
    rows, width = flow.shape
    tokens = rows // seqs
    cols = tokens + 8
    cols += -cols % LANES

    def kernel(flow_ref, *refs):
        vector_refs, (near_ref, far_ref) = refs[:-2], refs[-2:]
        posit = flow_ref[:tokens]
        for seq in range(1, seqs):
            posit = posit + flow_ref[seq * tokens : (seq + 1) * tokens]
        fill = jnp.zeros((cols - tokens - len(vector_refs), width), full_type)
        table = jnp.concatenate([posit] + [ref[...] for ref in vector_refs] + [fill], axis=0).T
        near_ref[...] = table[: width // 2]
        far_ref[...] = half(table[width // 2 :])

    shapes = [shape_of((width // 2, cols), kind) for kind in (full_type, half_type)]
    return tuple(
        pl.pallas_call(
            kernel,
            grid=(1,),
            in_specs=[whole_block(flow.shape)] + [whole_block((1, width)) for _ in vectors],
            out_specs=[whole_block(shape.shape) for shape in shapes],
            out_shape=shapes,
            cost_estimate=cost(2 * rows * width, 8 * rows * width),
            compiler_params=grant(16),
        name="small_grads",
        )(flow, *vectors)
    )


class Plan:
    def __init__(self):
        self.seq_size = lax.axis_size("seq")
        self.count = lax.axis_size("dp") * self.seq_size
        self.bits = self.count.bit_length() - 1
        self.early = list(range(self.bits - 1, 2, -1))

        def flips(pick):
            return [(i, i ^ (1 << pick((i >> 1) & 1))) for i in range(self.count)]

        self.stages = [flips(lambda core, b=b: b) for b in self.early]
        self.stages.append(flips(lambda core: 0 if core else 2))
        self.stages.append(flips(lambda core: 2 if core else 0))
        self.core_stage = flips(lambda core: 1)
        self.index = lax.axis_index("dp") * self.seq_size + lax.axis_index("seq")

    def swap(self, value, perm):
        return lax.ppermute(value, AXES, perm)

    def row_table(self, width):
        rows = width // self.count
        place = lax.broadcasted_iota(jnp.int32, (1, width), 1)
        spot = place // rows
        early_count = len(self.early)
        other = (spot >> (self.bits - 1)) & 1
        holder_core = ((self.index >> 1) & 1) ^ other
        block = self.index ^ (other << 1)
        for step, bit in enumerate(self.early):
            block = block ^ (((spot >> step) & 1) << bit)
        first = (spot >> early_count) & 1
        second = (spot >> (early_count + 1)) & 1
        block = block ^ jnp.where(holder_core == 0, first << 2, first)
        block = block ^ jnp.where(holder_core == 0, second, second << 2)
        return block * rows + place % rows

    def mover(self, width):
        table = self.row_table(width)
        whole = lax.broadcasted_iota(jnp.int32, (width, width), 0)
        return (whole == table).astype(half_type)


class Pump:
    def __init__(self, plan):
        self.plan = plan
        self.jobs = []

    def add(self, steps, done, ticks=()):
        self.jobs.append(
            {"steps": steps, "sends": next(steps), "done": done, "stage": 0, "ticks": dict(ticks)}
        )

    def start(self, job):
        job["gots"] = [self.plan.swap(value, perm) for value, perm in job["sends"]]
        job["left"] = job["ticks"].get(job["stage"], 1)

    def advance(self, job, gots):
        job["stage"] += 1
        job["gots"] = None
        try:
            job["sends"] = job["steps"].send(gots)
            return True
        except StopIteration as stop:
            job["done"](stop.value)
            return False

    def begin(self):
        for job in self.jobs:
            if job.get("gots") is None:
                self.start(job)

    def end(self, values=()):
        due = []
        for job in self.jobs:
            job["left"] -= 1
            if job["left"] == 0:
                due.append(job)
        flying, values = lax.optimization_barrier(([job["gots"] for job in due], values))
        over = [job for job, gots in zip(due, flying) if not self.advance(job, gots)]
        self.jobs = [job for job in self.jobs if job not in over]
        return values

    def drain(self):
        newest = self.jobs[-1]
        while self.jobs:
            self.begin()
            if self.jobs[-1] is newest:
                if self.advance(newest, newest["gots"]):
                    self.start(newest)
                else:
                    self.jobs.pop()
            self.end()


def scatter_steps(plan, pieces, narrow):
    gots = yield [(far, plan.core_stage) for _, far in pieces]
    quarter = pieces[0][0].shape[0] // 2
    sums = [
        (half(near[quarter:] + got[quarter:]), near[:quarter] + got[:quarter])
        for (near, _), got in zip(pieces, gots)
    ]
    send = jnp.concatenate([part for part, _ in sums], axis=1)
    keep = jnp.concatenate([part for _, part in sums], axis=1)
    stages = plan.stages[::-1]
    for step, perm in enumerate(stages):
        (got,) = yield [(send, perm)]
        if step == len(stages) - 1:
            return keep + got
        middle = keep.shape[0] // 2
        send = keep[middle:] + got[middle:]
        if step < narrow - 1:
            send = half(send)
        keep = keep[:middle] + got[:middle]


def adam_step(weight, first_mom, second_mom, teacher, gradient):
    first_new = first_decay * first_mom + (1.0 - first_decay) * gradient
    second_new = second_decay * second_mom + (1.0 - second_decay) * gradient * gradient
    weight_new = weight - learn_rate * (
        first_new / (jnp.sqrt(second_new) + adam_eps) + weight_decay * weight
    )
    teacher_new = teacher_keep * teacher + (1.0 - teacher_keep) * weight_new
    return (weight_new, first_new, second_new, teacher_new)


def norm_totals(edge, attn_zero, attn_one, mlp_zero, mlp_one, loss_row, width, tokens):
    stop = 4 * width

    def kernel(edge_ref, first_ref, second_ref, zero_ref, one_ref, loss_ref, out_ref):
        def square(value):
            return jnp.sum(value * value)

        small = edge_ref[:, width:]
        lane = lax.broadcasted_iota(jnp.int32, small.shape, 1)
        posit = jnp.where(lane < tokens, small, 0.0)
        vecs = jnp.where(lane >= tokens, small, 0.0)
        parts = [
            jnp.sum(loss_ref[...]),
            square(edge_ref[:, :width]) + square(second_ref[:, stop:]),
            square(first_ref[...]) + square(second_ref[:, :stop]),
            square(zero_ref[...]) + square(one_ref[...]),
            square(posit),
            square(vecs),
        ]
        row = lax.broadcasted_iota(jnp.int32, (8, LANES), 0)
        out = jnp.zeros((8, LANES), full_type)
        for place, part in enumerate(parts):
            out = jnp.where(row == place, part, out)
        out_ref[...] = out

    args = (edge, attn_zero, attn_one, mlp_zero, mlp_one, loss_row)
    return pl.pallas_call(
        kernel,
        grid=(1,),
        in_specs=[whole_block(arg.shape) for arg in args],
        out_specs=whole_block((8, LANES)),
        out_shape=shape_of((8, LANES), full_type),
        compiler_params=grant(16),
        name="norm_totals",
    )(*args)


def update(totals, edge, attn_zero, attn_one, mlp_zero, mlp_one, groups, sizes, width, tokens):
    stop = mlp_zero.shape[1]

    def kernel(total_ref, edge_ref, first_ref, second_ref, zero_ref, one_ref, *refs):
        ins, outs = refs[:20], refs[20:]

        def step(group, gradient, cols=slice(None)):
            limit = entry_clip * sizes[group] ** 0.5
            norm_value = jnp.sqrt(total_ref[group + 1 : group + 2, 0:1])
            gradient = gradient * (limit / jnp.maximum(norm_value, limit))
            weight, first, second, teacher = (
                ref[:, cols] for ref in ins[4 * group : 4 * group + 4]
            )
            news = adam_step(weight, first, second, teacher, gradient)
            for ref, new in zip(outs[4 * group : 4 * group + 4], news):
                ref[:, cols] = new

        step(0, edge_ref[:, :width], slice(0, width))
        step(0, second_ref[:, 4 * width :], slice(width, 2 * width))
        step(1, first_ref[...], slice(0, 4 * width))
        step(1, second_ref[:, : 4 * width], slice(4 * width, 8 * width))
        step(2, zero_ref[...], slice(0, stop))
        step(2, one_ref[...], slice(stop, 2 * stop))
        step(3, edge_ref[:, width : width + tokens])
        start = tokens // LANES * LANES
        turned = edge_ref[:, width + start : width + start + LANES].T
        count = ins[16].shape[0]
        step(4, turned[tokens - start : tokens - start + count])

    args = [totals, edge, attn_zero, attn_one, mlp_zero, mlp_one] + [part for group in groups for part in group]
    outs = [shape_of(part.shape, full_type) for group in groups for part in group]
    return pl.pallas_call(
        kernel,
        grid=(1,),
        in_specs=[whole_block(arg.shape) for arg in args],
        out_specs=[whole_block(out.shape) for out in outs],
        out_shape=outs,
        compiler_params=grant(40),
        name="update",
    )(*args)


def pad_lanes(value):
    extra = -value.shape[1] % LANES
    return jnp.pad(value, ((0, 0), (0, extra)))


def local(
    patches,
    masked_at,
    edge_w,
    attn_w,
    mlp_w,
    posit_w,
    vecs_w,
    edge_m,
    attn_m,
    mlp_m,
    posit_m,
    vecs_m,
    edge_v,
    attn_v,
    mlp_v,
    posit_v,
    vecs_v,
    edge_t,
    attn_t,
    mlp_t,
    posit_t,
    vecs_t,
):
    seqs, tokens, width = patches.shape
    plan = Plan()
    total_masked = seqs * plan.count * tokens // 2
    ff_width = mlp_w.shape[1] // (2 * LAYERS)
    small_cols = tokens + vecs_w.shape[1]
    flat_patch = patches.reshape(-1, width)
    mask_flat = masked_at.astype(full_type).reshape(-1, 1)
    mover = plan.mover(width)

    def shards(edge, attn, mlp, posit, vecs):
        small = pad_lanes(jnp.concatenate([posit, vecs], axis=1))
        return [edge[:, :width], edge[:, width:], small] + [
            [
                part[:, layer * part.shape[1] // LAYERS : (layer + 1) * part.shape[1] // LAYERS]
                for part in (attn, mlp)
            ]
            for layer in range(LAYERS)
        ]

    def joined(parts):
        return jnp.concatenate([half(part) for part in parts], axis=1)

    t_patch, _, t_small, t_one, t_two = shards(edge_t, attn_t, mlp_t, posit_t, vecs_t)
    s_patch, s_head, s_small, s_one, s_two = shards(edge_w, attn_w, mlp_w, posit_w, vecs_w)
    chunks = [
        [t_patch, t_one[0], t_small],
        [t_one[1]],
        t_two,
        [s_patch, s_one[0], s_small],
        [s_one[1]],
        [s_two[0], s_head],
        [s_two[1]],
    ]
    groups = [[0], [1], [2], [3], [4, 5, 6]]
    group_start = [0, 1, 2, 3, 4]

    def attn_weights(blocks, start):
        return Weight(blocks, start, 3 * width), Weight(blocks, start + 3 * width, width)

    def mlp_weights(blocks, start):
        return Weight(blocks, start, ff_width), Weight(blocks, start + ff_width, ff_width)

    def small_of(blocks):
        start = blocks[0].shape[1] - t_small.shape[1]
        return [block[:, start:] for block in blocks]

    def finish(blocks):
        return list(blocks) + [plan.swap(blocks[1], plan.core_stage)]

    def attend_forward(states, table, layer, w_qkv, w_out, keep, outs=None):
        if outs is None:
            outs = norm_project(states, table, layer, w_qkv, keep)
        projected = outs[0].reshape(seqs, tokens, w_qkv.cols)
        mixed = attend(projected).reshape(-1, width)
        results = mix_out(mixed, states, mover, table, LAYERS + layer, w_out, keep)
        if keep:
            return results[0], results[1], (states, outs[1], projected) + tuple(results[2:])
        return results[0], results[1], ()

    saved_attn = [None] * LAYERS
    saved_mlp = [None] * LAYERS

    def segment_t0(_, blocks):
        patch = Weight(blocks, 0, width)
        states, table, patch_rel = embed(
            flat_patch, None, mover, patch, small_of(blocks), True
        )
        weights = attn_weights(blocks, width)
        return states, table, patch_rel, norm_project(states, table, 0, weights[0], False)

    def segment_t0_rest(values, blocks):
        states, table, patch_rel, outs = values
        weights = attn_weights(blocks, width)
        middle, normed, _ = attend_forward(states, table, 0, *weights, False, outs)
        return middle, normed, table, patch_rel

    def segment_t1(values, blocks):
        middle, normed, table, patch_rel = values
        (states,) = feed_forward(normed, middle, *mlp_weights(blocks, 0), False)
        return states, table, patch_rel

    def segment_t2(values, blocks):
        first, table, patch_rel = values
        middle, normed, _ = attend_forward(first, table, 1, *attn_weights(blocks, 0), False)
        (second,) = feed_forward(normed, middle, *mlp_weights(blocks, 4 * width), False)
        return make_target(first, second, seqs), patch_rel

    def segment_s0(values, blocks):
        target, patch_rel = values
        patch = Weight(blocks, 0, width)
        states, table = embed(flat_patch, mask_flat, mover, patch, small_of(blocks), False)
        weights = attn_weights(blocks, width)
        middle, normed, saved = attend_forward(states, table, 0, *weights, True)
        saved_attn[0] = (weights[0], saved)
        return target, patch_rel, table, middle, normed

    def segment_s1(values, blocks):
        target, patch_rel, table, middle, normed = values
        weights = mlp_weights(blocks, 0)
        states, active, slope = feed_forward(normed, middle, *weights, True)
        saved_mlp[0] = (weights, middle, normed, active, slope)
        return target, patch_rel, table, states

    def segment_s2(values, blocks):
        target, patch_rel, table, states = values
        weights = attn_weights(blocks, 0)
        middle, normed, saved = attend_forward(states, table, 1, *weights, True)
        saved_attn[1] = (weights[0], saved)
        return target, patch_rel, table, middle, normed, blocks

    segments = [segment_t0_rest, segment_t1, segment_t2, segment_s0, segment_s1, segment_s2]
    early = len(plan.early)
    group_values = [joined([part for c in group for part in chunks[c]]) for group in groups]
    own = [None] * len(chunks)
    blocks = [None] * len(chunks)
    values = ()
    for tick in range(len(chunks) + early + 1):
        sends = {}
        for group, start in enumerate(group_start):
            if 0 <= tick - start < early:
                sends["early", group] = (group_values[group], plan.stages[tick - start])
        for chunk in range(len(chunks)):
            if tick == chunk + early:
                sends["first", chunk] = (own[chunk], plan.stages[early])
            if tick == chunk + early + 1:
                sends["second", chunk] = (own[chunk], plan.stages[early + 1])
                sends["core", chunk] = (own[chunk], plan.core_stage)
        gots = {key: plan.swap(value, perm) for key, (value, perm) in sends.items()}
        place = tick - early - 2
        if 0 <= place < len(segments):
            values = segments[place](values, finish(blocks[place]))
        if tick == early + 1:
            first_blocks = (own[0], gots["second", 0], gots["core", 0])
            values = segment_t0(values, finish(first_blocks))
        apart = {key: got for key, got in gots.items() if FAST_LANE and key[1] == 0 and tick}
        gots = {key: got for key, got in gots.items() if key not in apart}
        later = [g for g in range(len(groups)) if group_start[g] > tick]
        idle = [c for c in range(1, len(chunks)) if own[c] is not None and c + early > tick]
        gots, values, held, held_own, _ = lax.optimization_barrier(
            (gots, values, [group_values[g] for g in later], [own[c] for c in idle], apart)
        )
        for g, value in zip(later, held):
            group_values[g] = value
        for c, value in zip(idle, held_own):
            own[c] = value
        gots.update(apart)
        for (kind, index), got in gots.items():
            if kind == "early":
                group_values[index] = jnp.concatenate([group_values[index], got], axis=0)
                if tick - group_start[index] == early - 1:
                    start = 0
                    for chunk in groups[index]:
                        stop = start + sum(part.shape[1] for part in chunks[chunk])
                        own[chunk] = group_values[index][:, start:stop]
                        start = stop
            elif kind == "first":
                own[index] = jnp.concatenate([own[index], got], axis=0)
        for chunk in range(len(chunks)):
            if ("second", chunk) in gots:
                blocks[chunk] = (own[chunk], gots["second", chunk], gots["core", chunk])
    pump = Pump(plan)
    target, patch_rel, table, middle, normed, head_blocks = values
    weights = mlp_weights(finish(blocks[-1]), 0)
    states, active, slope = feed_forward(normed, middle, *weights, True)
    saved_mlp[1] = (weights, middle, normed, active, slope)
    flow, final_normed, grad_pred, grad_gain_final, loss_row = head_step(
        states,
        table,
        mover,
        Weight(head_blocks, 4 * width, width),
        target,
        mask_flat,
        total_masked,
    )

    gain_ones = [None] * LAYERS
    gain_twos = [None] * LAYERS
    shards = {}
    last_stage = len(plan.stages)

    def send_off(name, pieces, narrow, ticks=()):
        pump.add(
            scatter_steps(plan, pieces, narrow), lambda out: shards.__setitem__(name, out), ticks
        )

    for layer in reversed(range(LAYERS)):
        w_qkv, (states, normed_one, projected, mixed_rel, w_out_rel) = saved_attn[layer]
        (w_up, w_down), middle, normed_two, active, slope = saved_mlp[layer]
        pump.begin()
        grad_hidden, grad_down, grad_middle, grad_branch, gain_twos[layer] = feed_back(
            flow, slope, middle, table, LAYERS + layer, w_up, w_down
        )
        grad_hidden, grad_down, grad_middle, grad_branch = pump.end(
            (grad_hidden, grad_down, grad_middle, grad_branch)
        )
        pump.begin()
        piece = weight_grads([(normed_two, [grad_hidden]), (grad_down, [active])])
        piece, grad_branch = pump.end((piece, grad_branch))
        send_off(
            ("mlp", layer), [piece], 3, {1: 2, last_stage: 2} if layer else {last_stage: 2}
        )
        pump.begin()
        grad_mixed, branch_whole = mix_back(grad_branch, w_out_rel, mover)
        grad_mixed = grad_mixed.reshape(seqs, tokens, width)
        grad_proj = ()
        for seq in range(seqs - 1):
            grad_proj = attend_back(projected, grad_mixed, seq, tuple(grad_proj))
        grad_proj, grad_mixed, branch_whole = pump.end((grad_proj, grad_mixed, branch_whole))
        pump.begin()
        grad_proj = attend_back(projected, grad_mixed, seqs - 1, tuple(grad_proj))
        grad_proj = [part.reshape(-1, width) for part in grad_proj]
        pairs = [(normed_one, grad_proj), (mixed_rel, [branch_whole])]
        if layer == 0:
            piece = weight_grads(pairs)
            piece, grad_proj = pump.end((piece, grad_proj))
            send_off(("attn", 0), [piece], 3)
            pump.begin()
        results = project_back(
            grad_proj,
            grad_middle,
            states,
            table,
            layer,
            w_qkv,
            mover,
            None if layer else mask_flat,
        )
        flow, gain_ones[layer] = results[:2]
        if layer:
            flow, grad_proj = pump.end((flow, grad_proj))
            pairs = [(normed_one, grad_proj), (mixed_rel, [branch_whole])]
            pairs.append((final_normed, [grad_pred]))
            pump.begin()
            piece = weight_grads(pairs)
            piece, flow = pump.end((piece, flow))
            send_off(("attn", layer), [piece], 2)
    grad_embed, grad_maskvec = results[2:]
    vectors = gain_ones + gain_twos + [grad_gain_final, grad_maskvec]
    pieces = pump.end(
        [weight_grads([(patch_rel, [grad_embed])]), small_grads(flow, vectors, seqs)]
    )
    send_off("edge", pieces, 2)
    pump.drain()
    pieces = (
        shards["edge"],
        shards["attn", 0],
        shards["attn", 1],
        shards["mlp", 0],
        shards["mlp", 1],
    )
    totals = norm_totals(*pieces, loss_row, width, tokens)
    for perm in [plan.core_stage] + plan.stages:
        totals = totals + plan.swap(totals, perm)
    groups = [
        (edge_w, edge_m, edge_v, edge_t),
        (attn_w, attn_m, attn_v, attn_t),
        (mlp_w, mlp_m, mlp_v, mlp_t),
        (posit_w, posit_m, posit_v, posit_t),
        (vecs_w.T, vecs_m.T, vecs_v.T, vecs_t.T),
    ]
    sizes = [group[0].size * plan.count for group in groups]
    news = update(totals, *pieces, groups, sizes, width, tokens)
    news = [
        [news[4 * group + part] for group in range(4)] + [news[16 + part].T] for part in range(4)
    ]
    return (totals[0, 0] / total_masked,) + tuple(new for part in news for new in part)


def solution(mesh):
    rows = P(AXES, None)
    in_specs = (P(AXES, None, None),) + (rows,) * 21
    out_specs = (P(),) + (rows,) * 20
    return jax.shard_map(local, mesh=mesh, in_specs=in_specs, out_specs=out_specs, check_vma=False)
```

```python
import jax
import jax.numpy as jnp
from jax import lax
from jax.experimental import pallas as pl
from jax.experimental.pallas import tpu as pltpu
from jax.sharding import PartitionSpec as P

HDIM = 64
LAYERS = 2
TOPK = 2
LANES = 128
FF_TILE = 512
SMALL_TILE = 256
ROW_TILE = 64
PAIRS = 2
FAST_LANE = True

ln_eps = 1e-05
in_eps = 1e-05
learn_rate = 0.02
first_decay = 0.5
second_decay = 0.5
adam_eps = 1e-08
weight_decay = 0.1
teacher_keep = 0.5
huber_beta = 1.0
score_scale = 0.125
entry_clip = 1e-05
half_type = jnp.bfloat16
full_type = jnp.float32
AXES = ("dp", "seq")


def contract(left, right, left_dim, right_dim):
    return lax.dot_general(
        left,
        right,
        (((left_dim,), (right_dim,)), ((), ())),
        preferred_element_type=full_type,
    )


def head_mask(which, width):
    lane = lax.broadcasted_iota(jnp.int32, (1, width), 1)
    return (lane // HDIM) == which


def head_part(values, which):
    return jnp.where(head_mask(which, LANES), values, jnp.zeros_like(values))


def softmax_rows(scores):
    exps = jnp.exp(scores - jnp.max(scores, axis=1, keepdims=True))
    return exps * (1.0 / jnp.sum(exps, axis=1, keepdims=True))


def attend_kernel(q_ref, k_ref, v_ref, o_ref, score_ref, prob_ref):
    tokens = q_ref.shape[1]
    heads = LANES // HDIM
    for start in range(0, q_ref.shape[2], LANES):
        cols = slice(start, start + LANES)
        queries = q_ref[0, :, cols] * jnp.asarray(score_scale, half_type)
        for which in range(heads):
            score_ref[which] = contract(head_part(queries, which), k_ref[0, :, cols], 1, 1)
        for which in range(heads):
            for row in range(0, tokens, ROW_TILE):
                rows = slice(row, row + ROW_TILE)
                prob_ref[which, rows] = softmax_rows(score_ref[which, rows]).astype(half_type)
        mixed = None
        for which in range(heads):
            out = contract(prob_ref[which], v_ref[0, :, cols], 1, 0)
            mixed = out if mixed is None else jnp.where(head_mask(which, LANES), out, mixed)
        o_ref[0, :, cols] = mixed.astype(half_type)


def attend_back_kernel(q_ref, k_ref, v_ref, do_ref, dq_ref, dk_ref, dv_ref, *scratch):
    score_ref, grad_ref, prob_ref, back_ref = scratch
    tokens = q_ref.shape[1]
    heads = LANES // HDIM
    for start in range(0, q_ref.shape[2], LANES):
        cols = slice(start, start + LANES)
        queries = q_ref[0, :, cols] * jnp.asarray(score_scale, half_type)
        keys_now = k_ref[0, :, cols]
        grad_out = do_ref[0, :, cols]
        for which in range(heads):
            score_ref[which] = contract(head_part(queries, which), keys_now, 1, 1)
            grad_ref[which] = contract(head_part(grad_out, which), v_ref[0, :, cols], 1, 1)
        for which in range(heads):
            for row in range(0, tokens, ROW_TILE):
                rows = slice(row, row + ROW_TILE)
                probs = softmax_rows(score_ref[which, rows])
                prob_ref[which, rows] = probs.astype(half_type)
                prods = probs * grad_ref[which, rows]
                back_ref[which, rows] = (
                    prods - probs * jnp.sum(prods, axis=1, keepdims=True)
                ).astype(half_type)
        turned_k = []
        turned_v = []
        grad_q = None
        for which in range(heads):
            part = slice(which * HDIM, (which + 1) * HDIM)
            turned_v.append(contract(grad_out, prob_ref[which], 0, 0)[part])
            turned_k.append(contract(queries, back_ref[which], 0, 0)[part])
            out = contract(back_ref[which], keys_now, 1, 0)
            grad_q = out if grad_q is None else jnp.where(head_mask(which, LANES), out, grad_q)
        dq_ref[0, :, cols] = (grad_q * score_scale).astype(half_type)
        dk_ref[0, :, cols] = jnp.concatenate(turned_k, axis=0).T.astype(half_type)
        dv_ref[0, :, cols] = jnp.concatenate(turned_v, axis=0).T.astype(half_type)


def attend(projected):
    seqs, tokens, width3 = projected.shape
    width = width3 // 3
    wide = PAIRS * LANES
    blocks = width // wide
    specs = [
        pl.BlockSpec((1, tokens, wide), lambda s, j, off=off: (s, 0, off * blocks + j))
        for off in range(3)
    ]
    heads = LANES // HDIM
    return pl.pallas_call(
        attend_kernel,
        grid=(seqs, blocks),
        in_specs=specs,
        out_specs=pl.BlockSpec((1, tokens, wide), lambda s, j: (s, 0, j)),
        out_shape=jax.ShapeDtypeStruct((seqs, tokens, width), half_type),
        scratch_shapes=[
            pltpu.VMEM((heads, tokens, tokens), full_type),
            pltpu.VMEM((heads, tokens, tokens), half_type),
        ],
        cost_estimate=pl.CostEstimate(
            flops=16 * seqs * tokens * tokens * width,
            transcendentals=seqs * tokens * tokens * width // HDIM,
            bytes_accessed=8 * seqs * tokens * width,
        ),
        compiler_params=grant(16),
        name="attend",
    )(projected, projected, projected)


def attend_back(projected, grad_mixed, seq, into=()):
    seqs, tokens, width3 = projected.shape
    width = width3 // 3
    wide = PAIRS * LANES
    blocks = width // wide
    block = pl.BlockSpec((1, tokens, wide), lambda j: (seq, 0, j))
    specs = [
        pl.BlockSpec((1, tokens, wide), lambda j, off=off: (seq, 0, off * blocks + j))
        for off in range(3)
    ]
    heads = LANES // HDIM
    skip = len(into)

    def kernel(q_ref, k_ref, v_ref, do_ref, *refs):
        attend_back_kernel(q_ref, k_ref, v_ref, do_ref, *refs[skip:])

    shape = kept_shape((seqs, tokens, width), half_type)
    return pl.pallas_call(
        kernel,
        grid=(blocks,),
        in_specs=specs + [block] + [pl.BlockSpec(memory_space=pl.ANY)] * skip,
        out_specs=[block, block, block],
        out_shape=[shape, shape, shape],
        input_output_aliases={4 + place: place for place in range(skip)},
        scratch_shapes=[
            pltpu.VMEM((heads, tokens, tokens), kind)
            for kind in (full_type, full_type, half_type, half_type)
        ],
        cost_estimate=pl.CostEstimate(
            flops=32 * tokens * tokens * width,
            transcendentals=tokens * tokens * width // HDIM,
            bytes_accessed=14 * tokens * width,
        ),
        compiler_params=grant(20),
        name="attend_back",
    )(projected, projected, projected, grad_mixed, *into)


def normal_cdf(values):
    return 0.5 + 0.5 * lax.erf(values * (0.5**0.5))


def whole_block(shape):
    zeros = (0,) * len(shape)
    return pl.BlockSpec(shape, lambda *_: zeros, pipeline_mode=pl.Buffered(1))


def grant(mib):
    return pltpu.CompilerParams(vmem_limit_bytes=mib << 20)


def stacked(*refs):
    return jnp.concatenate([ref[...] for ref in refs], axis=0)


def unit_of(values):
    centre = values - jnp.mean(values, axis=1, keepdims=True)
    inv_scale = lax.rsqrt(jnp.mean(centre * centre, axis=1, keepdims=True) + ln_eps)
    return centre * inv_scale, inv_scale


def norm_back(grad_out, gain, values):
    unit, inv_scale = unit_of(values)
    grad_unit = grad_out * gain
    inner_mean = jnp.mean(grad_unit, axis=1, keepdims=True)
    along_mean = jnp.mean(grad_unit * unit, axis=1, keepdims=True)
    grad_in = (grad_unit - inner_mean - unit * along_mean) * inv_scale
    return grad_in, jnp.sum(grad_out * unit, axis=0, keepdims=True)


def half(values):
    return values.astype(half_type)


def shape_of(shape, kind):
    return jax.ShapeDtypeStruct(shape, kind)


def kept_shape(shape, kind):
    return pltpu.HBM(shape, kind)


def cost(flops, moved):
    return pl.CostEstimate(flops=flops, transcendentals=0, bytes_accessed=moved)


def in_hbm(value):
    return pltpu.with_memory_space_constraint(value, pltpu.HBM)


class Weight:
    def __init__(self, blocks, start, cols):
        self.blocks, self.start, self.cols = list(blocks), start, cols

    def specs(self, width, index=lambda j: j):
        base = self.start // width
        spec = pl.BlockSpec(
            (self.blocks[0].shape[0], width), lambda j, base=base: (0, base + index(j))
        )
        return [spec] * len(self.blocks)

    def refs(self):
        return [in_hbm(block) for block in self.blocks[:-1]] + self.blocks[-1:]


def embed(patches, mask, mover, weight, small, keep_patches):
    rows, width = patches.shape
    tokens = rows // 2
    masked = mask is not None
    pieces = small.cols // SMALL_TILE

    def kernel(*refs):
        x_ref, mover_ref = refs[:2]
        w_refs, small_refs, refs = refs[2:6], refs[6 : 6 + 4 * pieces], refs[6 + 4 * pieces :]
        if masked:
            mask_ref, refs = refs[0], refs[1:]
        h_ref, table_ref = refs[:2]
        x_rel = half(contract(x_ref[...], mover_ref[...], 1, 0))
        if keep_patches:
            refs[2][...] = x_rel
        w_rel = half(contract(stacked(*w_refs), mover_ref[...], 1, 0))
        small_parts = [stacked(*small_refs[4 * k : 4 * k + 4]) for k in range(pieces)]
        small_t = jnp.concatenate(small_parts, axis=1).astype(full_type).T
        posit = small_t[:tokens]
        table = small_t[tokens : tokens + 8]
        table_ref[...] = table
        states = contract(x_rel, w_rel, 1, 0)
        for seq in range(rows // tokens):
            part = slice(seq * tokens, (seq + 1) * tokens)
            state = states[part]
            if masked:
                flag = mask_ref[part, :]
                state = state * (1.0 - flag) + flag * table[2 * LAYERS + 1 : 2 * LAYERS + 2]
            h_ref[part, :] = state + posit

    outs = [shape_of((rows, width), full_type), shape_of((8, width), full_type)]
    if keep_patches:
        outs.append(kept_shape((rows, width), half_type))
    args = [patches, mover] + weight.refs() + small.refs() * pieces + ([mask] if masked else [])
    specs = [whole_block(patches.shape), whole_block(mover.shape)] + weight.specs(width)
    for k in range(pieces):
        specs += small.specs(SMALL_TILE, lambda j, k=k: k)
    if masked:
        specs.append(whole_block(mask.shape))
    return pl.pallas_call(
        kernel,
        grid=(1,),
        in_specs=specs,
        out_specs=[whole_block(out.shape) for out in outs],
        out_shape=outs,
        cost_estimate=cost(6 * rows * width * width, 12 * rows * width),
        compiler_params=grant(28),
        name="embed",
    )(*args)


def norm_project(states, table, row, weight, keep):
    rows, width = states.shape
    steps = weight.cols // width

    def kernel(h_ref, table_ref, own_ref, own2_ref, got_ref, got2_ref, out_ref, a_ref):
        @pl.when(pl.program_id(0) == 0)
        def _():
            unit, _ = unit_of(h_ref[...])
            a_ref[...] = half(unit * table_ref[row : row + 1, :])

        out_ref[...] = half(contract(a_ref[...], stacked(own_ref, own2_ref, got_ref, got2_ref), 1, 0))

    outs = [shape_of((rows, weight.cols), half_type)]
    out_specs = [pl.BlockSpec((rows, width), lambda j: (0, j))]
    scratch = []
    if keep:
        outs.append(kept_shape((rows, width), half_type))
        out_specs.append(whole_block((rows, width)))
    else:
        scratch.append(pltpu.VMEM((rows, width), half_type))
    return pl.pallas_call(
        kernel,
        grid=(steps,),
        in_specs=[whole_block(states.shape), whole_block(table.shape)] + weight.specs(width),
        out_specs=out_specs,
        out_shape=outs,
        scratch_shapes=scratch,
        cost_estimate=cost(2 * rows * width * weight.cols, 12 * rows * width),
        compiler_params=grant(24),
        name="norm_project",
    )(states, table, *weight.refs())


def mix_out(mixed, states, mover, table, row, weight, keep):
    rows, width = states.shape
    tile = rows // 2

    def kernel(o_ref, h_ref, mover_ref, table_ref, own_ref, own2_ref, got_ref, got2_ref, m_ref, b_ref, *rest):
        if keep:
            rel_ref, w_ref = rest
        else:
            (w_ref,) = rest

        @pl.when(pl.program_id(0) == 0)
        def _():
            w_ref[...] = half(contract(stacked(own_ref, own2_ref, got_ref, got2_ref), mover_ref[...], 1, 0))

        mixed_rel = half(contract(o_ref[...], mover_ref[...], 1, 0))
        if keep:
            rel_ref[...] = mixed_rel
        middle = h_ref[...] + contract(mixed_rel, w_ref[...], 1, 0)
        m_ref[...] = middle
        unit, _ = unit_of(middle)
        b_ref[...] = half(unit * table_ref[row : row + 1, :])

    part = pl.BlockSpec((tile, width), lambda j: (j, 0))
    outs = [shape_of((rows, width), full_type), shape_of((rows, width), half_type)]
    out_specs = [part, part]
    scratch = []
    if keep:
        outs += [kept_shape((rows, width), half_type), kept_shape((width, width), half_type)]
        out_specs += [part, whole_block((width, width))]
    else:
        scratch.append(pltpu.VMEM((width, width), half_type))
    return pl.pallas_call(
        kernel,
        grid=(2,),
        in_specs=[part, part, whole_block(mover.shape), whole_block(table.shape)]
        + weight.specs(width, lambda j: 0),
        out_specs=out_specs,
        out_shape=outs,
        scratch_shapes=scratch,
        cost_estimate=cost(6 * rows * width * width, 14 * rows * width),
        compiler_params=grant(24),
        name="mix_out",
    )(mixed, states, mover, table, *weight.refs())


def feed_forward(normed, middle, w_up, w_down, keep):
    rows, width = middle.shape
    tile = FF_TILE
    steps = w_up.cols // tile

    def kernel(b_ref, m_ref, uown_ref, uown2_ref, ugot_ref, ugot2_ref, down_ref, down2_ref, dgot_ref, dgot2_ref, out_ref, *rest):
        step = pl.program_id(0)
        hidden = contract(b_ref[...], stacked(uown_ref, uown2_ref, ugot_ref, ugot2_ref), 1, 0)
        cdf = normal_cdf(hidden)
        active = half(hidden * cdf)
        if keep:
            rest[0][...] = active
            rest[1][...] = cdf + hidden * (
                jnp.exp(-0.5 * hidden * hidden) * ((0.5 / jnp.pi) ** 0.5)
            )
        part = contract(active, stacked(down_ref, down2_ref, dgot_ref, dgot2_ref), 1, 1)

        @pl.when(step == 0)
        def _():
            out_ref[...] = m_ref[...] + part

        @pl.when(step > 0)
        def _():
            out_ref[...] += part

    outs = [shape_of((rows, width), full_type)]
    out_specs = [whole_block((rows, width))]
    if keep:
        outs += [kept_shape((rows, w_up.cols), half_type), kept_shape((rows, w_up.cols), full_type)]
        out_specs += [pl.BlockSpec((rows, tile), lambda j: (0, j))] * 2
    return pl.pallas_call(
        kernel,
        grid=(steps,),
        in_specs=[whole_block(normed.shape), whole_block(middle.shape)]
        + w_up.specs(tile)
        + w_down.specs(tile),
        out_specs=out_specs,
        out_shape=outs,
        cost_estimate=cost(4 * rows * width * w_up.cols, 12 * rows * width + 16 * width * w_up.cols),
        compiler_params=grant(30),
        name="feed_forward",
    )(normed, middle, *w_up.refs(), *w_down.refs())


def make_target(first, second, seqs):
    rows, width = first.shape
    tokens = rows // seqs
    cols = width // 2

    def kernel(one_ref, two_ref, out_ref):
        total = None
        for ref in (one_ref, two_ref):
            values = ref[...]
            centre = values - jnp.mean(values, axis=0, keepdims=True)
            variance = jnp.mean(centre * centre, axis=0, keepdims=True)
            term = centre * lax.rsqrt(variance + in_eps)
            total = term if total is None else total + term
        out_ref[...] = total * (1.0 / TOPK)

    block = pl.BlockSpec((tokens, cols), lambda s, j: (s, j))
    return pl.pallas_call(
        kernel,
        grid=(seqs, 2),
        in_specs=[block, block],
        out_specs=block,
        out_shape=shape_of((rows, width), full_type),
        cost_estimate=cost(20 * rows * width, 12 * rows * width),
        compiler_params=grant(16),
        name="make_target",
    )(first, second)


def head_step(states, table, mover, weight, target, mask, total_masked):
    rows, width = states.shape
    tile = rows // 2
    final_row = 2 * LAYERS

    def kernel(
        h_ref, table_ref, mover_ref, own_ref, own2_ref, got_ref, got2_ref, t_ref, mask_ref,
        flow_ref, f_ref, pred_ref, gain_ref, loss_ref, w_ref,
    ):
        step = pl.program_id(0)

        @pl.when(step == 0)
        def _():
            w_ref[...] = half(contract(stacked(own_ref, own2_ref, got_ref, got2_ref), mover_ref[...], 1, 0))
            gain_ref[...] = jnp.zeros_like(gain_ref)
            loss_ref[...] = jnp.zeros_like(loss_ref)

        states_now = h_ref[...]
        gain = table_ref[final_row : final_row + 1, :]
        unit, _ = unit_of(states_now)
        final_normed = half(unit * gain)
        f_ref[...] = final_normed
        flag = mask_ref[...]
        differ = contract(final_normed, w_ref[...], 1, 0) - t_ref[...]
        magnitude = jnp.abs(differ)
        terms = jnp.where(
            magnitude < huber_beta,
            0.5 * differ * differ / huber_beta,
            magnitude - 0.5 * huber_beta,
        )
        loss_ref[...] += jnp.sum(terms * flag, axis=0, keepdims=True)
        grad_pred = half(flag * jnp.clip(differ / huber_beta, -1.0, 1.0) / total_masked)
        pred_ref[...] = half(contract(grad_pred, mover_ref[...], 1, 1))
        grad_in, grad_gain = norm_back(contract(grad_pred, w_ref[...], 1, 1), gain, states_now)
        flow_ref[...] = grad_in
        gain_ref[...] += grad_gain

    part = pl.BlockSpec((tile, width), lambda j: (j, 0))
    row = whole_block((1, width))
    return pl.pallas_call(
        kernel,
        grid=(2,),
        in_specs=[part, whole_block(table.shape), whole_block(mover.shape)]
        + weight.specs(width, lambda j: 0)
        + [part, pl.BlockSpec((tile, 1), lambda j: (j, 0))],
        out_specs=[part, part, part, row, row],
        out_shape=[
            shape_of((rows, width), full_type),
            kept_shape((rows, width), half_type),
            kept_shape((rows, width), half_type),
            shape_of((1, width), full_type),
            shape_of((1, width), full_type),
        ],
        scratch_shapes=[pltpu.VMEM((width, width), half_type)],
        cost_estimate=cost(8 * rows * width * width, 16 * rows * width),
        compiler_params=grant(30),
        name="head_step",
    )(states, table, mover, *weight.refs(), target, mask)


def feed_back(flow, slope, middle, table, row, w_up, w_down):
    rows, width = flow.shape
    tile = FF_TILE
    steps = w_up.cols // tile

    def kernel(
        flow_ref, slope_ref, m_ref, table_ref, uown_ref, uown2_ref, ugot_ref, ugot2_ref, down_ref, down2_ref, dgot_ref, dgot2_ref,
        du_ref, dy_ref, dm_ref, dz_ref, gain_ref, acc_ref,
    ):
        step = pl.program_id(0)

        @pl.when(step == 0)
        def _():
            dy_ref[...] = half(flow_ref[...])

        grad_active = contract(dy_ref[...], stacked(down_ref, down2_ref, dgot_ref, dgot2_ref), 1, 0)
        grad_hidden = half(grad_active * slope_ref[...])
        du_ref[...] = grad_hidden
        part = contract(grad_hidden, stacked(uown_ref, uown2_ref, ugot_ref, ugot2_ref), 1, 1)

        @pl.when(step == 0)
        def _():
            acc_ref[...] = part

        @pl.when(step > 0)
        def _():
            acc_ref[...] += part

        @pl.when(step == steps - 1)
        def _():
            grad_in, grad_gain = norm_back(
                acc_ref[...], table_ref[row : row + 1, :], m_ref[...]
            )
            grad_middle = flow_ref[...] + grad_in
            dm_ref[...] = grad_middle
            dz_ref[...] = half(grad_middle)
            gain_ref[...] = grad_gain

    full = whole_block((rows, width))
    column = pl.BlockSpec((rows, tile), lambda j: (0, j))
    return pl.pallas_call(
        kernel,
        grid=(steps,),
        in_specs=[full, column, full, whole_block(table.shape)]
        + w_up.specs(tile)
        + w_down.specs(tile),
        out_specs=[column, full, full, full, whole_block((1, width))],
        out_shape=[
            kept_shape((rows, w_up.cols), half_type),
            kept_shape((rows, width), half_type),
            shape_of((rows, width), full_type),
            shape_of((rows, width), half_type),
            shape_of((1, width), full_type),
        ],
        scratch_shapes=[pltpu.VMEM((rows, width), full_type)],
        cost_estimate=cost(4 * rows * width * w_up.cols, 40 * rows * width + 8 * width * w_up.cols),
        compiler_params=grant(32),
        name="feed_back",
    )(flow, in_hbm(slope), middle, table, *w_up.refs(), *w_down.refs())


def mix_back(grad_branch, w_rel, mover):
    rows, width = grad_branch.shape
    tile = rows // 2

    def kernel(dz_ref, w_ref, mover_ref, do_ref, nat_ref):
        branch = dz_ref[...]
        grad_rel = half(contract(branch, w_ref[...], 1, 1))
        do_ref[...] = half(contract(grad_rel, mover_ref[...], 1, 1))
        nat_ref[...] = half(contract(branch, mover_ref[...], 1, 1))

    part = pl.BlockSpec((tile, width), lambda j: (j, 0))
    square = whole_block((width, width))
    return pl.pallas_call(
        kernel,
        grid=(2,),
        in_specs=[part, square, square],
        out_specs=[part, part],
        out_shape=[shape_of((rows, width), half_type), kept_shape((rows, width), half_type)],
        cost_estimate=cost(6 * rows * width * width, 10 * rows * width),
        compiler_params=grant(16),
        name="mix_back",
    )(grad_branch, w_rel, mover)


def project_back(grads, grad_middle, states, table, row, weight, mover, mask):
    rows, width = states.shape
    tile = rows // 2
    count = len(grads)
    first = mask is not None

    def kernel(*refs):
        grad_refs, refs = refs[:count], refs[count:]
        w_refs, refs = refs[: 4 * count], refs[4 * count :]
        dm_ref, h_ref, table_ref = refs[:3]
        refs = refs[3:]
        if first:
            mover_ref, mask_ref = refs[:2]
            refs = refs[2:]
        dh_ref, gain_ref = refs[:2]
        step = pl.program_id(0)

        @pl.when(step == 0)
        def _():
            for ref in (gain_ref,) + ((refs[3],) if first else ()):
                ref[...] = jnp.zeros_like(ref)

        total = None
        for place in range(count):
            part = contract(
                grad_refs[place][...], stacked(*w_refs[4 * place : 4 * place + 4]), 1, 1
            )
            total = part if total is None else total + part
        grad_in, grad_gain = norm_back(total, table_ref[row : row + 1, :], h_ref[...])
        flow = dm_ref[...] + grad_in
        dh_ref[...] = flow
        gain_ref[...] += grad_gain
        if first:
            flag = mask_ref[...]
            refs[2][...] = half(contract(half(flow * (1.0 - flag)), mover_ref[...], 1, 1))
            refs[3][...] += jnp.sum(flow * flag, axis=0, keepdims=True)

    part = pl.BlockSpec((tile, width), lambda j: (j, 0))
    vector = whole_block((1, width))
    specs = [part] * count
    args = [in_hbm(grad) for grad in grads]
    for place in range(count):
        specs += weight.specs(width, lambda j, place=place: place)
        args += weight.refs()
    specs += [part, part, whole_block(table.shape)]
    args += [grad_middle, states, table]
    outs = [shape_of((rows, width), full_type), shape_of((1, width), full_type)]
    out_specs = [part, vector]
    if first:
        specs += [whole_block(mover.shape), pl.BlockSpec((tile, 1), lambda j: (j, 0))]
        args += [mover, mask]
        outs += [kept_shape((rows, width), half_type), shape_of((1, width), full_type)]
        out_specs += [part, vector]
    return pl.pallas_call(
        kernel,
        grid=(2,),
        in_specs=specs,
        out_specs=out_specs,
        out_shape=outs,
        cost_estimate=cost(2 * rows * width * weight.cols, 22 * rows * width),
        compiler_params=grant(30),
        name="project_back",
    )(*args)


def weight_grads(pairs):
    rows, width = pairs[0][0].shape
    plan = []
    start = 0
    for place, (_, rights) in enumerate(pairs):
        first = start
        for right in rights:
            tiles = right.shape[1] // width
            plan.append((place, start, tiles, start == first))
            start += tiles
    total = start
    near_rows = width // 2

    def kernel(*refs):
        left_refs, refs = refs[: len(pairs)], refs[len(pairs) :]
        right_refs, refs = refs[: len(plan)], refs[len(plan) :]
        near_ref, far_ref, turned_ref = refs
        step = pl.program_id(0)
        for (place, begin, tiles, fresh), right_ref in zip(plan, right_refs):
            if fresh:

                @pl.when(step == begin)
                def _(place=place):
                    turned_ref[...] = left_refs[place][...].T

            @pl.when((step >= begin) & (step < begin + tiles))
            def _(right_ref=right_ref):
                out = contract(turned_ref[...], right_ref[...], 1, 0)
                near_ref[...] = out[:near_rows]
                far_ref[...] = half(out[near_rows:])

    specs = [whole_block((rows, width)) for _ in pairs]
    args = [left for left, _ in pairs]
    for (_, rights) in pairs:
        args += list(rights)
    for _, begin, tiles, _ in plan:
        specs.append(
            pl.BlockSpec(
                (rows, width),
                lambda j, begin=begin, tiles=tiles: (0, jnp.clip(j - begin, 0, tiles - 1)),
            )
        )
    block = pl.BlockSpec((near_rows, width), lambda j: (0, j))
    shapes = [
        kept_shape((near_rows, total * width), full_type),
        shape_of((near_rows, total * width), half_type),
    ]
    return tuple(
        pl.pallas_call(
            kernel,
            grid=(total,),
            in_specs=specs,
            out_specs=[block, block],
            out_shape=shapes,
            scratch_shapes=[pltpu.VMEM((width, rows), half_type)],
            cost_estimate=cost(
                2 * rows * width * width * total, width * total * (4 * width + 2 * rows)
            ),
            compiler_params=grant(30),
        name="weight_grads",
        )(*[in_hbm(arg) for arg in args])
    )


def small_grads(flow, vectors, seqs):
    rows, width = flow.shape
    tokens = rows // seqs
    cols = tokens + 8
    cols += -cols % LANES

    def kernel(flow_ref, *refs):
        vector_refs, (near_ref, far_ref) = refs[:-2], refs[-2:]
        posit = flow_ref[:tokens]
        for seq in range(1, seqs):
            posit = posit + flow_ref[seq * tokens : (seq + 1) * tokens]
        fill = jnp.zeros((cols - tokens - len(vector_refs), width), full_type)
        table = jnp.concatenate([posit] + [ref[...] for ref in vector_refs] + [fill], axis=0).T
        near_ref[...] = table[: width // 2]
        far_ref[...] = half(table[width // 2 :])

    shapes = [shape_of((width // 2, cols), kind) for kind in (full_type, half_type)]
    return tuple(
        pl.pallas_call(
            kernel,
            grid=(1,),
            in_specs=[whole_block(flow.shape)] + [whole_block((1, width)) for _ in vectors],
            out_specs=[whole_block(shape.shape) for shape in shapes],
            out_shape=shapes,
            cost_estimate=cost(2 * rows * width, 8 * rows * width),
            compiler_params=grant(16),
        name="small_grads",
        )(flow, *vectors)
    )


class Plan:
    def __init__(self):
        self.seq_size = lax.axis_size("seq")
        self.count = lax.axis_size("dp") * self.seq_size
        self.bits = self.count.bit_length() - 1
        self.early = list(range(self.bits - 1, 2, -1))

        def flips(pick):
            return [(i, i ^ (1 << pick((i >> 1) & 1))) for i in range(self.count)]

        self.stages = [flips(lambda core, b=b: b) for b in self.early]
        self.stages.append(flips(lambda core: 0 if core else 2))
        self.stages.append(flips(lambda core: 2 if core else 0))
        self.core_stage = flips(lambda core: 1)
        self.index = lax.axis_index("dp") * self.seq_size + lax.axis_index("seq")

    def swap(self, value, perm):
        return lax.ppermute(value, AXES, perm)

    def row_table(self, width):
        rows = width // self.count
        place = lax.broadcasted_iota(jnp.int32, (1, width), 1)
        spot = place // rows
        early_count = len(self.early)
        other = (spot >> (self.bits - 1)) & 1
        holder_core = ((self.index >> 1) & 1) ^ other
        block = self.index ^ (other << 1)
        for step, bit in enumerate(self.early):
            block = block ^ (((spot >> step) & 1) << bit)
        first = (spot >> early_count) & 1
        second = (spot >> (early_count + 1)) & 1
        block = block ^ jnp.where(holder_core == 0, first << 2, first)
        block = block ^ jnp.where(holder_core == 0, second, second << 2)
        return block * rows + place % rows

    def mover(self, width):
        table = self.row_table(width)
        whole = lax.broadcasted_iota(jnp.int32, (width, width), 0)
        return (whole == table).astype(half_type)


class Pump:
    def __init__(self, plan):
        self.plan = plan
        self.jobs = []

    def add(self, steps, done, ticks=()):
        self.jobs.append(
            {"steps": steps, "sends": next(steps), "done": done, "stage": 0, "ticks": dict(ticks)}
        )

    def start(self, job):
        job["gots"] = [self.plan.swap(value, perm) for value, perm in job["sends"]]
        job["left"] = job["ticks"].get(job["stage"], 1)

    def advance(self, job, gots):
        job["stage"] += 1
        job["gots"] = None
        try:
            job["sends"] = job["steps"].send(gots)
            return True
        except StopIteration as stop:
            job["done"](stop.value)
            return False

    def begin(self):
        for job in self.jobs:
            if job.get("gots") is None:
                self.start(job)

    def end(self, values=()):
        due = []
        for job in self.jobs:
            job["left"] -= 1
            if job["left"] == 0:
                due.append(job)
        flying, values = lax.optimization_barrier(([job["gots"] for job in due], values))
        over = [job for job, gots in zip(due, flying) if not self.advance(job, gots)]
        self.jobs = [job for job in self.jobs if job not in over]
        return values

    def drain(self):
        newest = self.jobs[-1]
        while self.jobs:
            self.begin()
            if self.jobs[-1] is newest:
                if self.advance(newest, newest["gots"]):
                    self.start(newest)
                else:
                    self.jobs.pop()
            self.end()


def scatter_steps(plan, pieces, narrow):
    gots = yield [(far, plan.core_stage) for _, far in pieces]
    quarter = pieces[0][0].shape[0] // 2
    sums = [
        (half(near[quarter:] + got[quarter:]), near[:quarter] + got[:quarter])
        for (near, _), got in zip(pieces, gots)
    ]
    send = jnp.concatenate([part for part, _ in sums], axis=1)
    keep = jnp.concatenate([part for _, part in sums], axis=1)
    stages = plan.stages[::-1]
    for step, perm in enumerate(stages):
        (got,) = yield [(send, perm)]
        if step == len(stages) - 1:
            return keep + got
        middle = keep.shape[0] // 2
        send = keep[middle:] + got[middle:]
        if step < narrow - 1:
            send = half(send)
        keep = keep[:middle] + got[:middle]


def adam_step(weight, first_mom, second_mom, teacher, gradient):
    first_new = first_decay * first_mom + (1.0 - first_decay) * gradient
    second_new = second_decay * second_mom + (1.0 - second_decay) * gradient * gradient
    weight_new = weight - learn_rate * (
        first_new / (jnp.sqrt(second_new) + adam_eps) + weight_decay * weight
    )
    teacher_new = teacher_keep * teacher + (1.0 - teacher_keep) * weight_new
    return (weight_new, first_new, second_new, teacher_new)


def norm_totals(edge, attn_zero, attn_one, mlp_zero, mlp_one, loss_row, width, tokens):
    stop = 4 * width

    def kernel(edge_ref, first_ref, second_ref, zero_ref, one_ref, loss_ref, out_ref):
        def square(value):
            return jnp.sum(value * value)

        small = edge_ref[:, width:]
        lane = lax.broadcasted_iota(jnp.int32, small.shape, 1)
        posit = jnp.where(lane < tokens, small, 0.0)
        vecs = jnp.where(lane >= tokens, small, 0.0)
        parts = [
            jnp.sum(loss_ref[...]),
            square(edge_ref[:, :width]) + square(second_ref[:, stop:]),
            square(first_ref[...]) + square(second_ref[:, :stop]),
            square(zero_ref[...]) + square(one_ref[...]),
            square(posit),
            square(vecs),
        ]
        row = lax.broadcasted_iota(jnp.int32, (8, LANES), 0)
        out = jnp.zeros((8, LANES), full_type)
        for place, part in enumerate(parts):
            out = jnp.where(row == place, part, out)
        out_ref[...] = out

    args = (edge, attn_zero, attn_one, mlp_zero, mlp_one, loss_row)
    return pl.pallas_call(
        kernel,
        grid=(1,),
        in_specs=[whole_block(arg.shape) for arg in args],
        out_specs=whole_block((8, LANES)),
        out_shape=shape_of((8, LANES), full_type),
        compiler_params=grant(16),
        name="norm_totals",
    )(*args)


def update(totals, edge, attn_zero, attn_one, mlp_zero, mlp_one, groups, sizes, width, tokens):
    stop = mlp_zero.shape[1]

    def kernel(total_ref, edge_ref, first_ref, second_ref, zero_ref, one_ref, *refs):
        ins, outs = refs[:20], refs[20:]

        def step(group, gradient, cols=slice(None)):
            limit = entry_clip * sizes[group] ** 0.5
            norm_value = jnp.sqrt(total_ref[group + 1 : group + 2, 0:1])
            gradient = gradient * (limit / jnp.maximum(norm_value, limit))
            weight, first, second, teacher = (
                ref[:, cols] for ref in ins[4 * group : 4 * group + 4]
            )
            news = adam_step(weight, first, second, teacher, gradient)
            for ref, new in zip(outs[4 * group : 4 * group + 4], news):
                ref[:, cols] = new

        step(0, edge_ref[:, :width], slice(0, width))
        step(0, second_ref[:, 4 * width :], slice(width, 2 * width))
        step(1, first_ref[...], slice(0, 4 * width))
        step(1, second_ref[:, : 4 * width], slice(4 * width, 8 * width))
        step(2, zero_ref[...], slice(0, stop))
        step(2, one_ref[...], slice(stop, 2 * stop))
        step(3, edge_ref[:, width : width + tokens])
        start = tokens // LANES * LANES
        turned = edge_ref[:, width + start : width + start + LANES].T
        count = ins[16].shape[0]
        step(4, turned[tokens - start : tokens - start + count])

    args = [totals, edge, attn_zero, attn_one, mlp_zero, mlp_one] + [part for group in groups for part in group]
    outs = [shape_of(part.shape, full_type) for group in groups for part in group]
    return pl.pallas_call(
        kernel,
        grid=(1,),
        in_specs=[whole_block(arg.shape) for arg in args],
        out_specs=[whole_block(out.shape) for out in outs],
        out_shape=outs,
        compiler_params=grant(40),
        name="update",
    )(*args)


def pad_lanes(value):
    extra = -value.shape[1] % LANES
    return jnp.pad(value, ((0, 0), (0, extra)))


def local(
    patches,
    masked_at,
    edge_w,
    attn_w,
    mlp_w,
    posit_w,
    vecs_w,
    edge_m,
    attn_m,
    mlp_m,
    posit_m,
    vecs_m,
    edge_v,
    attn_v,
    mlp_v,
    posit_v,
    vecs_v,
    edge_t,
    attn_t,
    mlp_t,
    posit_t,
    vecs_t,
):
    seqs, tokens, width = patches.shape
    plan = Plan()
    total_masked = seqs * plan.count * tokens // 2
    ff_width = mlp_w.shape[1] // (2 * LAYERS)
    small_cols = tokens + vecs_w.shape[1]
    flat_patch = patches.reshape(-1, width)
    mask_flat = masked_at.astype(full_type).reshape(-1, 1)
    mover = plan.mover(width)

    def shards(edge, attn, mlp, posit, vecs):
        small = pad_lanes(jnp.concatenate([posit, vecs], axis=1))
        return [edge[:, :width], edge[:, width:], small] + [
            [
                part[:, layer * part.shape[1] // LAYERS : (layer + 1) * part.shape[1] // LAYERS]
                for part in (attn, mlp)
            ]
            for layer in range(LAYERS)
        ]

    def joined(parts):
        return jnp.concatenate([half(part) for part in parts], axis=1)

    t_patch, _, t_small, t_one, t_two = shards(edge_t, attn_t, mlp_t, posit_t, vecs_t)
    s_patch, s_head, s_small, s_one, s_two = shards(edge_w, attn_w, mlp_w, posit_w, vecs_w)
    chunks = [
        [t_patch, t_one[0], t_small],
        [t_one[1]],
        t_two,
        [s_patch, s_one[0], s_small],
        [s_one[1]],
        [s_two[0], s_head],
        [s_two[1]],
    ]
    groups = [[0], [1], [2], [3], [4, 5, 6]]
    group_start = [0, 1, 2, 3, 4]

    def attn_weights(blocks, start):
        return Weight(blocks, start, 3 * width), Weight(blocks, start + 3 * width, width)

    def mlp_weights(blocks, start):
        return Weight(blocks, start, ff_width), Weight(blocks, start + ff_width, ff_width)

    def small_of(blocks):
        return Weight(blocks, 5 * width, t_small.shape[1])

    def finish(blocks):
        return list(blocks) + [plan.swap(blocks[1], plan.core_stage)]

    def attend_forward(states, table, layer, w_qkv, w_out, keep, outs=None):
        if outs is None:
            outs = norm_project(states, table, layer, w_qkv, keep)
        projected = outs[0].reshape(seqs, tokens, w_qkv.cols)
        mixed = attend(projected).reshape(-1, width)
        results = mix_out(mixed, states, mover, table, LAYERS + layer, w_out, keep)
        if keep:
            return results[0], results[1], (states, outs[1], projected) + tuple(results[2:])
        return results[0], results[1], ()

    saved_attn = [None] * LAYERS
    saved_mlp = [None] * LAYERS

    def segment_t0(_, blocks):
        patch = Weight(blocks, 0, width)
        states, table, patch_rel = embed(
            flat_patch, None, mover, patch, small_of(blocks), True
        )
        weights = attn_weights(blocks, width)
        return states, table, patch_rel, norm_project(states, table, 0, weights[0], False)

    def segment_t0_rest(values, blocks):
        states, table, patch_rel, outs = values
        weights = attn_weights(blocks, width)
        middle, normed, _ = attend_forward(states, table, 0, *weights, False, outs)
        return middle, normed, table, patch_rel

    def segment_t1(values, blocks):
        middle, normed, table, patch_rel = values
        (states,) = feed_forward(normed, middle, *mlp_weights(blocks, 0), False)
        return states, table, patch_rel

    def segment_t2(values, blocks):
        first, table, patch_rel = values
        middle, normed, _ = attend_forward(first, table, 1, *attn_weights(blocks, 0), False)
        (second,) = feed_forward(normed, middle, *mlp_weights(blocks, 4 * width), False)
        return make_target(first, second, seqs), patch_rel

    def segment_s0(values, blocks):
        target, patch_rel = values
        patch = Weight(blocks, 0, width)
        states, table = embed(flat_patch, mask_flat, mover, patch, small_of(blocks), False)
        weights = attn_weights(blocks, width)
        middle, normed, saved = attend_forward(states, table, 0, *weights, True)
        saved_attn[0] = (weights[0], saved)
        return target, patch_rel, table, middle, normed

    def segment_s1(values, blocks):
        target, patch_rel, table, middle, normed = values
        weights = mlp_weights(blocks, 0)
        states, active, slope = feed_forward(normed, middle, *weights, True)
        saved_mlp[0] = (weights, middle, normed, active, slope)
        return target, patch_rel, table, states

    def segment_s2(values, blocks):
        target, patch_rel, table, states = values
        weights = attn_weights(blocks, 0)
        middle, normed, saved = attend_forward(states, table, 1, *weights, True)
        saved_attn[1] = (weights[0], saved)
        return target, patch_rel, table, middle, normed, blocks

    segments = [segment_t0_rest, segment_t1, segment_t2, segment_s0, segment_s1, segment_s2]
    early = len(plan.early)
    group_values = [joined([part for c in group for part in chunks[c]]) for group in groups]
    own = [None] * len(chunks)
    blocks = [None] * len(chunks)
    values = ()
    for tick in range(len(chunks) + early + 1):
        sends = {}
        for group, start in enumerate(group_start):
            if 0 <= tick - start < early:
                sends["early", group] = (group_values[group], plan.stages[tick - start])
        for chunk in range(len(chunks)):
            if tick == chunk + early:
                sends["first", chunk] = (own[chunk], plan.stages[early])
            if tick == chunk + early + 1:
                sends["second", chunk] = (own[chunk], plan.stages[early + 1])
                sends["core", chunk] = (own[chunk], plan.core_stage)
        gots = {key: plan.swap(value, perm) for key, (value, perm) in sends.items()}
        place = tick - early - 2
        if 0 <= place < len(segments):
            values = segments[place](values, finish(blocks[place]))
        if tick == early + 1:
            first_blocks = (own[0], gots["second", 0], gots["core", 0])
            values = segment_t0(values, finish(first_blocks))
        apart = {key: got for key, got in gots.items() if FAST_LANE and key[1] == 0 and tick}
        gots = {key: got for key, got in gots.items() if key not in apart}
        later = [g for g in range(len(groups)) if group_start[g] > tick]
        idle = [c for c in range(1, len(chunks)) if own[c] is not None and c + early > tick]
        gots, values, held, held_own, _ = lax.optimization_barrier(
            (gots, values, [group_values[g] for g in later], [own[c] for c in idle], apart)
        )
        for g, value in zip(later, held):
            group_values[g] = value
        for c, value in zip(idle, held_own):
            own[c] = value
        gots.update(apart)
        for (kind, index), got in gots.items():
            if kind == "early":
                group_values[index] = jnp.concatenate([group_values[index], got], axis=0)
                if tick - group_start[index] == early - 1:
                    start = 0
                    for chunk in groups[index]:
                        stop = start + sum(part.shape[1] for part in chunks[chunk])
                        own[chunk] = group_values[index][:, start:stop]
                        start = stop
            elif kind == "first":
                own[index] = jnp.concatenate([own[index], got], axis=0)
        for chunk in range(len(chunks)):
            if ("second", chunk) in gots:
                blocks[chunk] = (own[chunk], gots["second", chunk], gots["core", chunk])
    pump = Pump(plan)
    target, patch_rel, table, middle, normed, head_blocks = values
    weights = mlp_weights(finish(blocks[-1]), 0)
    states, active, slope = feed_forward(normed, middle, *weights, True)
    saved_mlp[1] = (weights, middle, normed, active, slope)
    flow, final_normed, grad_pred, grad_gain_final, loss_row = head_step(
        states,
        table,
        mover,
        Weight(head_blocks, 4 * width, width),
        target,
        mask_flat,
        total_masked,
    )

    gain_ones = [None] * LAYERS
    gain_twos = [None] * LAYERS
    shards = {}
    last_stage = len(plan.stages)

    def send_off(name, pieces, narrow, ticks=()):
        pump.add(
            scatter_steps(plan, pieces, narrow), lambda out: shards.__setitem__(name, out), ticks
        )

    for layer in reversed(range(LAYERS)):
        w_qkv, (states, normed_one, projected, mixed_rel, w_out_rel) = saved_attn[layer]
        (w_up, w_down), middle, normed_two, active, slope = saved_mlp[layer]
        pump.begin()
        grad_hidden, grad_down, grad_middle, grad_branch, gain_twos[layer] = feed_back(
            flow, slope, middle, table, LAYERS + layer, w_up, w_down
        )
        grad_hidden, grad_down, grad_middle, grad_branch = pump.end(
            (grad_hidden, grad_down, grad_middle, grad_branch)
        )
        pump.begin()
        piece = weight_grads([(normed_two, [grad_hidden]), (grad_down, [active])])
        piece, grad_branch = pump.end((piece, grad_branch))
        send_off(
            ("mlp", layer), [piece], 3, {1: 2, last_stage: 2} if layer else {last_stage: 2}
        )
        pump.begin()
        grad_mixed, branch_whole = mix_back(grad_branch, w_out_rel, mover)
        grad_mixed = grad_mixed.reshape(seqs, tokens, width)
        grad_proj = ()
        for seq in range(seqs - 1):
            grad_proj = attend_back(projected, grad_mixed, seq, tuple(grad_proj))
        grad_proj, grad_mixed, branch_whole = pump.end((grad_proj, grad_mixed, branch_whole))
        pump.begin()
        grad_proj = attend_back(projected, grad_mixed, seqs - 1, tuple(grad_proj))
        grad_proj = [part.reshape(-1, width) for part in grad_proj]
        pairs = [(normed_one, grad_proj), (mixed_rel, [branch_whole])]
        if layer == 0:
            piece = weight_grads(pairs)
            piece, grad_proj = pump.end((piece, grad_proj))
            send_off(("attn", 0), [piece], 3)
            pump.begin()
        results = project_back(
            grad_proj,
            grad_middle,
            states,
            table,
            layer,
            w_qkv,
            mover,
            None if layer else mask_flat,
        )
        flow, gain_ones[layer] = results[:2]
        if layer:
            flow, grad_proj = pump.end((flow, grad_proj))
            pairs = [(normed_one, grad_proj), (mixed_rel, [branch_whole])]
            pairs.append((final_normed, [grad_pred]))
            pump.begin()
            piece = weight_grads(pairs)
            piece, flow = pump.end((piece, flow))
            send_off(("attn", layer), [piece], 2)
    grad_embed, grad_maskvec = results[2:]
    vectors = gain_ones + gain_twos + [grad_gain_final, grad_maskvec]
    pieces = pump.end(
        [weight_grads([(patch_rel, [grad_embed])]), small_grads(flow, vectors, seqs)]
    )
    send_off("edge", pieces, 2)
    pump.drain()
    pieces = (
        shards["edge"],
        shards["attn", 0],
        shards["attn", 1],
        shards["mlp", 0],
        shards["mlp", 1],
    )
    totals = norm_totals(*pieces, loss_row, width, tokens)
    for perm in [plan.core_stage] + plan.stages:
        totals = totals + plan.swap(totals, perm)
    groups = [
        (edge_w, edge_m, edge_v, edge_t),
        (attn_w, attn_m, attn_v, attn_t),
        (mlp_w, mlp_m, mlp_v, mlp_t),
        (posit_w, posit_m, posit_v, posit_t),
        (vecs_w.T, vecs_m.T, vecs_v.T, vecs_t.T),
    ]
    sizes = [group[0].size * plan.count for group in groups]
    news = update(totals, *pieces, groups, sizes, width, tokens)
    news = [
        [news[4 * group + part] for group in range(4)] + [news[16 + part].T] for part in range(4)
    ]
    return (totals[0, 0] / total_masked,) + tuple(new for part in news for new in part)


def solution(mesh):
    rows = P(AXES, None)
    in_specs = (P(AXES, None, None),) + (rows,) * 21
    out_specs = (P(),) + (rows,) * 20
    return jax.shard_map(local, mesh=mesh, in_specs=in_specs, out_specs=out_specs, check_vma=False)
```

```python
import jax
import jax.numpy as jnp
from jax import lax
from jax.experimental import pallas as pl
from jax.experimental.pallas import tpu as pltpu
from jax.sharding import PartitionSpec as P

HDIM = 64
LAYERS = 2
TOPK = 2
LANES = 128
FF_TILE = 512
SMALL_TILE = 256
ROW_TILE = 64
PAIRS = 2
FAST_LANE = True

ln_eps = 1e-05
in_eps = 1e-05
learn_rate = 0.02
first_decay = 0.5
second_decay = 0.5
adam_eps = 1e-08
weight_decay = 0.1
teacher_keep = 0.5
huber_beta = 1.0
score_scale = 0.125
entry_clip = 1e-05
half_type = jnp.bfloat16
full_type = jnp.float32
AXES = ("dp", "seq")


def contract(left, right, left_dim, right_dim):
    return lax.dot_general(
        left,
        right,
        (((left_dim,), (right_dim,)), ((), ())),
        preferred_element_type=full_type,
    )


def head_mask(which, width):
    lane = lax.broadcasted_iota(jnp.int32, (1, width), 1)
    return (lane // HDIM) == which


def head_part(values, which):
    return jnp.where(head_mask(which, LANES), values, jnp.zeros_like(values))


def softmax_rows(scores):
    exps = jnp.exp(scores - jnp.max(scores, axis=1, keepdims=True))
    return exps * (1.0 / jnp.sum(exps, axis=1, keepdims=True))


def attend_kernel(q_ref, k_ref, v_ref, o_ref, score_ref, prob_ref):
    tokens = q_ref.shape[1]
    heads = LANES // HDIM
    for start in range(0, q_ref.shape[2], LANES):
        cols = slice(start, start + LANES)
        queries = q_ref[0, :, cols] * jnp.asarray(score_scale, half_type)
        for which in range(heads):
            score_ref[which] = contract(head_part(queries, which), k_ref[0, :, cols], 1, 1)
        for which in range(heads):
            for row in range(0, tokens, ROW_TILE):
                rows = slice(row, row + ROW_TILE)
                prob_ref[which, rows] = softmax_rows(score_ref[which, rows]).astype(half_type)
        mixed = None
        for which in range(heads):
            out = contract(prob_ref[which], v_ref[0, :, cols], 1, 0)
            mixed = out if mixed is None else jnp.where(head_mask(which, LANES), out, mixed)
        o_ref[0, :, cols] = mixed.astype(half_type)


def attend_back_kernel(q_ref, k_ref, v_ref, do_ref, dq_ref, dk_ref, dv_ref, *scratch):
    score_ref, grad_ref, prob_ref, back_ref = scratch
    tokens = q_ref.shape[1]
    heads = LANES // HDIM
    for start in range(0, q_ref.shape[2], LANES):
        cols = slice(start, start + LANES)
        queries = q_ref[0, :, cols] * jnp.asarray(score_scale, half_type)
        keys_now = k_ref[0, :, cols]
        grad_out = do_ref[0, :, cols]
        for which in range(heads):
            score_ref[which] = contract(head_part(queries, which), keys_now, 1, 1)
            grad_ref[which] = contract(head_part(grad_out, which), v_ref[0, :, cols], 1, 1)
        for which in range(heads):
            for row in range(0, tokens, ROW_TILE):
                rows = slice(row, row + ROW_TILE)
                probs = softmax_rows(score_ref[which, rows])
                prob_ref[which, rows] = probs.astype(half_type)
                prods = probs * grad_ref[which, rows]
                back_ref[which, rows] = (
                    prods - probs * jnp.sum(prods, axis=1, keepdims=True)
                ).astype(half_type)
        turned_k = []
        turned_v = []
        grad_q = None
        for which in range(heads):
            part = slice(which * HDIM, (which + 1) * HDIM)
            turned_v.append(contract(grad_out, prob_ref[which], 0, 0)[part])
            turned_k.append(contract(queries, back_ref[which], 0, 0)[part])
            out = contract(back_ref[which], keys_now, 1, 0)
            grad_q = out if grad_q is None else jnp.where(head_mask(which, LANES), out, grad_q)
        dq_ref[0, :, cols] = (grad_q * score_scale).astype(half_type)
        dk_ref[0, :, cols] = jnp.concatenate(turned_k, axis=0).T.astype(half_type)
        dv_ref[0, :, cols] = jnp.concatenate(turned_v, axis=0).T.astype(half_type)


def attend(projected):
    seqs, tokens, width3 = projected.shape
    width = width3 // 3
    wide = PAIRS * LANES
    blocks = width // wide
    specs = [
        pl.BlockSpec((1, tokens, wide), lambda s, j, off=off: (s, 0, off * blocks + j))
        for off in range(3)
    ]
    heads = LANES // HDIM
    return pl.pallas_call(
        attend_kernel,
        grid=(seqs, blocks),
        in_specs=specs,
        out_specs=pl.BlockSpec((1, tokens, wide), lambda s, j: (s, 0, j)),
        out_shape=jax.ShapeDtypeStruct((seqs, tokens, width), half_type),
        scratch_shapes=[
            pltpu.VMEM((heads, tokens, tokens), full_type),
            pltpu.VMEM((heads, tokens, tokens), half_type),
        ],
        cost_estimate=pl.CostEstimate(
            flops=16 * seqs * tokens * tokens * width,
            transcendentals=seqs * tokens * tokens * width // HDIM,
            bytes_accessed=8 * seqs * tokens * width,
        ),
        compiler_params=grant(16),
        name="attend",
    )(projected, projected, projected)


def attend_back(projected, grad_mixed, seq, into=()):
    seqs, tokens, width3 = projected.shape
    width = width3 // 3
    wide = PAIRS * LANES
    blocks = width // wide
    block = pl.BlockSpec((1, tokens, wide), lambda j: (seq, 0, j))
    specs = [
        pl.BlockSpec((1, tokens, wide), lambda j, off=off: (seq, 0, off * blocks + j))
        for off in range(3)
    ]
    heads = LANES // HDIM
    skip = len(into)

    def kernel(q_ref, k_ref, v_ref, do_ref, *refs):
        attend_back_kernel(q_ref, k_ref, v_ref, do_ref, *refs[skip:])

    shape = kept_shape((seqs, tokens, width), half_type)
    return pl.pallas_call(
        kernel,
        grid=(blocks,),
        in_specs=specs + [block] + [pl.BlockSpec(memory_space=pl.ANY)] * skip,
        out_specs=[block, block, block],
        out_shape=[shape, shape, shape],
        input_output_aliases={4 + place: place for place in range(skip)},
        scratch_shapes=[
            pltpu.VMEM((heads, tokens, tokens), kind)
            for kind in (full_type, full_type, half_type, half_type)
        ],
        cost_estimate=pl.CostEstimate(
            flops=32 * tokens * tokens * width,
            transcendentals=tokens * tokens * width // HDIM,
            bytes_accessed=14 * tokens * width,
        ),
        compiler_params=grant(20),
        name="attend_back",
    )(projected, projected, projected, grad_mixed, *into)


def normal_cdf(values):
    return 0.5 + 0.5 * lax.erf(values * (0.5**0.5))


def whole_block(shape):
    zeros = (0,) * len(shape)
    return pl.BlockSpec(shape, lambda *_: zeros, pipeline_mode=pl.Buffered(1))


def grant(mib):
    return pltpu.CompilerParams(vmem_limit_bytes=mib << 20)


def stacked(*refs):
    return jnp.concatenate([ref[...] for ref in refs], axis=0)


def unit_of(values):
    centre = values - jnp.mean(values, axis=1, keepdims=True)
    inv_scale = lax.rsqrt(jnp.mean(centre * centre, axis=1, keepdims=True) + ln_eps)
    return centre * inv_scale, inv_scale


def norm_back(grad_out, gain, values):
    unit, inv_scale = unit_of(values)
    grad_unit = grad_out * gain
    inner_mean = jnp.mean(grad_unit, axis=1, keepdims=True)
    along_mean = jnp.mean(grad_unit * unit, axis=1, keepdims=True)
    grad_in = (grad_unit - inner_mean - unit * along_mean) * inv_scale
    return grad_in, jnp.sum(grad_out * unit, axis=0, keepdims=True)


def half(values):
    return values.astype(half_type)


def shape_of(shape, kind):
    return jax.ShapeDtypeStruct(shape, kind)


def kept_shape(shape, kind):
    return pltpu.HBM(shape, kind)


def cost(flops, moved):
    return pl.CostEstimate(flops=flops, transcendentals=0, bytes_accessed=moved)


def in_hbm(value):
    return pltpu.with_memory_space_constraint(value, pltpu.HBM)


class Weight:
    def __init__(self, blocks, start, cols):
        self.blocks, self.start, self.cols = list(blocks), start, cols

    def specs(self, width, index=lambda j: j):
        base = self.start // width
        spec = pl.BlockSpec(
            (self.blocks[0].shape[0], width), lambda j, base=base: (0, base + index(j))
        )
        return [spec] * len(self.blocks)

    def refs(self):
        return [in_hbm(block) for block in self.blocks[:-1]] + self.blocks[-1:]


def embed(patches, mask, mover, weight, small, keep_patches):
    rows, width = patches.shape
    tokens = rows // 2
    masked = mask is not None
    pieces = small.cols // SMALL_TILE

    def kernel(*refs):
        x_ref, mover_ref = refs[:2]
        w_refs, small_refs, refs = refs[2:6], refs[6 : 6 + 4 * pieces], refs[6 + 4 * pieces :]
        if masked:
            mask_ref, refs = refs[0], refs[1:]
        h_ref, table_ref = refs[:2]
        x_rel = half(contract(x_ref[...], mover_ref[...], 1, 0))
        if keep_patches:
            refs[2][...] = x_rel
        w_rel = half(contract(stacked(*w_refs), mover_ref[...], 1, 0))
        small_parts = [stacked(*small_refs[4 * k : 4 * k + 4]) for k in range(pieces)]
        small_t = jnp.concatenate(small_parts, axis=1).astype(full_type).T
        posit = small_t[:tokens]
        table = small_t[tokens : tokens + 8]
        table_ref[...] = table
        states = contract(x_rel, w_rel, 1, 0)
        for seq in range(rows // tokens):
            part = slice(seq * tokens, (seq + 1) * tokens)
            state = states[part]
            if masked:
                flag = mask_ref[part, :]
                state = state * (1.0 - flag) + flag * table[2 * LAYERS + 1 : 2 * LAYERS + 2]
            h_ref[part, :] = state + posit

    outs = [shape_of((rows, width), full_type), shape_of((8, width), full_type)]
    if keep_patches:
        outs.append(kept_shape((rows, width), half_type))
    args = [patches, mover] + weight.refs() + small.refs() * pieces + ([mask] if masked else [])
    specs = [whole_block(patches.shape), whole_block(mover.shape)] + weight.specs(width)
    for k in range(pieces):
        specs += small.specs(SMALL_TILE, lambda j, k=k: k)
    if masked:
        specs.append(whole_block(mask.shape))
    return pl.pallas_call(
        kernel,
        grid=(1,),
        in_specs=specs,
        out_specs=[whole_block(out.shape) for out in outs],
        out_shape=outs,
        cost_estimate=cost(6 * rows * width * width, 12 * rows * width),
        compiler_params=grant(28),
        name="embed",
    )(*args)


def norm_project(states, table, row, weight, keep):
    rows, width = states.shape
    steps = weight.cols // width

    def kernel(h_ref, table_ref, own_ref, own2_ref, got_ref, got2_ref, out_ref, a_ref):
        @pl.when(pl.program_id(0) == 0)
        def _():
            unit, _ = unit_of(h_ref[...])
            a_ref[...] = half(unit * table_ref[row : row + 1, :])

        out_ref[...] = half(contract(a_ref[...], stacked(own_ref, own2_ref, got_ref, got2_ref), 1, 0))

    outs = [shape_of((rows, weight.cols), half_type)]
    out_specs = [pl.BlockSpec((rows, width), lambda j: (0, j))]
    scratch = []
    if keep:
        outs.append(kept_shape((rows, width), half_type))
        out_specs.append(whole_block((rows, width)))
    else:
        scratch.append(pltpu.VMEM((rows, width), half_type))
    return pl.pallas_call(
        kernel,
        grid=(steps,),
        in_specs=[whole_block(states.shape), whole_block(table.shape)] + weight.specs(width),
        out_specs=out_specs,
        out_shape=outs,
        scratch_shapes=scratch,
        cost_estimate=cost(2 * rows * width * weight.cols, 12 * rows * width),
        compiler_params=grant(24),
        name="norm_project",
    )(states, table, *weight.refs())


def mix_out(mixed, states, mover, table, row, weight, keep):
    rows, width = states.shape
    tile = rows // 2

    def kernel(o_ref, h_ref, mover_ref, table_ref, own_ref, own2_ref, got_ref, got2_ref, m_ref, b_ref, *rest):
        if keep:
            rel_ref, w_ref = rest
        else:
            (w_ref,) = rest

        @pl.when(pl.program_id(0) == 0)
        def _():
            w_ref[...] = half(contract(stacked(own_ref, own2_ref, got_ref, got2_ref), mover_ref[...], 1, 0))

        mixed_rel = half(contract(o_ref[...], mover_ref[...], 1, 0))
        if keep:
            rel_ref[...] = mixed_rel
        middle = h_ref[...] + contract(mixed_rel, w_ref[...], 1, 0)
        m_ref[...] = middle
        unit, _ = unit_of(middle)
        b_ref[...] = half(unit * table_ref[row : row + 1, :])

    part = pl.BlockSpec((tile, width), lambda j: (j, 0))
    outs = [shape_of((rows, width), full_type), shape_of((rows, width), half_type)]
    out_specs = [part, part]
    scratch = []
    if keep:
        outs += [kept_shape((rows, width), half_type), kept_shape((width, width), half_type)]
        out_specs += [part, whole_block((width, width))]
    else:
        scratch.append(pltpu.VMEM((width, width), half_type))
    return pl.pallas_call(
        kernel,
        grid=(2,),
        in_specs=[part, part, whole_block(mover.shape), whole_block(table.shape)]
        + weight.specs(width, lambda j: 0),
        out_specs=out_specs,
        out_shape=outs,
        scratch_shapes=scratch,
        cost_estimate=cost(6 * rows * width * width, 14 * rows * width),
        compiler_params=grant(24),
        name="mix_out",
    )(mixed, states, mover, table, *weight.refs())


def feed_forward(normed, middle, w_up, w_down, keep):
    rows, width = middle.shape
    tile = FF_TILE
    steps = w_up.cols // tile

    def kernel(b_ref, m_ref, uown_ref, uown2_ref, ugot_ref, ugot2_ref, down_ref, down2_ref, dgot_ref, dgot2_ref, out_ref, *rest):
        step = pl.program_id(0)
        hidden = contract(b_ref[...], stacked(uown_ref, uown2_ref, ugot_ref, ugot2_ref), 1, 0)
        cdf = normal_cdf(hidden)
        active = half(hidden * cdf)
        if keep:
            rest[0][...] = active
            rest[1][...] = cdf + hidden * (
                jnp.exp(-0.5 * hidden * hidden) * ((0.5 / jnp.pi) ** 0.5)
            )
        part = contract(active, stacked(down_ref, down2_ref, dgot_ref, dgot2_ref), 1, 1)

        @pl.when(step == 0)
        def _():
            out_ref[...] = m_ref[...] + part

        @pl.when(step > 0)
        def _():
            out_ref[...] += part

    outs = [shape_of((rows, width), full_type)]
    out_specs = [whole_block((rows, width))]
    if keep:
        outs += [kept_shape((rows, w_up.cols), half_type), kept_shape((rows, w_up.cols), full_type)]
        out_specs += [pl.BlockSpec((rows, tile), lambda j: (0, j))] * 2
    return pl.pallas_call(
        kernel,
        grid=(steps,),
        in_specs=[whole_block(normed.shape), whole_block(middle.shape)]
        + w_up.specs(tile)
        + w_down.specs(tile),
        out_specs=out_specs,
        out_shape=outs,
        cost_estimate=cost(4 * rows * width * w_up.cols, 12 * rows * width + 16 * width * w_up.cols),
        compiler_params=grant(30),
        name="feed_forward",
    )(normed, middle, *w_up.refs(), *w_down.refs())


def make_target(first, second, seqs):
    rows, width = first.shape
    tokens = rows // seqs
    cols = width // 2

    def kernel(one_ref, two_ref, out_ref):
        total = None
        for ref in (one_ref, two_ref):
            values = ref[...]
            centre = values - jnp.mean(values, axis=0, keepdims=True)
            variance = jnp.mean(centre * centre, axis=0, keepdims=True)
            term = centre * lax.rsqrt(variance + in_eps)
            total = term if total is None else total + term
        out_ref[...] = total * (1.0 / TOPK)

    block = pl.BlockSpec((tokens, cols), lambda s, j: (s, j))
    return pl.pallas_call(
        kernel,
        grid=(seqs, 2),
        in_specs=[block, block],
        out_specs=block,
        out_shape=shape_of((rows, width), full_type),
        cost_estimate=cost(20 * rows * width, 12 * rows * width),
        compiler_params=grant(16),
        name="make_target",
    )(first, second)


def head_step(states, table, mover, weight, target, mask, total_masked):
    rows, width = states.shape
    tile = rows // 2
    final_row = 2 * LAYERS

    def kernel(
        h_ref, table_ref, mover_ref, own_ref, own2_ref, got_ref, got2_ref, t_ref, mask_ref,
        flow_ref, f_ref, pred_ref, gain_ref, loss_ref, w_ref,
    ):
        step = pl.program_id(0)

        @pl.when(step == 0)
        def _():
            w_ref[...] = half(contract(stacked(own_ref, own2_ref, got_ref, got2_ref), mover_ref[...], 1, 0))
            gain_ref[...] = jnp.zeros_like(gain_ref)
            loss_ref[...] = jnp.zeros_like(loss_ref)

        states_now = h_ref[...]
        gain = table_ref[final_row : final_row + 1, :]
        unit, _ = unit_of(states_now)
        final_normed = half(unit * gain)
        f_ref[...] = final_normed
        flag = mask_ref[...]
        differ = contract(final_normed, w_ref[...], 1, 0) - t_ref[...]
        magnitude = jnp.abs(differ)
        terms = jnp.where(
            magnitude < huber_beta,
            0.5 * differ * differ / huber_beta,
            magnitude - 0.5 * huber_beta,
        )
        loss_ref[...] += jnp.sum(terms * flag, axis=0, keepdims=True)
        grad_pred = half(flag * jnp.clip(differ / huber_beta, -1.0, 1.0) / total_masked)
        pred_ref[...] = half(contract(grad_pred, mover_ref[...], 1, 1))
        grad_in, grad_gain = norm_back(contract(grad_pred, w_ref[...], 1, 1), gain, states_now)
        flow_ref[...] = grad_in
        gain_ref[...] += grad_gain

    part = pl.BlockSpec((tile, width), lambda j: (j, 0))
    row = whole_block((1, width))
    return pl.pallas_call(
        kernel,
        grid=(2,),
        in_specs=[part, whole_block(table.shape), whole_block(mover.shape)]
        + weight.specs(width, lambda j: 0)
        + [part, pl.BlockSpec((tile, 1), lambda j: (j, 0))],
        out_specs=[part, part, part, row, row],
        out_shape=[
            shape_of((rows, width), full_type),
            kept_shape((rows, width), half_type),
            kept_shape((rows, width), half_type),
            shape_of((1, width), full_type),
            shape_of((1, width), full_type),
        ],
        scratch_shapes=[pltpu.VMEM((width, width), half_type)],
        cost_estimate=cost(8 * rows * width * width, 16 * rows * width),
        compiler_params=grant(30),
        name="head_step",
    )(states, table, mover, *weight.refs(), target, mask)


def feed_back(flow, slope, middle, table, row, w_up, w_down):
    rows, width = flow.shape
    tile = FF_TILE
    steps = w_up.cols // tile

    def kernel(
        flow_ref, slope_ref, m_ref, table_ref, uown_ref, uown2_ref, ugot_ref, ugot2_ref, down_ref, down2_ref, dgot_ref, dgot2_ref,
        du_ref, dy_ref, dm_ref, dz_ref, gain_ref, acc_ref,
    ):
        step = pl.program_id(0)

        @pl.when(step == 0)
        def _():
            dy_ref[...] = half(flow_ref[...])

        grad_active = contract(dy_ref[...], stacked(down_ref, down2_ref, dgot_ref, dgot2_ref), 1, 0)
        grad_hidden = half(grad_active * slope_ref[...])
        du_ref[...] = grad_hidden
        part = contract(grad_hidden, stacked(uown_ref, uown2_ref, ugot_ref, ugot2_ref), 1, 1)

        @pl.when(step == 0)
        def _():
            acc_ref[...] = part

        @pl.when(step > 0)
        def _():
            acc_ref[...] += part

        @pl.when(step == steps - 1)
        def _():
            grad_in, grad_gain = norm_back(
                acc_ref[...], table_ref[row : row + 1, :], m_ref[...]
            )
            grad_middle = flow_ref[...] + grad_in
            dm_ref[...] = grad_middle
            dz_ref[...] = half(grad_middle)
            gain_ref[...] = grad_gain

    full = whole_block((rows, width))
    column = pl.BlockSpec((rows, tile), lambda j: (0, j))
    return pl.pallas_call(
        kernel,
        grid=(steps,),
        in_specs=[full, column, full, whole_block(table.shape)]
        + w_up.specs(tile)
        + w_down.specs(tile),
        out_specs=[column, full, full, full, whole_block((1, width))],
        out_shape=[
            kept_shape((rows, w_up.cols), half_type),
            kept_shape((rows, width), half_type),
            shape_of((rows, width), full_type),
            shape_of((rows, width), half_type),
            shape_of((1, width), full_type),
        ],
        scratch_shapes=[pltpu.VMEM((rows, width), full_type)],
        cost_estimate=cost(4 * rows * width * w_up.cols, 40 * rows * width + 8 * width * w_up.cols),
        compiler_params=grant(32),
        name="feed_back",
    )(flow, in_hbm(slope), middle, table, *w_up.refs(), *w_down.refs())


def mix_back(grad_branch, w_rel, mover):
    rows, width = grad_branch.shape
    tile = rows // 2

    def kernel(dz_ref, w_ref, mover_ref, do_ref, nat_ref):
        branch = dz_ref[...]
        grad_rel = half(contract(branch, w_ref[...], 1, 1))
        do_ref[...] = half(contract(grad_rel, mover_ref[...], 1, 1))
        nat_ref[...] = half(contract(branch, mover_ref[...], 1, 1))

    part = pl.BlockSpec((tile, width), lambda j: (j, 0))
    square = whole_block((width, width))
    return pl.pallas_call(
        kernel,
        grid=(2,),
        in_specs=[part, square, square],
        out_specs=[part, part],
        out_shape=[shape_of((rows, width), half_type), kept_shape((rows, width), half_type)],
        cost_estimate=cost(6 * rows * width * width, 10 * rows * width),
        compiler_params=grant(16),
        name="mix_back",
    )(grad_branch, w_rel, mover)


def project_back(grads, grad_middle, states, table, row, weight, mover, mask):
    rows, width = states.shape
    tile = rows // 2
    count = len(grads)
    first = mask is not None

    def kernel(*refs):
        grad_refs, refs = refs[:count], refs[count:]
        w_refs, refs = refs[: 4 * count], refs[4 * count :]
        dm_ref, h_ref, table_ref = refs[:3]
        refs = refs[3:]
        if first:
            mover_ref, mask_ref = refs[:2]
            refs = refs[2:]
        dh_ref, gain_ref = refs[:2]
        step = pl.program_id(0)

        @pl.when(step == 0)
        def _():
            for ref in (gain_ref,) + ((refs[3],) if first else ()):
                ref[...] = jnp.zeros_like(ref)

        total = None
        for place in range(count):
            part = contract(
                grad_refs[place][...], stacked(*w_refs[4 * place : 4 * place + 4]), 1, 1
            )
            total = part if total is None else total + part
        grad_in, grad_gain = norm_back(total, table_ref[row : row + 1, :], h_ref[...])
        flow = dm_ref[...] + grad_in
        dh_ref[...] = flow
        gain_ref[...] += grad_gain
        if first:
            flag = mask_ref[...]
            refs[2][...] = half(contract(half(flow * (1.0 - flag)), mover_ref[...], 1, 1))
            refs[3][...] += jnp.sum(flow * flag, axis=0, keepdims=True)

    part = pl.BlockSpec((tile, width), lambda j: (j, 0))
    vector = whole_block((1, width))
    specs = [part] * count
    args = [in_hbm(grad) for grad in grads]
    for place in range(count):
        specs += weight.specs(width, lambda j, place=place: place)
        args += weight.refs()
    specs += [part, part, whole_block(table.shape)]
    args += [grad_middle, states, table]
    outs = [shape_of((rows, width), full_type), shape_of((1, width), full_type)]
    out_specs = [part, vector]
    if first:
        specs += [whole_block(mover.shape), pl.BlockSpec((tile, 1), lambda j: (j, 0))]
        args += [mover, mask]
        outs += [kept_shape((rows, width), half_type), shape_of((1, width), full_type)]
        out_specs += [part, vector]
    return pl.pallas_call(
        kernel,
        grid=(2,),
        in_specs=specs,
        out_specs=out_specs,
        out_shape=outs,
        cost_estimate=cost(2 * rows * width * weight.cols, 22 * rows * width),
        compiler_params=grant(30),
        name="project_back",
    )(*args)


def weight_grads(pairs):
    rows, width = pairs[0][0].shape
    plan = []
    start = 0
    for place, (_, rights) in enumerate(pairs):
        first = start
        for right in rights:
            tiles = right.shape[1] // width
            plan.append((place, start, tiles, start == first))
            start += tiles
    total = start
    near_rows = width // 2

    def kernel(*refs):
        left_refs, refs = refs[: len(pairs)], refs[len(pairs) :]
        right_refs, refs = refs[: len(plan)], refs[len(plan) :]
        near_ref, far_ref, turned_ref = refs
        step = pl.program_id(0)
        for (place, begin, tiles, fresh), right_ref in zip(plan, right_refs):
            if fresh:

                @pl.when(step == begin)
                def _(place=place):
                    turned_ref[...] = left_refs[place][...].T

            @pl.when((step >= begin) & (step < begin + tiles))
            def _(right_ref=right_ref):
                out = contract(turned_ref[...], right_ref[...], 1, 0)
                near_ref[...] = out[:near_rows]
                far_ref[...] = half(out[near_rows:])

    specs = [whole_block((rows, width)) for _ in pairs]
    args = [left for left, _ in pairs]
    for (_, rights) in pairs:
        args += list(rights)
    for _, begin, tiles, _ in plan:
        specs.append(
            pl.BlockSpec(
                (rows, width),
                lambda j, begin=begin, tiles=tiles: (0, jnp.clip(j - begin, 0, tiles - 1)),
            )
        )
    block = pl.BlockSpec((near_rows, width), lambda j: (0, j))
    shapes = [
        kept_shape((near_rows, total * width), full_type),
        shape_of((near_rows, total * width), half_type),
    ]
    return tuple(
        pl.pallas_call(
            kernel,
            grid=(total,),
            in_specs=specs,
            out_specs=[block, block],
            out_shape=shapes,
            scratch_shapes=[pltpu.VMEM((width, rows), half_type)],
            cost_estimate=cost(
                2 * rows * width * width * total, width * total * (4 * width + 2 * rows)
            ),
            compiler_params=grant(30),
        name="weight_grads",
        )(*[in_hbm(arg) for arg in args])
    )


def small_grads(flow, vectors, seqs):
    rows, width = flow.shape
    tokens = rows // seqs
    cols = tokens + 8
    cols += -cols % LANES

    def kernel(flow_ref, *refs):
        vector_refs, (near_ref, far_ref) = refs[:-2], refs[-2:]
        posit = flow_ref[:tokens]
        for seq in range(1, seqs):
            posit = posit + flow_ref[seq * tokens : (seq + 1) * tokens]
        fill = jnp.zeros((cols - tokens - len(vector_refs), width), full_type)
        table = jnp.concatenate([posit] + [ref[...] for ref in vector_refs] + [fill], axis=0).T
        near_ref[...] = table[: width // 2]
        far_ref[...] = half(table[width // 2 :])

    shapes = [shape_of((width // 2, cols), kind) for kind in (full_type, half_type)]
    return tuple(
        pl.pallas_call(
            kernel,
            grid=(1,),
            in_specs=[whole_block(flow.shape)] + [whole_block((1, width)) for _ in vectors],
            out_specs=[whole_block(shape.shape) for shape in shapes],
            out_shape=shapes,
            cost_estimate=cost(2 * rows * width, 8 * rows * width),
            compiler_params=grant(16),
        name="small_grads",
        )(flow, *vectors)
    )


class Plan:
    def __init__(self):
        self.seq_size = lax.axis_size("seq")
        self.count = lax.axis_size("dp") * self.seq_size
        self.bits = self.count.bit_length() - 1
        self.early = list(range(self.bits - 1, 2, -1))

        def flips(pick):
            return [(i, i ^ (1 << pick((i >> 1) & 1))) for i in range(self.count)]

        self.stages = [flips(lambda core, b=b: b) for b in self.early]
        self.stages.append(flips(lambda core: 0 if core else 2))
        self.stages.append(flips(lambda core: 2 if core else 0))
        self.core_stage = flips(lambda core: 1)
        self.index = lax.axis_index("dp") * self.seq_size + lax.axis_index("seq")

    def swap(self, value, perm):
        return lax.ppermute(value, AXES, perm)

    def row_table(self, width):
        rows = width // self.count
        place = lax.broadcasted_iota(jnp.int32, (1, width), 1)
        spot = place // rows
        early_count = len(self.early)
        other = (spot >> (self.bits - 1)) & 1
        holder_core = ((self.index >> 1) & 1) ^ other
        block = self.index ^ (other << 1)
        for step, bit in enumerate(self.early):
            block = block ^ (((spot >> step) & 1) << bit)
        first = (spot >> early_count) & 1
        second = (spot >> (early_count + 1)) & 1
        block = block ^ jnp.where(holder_core == 0, first << 2, first)
        block = block ^ jnp.where(holder_core == 0, second, second << 2)
        return block * rows + place % rows

    def mover(self, width):
        table = self.row_table(width)
        whole = lax.broadcasted_iota(jnp.int32, (width, width), 0)
        return (whole == table).astype(half_type)


class Pump:
    def __init__(self, plan):
        self.plan = plan
        self.jobs = []

    def add(self, steps, done, ticks=()):
        self.jobs.append(
            {"steps": steps, "sends": next(steps), "done": done, "stage": 0, "ticks": dict(ticks)}
        )

    def start(self, job):
        job["gots"] = [self.plan.swap(value, perm) for value, perm in job["sends"]]
        job["left"] = job["ticks"].get(job["stage"], 1)

    def advance(self, job, gots):
        job["stage"] += 1
        job["gots"] = None
        try:
            job["sends"] = job["steps"].send(gots)
            return True
        except StopIteration as stop:
            job["done"](stop.value)
            return False

    def begin(self):
        for job in self.jobs:
            if job.get("gots") is None:
                self.start(job)

    def end(self, values=()):
        due = []
        for job in self.jobs:
            job["left"] -= 1
            if job["left"] == 0:
                due.append(job)
        flying, values = lax.optimization_barrier(([job["gots"] for job in due], values))
        over = [job for job, gots in zip(due, flying) if not self.advance(job, gots)]
        self.jobs = [job for job in self.jobs if job not in over]
        return values

    def drain(self):
        newest = self.jobs[-1]
        while self.jobs:
            self.begin()
            if self.jobs[-1] is newest:
                if self.advance(newest, newest["gots"]):
                    self.start(newest)
                else:
                    self.jobs.pop()
            self.end()


def scatter_steps(plan, pieces, narrow):
    gots = yield [(far, plan.core_stage) for _, far in pieces]
    quarter = pieces[0][0].shape[0] // 2
    sums = [
        (half(near[quarter:] + got[quarter:]), near[:quarter] + got[:quarter])
        for (near, _), got in zip(pieces, gots)
    ]
    send = jnp.concatenate([part for part, _ in sums], axis=1)
    keep = jnp.concatenate([part for _, part in sums], axis=1)
    stages = plan.stages[::-1]
    for step, perm in enumerate(stages):
        (got,) = yield [(send, perm)]
        if step == len(stages) - 1:
            return keep + got
        middle = keep.shape[0] // 2
        send = keep[middle:] + got[middle:]
        if step < narrow - 1:
            send = half(send)
        keep = keep[:middle] + got[:middle]


def adam_step(weight, first_mom, second_mom, teacher, gradient):
    first_new = first_decay * first_mom + (1.0 - first_decay) * gradient
    second_new = second_decay * second_mom + (1.0 - second_decay) * gradient * gradient
    weight_new = weight - learn_rate * (
        first_new / (jnp.sqrt(second_new) + adam_eps) + weight_decay * weight
    )
    teacher_new = teacher_keep * teacher + (1.0 - teacher_keep) * weight_new
    return (weight_new, first_new, second_new, teacher_new)


def norm_totals(edge, attn_zero, attn_one, mlp_zero, mlp_one, loss_row, width, tokens):
    stop = 4 * width

    def kernel(edge_ref, first_ref, second_ref, zero_ref, one_ref, loss_ref, out_ref):
        def square(value):
            return jnp.sum(value * value)

        small = edge_ref[:, width:]
        lane = lax.broadcasted_iota(jnp.int32, small.shape, 1)
        posit = jnp.where(lane < tokens, small, 0.0)
        vecs = jnp.where(lane >= tokens, small, 0.0)
        parts = [
            jnp.sum(loss_ref[...]),
            square(edge_ref[:, :width]) + square(second_ref[:, stop:]),
            square(first_ref[...]) + square(second_ref[:, :stop]),
            square(zero_ref[...]) + square(one_ref[...]),
            square(posit),
            square(vecs),
        ]
        row = lax.broadcasted_iota(jnp.int32, (8, LANES), 0)
        out = jnp.zeros((8, LANES), full_type)
        for place, part in enumerate(parts):
            out = jnp.where(row == place, part, out)
        out_ref[...] = out

    args = (edge, attn_zero, attn_one, mlp_zero, mlp_one, loss_row)
    return pl.pallas_call(
        kernel,
        grid=(1,),
        in_specs=[whole_block(arg.shape) for arg in args],
        out_specs=whole_block((8, LANES)),
        out_shape=shape_of((8, LANES), full_type),
        compiler_params=grant(16),
        name="norm_totals",
    )(*args)


def update(totals, edge, attn_zero, attn_one, mlp_zero, mlp_one, groups, sizes, width, tokens):
    stop = mlp_zero.shape[1]

    def kernel(total_ref, edge_ref, first_ref, second_ref, zero_ref, one_ref, *refs):
        ins, outs = refs[:20], refs[20:]

        def step(group, gradient, cols=slice(None)):
            limit = entry_clip * sizes[group] ** 0.5
            norm_value = jnp.sqrt(total_ref[group + 1 : group + 2, 0:1])
            gradient = gradient * (limit / jnp.maximum(norm_value, limit))
            weight, first, second, teacher = (
                ref[:, cols] for ref in ins[4 * group : 4 * group + 4]
            )
            news = adam_step(weight, first, second, teacher, gradient)
            for ref, new in zip(outs[4 * group : 4 * group + 4], news):
                ref[:, cols] = new

        step(0, edge_ref[:, :width], slice(0, width))
        step(0, second_ref[:, 4 * width :], slice(width, 2 * width))
        step(1, first_ref[...], slice(0, 4 * width))
        step(1, second_ref[:, : 4 * width], slice(4 * width, 8 * width))
        step(2, zero_ref[...], slice(0, stop))
        step(2, one_ref[...], slice(stop, 2 * stop))
        step(3, edge_ref[:, width : width + tokens])
        start = tokens // LANES * LANES
        turned = edge_ref[:, width + start : width + start + LANES].T
        count = ins[16].shape[0]
        step(4, turned[tokens - start : tokens - start + count])

    args = [totals, edge, attn_zero, attn_one, mlp_zero, mlp_one] + [part for group in groups for part in group]
    outs = [shape_of(part.shape, full_type) for group in groups for part in group]
    return pl.pallas_call(
        kernel,
        grid=(1,),
        in_specs=[whole_block(arg.shape) for arg in args],
        out_specs=[whole_block(out.shape) for out in outs],
        out_shape=outs,
        compiler_params=grant(40),
        name="update",
    )(*args)


def pad_lanes(value):
    extra = -value.shape[1] % LANES
    return jnp.pad(value, ((0, 0), (0, extra)))


def local(
    patches,
    masked_at,
    edge_w,
    attn_w,
    mlp_w,
    posit_w,
    vecs_w,
    edge_m,
    attn_m,
    mlp_m,
    posit_m,
    vecs_m,
    edge_v,
    attn_v,
    mlp_v,
    posit_v,
    vecs_v,
    edge_t,
    attn_t,
    mlp_t,
    posit_t,
    vecs_t,
):
    seqs, tokens, width = patches.shape
    plan = Plan()
    total_masked = seqs * plan.count * tokens // 2
    ff_width = mlp_w.shape[1] // (2 * LAYERS)
    small_cols = tokens + vecs_w.shape[1]
    flat_patch = patches.reshape(-1, width)
    mask_flat = masked_at.astype(full_type).reshape(-1, 1)
    mover = plan.mover(width)

    def shards(edge, attn, mlp, posit, vecs):
        small = pad_lanes(jnp.concatenate([posit, vecs], axis=1))
        return [edge[:, :width], edge[:, width:], small] + [
            [
                part[:, layer * part.shape[1] // LAYERS : (layer + 1) * part.shape[1] // LAYERS]
                for part in (attn, mlp)
            ]
            for layer in range(LAYERS)
        ]

    def joined(parts):
        return jnp.concatenate([half(part) for part in parts], axis=1)

    t_patch, _, t_small, t_one, t_two = shards(edge_t, attn_t, mlp_t, posit_t, vecs_t)
    s_patch, s_head, s_small, s_one, s_two = shards(edge_w, attn_w, mlp_w, posit_w, vecs_w)
    chunks = [
        [t_patch, t_one[0], t_small],
        [t_one[1]],
        t_two,
        [s_patch, s_one[0], s_small],
        [s_one[1]],
        [s_two[0], s_head],
        [s_two[1]],
    ]
    groups = [[0], [1], [2], [3], [4, 5, 6]]
    group_start = [0, 1, 2, 3, 4]

    def attn_weights(blocks, start):
        return Weight(blocks, start, 3 * width), Weight(blocks, start + 3 * width, width)

    def mlp_weights(blocks, start):
        return Weight(blocks, start, ff_width), Weight(blocks, start + ff_width, ff_width)

    def small_of(blocks):
        return Weight(blocks, 5 * width, t_small.shape[1])

    def finish(blocks):
        return list(blocks) + [plan.swap(blocks[1], plan.core_stage)]

    def attend_forward(states, table, layer, w_qkv, w_out, keep, outs=None):
        if outs is None:
            outs = norm_project(states, table, layer, w_qkv, keep)
        projected = outs[0].reshape(seqs, tokens, w_qkv.cols)
        mixed = attend(projected).reshape(-1, width)
        results = mix_out(mixed, states, mover, table, LAYERS + layer, w_out, keep)
        if keep:
            return results[0], results[1], (states, outs[1], projected) + tuple(results[2:])
        return results[0], results[1], ()

    saved_attn = [None] * LAYERS
    saved_mlp = [None] * LAYERS

    def segment_t0(_, blocks):
        patch = Weight(blocks, 0, width)
        states, table, patch_rel = embed(
            flat_patch, None, mover, patch, small_of(blocks), True
        )
        weights = attn_weights(blocks, width)
        return states, table, patch_rel, norm_project(states, table, 0, weights[0], False)

    def segment_t0_rest(values, blocks):
        states, table, patch_rel, outs = values
        weights = attn_weights(blocks, width)
        middle, normed, _ = attend_forward(states, table, 0, *weights, False, outs)
        return middle, normed, table, patch_rel

    def segment_t1(values, blocks):
        middle, normed, table, patch_rel = values
        (states,) = feed_forward(normed, middle, *mlp_weights(blocks, 0), False)
        return states, table, patch_rel

    def segment_t2(values, blocks):
        first, table, patch_rel = values
        middle, normed, _ = attend_forward(first, table, 1, *attn_weights(blocks, 0), False)
        (second,) = feed_forward(normed, middle, *mlp_weights(blocks, 4 * width), False)
        return make_target(first, second, seqs), patch_rel

    def segment_s0(values, blocks):
        target, patch_rel = values
        patch = Weight(blocks, 0, width)
        states, table = embed(flat_patch, mask_flat, mover, patch, small_of(blocks), False)
        weights = attn_weights(blocks, width)
        middle, normed, saved = attend_forward(states, table, 0, *weights, True)
        saved_attn[0] = (weights[0], saved)
        return target, patch_rel, table, middle, normed

    def segment_s1(values, blocks):
        target, patch_rel, table, middle, normed = values
        weights = mlp_weights(blocks, 0)
        states, active, slope = feed_forward(normed, middle, *weights, True)
        saved_mlp[0] = (weights, middle, normed, active, slope)
        return target, patch_rel, table, states

    def segment_s2(values, blocks):
        target, patch_rel, table, states = values
        weights = attn_weights(blocks, 0)
        middle, normed, saved = attend_forward(states, table, 1, *weights, True)
        saved_attn[1] = (weights[0], saved)
        return target, patch_rel, table, middle, normed, blocks

    segments = [segment_t0_rest, segment_t1, segment_t2, segment_s0, segment_s1, segment_s2]
    early = len(plan.early)
    group_values = [joined([part for c in group for part in chunks[c]]) for group in groups]
    own = [None] * len(chunks)
    blocks = [None] * len(chunks)
    values = ()
    ahead = {}
    for tick in range(len(chunks) + early + 1):
        sends = {}
        for group, start in enumerate(group_start):
            if 0 <= tick - start < early:
                sends["early", group] = (group_values[group], plan.stages[tick - start])
        for chunk in range(len(chunks)):
            if tick == chunk + early:
                sends["first", chunk] = (own[chunk], plan.stages[early])
            if tick == chunk + early + 1 and ("second", chunk) not in ahead:
                sends["second", chunk] = (own[chunk], plan.stages[early + 1])
                sends["core", chunk] = (own[chunk], plan.core_stage)
        gots = {key: plan.swap(value, perm) for key, (value, perm) in sends.items()}
        if tick == early + 2:
            gots.update(ahead)
        place = tick - early - 2
        if 0 <= place < len(segments):
            values = segments[place](values, finish(blocks[place]))
        if tick == early + 1:
            lead = [gots.pop(key) for key in (("second", 0), ("core", 0), ("first", 1))]
            later = [g for g in range(len(groups)) if group_start[g] > tick]
            lead, held = lax.optimization_barrier((lead, [group_values[g] for g in later]))
            for g, value in zip(later, held):
                group_values[g] = value
            own[1] = jnp.concatenate([own[1], lead[2]], axis=0)
            ahead = {
                ("second", 1): plan.swap(own[1], plan.stages[early + 1]),
                ("core", 1): plan.swap(own[1], plan.core_stage),
            }
            blocks[0] = (own[0], lead[0], lead[1])
            values = segment_t0(values, finish(blocks[0]))
        apart = {key: got for key, got in gots.items() if FAST_LANE and key[1] == 0 and tick}
        gots = {key: got for key, got in gots.items() if key not in apart}
        later = [g for g in range(len(groups)) if group_start[g] > tick]
        idle = [c for c in range(1, len(chunks)) if own[c] is not None and c + early > tick]
        gots, values, held, held_own, _ = lax.optimization_barrier(
            (gots, values, [group_values[g] for g in later], [own[c] for c in idle], apart)
        )
        for g, value in zip(later, held):
            group_values[g] = value
        for c, value in zip(idle, held_own):
            own[c] = value
        gots.update(apart)
        for (kind, index), got in gots.items():
            if kind == "early":
                group_values[index] = jnp.concatenate([group_values[index], got], axis=0)
                if tick - group_start[index] == early - 1:
                    start = 0
                    for chunk in groups[index]:
                        stop = start + sum(part.shape[1] for part in chunks[chunk])
                        own[chunk] = group_values[index][:, start:stop]
                        start = stop
            elif kind == "first":
                own[index] = jnp.concatenate([own[index], got], axis=0)
        for chunk in range(len(chunks)):
            if ("second", chunk) in gots:
                blocks[chunk] = (own[chunk], gots["second", chunk], gots["core", chunk])
    pump = Pump(plan)
    target, patch_rel, table, middle, normed, head_blocks = values
    weights = mlp_weights(finish(blocks[-1]), 0)
    states, active, slope = feed_forward(normed, middle, *weights, True)
    saved_mlp[1] = (weights, middle, normed, active, slope)
    flow, final_normed, grad_pred, grad_gain_final, loss_row = head_step(
        states,
        table,
        mover,
        Weight(head_blocks, 4 * width, width),
        target,
        mask_flat,
        total_masked,
    )

    gain_ones = [None] * LAYERS
    gain_twos = [None] * LAYERS
    shards = {}
    last_stage = len(plan.stages)

    def send_off(name, pieces, narrow, ticks=()):
        pump.add(
            scatter_steps(plan, pieces, narrow), lambda out: shards.__setitem__(name, out), ticks
        )

    for layer in reversed(range(LAYERS)):
        w_qkv, (states, normed_one, projected, mixed_rel, w_out_rel) = saved_attn[layer]
        (w_up, w_down), middle, normed_two, active, slope = saved_mlp[layer]
        pump.begin()
        grad_hidden, grad_down, grad_middle, grad_branch, gain_twos[layer] = feed_back(
            flow, slope, middle, table, LAYERS + layer, w_up, w_down
        )
        grad_hidden, grad_down, grad_middle, grad_branch = pump.end(
            (grad_hidden, grad_down, grad_middle, grad_branch)
        )
        pump.begin()
        piece = weight_grads([(normed_two, [grad_hidden]), (grad_down, [active])])
        piece, grad_branch = pump.end((piece, grad_branch))
        send_off(
            ("mlp", layer), [piece], 3, {1: 2, last_stage: 2} if layer else {last_stage: 2}
        )
        pump.begin()
        grad_mixed, branch_whole = mix_back(grad_branch, w_out_rel, mover)
        grad_mixed = grad_mixed.reshape(seqs, tokens, width)
        grad_proj = ()
        for seq in range(seqs - 1):
            grad_proj = attend_back(projected, grad_mixed, seq, tuple(grad_proj))
        grad_proj, grad_mixed, branch_whole = pump.end((grad_proj, grad_mixed, branch_whole))
        pump.begin()
        grad_proj = attend_back(projected, grad_mixed, seqs - 1, tuple(grad_proj))
        grad_proj = [part.reshape(-1, width) for part in grad_proj]
        pairs = [(normed_one, grad_proj), (mixed_rel, [branch_whole])]
        if layer == 0:
            piece = weight_grads(pairs)
            piece, grad_proj = pump.end((piece, grad_proj))
            send_off(("attn", 0), [piece], 3)
            pump.begin()
        results = project_back(
            grad_proj,
            grad_middle,
            states,
            table,
            layer,
            w_qkv,
            mover,
            None if layer else mask_flat,
        )
        flow, gain_ones[layer] = results[:2]
        if layer:
            flow, grad_proj = pump.end((flow, grad_proj))
            pairs = [(normed_one, grad_proj), (mixed_rel, [branch_whole])]
            pairs.append((final_normed, [grad_pred]))
            pump.begin()
            piece = weight_grads(pairs)
            piece, flow = pump.end((piece, flow))
            send_off(("attn", layer), [piece], 2)
    grad_embed, grad_maskvec = results[2:]
    vectors = gain_ones + gain_twos + [grad_gain_final, grad_maskvec]
    pieces = pump.end(
        [weight_grads([(patch_rel, [grad_embed])]), small_grads(flow, vectors, seqs)]
    )
    send_off("edge", pieces, 2)
    pump.drain()
    pieces = (
        shards["edge"],
        shards["attn", 0],
        shards["attn", 1],
        shards["mlp", 0],
        shards["mlp", 1],
    )
    totals = norm_totals(*pieces, loss_row, width, tokens)
    for perm in [plan.core_stage] + plan.stages:
        totals = totals + plan.swap(totals, perm)
    groups = [
        (edge_w, edge_m, edge_v, edge_t),
        (attn_w, attn_m, attn_v, attn_t),
        (mlp_w, mlp_m, mlp_v, mlp_t),
        (posit_w, posit_m, posit_v, posit_t),
        (vecs_w.T, vecs_m.T, vecs_v.T, vecs_t.T),
    ]
    sizes = [group[0].size * plan.count for group in groups]
    news = update(totals, *pieces, groups, sizes, width, tokens)
    news = [
        [news[4 * group + part] for group in range(4)] + [news[16 + part].T] for part in range(4)
    ]
    return (totals[0, 0] / total_masked,) + tuple(new for part in news for new in part)


def solution(mesh):
    rows = P(AXES, None)
    in_specs = (P(AXES, None, None),) + (rows,) * 21
    out_specs = (P(),) + (rows,) * 20
    return jax.shard_map(local, mesh=mesh, in_specs=in_specs, out_specs=out_specs, check_vma=False)
```

```python
import jax
import jax.numpy as jnp
from jax import lax
from jax.experimental import pallas as pl
from jax.experimental.pallas import tpu as pltpu
from jax.sharding import PartitionSpec as P

HDIM = 64
LAYERS = 2
TOPK = 2
LANES = 128
FF_TILE = 512
SMALL_TILE = 256
ROW_TILE = 64
PAIRS = 2
FAST_LANE = True

ln_eps = 1e-05
in_eps = 1e-05
learn_rate = 0.02
first_decay = 0.5
second_decay = 0.5
adam_eps = 1e-08
weight_decay = 0.1
teacher_keep = 0.5
huber_beta = 1.0
score_scale = 0.125
entry_clip = 1e-05
half_type = jnp.bfloat16
full_type = jnp.float32
AXES = ("dp", "seq")


def contract(left, right, left_dim, right_dim):
    return lax.dot_general(
        left,
        right,
        (((left_dim,), (right_dim,)), ((), ())),
        preferred_element_type=full_type,
    )


def head_mask(which, width):
    lane = lax.broadcasted_iota(jnp.int32, (1, width), 1)
    return (lane // HDIM) == which


def head_part(values, which):
    return jnp.where(head_mask(which, LANES), values, jnp.zeros_like(values))


def softmax_rows(scores):
    exps = jnp.exp(scores - jnp.max(scores, axis=1, keepdims=True))
    return exps * (1.0 / jnp.sum(exps, axis=1, keepdims=True))


def attend_kernel(q_ref, k_ref, v_ref, o_ref, score_ref, prob_ref):
    tokens = q_ref.shape[1]
    heads = LANES // HDIM
    for start in range(0, q_ref.shape[2], LANES):
        cols = slice(start, start + LANES)
        queries = q_ref[0, :, cols] * jnp.asarray(score_scale, half_type)
        for which in range(heads):
            score_ref[which] = contract(head_part(queries, which), k_ref[0, :, cols], 1, 1)
        for which in range(heads):
            for row in range(0, tokens, ROW_TILE):
                rows = slice(row, row + ROW_TILE)
                prob_ref[which, rows] = softmax_rows(score_ref[which, rows]).astype(half_type)
        mixed = None
        for which in range(heads):
            out = contract(prob_ref[which], v_ref[0, :, cols], 1, 0)
            mixed = out if mixed is None else jnp.where(head_mask(which, LANES), out, mixed)
        o_ref[0, :, cols] = mixed.astype(half_type)


def attend_back_kernel(q_ref, k_ref, v_ref, do_ref, dq_ref, dk_ref, dv_ref, *scratch):
    score_ref, grad_ref, prob_ref, back_ref = scratch
    tokens = q_ref.shape[1]
    heads = LANES // HDIM
    for start in range(0, q_ref.shape[2], LANES):
        cols = slice(start, start + LANES)
        queries = q_ref[0, :, cols] * jnp.asarray(score_scale, half_type)
        keys_now = k_ref[0, :, cols]
        grad_out = do_ref[0, :, cols]
        for which in range(heads):
            score_ref[which] = contract(head_part(queries, which), keys_now, 1, 1)
            grad_ref[which] = contract(head_part(grad_out, which), v_ref[0, :, cols], 1, 1)
        for which in range(heads):
            for row in range(0, tokens, ROW_TILE):
                rows = slice(row, row + ROW_TILE)
                probs = softmax_rows(score_ref[which, rows])
                prob_ref[which, rows] = probs.astype(half_type)
                prods = probs * grad_ref[which, rows]
                back_ref[which, rows] = (
                    prods - probs * jnp.sum(prods, axis=1, keepdims=True)
                ).astype(half_type)
        turned_k = []
        turned_v = []
        grad_q = None
        for which in range(heads):
            part = slice(which * HDIM, (which + 1) * HDIM)
            turned_v.append(contract(grad_out, prob_ref[which], 0, 0)[part])
            turned_k.append(contract(queries, back_ref[which], 0, 0)[part])
            out = contract(back_ref[which], keys_now, 1, 0)
            grad_q = out if grad_q is None else jnp.where(head_mask(which, LANES), out, grad_q)
        dq_ref[0, :, cols] = (grad_q * score_scale).astype(half_type)
        dk_ref[0, :, cols] = jnp.concatenate(turned_k, axis=0).T.astype(half_type)
        dv_ref[0, :, cols] = jnp.concatenate(turned_v, axis=0).T.astype(half_type)


def attend(projected):
    seqs, tokens, width3 = projected.shape
    width = width3 // 3
    wide = PAIRS * LANES
    blocks = width // wide
    specs = [
        pl.BlockSpec((1, tokens, wide), lambda s, j, off=off: (s, 0, off * blocks + j))
        for off in range(3)
    ]
    heads = LANES // HDIM
    return pl.pallas_call(
        attend_kernel,
        grid=(seqs, blocks),
        in_specs=specs,
        out_specs=pl.BlockSpec((1, tokens, wide), lambda s, j: (s, 0, j)),
        out_shape=jax.ShapeDtypeStruct((seqs, tokens, width), half_type),
        scratch_shapes=[
            pltpu.VMEM((heads, tokens, tokens), full_type),
            pltpu.VMEM((heads, tokens, tokens), half_type),
        ],
        cost_estimate=pl.CostEstimate(
            flops=16 * seqs * tokens * tokens * width,
            transcendentals=seqs * tokens * tokens * width // HDIM,
            bytes_accessed=8 * seqs * tokens * width,
        ),
        compiler_params=grant(16),
        name="attend",
    )(projected, projected, projected)


def attend_back(projected, grad_mixed, seq, into=()):
    seqs, tokens, width3 = projected.shape
    width = width3 // 3
    wide = PAIRS * LANES
    blocks = width // wide
    block = pl.BlockSpec((1, tokens, wide), lambda j: (seq, 0, j))
    specs = [
        pl.BlockSpec((1, tokens, wide), lambda j, off=off: (seq, 0, off * blocks + j))
        for off in range(3)
    ]
    heads = LANES // HDIM
    skip = len(into)

    def kernel(q_ref, k_ref, v_ref, do_ref, *refs):
        attend_back_kernel(q_ref, k_ref, v_ref, do_ref, *refs[skip:])

    shape = kept_shape((seqs, tokens, width), half_type)
    return pl.pallas_call(
        kernel,
        grid=(blocks,),
        in_specs=specs + [block] + [pl.BlockSpec(memory_space=pl.ANY)] * skip,
        out_specs=[block, block, block],
        out_shape=[shape, shape, shape],
        input_output_aliases={4 + place: place for place in range(skip)},
        scratch_shapes=[
            pltpu.VMEM((heads, tokens, tokens), kind)
            for kind in (full_type, full_type, half_type, half_type)
        ],
        cost_estimate=pl.CostEstimate(
            flops=32 * tokens * tokens * width,
            transcendentals=tokens * tokens * width // HDIM,
            bytes_accessed=14 * tokens * width,
        ),
        compiler_params=grant(20),
        name="attend_back",
    )(projected, projected, projected, grad_mixed, *into)


def normal_cdf(values):
    return 0.5 + 0.5 * lax.erf(values * (0.5**0.5))


def whole_block(shape):
    zeros = (0,) * len(shape)
    return pl.BlockSpec(shape, lambda *_: zeros, pipeline_mode=pl.Buffered(1))


def grant(mib):
    return pltpu.CompilerParams(vmem_limit_bytes=mib << 20)


def stacked(*refs):
    return jnp.concatenate([ref[...] for ref in refs], axis=0)


def unit_of(values):
    centre = values - jnp.mean(values, axis=1, keepdims=True)
    inv_scale = lax.rsqrt(jnp.mean(centre * centre, axis=1, keepdims=True) + ln_eps)
    return centre * inv_scale, inv_scale


def norm_back(grad_out, gain, values):
    unit, inv_scale = unit_of(values)
    grad_unit = grad_out * gain
    inner_mean = jnp.mean(grad_unit, axis=1, keepdims=True)
    along_mean = jnp.mean(grad_unit * unit, axis=1, keepdims=True)
    grad_in = (grad_unit - inner_mean - unit * along_mean) * inv_scale
    return grad_in, jnp.sum(grad_out * unit, axis=0, keepdims=True)


def half(values):
    return values.astype(half_type)


def shape_of(shape, kind):
    return jax.ShapeDtypeStruct(shape, kind)


def kept_shape(shape, kind):
    return pltpu.HBM(shape, kind)


def cost(flops, moved):
    return pl.CostEstimate(flops=flops, transcendentals=0, bytes_accessed=moved)


def in_hbm(value):
    return pltpu.with_memory_space_constraint(value, pltpu.HBM)


class Weight:
    def __init__(self, blocks, start, cols):
        self.blocks, self.start, self.cols = list(blocks), start, cols

    def specs(self, width, index=lambda j: j):
        base = self.start // width
        spec = pl.BlockSpec(
            (self.blocks[0].shape[0], width), lambda j, base=base: (0, base + index(j))
        )
        return [spec] * len(self.blocks)

    def refs(self):
        return [in_hbm(block) for block in self.blocks[:-1]] + self.blocks[-1:]


def embed(patches, mask, mover, weight, small, keep_patches):
    rows, width = patches.shape
    tokens = rows // 2
    masked = mask is not None
    pieces = small.cols // SMALL_TILE

    def kernel(*refs):
        x_ref, mover_ref = refs[:2]
        w_refs, small_refs, refs = refs[2:6], refs[6 : 6 + 4 * pieces], refs[6 + 4 * pieces :]
        if masked:
            mask_ref, refs = refs[0], refs[1:]
        h_ref, table_ref = refs[:2]
        x_rel = half(contract(x_ref[...], mover_ref[...], 1, 0))
        if keep_patches:
            refs[2][...] = x_rel
        w_rel = half(contract(stacked(*w_refs), mover_ref[...], 1, 0))
        small_parts = [stacked(*small_refs[4 * k : 4 * k + 4]) for k in range(pieces)]
        small_t = jnp.concatenate(small_parts, axis=1).astype(full_type).T
        posit = small_t[:tokens]
        table = small_t[tokens : tokens + 8]
        table_ref[...] = table
        states = contract(x_rel, w_rel, 1, 0)
        for seq in range(rows // tokens):
            part = slice(seq * tokens, (seq + 1) * tokens)
            state = states[part]
            if masked:
                flag = mask_ref[part, :]
                state = state * (1.0 - flag) + flag * table[2 * LAYERS + 1 : 2 * LAYERS + 2]
            h_ref[part, :] = state + posit

    outs = [shape_of((rows, width), full_type), shape_of((8, width), full_type)]
    if keep_patches:
        outs.append(kept_shape((rows, width), half_type))
    args = [patches, mover] + weight.refs() + small.refs() * pieces + ([mask] if masked else [])
    specs = [whole_block(patches.shape), whole_block(mover.shape)] + weight.specs(width)
    for k in range(pieces):
        specs += small.specs(SMALL_TILE, lambda j, k=k: k)
    if masked:
        specs.append(whole_block(mask.shape))
    return pl.pallas_call(
        kernel,
        grid=(1,),
        in_specs=specs,
        out_specs=[whole_block(out.shape) for out in outs],
        out_shape=outs,
        cost_estimate=cost(6 * rows * width * width, 12 * rows * width),
        compiler_params=grant(28),
        name="embed",
    )(*args)


def norm_project(states, table, row, weight, keep):
    rows, width = states.shape
    steps = weight.cols // width

    def kernel(h_ref, table_ref, own_ref, own2_ref, got_ref, got2_ref, out_ref, a_ref):
        @pl.when(pl.program_id(0) == 0)
        def _():
            unit, _ = unit_of(h_ref[...])
            a_ref[...] = half(unit * table_ref[row : row + 1, :])

        out_ref[...] = half(contract(a_ref[...], stacked(own_ref, own2_ref, got_ref, got2_ref), 1, 0))

    outs = [shape_of((rows, weight.cols), half_type)]
    out_specs = [pl.BlockSpec((rows, width), lambda j: (0, j))]
    scratch = []
    if keep:
        outs.append(kept_shape((rows, width), half_type))
        out_specs.append(whole_block((rows, width)))
    else:
        scratch.append(pltpu.VMEM((rows, width), half_type))
    return pl.pallas_call(
        kernel,
        grid=(steps,),
        in_specs=[whole_block(states.shape), whole_block(table.shape)] + weight.specs(width),
        out_specs=out_specs,
        out_shape=outs,
        scratch_shapes=scratch,
        cost_estimate=cost(2 * rows * width * weight.cols, 12 * rows * width),
        compiler_params=grant(24),
        name="norm_project",
    )(states, table, *weight.refs())


def mix_out(mixed, states, mover, table, row, weight, keep):
    rows, width = states.shape
    tile = rows // 2

    def kernel(o_ref, h_ref, mover_ref, table_ref, own_ref, own2_ref, got_ref, got2_ref, m_ref, b_ref, *rest):
        if keep:
            rel_ref, w_ref = rest
        else:
            (w_ref,) = rest

        @pl.when(pl.program_id(0) == 0)
        def _():
            w_ref[...] = half(contract(stacked(own_ref, own2_ref, got_ref, got2_ref), mover_ref[...], 1, 0))

        mixed_rel = half(contract(o_ref[...], mover_ref[...], 1, 0))
        if keep:
            rel_ref[...] = mixed_rel
        middle = h_ref[...] + contract(mixed_rel, w_ref[...], 1, 0)
        m_ref[...] = middle
        unit, _ = unit_of(middle)
        b_ref[...] = half(unit * table_ref[row : row + 1, :])

    part = pl.BlockSpec((tile, width), lambda j: (j, 0))
    outs = [shape_of((rows, width), full_type), shape_of((rows, width), half_type)]
    out_specs = [part, part]
    scratch = []
    if keep:
        outs += [kept_shape((rows, width), half_type), kept_shape((width, width), half_type)]
        out_specs += [part, whole_block((width, width))]
    else:
        scratch.append(pltpu.VMEM((width, width), half_type))
    return pl.pallas_call(
        kernel,
        grid=(2,),
        in_specs=[part, part, whole_block(mover.shape), whole_block(table.shape)]
        + weight.specs(width, lambda j: 0),
        out_specs=out_specs,
        out_shape=outs,
        scratch_shapes=scratch,
        cost_estimate=cost(6 * rows * width * width, 14 * rows * width),
        compiler_params=grant(24),
        name="mix_out",
    )(mixed, states, mover, table, *weight.refs())


def feed_forward(normed, middle, w_up, w_down, keep):
    rows, width = middle.shape
    tile = FF_TILE
    steps = w_up.cols // tile

    def kernel(b_ref, m_ref, uown_ref, uown2_ref, ugot_ref, ugot2_ref, down_ref, down2_ref, dgot_ref, dgot2_ref, out_ref, *rest):
        step = pl.program_id(0)
        hidden = contract(b_ref[...], stacked(uown_ref, uown2_ref, ugot_ref, ugot2_ref), 1, 0)
        cdf = normal_cdf(hidden)
        active = half(hidden * cdf)
        if keep:
            rest[0][...] = active
            rest[1][...] = cdf + hidden * (
                jnp.exp(-0.5 * hidden * hidden) * ((0.5 / jnp.pi) ** 0.5)
            )
        part = contract(active, stacked(down_ref, down2_ref, dgot_ref, dgot2_ref), 1, 1)

        @pl.when(step == 0)
        def _():
            out_ref[...] = m_ref[...] + part

        @pl.when(step > 0)
        def _():
            out_ref[...] += part

    outs = [shape_of((rows, width), full_type)]
    out_specs = [whole_block((rows, width))]
    if keep:
        outs += [kept_shape((rows, w_up.cols), half_type), kept_shape((rows, w_up.cols), full_type)]
        out_specs += [pl.BlockSpec((rows, tile), lambda j: (0, j))] * 2
    return pl.pallas_call(
        kernel,
        grid=(steps,),
        in_specs=[whole_block(normed.shape), whole_block(middle.shape)]
        + w_up.specs(tile)
        + w_down.specs(tile),
        out_specs=out_specs,
        out_shape=outs,
        cost_estimate=cost(4 * rows * width * w_up.cols, 12 * rows * width + 16 * width * w_up.cols),
        compiler_params=grant(30),
        name="feed_forward",
    )(normed, middle, *w_up.refs(), *w_down.refs())


def make_target(first, second, seqs):
    rows, width = first.shape
    tokens = rows // seqs
    cols = width // 2

    def kernel(one_ref, two_ref, out_ref):
        total = None
        for ref in (one_ref, two_ref):
            values = ref[...]
            centre = values - jnp.mean(values, axis=0, keepdims=True)
            variance = jnp.mean(centre * centre, axis=0, keepdims=True)
            term = centre * lax.rsqrt(variance + in_eps)
            total = term if total is None else total + term
        out_ref[...] = total * (1.0 / TOPK)

    block = pl.BlockSpec((tokens, cols), lambda s, j: (s, j))
    return pl.pallas_call(
        kernel,
        grid=(seqs, 2),
        in_specs=[block, block],
        out_specs=block,
        out_shape=shape_of((rows, width), full_type),
        cost_estimate=cost(20 * rows * width, 12 * rows * width),
        compiler_params=grant(16),
        name="make_target",
    )(first, second)


def head_step(states, table, mover, weight, target, mask, total_masked):
    rows, width = states.shape
    tile = rows // 2
    final_row = 2 * LAYERS

    def kernel(
        h_ref, table_ref, mover_ref, own_ref, own2_ref, got_ref, got2_ref, t_ref, mask_ref,
        flow_ref, f_ref, pred_ref, gain_ref, loss_ref, w_ref,
    ):
        step = pl.program_id(0)

        @pl.when(step == 0)
        def _():
            w_ref[...] = half(contract(stacked(own_ref, own2_ref, got_ref, got2_ref), mover_ref[...], 1, 0))
            gain_ref[...] = jnp.zeros_like(gain_ref)
            loss_ref[...] = jnp.zeros_like(loss_ref)

        states_now = h_ref[...]
        gain = table_ref[final_row : final_row + 1, :]
        unit, _ = unit_of(states_now)
        final_normed = half(unit * gain)
        f_ref[...] = final_normed
        flag = mask_ref[...]
        differ = contract(final_normed, w_ref[...], 1, 0) - t_ref[...]
        magnitude = jnp.abs(differ)
        terms = jnp.where(
            magnitude < huber_beta,
            0.5 * differ * differ / huber_beta,
            magnitude - 0.5 * huber_beta,
        )
        loss_ref[...] += jnp.sum(terms * flag, axis=0, keepdims=True)
        grad_pred = half(flag * jnp.clip(differ / huber_beta, -1.0, 1.0) / total_masked)
        pred_ref[...] = half(contract(grad_pred, mover_ref[...], 1, 1))
        grad_in, grad_gain = norm_back(contract(grad_pred, w_ref[...], 1, 1), gain, states_now)
        flow_ref[...] = grad_in
        gain_ref[...] += grad_gain

    part = pl.BlockSpec((tile, width), lambda j: (j, 0))
    row = whole_block((1, width))
    return pl.pallas_call(
        kernel,
        grid=(2,),
        in_specs=[part, whole_block(table.shape), whole_block(mover.shape)]
        + weight.specs(width, lambda j: 0)
        + [part, pl.BlockSpec((tile, 1), lambda j: (j, 0))],
        out_specs=[part, part, part, row, row],
        out_shape=[
            shape_of((rows, width), full_type),
            kept_shape((rows, width), half_type),
            kept_shape((rows, width), half_type),
            shape_of((1, width), full_type),
            shape_of((1, width), full_type),
        ],
        scratch_shapes=[pltpu.VMEM((width, width), half_type)],
        cost_estimate=cost(8 * rows * width * width, 16 * rows * width),
        compiler_params=grant(30),
        name="head_step",
    )(states, table, mover, *weight.refs(), target, mask)


def feed_back(flow, slope, middle, table, row, w_up, w_down):
    rows, width = flow.shape
    tile = FF_TILE
    steps = w_up.cols // tile

    def kernel(
        flow_ref, slope_ref, m_ref, table_ref, uown_ref, uown2_ref, ugot_ref, ugot2_ref, down_ref, down2_ref, dgot_ref, dgot2_ref,
        du_ref, dy_ref, dm_ref, dz_ref, gain_ref, acc_ref,
    ):
        step = pl.program_id(0)

        @pl.when(step == 0)
        def _():
            dy_ref[...] = half(flow_ref[...])

        grad_active = contract(dy_ref[...], stacked(down_ref, down2_ref, dgot_ref, dgot2_ref), 1, 0)
        grad_hidden = half(grad_active * slope_ref[...])
        du_ref[...] = grad_hidden
        part = contract(grad_hidden, stacked(uown_ref, uown2_ref, ugot_ref, ugot2_ref), 1, 1)

        @pl.when(step == 0)
        def _():
            acc_ref[...] = part

        @pl.when(step > 0)
        def _():
            acc_ref[...] += part

        @pl.when(step == steps - 1)
        def _():
            grad_in, grad_gain = norm_back(
                acc_ref[...], table_ref[row : row + 1, :], m_ref[...]
            )
            grad_middle = flow_ref[...] + grad_in
            dm_ref[...] = grad_middle
            dz_ref[...] = half(grad_middle)
            gain_ref[...] = grad_gain

    full = whole_block((rows, width))
    column = pl.BlockSpec((rows, tile), lambda j: (0, j))
    return pl.pallas_call(
        kernel,
        grid=(steps,),
        in_specs=[full, column, full, whole_block(table.shape)]
        + w_up.specs(tile)
        + w_down.specs(tile),
        out_specs=[column, full, full, full, whole_block((1, width))],
        out_shape=[
            kept_shape((rows, w_up.cols), half_type),
            kept_shape((rows, width), half_type),
            shape_of((rows, width), full_type),
            shape_of((rows, width), half_type),
            shape_of((1, width), full_type),
        ],
        scratch_shapes=[pltpu.VMEM((rows, width), full_type)],
        cost_estimate=cost(4 * rows * width * w_up.cols, 40 * rows * width + 8 * width * w_up.cols),
        compiler_params=grant(32),
        name="feed_back",
    )(flow, in_hbm(slope), middle, table, *w_up.refs(), *w_down.refs())


def mix_back(grad_branch, w_rel, mover):
    rows, width = grad_branch.shape
    tile = rows // 2

    def kernel(dz_ref, w_ref, mover_ref, do_ref, nat_ref):
        branch = dz_ref[...]
        grad_rel = half(contract(branch, w_ref[...], 1, 1))
        do_ref[...] = half(contract(grad_rel, mover_ref[...], 1, 1))
        nat_ref[...] = half(contract(branch, mover_ref[...], 1, 1))

    part = pl.BlockSpec((tile, width), lambda j: (j, 0))
    square = whole_block((width, width))
    return pl.pallas_call(
        kernel,
        grid=(2,),
        in_specs=[part, square, square],
        out_specs=[part, part],
        out_shape=[shape_of((rows, width), half_type), kept_shape((rows, width), half_type)],
        cost_estimate=cost(6 * rows * width * width, 10 * rows * width),
        compiler_params=grant(16),
        name="mix_back",
    )(grad_branch, w_rel, mover)


def project_back(grads, grad_middle, states, table, row, weight, mover, mask):
    rows, width = states.shape
    tile = rows // 2
    count = len(grads)
    first = mask is not None

    def kernel(*refs):
        grad_refs, refs = refs[:count], refs[count:]
        w_refs, refs = refs[: 4 * count], refs[4 * count :]
        dm_ref, h_ref, table_ref = refs[:3]
        refs = refs[3:]
        if first:
            mover_ref, mask_ref = refs[:2]
            refs = refs[2:]
        dh_ref, gain_ref = refs[:2]
        step = pl.program_id(0)

        @pl.when(step == 0)
        def _():
            for ref in (gain_ref,) + ((refs[3],) if first else ()):
                ref[...] = jnp.zeros_like(ref)

        total = None
        for place in range(count):
            part = contract(
                grad_refs[place][...], stacked(*w_refs[4 * place : 4 * place + 4]), 1, 1
            )
            total = part if total is None else total + part
        grad_in, grad_gain = norm_back(total, table_ref[row : row + 1, :], h_ref[...])
        flow = dm_ref[...] + grad_in
        dh_ref[...] = flow
        gain_ref[...] += grad_gain
        if first:
            flag = mask_ref[...]
            refs[2][...] = half(contract(half(flow * (1.0 - flag)), mover_ref[...], 1, 1))
            refs[3][...] += jnp.sum(flow * flag, axis=0, keepdims=True)

    part = pl.BlockSpec((tile, width), lambda j: (j, 0))
    vector = whole_block((1, width))
    specs = [part] * count
    args = [in_hbm(grad) for grad in grads]
    for place in range(count):
        specs += weight.specs(width, lambda j, place=place: place)
        args += weight.refs()
    specs += [part, part, whole_block(table.shape)]
    args += [grad_middle, states, table]
    outs = [shape_of((rows, width), full_type), shape_of((1, width), full_type)]
    out_specs = [part, vector]
    if first:
        specs += [whole_block(mover.shape), pl.BlockSpec((tile, 1), lambda j: (j, 0))]
        args += [mover, mask]
        outs += [kept_shape((rows, width), half_type), shape_of((1, width), full_type)]
        out_specs += [part, vector]
    return pl.pallas_call(
        kernel,
        grid=(2,),
        in_specs=specs,
        out_specs=out_specs,
        out_shape=outs,
        cost_estimate=cost(2 * rows * width * weight.cols, 22 * rows * width),
        compiler_params=grant(30),
        name="project_back",
    )(*args)


def weight_grads(pairs):
    rows, width = pairs[0][0].shape
    plan = []
    start = 0
    for place, (_, rights) in enumerate(pairs):
        first = start
        for right in rights:
            tiles = right.shape[1] // width
            plan.append((place, start, tiles, start == first))
            start += tiles
    total = start
    near_rows = width // 2

    def kernel(*refs):
        left_refs, refs = refs[: len(pairs)], refs[len(pairs) :]
        right_refs, refs = refs[: len(plan)], refs[len(plan) :]
        near_ref, far_ref, turned_ref = refs
        step = pl.program_id(0)
        for (place, begin, tiles, fresh), right_ref in zip(plan, right_refs):
            if fresh:

                @pl.when(step == begin)
                def _(place=place):
                    turned_ref[...] = left_refs[place][...].T

            @pl.when((step >= begin) & (step < begin + tiles))
            def _(right_ref=right_ref):
                out = contract(turned_ref[...], right_ref[...], 1, 0)
                near_ref[...] = out[:near_rows]
                far_ref[...] = half(out[near_rows:])

    specs = [whole_block((rows, width)) for _ in pairs]
    args = [left for left, _ in pairs]
    for (_, rights) in pairs:
        args += list(rights)
    for _, begin, tiles, _ in plan:
        specs.append(
            pl.BlockSpec(
                (rows, width),
                lambda j, begin=begin, tiles=tiles: (0, jnp.clip(j - begin, 0, tiles - 1)),
            )
        )
    block = pl.BlockSpec((near_rows, width), lambda j: (0, j))
    shapes = [
        kept_shape((near_rows, total * width), full_type),
        shape_of((near_rows, total * width), half_type),
    ]
    return tuple(
        pl.pallas_call(
            kernel,
            grid=(total,),
            in_specs=specs,
            out_specs=[block, block],
            out_shape=shapes,
            scratch_shapes=[pltpu.VMEM((width, rows), half_type)],
            cost_estimate=cost(
                2 * rows * width * width * total, width * total * (4 * width + 2 * rows)
            ),
            compiler_params=grant(30),
        name="weight_grads",
        )(*[in_hbm(arg) for arg in args])
    )


def small_grads(flow, vectors, seqs):
    rows, width = flow.shape
    tokens = rows // seqs
    cols = tokens + 8
    cols += -cols % LANES

    def kernel(flow_ref, *refs):
        vector_refs, (near_ref, far_ref) = refs[:-2], refs[-2:]
        posit = flow_ref[:tokens]
        for seq in range(1, seqs):
            posit = posit + flow_ref[seq * tokens : (seq + 1) * tokens]
        fill = jnp.zeros((cols - tokens - len(vector_refs), width), full_type)
        table = jnp.concatenate([posit] + [ref[...] for ref in vector_refs] + [fill], axis=0).T
        near_ref[...] = table[: width // 2]
        far_ref[...] = half(table[width // 2 :])

    shapes = [shape_of((width // 2, cols), kind) for kind in (full_type, half_type)]
    return tuple(
        pl.pallas_call(
            kernel,
            grid=(1,),
            in_specs=[whole_block(flow.shape)] + [whole_block((1, width)) for _ in vectors],
            out_specs=[whole_block(shape.shape) for shape in shapes],
            out_shape=shapes,
            cost_estimate=cost(2 * rows * width, 8 * rows * width),
            compiler_params=grant(16),
        name="small_grads",
        )(flow, *vectors)
    )


class Plan:
    def __init__(self):
        self.seq_size = lax.axis_size("seq")
        self.count = lax.axis_size("dp") * self.seq_size
        self.bits = self.count.bit_length() - 1
        self.early = list(range(self.bits - 1, 2, -1))

        def flips(pick):
            return [(i, i ^ (1 << pick((i >> 1) & 1))) for i in range(self.count)]

        self.stages = [flips(lambda core, b=b: b) for b in self.early]
        self.stages.append(flips(lambda core: 0 if core else 2))
        self.stages.append(flips(lambda core: 2 if core else 0))
        self.core_stage = flips(lambda core: 1)
        self.index = lax.axis_index("dp") * self.seq_size + lax.axis_index("seq")

    def swap(self, value, perm):
        return lax.ppermute(value, AXES, perm)

    def row_table(self, width):
        rows = width // self.count
        place = lax.broadcasted_iota(jnp.int32, (1, width), 1)
        spot = place // rows
        early_count = len(self.early)
        other = (spot >> (self.bits - 1)) & 1
        holder_core = ((self.index >> 1) & 1) ^ other
        block = self.index ^ (other << 1)
        for step, bit in enumerate(self.early):
            block = block ^ (((spot >> step) & 1) << bit)
        first = (spot >> early_count) & 1
        second = (spot >> (early_count + 1)) & 1
        block = block ^ jnp.where(holder_core == 0, first << 2, first)
        block = block ^ jnp.where(holder_core == 0, second, second << 2)
        return block * rows + place % rows

    def mover(self, width):
        table = self.row_table(width)
        whole = lax.broadcasted_iota(jnp.int32, (width, width), 0)
        return (whole == table).astype(half_type)


class Pump:
    def __init__(self, plan):
        self.plan = plan
        self.jobs = []

    def add(self, steps, done, ticks=()):
        self.jobs.append(
            {"steps": steps, "sends": next(steps), "done": done, "stage": 0, "ticks": dict(ticks)}
        )

    def start(self, job):
        job["gots"] = [self.plan.swap(value, perm) for value, perm in job["sends"]]
        job["left"] = job["ticks"].get(job["stage"], 1)

    def advance(self, job, gots):
        job["stage"] += 1
        job["gots"] = None
        try:
            job["sends"] = job["steps"].send(gots)
            return True
        except StopIteration as stop:
            job["done"](stop.value)
            return False

    def begin(self):
        for job in self.jobs:
            if job.get("gots") is None:
                self.start(job)

    def end(self, values=()):
        due = []
        for job in self.jobs:
            job["left"] -= 1
            if job["left"] == 0:
                due.append(job)
        flying, values = lax.optimization_barrier(([job["gots"] for job in due], values))
        over = [job for job, gots in zip(due, flying) if not self.advance(job, gots)]
        self.jobs = [job for job in self.jobs if job not in over]
        return values

    def drain(self):
        newest = self.jobs[-1]
        while self.jobs:
            self.begin()
            if self.jobs[-1] is newest:
                if self.advance(newest, newest["gots"]):
                    self.start(newest)
                else:
                    self.jobs.pop()
            self.end()


def scatter_steps(plan, pieces, narrow):
    gots = yield [(far, plan.core_stage) for _, far in pieces]
    quarter = pieces[0][0].shape[0] // 2
    sums = [
        (half(near[quarter:] + got[quarter:]), near[:quarter] + got[:quarter])
        for (near, _), got in zip(pieces, gots)
    ]
    send = jnp.concatenate([part for part, _ in sums], axis=1)
    keep = jnp.concatenate([part for _, part in sums], axis=1)
    stages = plan.stages[::-1]
    for step, perm in enumerate(stages):
        (got,) = yield [(send, perm)]
        if step == len(stages) - 1:
            return keep + got
        middle = keep.shape[0] // 2
        send = keep[middle:] + got[middle:]
        if step < narrow - 1:
            send = half(send)
        keep = keep[:middle] + got[:middle]


def adam_step(weight, first_mom, second_mom, teacher, gradient):
    first_new = first_decay * first_mom + (1.0 - first_decay) * gradient
    second_new = second_decay * second_mom + (1.0 - second_decay) * gradient * gradient
    weight_new = weight - learn_rate * (
        first_new / (jnp.sqrt(second_new) + adam_eps) + weight_decay * weight
    )
    teacher_new = teacher_keep * teacher + (1.0 - teacher_keep) * weight_new
    return (weight_new, first_new, second_new, teacher_new)


def norm_totals(edge, attn_zero, attn_one, mlp_zero, mlp_one, loss_row, width, tokens):
    stop = 4 * width

    def kernel(edge_ref, first_ref, second_ref, zero_ref, one_ref, loss_ref, out_ref):
        def square(value):
            return jnp.sum(value * value)

        small = edge_ref[:, width:]
        lane = lax.broadcasted_iota(jnp.int32, small.shape, 1)
        posit = jnp.where(lane < tokens, small, 0.0)
        vecs = jnp.where(lane >= tokens, small, 0.0)
        parts = [
            jnp.sum(loss_ref[...]),
            square(edge_ref[:, :width]) + square(second_ref[:, stop:]),
            square(first_ref[...]) + square(second_ref[:, :stop]),
            square(zero_ref[...]) + square(one_ref[...]),
            square(posit),
            square(vecs),
        ]
        row = lax.broadcasted_iota(jnp.int32, (8, LANES), 0)
        out = jnp.zeros((8, LANES), full_type)
        for place, part in enumerate(parts):
            out = jnp.where(row == place, part, out)
        out_ref[...] = out

    args = (edge, attn_zero, attn_one, mlp_zero, mlp_one, loss_row)
    return pl.pallas_call(
        kernel,
        grid=(1,),
        in_specs=[whole_block(arg.shape) for arg in args],
        out_specs=whole_block((8, LANES)),
        out_shape=shape_of((8, LANES), full_type),
        compiler_params=grant(16),
        name="norm_totals",
    )(*args)


def update(totals, edge, attn_zero, attn_one, mlp_zero, mlp_one, groups, sizes, width, tokens):
    stop = mlp_zero.shape[1]

    def kernel(total_ref, edge_ref, first_ref, second_ref, zero_ref, one_ref, *refs):
        ins, outs = refs[:20], refs[20:]

        def step(group, gradient, cols=slice(None)):
            limit = entry_clip * sizes[group] ** 0.5
            norm_value = jnp.sqrt(total_ref[group + 1 : group + 2, 0:1])
            gradient = gradient * (limit / jnp.maximum(norm_value, limit))
            weight, first, second, teacher = (
                ref[:, cols] for ref in ins[4 * group : 4 * group + 4]
            )
            news = adam_step(weight, first, second, teacher, gradient)
            for ref, new in zip(outs[4 * group : 4 * group + 4], news):
                ref[:, cols] = new

        step(0, edge_ref[:, :width], slice(0, width))
        step(0, second_ref[:, 4 * width :], slice(width, 2 * width))
        step(1, first_ref[...], slice(0, 4 * width))
        step(1, second_ref[:, : 4 * width], slice(4 * width, 8 * width))
        step(2, zero_ref[...], slice(0, stop))
        step(2, one_ref[...], slice(stop, 2 * stop))
        step(3, edge_ref[:, width : width + tokens])
        start = tokens // LANES * LANES
        turned = edge_ref[:, width + start : width + start + LANES].T
        count = ins[16].shape[0]
        step(4, turned[tokens - start : tokens - start + count])

    args = [totals, edge, attn_zero, attn_one, mlp_zero, mlp_one] + [part for group in groups for part in group]
    outs = [shape_of(part.shape, full_type) for group in groups for part in group]
    return pl.pallas_call(
        kernel,
        grid=(1,),
        in_specs=[whole_block(arg.shape) for arg in args],
        out_specs=[whole_block(out.shape) for out in outs],
        out_shape=outs,
        compiler_params=grant(40),
        name="update",
    )(*args)


def pad_lanes(value):
    extra = -value.shape[1] % LANES
    return jnp.pad(value, ((0, 0), (0, extra)))


def local(
    patches,
    masked_at,
    edge_w,
    attn_w,
    mlp_w,
    posit_w,
    vecs_w,
    edge_m,
    attn_m,
    mlp_m,
    posit_m,
    vecs_m,
    edge_v,
    attn_v,
    mlp_v,
    posit_v,
    vecs_v,
    edge_t,
    attn_t,
    mlp_t,
    posit_t,
    vecs_t,
):
    seqs, tokens, width = patches.shape
    plan = Plan()
    total_masked = seqs * plan.count * tokens // 2
    ff_width = mlp_w.shape[1] // (2 * LAYERS)
    small_cols = tokens + vecs_w.shape[1]
    flat_patch = patches.reshape(-1, width)
    mask_flat = masked_at.astype(full_type).reshape(-1, 1)
    mover = plan.mover(width)

    def shards(edge, attn, mlp, posit, vecs):
        small = pad_lanes(jnp.concatenate([posit, vecs], axis=1))
        return [edge[:, :width], edge[:, width:], small] + [
            [
                part[:, layer * part.shape[1] // LAYERS : (layer + 1) * part.shape[1] // LAYERS]
                for part in (attn, mlp)
            ]
            for layer in range(LAYERS)
        ]

    def joined(parts):
        return jnp.concatenate([half(part) for part in parts], axis=1)

    t_patch, _, t_small, t_one, t_two = shards(edge_t, attn_t, mlp_t, posit_t, vecs_t)
    s_patch, s_head, s_small, s_one, s_two = shards(edge_w, attn_w, mlp_w, posit_w, vecs_w)
    chunks = [
        [t_patch, t_one[0], t_small],
        [t_one[1]],
        t_two,
        [s_patch, s_one[0], s_small],
        [s_one[1]],
        [s_two[0], s_head],
        [s_two[1]],
    ]
    groups = [[0], [1], [2], [3], [4, 5, 6]]
    group_start = [0, 1, 2, 3, 4]

    def attn_weights(blocks, start):
        return Weight(blocks, start, 3 * width), Weight(blocks, start + 3 * width, width)

    def mlp_weights(blocks, start):
        return Weight(blocks, start, ff_width), Weight(blocks, start + ff_width, ff_width)

    def small_of(blocks):
        return Weight(blocks, 5 * width, t_small.shape[1])

    def finish(blocks):
        return list(blocks) + [plan.swap(blocks[1], plan.core_stage)]

    def attend_forward(states, table, layer, w_qkv, w_out, keep, outs=None):
        if outs is None:
            outs = norm_project(states, table, layer, w_qkv, keep)
        projected = outs[0].reshape(seqs, tokens, w_qkv.cols)
        mixed = attend(projected).reshape(-1, width)
        results = mix_out(mixed, states, mover, table, LAYERS + layer, w_out, keep)
        if keep:
            return results[0], results[1], (states, outs[1], projected) + tuple(results[2:])
        return results[0], results[1], ()

    saved_attn = [None] * LAYERS
    saved_mlp = [None] * LAYERS

    def segment_t0(_, blocks):
        patch = Weight(blocks, 0, width)
        states, table, patch_rel = embed(
            flat_patch, None, mover, patch, small_of(blocks), True
        )
        weights = attn_weights(blocks, width)
        return states, table, patch_rel, norm_project(states, table, 0, weights[0], False)

    def segment_t0_rest(values, blocks):
        states, table, patch_rel, outs = values
        weights = attn_weights(blocks, width)
        middle, normed, _ = attend_forward(states, table, 0, *weights, False, outs)
        return middle, normed, table, patch_rel

    def segment_t1(values, blocks):
        middle, normed, table, patch_rel = values
        (states,) = feed_forward(normed, middle, *mlp_weights(blocks, 0), False)
        return states, table, patch_rel

    def segment_t2(values, blocks):
        first, table, patch_rel = values
        middle, normed, _ = attend_forward(first, table, 1, *attn_weights(blocks, 0), False)
        (second,) = feed_forward(normed, middle, *mlp_weights(blocks, 4 * width), False)
        return make_target(first, second, seqs), patch_rel

    def segment_s0(values, blocks):
        target, patch_rel = values
        patch = Weight(blocks, 0, width)
        states, table = embed(flat_patch, mask_flat, mover, patch, small_of(blocks), False)
        weights = attn_weights(blocks, width)
        middle, normed, saved = attend_forward(states, table, 0, *weights, True)
        saved_attn[0] = (weights[0], saved)
        return target, patch_rel, table, middle, normed

    def segment_s1(values, blocks):
        target, patch_rel, table, middle, normed = values
        weights = mlp_weights(blocks, 0)
        states, active, slope = feed_forward(normed, middle, *weights, True)
        saved_mlp[0] = (weights, middle, normed, active, slope)
        return target, patch_rel, table, states

    def segment_s2(values, blocks):
        target, patch_rel, table, states = values
        weights = attn_weights(blocks, 0)
        middle, normed, saved = attend_forward(states, table, 1, *weights, True)
        saved_attn[1] = (weights[0], saved)
        return target, patch_rel, table, middle, normed, blocks

    segments = [segment_t0_rest, segment_t1, segment_t2, segment_s0, segment_s1, segment_s2]
    early = len(plan.early)
    group_values = [joined([part for c in group for part in chunks[c]]) for group in groups]
    own = [None] * len(chunks)
    blocks = [None] * len(chunks)
    values = ()
    ahead = {}
    for tick in range(len(chunks) + early + 1):
        sends = {}
        for group, start in enumerate(group_start):
            if 0 <= tick - start < early:
                sends["early", group] = (group_values[group], plan.stages[tick - start])
        for chunk in range(len(chunks)):
            if tick == chunk + early:
                sends["first", chunk] = (own[chunk], plan.stages[early])
            if tick == chunk + early + 1 and ("second", chunk) not in ahead:
                sends["second", chunk] = (own[chunk], plan.stages[early + 1])
                sends["core", chunk] = (own[chunk], plan.core_stage)
        gots = {key: plan.swap(value, perm) for key, (value, perm) in sends.items()}
        if tick == early + 2:
            gots.update(ahead)
        place = tick - early - 2
        if 0 <= place < len(segments):
            values = segments[place](values, finish(blocks[place]))
        if tick == early + 1:
            lead = [gots.pop(key) for key in (("second", 0), ("core", 0), ("first", 1))]
            later = [g for g in range(len(groups)) if group_start[g] > tick]
            lead, held = lax.optimization_barrier((lead, [group_values[g] for g in later]))
            for g, value in zip(later, held):
                group_values[g] = value
            own[1] = jnp.concatenate([own[1], lead[2]], axis=0)
            ahead = {
                ("second", 1): plan.swap(own[1], plan.stages[early + 1]),
                ("core", 1): plan.swap(own[1], plan.core_stage),
            }
            blocks[0] = (own[0], lead[0], lead[1])
            values = segment_t0(values, finish(blocks[0]))
        apart = {key: got for key, got in gots.items() if FAST_LANE and key[1] == 0 and tick}
        gots = {key: got for key, got in gots.items() if key not in apart}
        later = [g for g in range(len(groups)) if group_start[g] > tick]
        idle = [c for c in range(1, len(chunks)) if own[c] is not None and c + early > tick]
        gots, values, held, held_own, _ = lax.optimization_barrier(
            (gots, values, [group_values[g] for g in later], [own[c] for c in idle], apart)
        )
        for g, value in zip(later, held):
            group_values[g] = value
        for c, value in zip(idle, held_own):
            own[c] = value
        gots.update(apart)
        for (kind, index), got in gots.items():
            if kind == "early":
                group_values[index] = jnp.concatenate([group_values[index], got], axis=0)
                if tick - group_start[index] == early - 1:
                    start = 0
                    for chunk in groups[index]:
                        stop = start + sum(part.shape[1] for part in chunks[chunk])
                        own[chunk] = group_values[index][:, start:stop]
                        start = stop
            elif kind == "first":
                own[index] = jnp.concatenate([own[index], got], axis=0)
        for chunk in range(len(chunks)):
            if ("second", chunk) in gots:
                blocks[chunk] = (own[chunk], gots["second", chunk], gots["core", chunk])
    pump = Pump(plan)
    target, patch_rel, table, middle, normed, head_blocks = values
    weights = mlp_weights(finish(blocks[-1]), 0)
    states, active, slope = feed_forward(normed, middle, *weights, True)
    saved_mlp[1] = (weights, middle, normed, active, slope)
    flow, final_normed, grad_pred, grad_gain_final, loss_row = head_step(
        states,
        table,
        mover,
        Weight(head_blocks, 4 * width, width),
        target,
        mask_flat,
        total_masked,
    )

    gain_ones = [None] * LAYERS
    gain_twos = [None] * LAYERS
    shards = {}
    last_stage = len(plan.stages)

    def send_off(name, pieces, narrow, ticks=()):
        pump.add(
            scatter_steps(plan, pieces, narrow), lambda out: shards.__setitem__(name, out), ticks
        )

    for layer in reversed(range(LAYERS)):
        w_qkv, (states, normed_one, projected, mixed_rel, w_out_rel) = saved_attn[layer]
        (w_up, w_down), middle, normed_two, active, slope = saved_mlp[layer]
        pump.begin()
        grad_hidden, grad_down, grad_middle, grad_branch, gain_twos[layer] = feed_back(
            flow, slope, middle, table, LAYERS + layer, w_up, w_down
        )
        grad_hidden, grad_down, grad_middle, grad_branch = pump.end(
            (grad_hidden, grad_down, grad_middle, grad_branch)
        )
        pump.begin()
        piece = weight_grads([(normed_two, [grad_hidden]), (grad_down, [active])])
        piece, grad_branch = pump.end((piece, grad_branch))
        send_off(
            ("mlp", layer), [piece], 2, {1: 2, last_stage: 2} if layer else {last_stage: 2}
        )
        pump.begin()
        grad_mixed, branch_whole = mix_back(grad_branch, w_out_rel, mover)
        grad_mixed = grad_mixed.reshape(seqs, tokens, width)
        grad_proj = ()
        for seq in range(seqs - 1):
            grad_proj = attend_back(projected, grad_mixed, seq, tuple(grad_proj))
        grad_proj, grad_mixed, branch_whole = pump.end((grad_proj, grad_mixed, branch_whole))
        pump.begin()
        grad_proj = attend_back(projected, grad_mixed, seqs - 1, tuple(grad_proj))
        grad_proj = [part.reshape(-1, width) for part in grad_proj]
        pairs = [(normed_one, grad_proj), (mixed_rel, [branch_whole])]
        if layer == 0:
            piece = weight_grads(pairs)
            piece, grad_proj = pump.end((piece, grad_proj))
            send_off(("attn", 0), [piece], 2)
            pump.begin()
        results = project_back(
            grad_proj,
            grad_middle,
            states,
            table,
            layer,
            w_qkv,
            mover,
            None if layer else mask_flat,
        )
        flow, gain_ones[layer] = results[:2]
        if layer:
            flow, grad_proj = pump.end((flow, grad_proj))
            pairs = [(normed_one, grad_proj), (mixed_rel, [branch_whole])]
            pairs.append((final_normed, [grad_pred]))
            pump.begin()
            piece = weight_grads(pairs)
            piece, flow = pump.end((piece, flow))
            send_off(("attn", layer), [piece], 2)
    grad_embed, grad_maskvec = results[2:]
    vectors = gain_ones + gain_twos + [grad_gain_final, grad_maskvec]
    pieces = pump.end(
        [weight_grads([(patch_rel, [grad_embed])]), small_grads(flow, vectors, seqs)]
    )
    send_off("edge", pieces, 2)
    pump.drain()
    pieces = (
        shards["edge"],
        shards["attn", 0],
        shards["attn", 1],
        shards["mlp", 0],
        shards["mlp", 1],
    )
    totals = norm_totals(*pieces, loss_row, width, tokens)
    for perm in [plan.core_stage] + plan.stages:
        totals = totals + plan.swap(totals, perm)
    groups = [
        (edge_w, edge_m, edge_v, edge_t),
        (attn_w, attn_m, attn_v, attn_t),
        (mlp_w, mlp_m, mlp_v, mlp_t),
        (posit_w, posit_m, posit_v, posit_t),
        (vecs_w.T, vecs_m.T, vecs_v.T, vecs_t.T),
    ]
    sizes = [group[0].size * plan.count for group in groups]
    news = update(totals, *pieces, groups, sizes, width, tokens)
    news = [
        [news[4 * group + part] for group in range(4)] + [news[16 + part].T] for part in range(4)
    ]
    return (totals[0, 0] / total_masked,) + tuple(new for part in news for new in part)


def solution(mesh):
    rows = P(AXES, None)
    in_specs = (P(AXES, None, None),) + (rows,) * 21
    out_specs = (P(),) + (rows,) * 20
    return jax.shard_map(local, mesh=mesh, in_specs=in_specs, out_specs=out_specs, check_vma=False)
```

```python
import jax
import jax.numpy as jnp
from jax import lax
from jax.experimental import pallas as pl
from jax.experimental.pallas import tpu as pltpu
from jax.sharding import PartitionSpec as P

HDIM = 64
LAYERS = 2
TOPK = 2
LANES = 128
FF_TILE = 1024
SMALL_TILE = 256
ROW_TILE = 64
PAIRS = 2
FAST_LANE = True

ln_eps = 1e-05
in_eps = 1e-05
learn_rate = 0.02
first_decay = 0.5
second_decay = 0.5
adam_eps = 1e-08
weight_decay = 0.1
teacher_keep = 0.5
huber_beta = 1.0
score_scale = 0.125
entry_clip = 1e-05
half_type = jnp.bfloat16
full_type = jnp.float32
AXES = ("dp", "seq")


def contract(left, right, left_dim, right_dim):
    return lax.dot_general(
        left,
        right,
        (((left_dim,), (right_dim,)), ((), ())),
        preferred_element_type=full_type,
    )


def head_mask(which, width):
    lane = lax.broadcasted_iota(jnp.int32, (1, width), 1)
    return (lane // HDIM) == which


def head_part(values, which):
    return jnp.where(head_mask(which, LANES), values, jnp.zeros_like(values))


def softmax_rows(scores):
    exps = jnp.exp(scores - jnp.max(scores, axis=1, keepdims=True))
    return exps * (1.0 / jnp.sum(exps, axis=1, keepdims=True))


def attend_kernel(q_ref, k_ref, v_ref, o_ref, score_ref, prob_ref):
    tokens = q_ref.shape[1]
    heads = LANES // HDIM
    for start in range(0, q_ref.shape[2], LANES):
        cols = slice(start, start + LANES)
        queries = q_ref[0, :, cols] * jnp.asarray(score_scale, half_type)
        for which in range(heads):
            score_ref[which] = contract(head_part(queries, which), k_ref[0, :, cols], 1, 1)
        for which in range(heads):
            for row in range(0, tokens, ROW_TILE):
                rows = slice(row, row + ROW_TILE)
                prob_ref[which, rows] = softmax_rows(score_ref[which, rows]).astype(half_type)
        mixed = None
        for which in range(heads):
            out = contract(prob_ref[which], v_ref[0, :, cols], 1, 0)
            mixed = out if mixed is None else jnp.where(head_mask(which, LANES), out, mixed)
        o_ref[0, :, cols] = mixed.astype(half_type)


def attend_back_kernel(q_ref, k_ref, v_ref, do_ref, dq_ref, dk_ref, dv_ref, *scratch):
    score_ref, grad_ref, prob_ref, back_ref = scratch
    tokens = q_ref.shape[1]
    heads = LANES // HDIM
    for start in range(0, q_ref.shape[2], LANES):
        cols = slice(start, start + LANES)
        queries = q_ref[0, :, cols] * jnp.asarray(score_scale, half_type)
        keys_now = k_ref[0, :, cols]
        grad_out = do_ref[0, :, cols]
        for which in range(heads):
            score_ref[which] = contract(head_part(queries, which), keys_now, 1, 1)
            grad_ref[which] = contract(head_part(grad_out, which), v_ref[0, :, cols], 1, 1)
        for which in range(heads):
            for row in range(0, tokens, ROW_TILE):
                rows = slice(row, row + ROW_TILE)
                probs = softmax_rows(score_ref[which, rows])
                prob_ref[which, rows] = probs.astype(half_type)
                prods = probs * grad_ref[which, rows]
                back_ref[which, rows] = (
                    prods - probs * jnp.sum(prods, axis=1, keepdims=True)
                ).astype(half_type)
        turned_k = []
        turned_v = []
        grad_q = None
        for which in range(heads):
            part = slice(which * HDIM, (which + 1) * HDIM)
            turned_v.append(contract(grad_out, prob_ref[which], 0, 0)[part])
            turned_k.append(contract(queries, back_ref[which], 0, 0)[part])
            out = contract(back_ref[which], keys_now, 1, 0)
            grad_q = out if grad_q is None else jnp.where(head_mask(which, LANES), out, grad_q)
        dq_ref[0, :, cols] = (grad_q * score_scale).astype(half_type)
        dk_ref[0, :, cols] = jnp.concatenate(turned_k, axis=0).T.astype(half_type)
        dv_ref[0, :, cols] = jnp.concatenate(turned_v, axis=0).T.astype(half_type)


def attend(projected):
    seqs, tokens, width3 = projected.shape
    width = width3 // 3
    wide = PAIRS * LANES
    blocks = width // wide
    specs = [
        pl.BlockSpec((1, tokens, wide), lambda s, j, off=off: (s, 0, off * blocks + j))
        for off in range(3)
    ]
    heads = LANES // HDIM
    return pl.pallas_call(
        attend_kernel,
        grid=(seqs, blocks),
        in_specs=specs,
        out_specs=pl.BlockSpec((1, tokens, wide), lambda s, j: (s, 0, j)),
        out_shape=jax.ShapeDtypeStruct((seqs, tokens, width), half_type),
        scratch_shapes=[
            pltpu.VMEM((heads, tokens, tokens), full_type),
            pltpu.VMEM((heads, tokens, tokens), half_type),
        ],
        cost_estimate=pl.CostEstimate(
            flops=16 * seqs * tokens * tokens * width,
            transcendentals=seqs * tokens * tokens * width // HDIM,
            bytes_accessed=8 * seqs * tokens * width,
        ),
        compiler_params=grant(16),
        name="attend",
    )(projected, projected, projected)


def attend_back(projected, grad_mixed, seq, into=()):
    seqs, tokens, width3 = projected.shape
    width = width3 // 3
    wide = PAIRS * LANES
    blocks = width // wide
    block = pl.BlockSpec((1, tokens, wide), lambda j: (seq, 0, j))
    specs = [
        pl.BlockSpec((1, tokens, wide), lambda j, off=off: (seq, 0, off * blocks + j))
        for off in range(3)
    ]
    heads = LANES // HDIM
    skip = len(into)

    def kernel(q_ref, k_ref, v_ref, do_ref, *refs):
        attend_back_kernel(q_ref, k_ref, v_ref, do_ref, *refs[skip:])

    shape = kept_shape((seqs, tokens, width), half_type)
    return pl.pallas_call(
        kernel,
        grid=(blocks,),
        in_specs=specs + [block] + [pl.BlockSpec(memory_space=pl.ANY)] * skip,
        out_specs=[block, block, block],
        out_shape=[shape, shape, shape],
        input_output_aliases={4 + place: place for place in range(skip)},
        scratch_shapes=[
            pltpu.VMEM((heads, tokens, tokens), kind)
            for kind in (full_type, full_type, half_type, half_type)
        ],
        cost_estimate=pl.CostEstimate(
            flops=32 * tokens * tokens * width,
            transcendentals=tokens * tokens * width // HDIM,
            bytes_accessed=14 * tokens * width,
        ),
        compiler_params=grant(20),
        name="attend_back",
    )(projected, projected, projected, grad_mixed, *into)


def normal_cdf(values):
    return 0.5 + 0.5 * lax.erf(values * (0.5**0.5))


def whole_block(shape):
    zeros = (0,) * len(shape)
    return pl.BlockSpec(shape, lambda *_: zeros, pipeline_mode=pl.Buffered(1))


def grant(mib):
    return pltpu.CompilerParams(vmem_limit_bytes=mib << 20)


def stacked(*refs):
    return jnp.concatenate([ref[...] for ref in refs], axis=0)


def unit_of(values):
    centre = values - jnp.mean(values, axis=1, keepdims=True)
    inv_scale = lax.rsqrt(jnp.mean(centre * centre, axis=1, keepdims=True) + ln_eps)
    return centre * inv_scale, inv_scale


def norm_back(grad_out, gain, values):
    unit, inv_scale = unit_of(values)
    grad_unit = grad_out * gain
    inner_mean = jnp.mean(grad_unit, axis=1, keepdims=True)
    along_mean = jnp.mean(grad_unit * unit, axis=1, keepdims=True)
    grad_in = (grad_unit - inner_mean - unit * along_mean) * inv_scale
    return grad_in, jnp.sum(grad_out * unit, axis=0, keepdims=True)


def half(values):
    return values.astype(half_type)


def shape_of(shape, kind):
    return jax.ShapeDtypeStruct(shape, kind)


def kept_shape(shape, kind):
    return pltpu.HBM(shape, kind)


def cost(flops, moved):
    return pl.CostEstimate(flops=flops, transcendentals=0, bytes_accessed=moved)


def in_hbm(value):
    return pltpu.with_memory_space_constraint(value, pltpu.HBM)


class Weight:
    def __init__(self, blocks, start, cols):
        self.blocks, self.start, self.cols = list(blocks), start, cols

    def specs(self, width, index=lambda j: j):
        base = self.start // width
        spec = pl.BlockSpec(
            (self.blocks[0].shape[0], width), lambda j, base=base: (0, base + index(j))
        )
        return [spec] * len(self.blocks)

    def refs(self):
        return [in_hbm(block) for block in self.blocks[:-1]] + self.blocks[-1:]


def embed(patches, mask, mover, weight, small, keep_patches):
    rows, width = patches.shape
    tokens = rows // 2
    masked = mask is not None
    pieces = small.cols // SMALL_TILE

    def kernel(*refs):
        x_ref, mover_ref = refs[:2]
        w_refs, small_refs, refs = refs[2:6], refs[6 : 6 + 4 * pieces], refs[6 + 4 * pieces :]
        if masked:
            mask_ref, refs = refs[0], refs[1:]
        h_ref, table_ref = refs[:2]
        x_rel = half(contract(x_ref[...], mover_ref[...], 1, 0))
        if keep_patches:
            refs[2][...] = x_rel
        w_rel = half(contract(stacked(*w_refs), mover_ref[...], 1, 0))
        small_parts = [stacked(*small_refs[4 * k : 4 * k + 4]) for k in range(pieces)]
        small_t = jnp.concatenate(small_parts, axis=1).astype(full_type).T
        posit = small_t[:tokens]
        table = small_t[tokens : tokens + 8]
        table_ref[...] = table
        states = contract(x_rel, w_rel, 1, 0)
        for seq in range(rows // tokens):
            part = slice(seq * tokens, (seq + 1) * tokens)
            state = states[part]
            if masked:
                flag = mask_ref[part, :]
                state = state * (1.0 - flag) + flag * table[2 * LAYERS + 1 : 2 * LAYERS + 2]
            h_ref[part, :] = state + posit

    outs = [shape_of((rows, width), full_type), shape_of((8, width), full_type)]
    if keep_patches:
        outs.append(kept_shape((rows, width), half_type))
    args = [patches, mover] + weight.refs() + small.refs() * pieces + ([mask] if masked else [])
    specs = [whole_block(patches.shape), whole_block(mover.shape)] + weight.specs(width)
    for k in range(pieces):
        specs += small.specs(SMALL_TILE, lambda j, k=k: k)
    if masked:
        specs.append(whole_block(mask.shape))
    return pl.pallas_call(
        kernel,
        grid=(1,),
        in_specs=specs,
        out_specs=[whole_block(out.shape) for out in outs],
        out_shape=outs,
        cost_estimate=cost(6 * rows * width * width, 12 * rows * width),
        compiler_params=grant(28),
        name="embed",
    )(*args)


def norm_project(states, table, row, weight, keep):
    rows, width = states.shape
    steps = weight.cols // width

    def kernel(h_ref, table_ref, own_ref, own2_ref, got_ref, got2_ref, out_ref, a_ref):
        @pl.when(pl.program_id(0) == 0)
        def _():
            unit, _ = unit_of(h_ref[...])
            a_ref[...] = half(unit * table_ref[row : row + 1, :])

        out_ref[...] = half(contract(a_ref[...], stacked(own_ref, own2_ref, got_ref, got2_ref), 1, 0))

    outs = [shape_of((rows, weight.cols), half_type)]
    out_specs = [pl.BlockSpec((rows, width), lambda j: (0, j))]
    scratch = []
    if keep:
        outs.append(kept_shape((rows, width), half_type))
        out_specs.append(whole_block((rows, width)))
    else:
        scratch.append(pltpu.VMEM((rows, width), half_type))
    return pl.pallas_call(
        kernel,
        grid=(steps,),
        in_specs=[whole_block(states.shape), whole_block(table.shape)] + weight.specs(width),
        out_specs=out_specs,
        out_shape=outs,
        scratch_shapes=scratch,
        cost_estimate=cost(2 * rows * width * weight.cols, 12 * rows * width),
        compiler_params=grant(24),
        name="norm_project",
    )(states, table, *weight.refs())


def mix_out(mixed, states, mover, table, row, weight, keep):
    rows, width = states.shape
    tile = rows // 2

    def kernel(o_ref, h_ref, mover_ref, table_ref, own_ref, own2_ref, got_ref, got2_ref, m_ref, b_ref, *rest):
        if keep:
            rel_ref, w_ref = rest
        else:
            (w_ref,) = rest

        @pl.when(pl.program_id(0) == 0)
        def _():
            w_ref[...] = half(contract(stacked(own_ref, own2_ref, got_ref, got2_ref), mover_ref[...], 1, 0))

        mixed_rel = half(contract(o_ref[...], mover_ref[...], 1, 0))
        if keep:
            rel_ref[...] = mixed_rel
        middle = h_ref[...] + contract(mixed_rel, w_ref[...], 1, 0)
        m_ref[...] = middle
        unit, _ = unit_of(middle)
        b_ref[...] = half(unit * table_ref[row : row + 1, :])

    part = pl.BlockSpec((tile, width), lambda j: (j, 0))
    outs = [shape_of((rows, width), full_type), shape_of((rows, width), half_type)]
    out_specs = [part, part]
    scratch = []
    if keep:
        outs += [kept_shape((rows, width), half_type), kept_shape((width, width), half_type)]
        out_specs += [part, whole_block((width, width))]
    else:
        scratch.append(pltpu.VMEM((width, width), half_type))
    return pl.pallas_call(
        kernel,
        grid=(2,),
        in_specs=[part, part, whole_block(mover.shape), whole_block(table.shape)]
        + weight.specs(width, lambda j: 0),
        out_specs=out_specs,
        out_shape=outs,
        scratch_shapes=scratch,
        cost_estimate=cost(6 * rows * width * width, 14 * rows * width),
        compiler_params=grant(24),
        name="mix_out",
    )(mixed, states, mover, table, *weight.refs())


def feed_forward(normed, middle, w_up, w_down, keep):
    rows, width = middle.shape
    tile = FF_TILE
    steps = w_up.cols // tile

    def kernel(b_ref, m_ref, uown_ref, uown2_ref, ugot_ref, ugot2_ref, down_ref, down2_ref, dgot_ref, dgot2_ref, out_ref, *rest):
        step = pl.program_id(0)
        hidden = contract(b_ref[...], stacked(uown_ref, uown2_ref, ugot_ref, ugot2_ref), 1, 0)
        cdf = normal_cdf(hidden)
        active = half(hidden * cdf)
        if keep:
            rest[0][...] = active
            rest[1][...] = cdf + hidden * (
                jnp.exp(-0.5 * hidden * hidden) * ((0.5 / jnp.pi) ** 0.5)
            )
        part = contract(active, stacked(down_ref, down2_ref, dgot_ref, dgot2_ref), 1, 1)

        @pl.when(step == 0)
        def _():
            out_ref[...] = m_ref[...] + part

        @pl.when(step > 0)
        def _():
            out_ref[...] += part

    outs = [shape_of((rows, width), full_type)]
    out_specs = [whole_block((rows, width))]
    if keep:
        outs += [kept_shape((rows, w_up.cols), half_type), kept_shape((rows, w_up.cols), full_type)]
        out_specs += [pl.BlockSpec((rows, tile), lambda j: (0, j))] * 2
    return pl.pallas_call(
        kernel,
        grid=(steps,),
        in_specs=[whole_block(normed.shape), whole_block(middle.shape)]
        + w_up.specs(tile)
        + w_down.specs(tile),
        out_specs=out_specs,
        out_shape=outs,
        cost_estimate=cost(4 * rows * width * w_up.cols, 12 * rows * width + 16 * width * w_up.cols),
        compiler_params=grant(42),
        name="feed_forward",
    )(normed, middle, *w_up.refs(), *w_down.refs())


def make_target(first, second, seqs):
    rows, width = first.shape
    tokens = rows // seqs
    cols = width // 2

    def kernel(one_ref, two_ref, out_ref):
        total = None
        for ref in (one_ref, two_ref):
            values = ref[...]
            centre = values - jnp.mean(values, axis=0, keepdims=True)
            variance = jnp.mean(centre * centre, axis=0, keepdims=True)
            term = centre * lax.rsqrt(variance + in_eps)
            total = term if total is None else total + term
        out_ref[...] = total * (1.0 / TOPK)

    block = pl.BlockSpec((tokens, cols), lambda s, j: (s, j))
    return pl.pallas_call(
        kernel,
        grid=(seqs, 2),
        in_specs=[block, block],
        out_specs=block,
        out_shape=shape_of((rows, width), full_type),
        cost_estimate=cost(20 * rows * width, 12 * rows * width),
        compiler_params=grant(16),
        name="make_target",
    )(first, second)


def head_step(states, table, mover, weight, target, mask, total_masked):
    rows, width = states.shape
    tile = rows // 2
    final_row = 2 * LAYERS

    def kernel(
        h_ref, table_ref, mover_ref, own_ref, own2_ref, got_ref, got2_ref, t_ref, mask_ref,
        flow_ref, f_ref, pred_ref, gain_ref, loss_ref, w_ref,
    ):
        step = pl.program_id(0)

        @pl.when(step == 0)
        def _():
            w_ref[...] = half(contract(stacked(own_ref, own2_ref, got_ref, got2_ref), mover_ref[...], 1, 0))
            gain_ref[...] = jnp.zeros_like(gain_ref)
            loss_ref[...] = jnp.zeros_like(loss_ref)

        states_now = h_ref[...]
        gain = table_ref[final_row : final_row + 1, :]
        unit, _ = unit_of(states_now)
        final_normed = half(unit * gain)
        f_ref[...] = final_normed
        flag = mask_ref[...]
        differ = contract(final_normed, w_ref[...], 1, 0) - t_ref[...]
        magnitude = jnp.abs(differ)
        terms = jnp.where(
            magnitude < huber_beta,
            0.5 * differ * differ / huber_beta,
            magnitude - 0.5 * huber_beta,
        )
        loss_ref[...] += jnp.sum(terms * flag, axis=0, keepdims=True)
        grad_pred = half(flag * jnp.clip(differ / huber_beta, -1.0, 1.0) / total_masked)
        pred_ref[...] = half(contract(grad_pred, mover_ref[...], 1, 1))
        grad_in, grad_gain = norm_back(contract(grad_pred, w_ref[...], 1, 1), gain, states_now)
        flow_ref[...] = grad_in
        gain_ref[...] += grad_gain

    part = pl.BlockSpec((tile, width), lambda j: (j, 0))
    row = whole_block((1, width))
    return pl.pallas_call(
        kernel,
        grid=(2,),
        in_specs=[part, whole_block(table.shape), whole_block(mover.shape)]
        + weight.specs(width, lambda j: 0)
        + [part, pl.BlockSpec((tile, 1), lambda j: (j, 0))],
        out_specs=[part, part, part, row, row],
        out_shape=[
            shape_of((rows, width), full_type),
            kept_shape((rows, width), half_type),
            kept_shape((rows, width), half_type),
            shape_of((1, width), full_type),
            shape_of((1, width), full_type),
        ],
        scratch_shapes=[pltpu.VMEM((width, width), half_type)],
        cost_estimate=cost(8 * rows * width * width, 16 * rows * width),
        compiler_params=grant(30),
        name="head_step",
    )(states, table, mover, *weight.refs(), target, mask)


def feed_back(flow, slope, middle, table, row, w_up, w_down):
    rows, width = flow.shape
    tile = FF_TILE
    steps = w_up.cols // tile

    def kernel(
        flow_ref, slope_ref, m_ref, table_ref, uown_ref, uown2_ref, ugot_ref, ugot2_ref, down_ref, down2_ref, dgot_ref, dgot2_ref,
        du_ref, dy_ref, dm_ref, dz_ref, gain_ref, acc_ref,
    ):
        step = pl.program_id(0)

        @pl.when(step == 0)
        def _():
            dy_ref[...] = half(flow_ref[...])

        grad_active = contract(dy_ref[...], stacked(down_ref, down2_ref, dgot_ref, dgot2_ref), 1, 0)
        grad_hidden = half(grad_active * slope_ref[...])
        du_ref[...] = grad_hidden
        part = contract(grad_hidden, stacked(uown_ref, uown2_ref, ugot_ref, ugot2_ref), 1, 1)

        @pl.when(step == 0)
        def _():
            acc_ref[...] = part

        @pl.when(step > 0)
        def _():
            acc_ref[...] += part

        @pl.when(step == steps - 1)
        def _():
            grad_in, grad_gain = norm_back(
                acc_ref[...], table_ref[row : row + 1, :], m_ref[...]
            )
            grad_middle = flow_ref[...] + grad_in
            dm_ref[...] = grad_middle
            dz_ref[...] = half(grad_middle)
            gain_ref[...] = grad_gain

    full = whole_block((rows, width))
    column = pl.BlockSpec((rows, tile), lambda j: (0, j))
    return pl.pallas_call(
        kernel,
        grid=(steps,),
        in_specs=[full, column, full, whole_block(table.shape)]
        + w_up.specs(tile)
        + w_down.specs(tile),
        out_specs=[column, full, full, full, whole_block((1, width))],
        out_shape=[
            kept_shape((rows, w_up.cols), half_type),
            kept_shape((rows, width), half_type),
            shape_of((rows, width), full_type),
            shape_of((rows, width), half_type),
            shape_of((1, width), full_type),
        ],
        scratch_shapes=[pltpu.VMEM((rows, width), full_type)],
        cost_estimate=cost(4 * rows * width * w_up.cols, 40 * rows * width + 8 * width * w_up.cols),
        compiler_params=grant(32),
        name="feed_back",
    )(flow, in_hbm(slope), middle, table, *w_up.refs(), *w_down.refs())


def mix_back(grad_branch, w_rel, mover):
    rows, width = grad_branch.shape
    tile = rows // 2

    def kernel(dz_ref, w_ref, mover_ref, do_ref, nat_ref):
        branch = dz_ref[...]
        grad_rel = half(contract(branch, w_ref[...], 1, 1))
        do_ref[...] = half(contract(grad_rel, mover_ref[...], 1, 1))
        nat_ref[...] = half(contract(branch, mover_ref[...], 1, 1))

    part = pl.BlockSpec((tile, width), lambda j: (j, 0))
    square = whole_block((width, width))
    return pl.pallas_call(
        kernel,
        grid=(2,),
        in_specs=[part, square, square],
        out_specs=[part, part],
        out_shape=[shape_of((rows, width), half_type), kept_shape((rows, width), half_type)],
        cost_estimate=cost(6 * rows * width * width, 10 * rows * width),
        compiler_params=grant(16),
        name="mix_back",
    )(grad_branch, w_rel, mover)


def project_back(grads, grad_middle, states, table, row, weight, mover, mask):
    rows, width = states.shape
    tile = rows // 2
    count = len(grads)
    first = mask is not None

    def kernel(*refs):
        grad_refs, refs = refs[:count], refs[count:]
        w_refs, refs = refs[: 4 * count], refs[4 * count :]
        dm_ref, h_ref, table_ref = refs[:3]
        refs = refs[3:]
        if first:
            mover_ref, mask_ref = refs[:2]
            refs = refs[2:]
        dh_ref, gain_ref = refs[:2]
        step = pl.program_id(0)

        @pl.when(step == 0)
        def _():
            for ref in (gain_ref,) + ((refs[3],) if first else ()):
                ref[...] = jnp.zeros_like(ref)

        total = None
        for place in range(count):
            part = contract(
                grad_refs[place][...], stacked(*w_refs[4 * place : 4 * place + 4]), 1, 1
            )
            total = part if total is None else total + part
        grad_in, grad_gain = norm_back(total, table_ref[row : row + 1, :], h_ref[...])
        flow = dm_ref[...] + grad_in
        dh_ref[...] = flow
        gain_ref[...] += grad_gain
        if first:
            flag = mask_ref[...]
            refs[2][...] = half(contract(half(flow * (1.0 - flag)), mover_ref[...], 1, 1))
            refs[3][...] += jnp.sum(flow * flag, axis=0, keepdims=True)

    part = pl.BlockSpec((tile, width), lambda j: (j, 0))
    vector = whole_block((1, width))
    specs = [part] * count
    args = [in_hbm(grad) for grad in grads]
    for place in range(count):
        specs += weight.specs(width, lambda j, place=place: place)
        args += weight.refs()
    specs += [part, part, whole_block(table.shape)]
    args += [grad_middle, states, table]
    outs = [shape_of((rows, width), full_type), shape_of((1, width), full_type)]
    out_specs = [part, vector]
    if first:
        specs += [whole_block(mover.shape), pl.BlockSpec((tile, 1), lambda j: (j, 0))]
        args += [mover, mask]
        outs += [kept_shape((rows, width), half_type), shape_of((1, width), full_type)]
        out_specs += [part, vector]
    return pl.pallas_call(
        kernel,
        grid=(2,),
        in_specs=specs,
        out_specs=out_specs,
        out_shape=outs,
        cost_estimate=cost(2 * rows * width * weight.cols, 22 * rows * width),
        compiler_params=grant(30),
        name="project_back",
    )(*args)


def weight_grads(pairs):
    rows, width = pairs[0][0].shape
    plan = []
    start = 0
    for place, (_, rights) in enumerate(pairs):
        first = start
        for right in rights:
            tiles = right.shape[1] // width
            plan.append((place, start, tiles, start == first))
            start += tiles
    total = start
    near_rows = width // 2

    def kernel(*refs):
        left_refs, refs = refs[: len(pairs)], refs[len(pairs) :]
        right_refs, refs = refs[: len(plan)], refs[len(plan) :]
        near_ref, far_ref, turned_ref = refs
        step = pl.program_id(0)
        for (place, begin, tiles, fresh), right_ref in zip(plan, right_refs):
            if fresh:

                @pl.when(step == begin)
                def _(place=place):
                    turned_ref[...] = left_refs[place][...].T

            @pl.when((step >= begin) & (step < begin + tiles))
            def _(right_ref=right_ref):
                out = contract(turned_ref[...], right_ref[...], 1, 0)
                near_ref[...] = out[:near_rows]
                far_ref[...] = half(out[near_rows:])

    specs = [whole_block((rows, width)) for _ in pairs]
    args = [left for left, _ in pairs]
    for (_, rights) in pairs:
        args += list(rights)
    for _, begin, tiles, _ in plan:
        specs.append(
            pl.BlockSpec(
                (rows, width),
                lambda j, begin=begin, tiles=tiles: (0, jnp.clip(j - begin, 0, tiles - 1)),
            )
        )
    block = pl.BlockSpec((near_rows, width), lambda j: (0, j))
    shapes = [
        kept_shape((near_rows, total * width), full_type),
        shape_of((near_rows, total * width), half_type),
    ]
    return tuple(
        pl.pallas_call(
            kernel,
            grid=(total,),
            in_specs=specs,
            out_specs=[block, block],
            out_shape=shapes,
            scratch_shapes=[pltpu.VMEM((width, rows), half_type)],
            cost_estimate=cost(
                2 * rows * width * width * total, width * total * (4 * width + 2 * rows)
            ),
            compiler_params=grant(30),
        name="weight_grads",
        )(*[in_hbm(arg) for arg in args])
    )


def small_grads(flow, vectors, seqs):
    rows, width = flow.shape
    tokens = rows // seqs
    cols = tokens + 8
    cols += -cols % LANES

    def kernel(flow_ref, *refs):
        vector_refs, (near_ref, far_ref) = refs[:-2], refs[-2:]
        posit = flow_ref[:tokens]
        for seq in range(1, seqs):
            posit = posit + flow_ref[seq * tokens : (seq + 1) * tokens]
        fill = jnp.zeros((cols - tokens - len(vector_refs), width), full_type)
        table = jnp.concatenate([posit] + [ref[...] for ref in vector_refs] + [fill], axis=0).T
        near_ref[...] = table[: width // 2]
        far_ref[...] = half(table[width // 2 :])

    shapes = [shape_of((width // 2, cols), kind) for kind in (full_type, half_type)]
    return tuple(
        pl.pallas_call(
            kernel,
            grid=(1,),
            in_specs=[whole_block(flow.shape)] + [whole_block((1, width)) for _ in vectors],
            out_specs=[whole_block(shape.shape) for shape in shapes],
            out_shape=shapes,
            cost_estimate=cost(2 * rows * width, 8 * rows * width),
            compiler_params=grant(16),
        name="small_grads",
        )(flow, *vectors)
    )


class Plan:
    def __init__(self):
        self.seq_size = lax.axis_size("seq")
        self.count = lax.axis_size("dp") * self.seq_size
        self.bits = self.count.bit_length() - 1
        self.early = list(range(self.bits - 1, 2, -1))

        def flips(pick):
            return [(i, i ^ (1 << pick((i >> 1) & 1))) for i in range(self.count)]

        self.stages = [flips(lambda core, b=b: b) for b in self.early]
        self.stages.append(flips(lambda core: 0 if core else 2))
        self.stages.append(flips(lambda core: 2 if core else 0))
        self.core_stage = flips(lambda core: 1)
        self.index = lax.axis_index("dp") * self.seq_size + lax.axis_index("seq")

    def swap(self, value, perm):
        return lax.ppermute(value, AXES, perm)

    def row_table(self, width):
        rows = width // self.count
        place = lax.broadcasted_iota(jnp.int32, (1, width), 1)
        spot = place // rows
        early_count = len(self.early)
        other = (spot >> (self.bits - 1)) & 1
        holder_core = ((self.index >> 1) & 1) ^ other
        block = self.index ^ (other << 1)
        for step, bit in enumerate(self.early):
            block = block ^ (((spot >> step) & 1) << bit)
        first = (spot >> early_count) & 1
        second = (spot >> (early_count + 1)) & 1
        block = block ^ jnp.where(holder_core == 0, first << 2, first)
        block = block ^ jnp.where(holder_core == 0, second, second << 2)
        return block * rows + place % rows

    def mover(self, width):
        table = self.row_table(width)
        whole = lax.broadcasted_iota(jnp.int32, (width, width), 0)
        return (whole == table).astype(half_type)


class Pump:
    def __init__(self, plan):
        self.plan = plan
        self.jobs = []

    def add(self, steps, done, ticks=()):
        self.jobs.append(
            {"steps": steps, "sends": next(steps), "done": done, "stage": 0, "ticks": dict(ticks)}
        )

    def start(self, job):
        job["gots"] = [self.plan.swap(value, perm) for value, perm in job["sends"]]
        job["left"] = job["ticks"].get(job["stage"], 1)

    def advance(self, job, gots):
        job["stage"] += 1
        job["gots"] = None
        try:
            job["sends"] = job["steps"].send(gots)
            return True
        except StopIteration as stop:
            job["done"](stop.value)
            return False

    def begin(self):
        for job in self.jobs:
            if job.get("gots") is None:
                self.start(job)

    def end(self, values=()):
        due = []
        for job in self.jobs:
            job["left"] -= 1
            if job["left"] == 0:
                due.append(job)
        flying, values = lax.optimization_barrier(([job["gots"] for job in due], values))
        over = [job for job, gots in zip(due, flying) if not self.advance(job, gots)]
        self.jobs = [job for job in self.jobs if job not in over]
        return values

    def drain(self):
        newest = self.jobs[-1]
        while self.jobs:
            self.begin()
            if self.jobs[-1] is newest:
                if self.advance(newest, newest["gots"]):
                    self.start(newest)
                else:
                    self.jobs.pop()
            self.end()


def scatter_steps(plan, pieces, narrow):
    gots = yield [(far, plan.core_stage) for _, far in pieces]
    quarter = pieces[0][0].shape[0] // 2
    sums = [
        (half(near[quarter:] + got[quarter:]), near[:quarter] + got[:quarter])
        for (near, _), got in zip(pieces, gots)
    ]
    send = jnp.concatenate([part for part, _ in sums], axis=1)
    keep = jnp.concatenate([part for _, part in sums], axis=1)
    stages = plan.stages[::-1]
    for step, perm in enumerate(stages):
        (got,) = yield [(send, perm)]
        if step == len(stages) - 1:
            return keep + got
        middle = keep.shape[0] // 2
        send = keep[middle:] + got[middle:]
        if step < narrow - 1:
            send = half(send)
        keep = keep[:middle] + got[:middle]


def adam_step(weight, first_mom, second_mom, teacher, gradient):
    first_new = first_decay * first_mom + (1.0 - first_decay) * gradient
    second_new = second_decay * second_mom + (1.0 - second_decay) * gradient * gradient
    weight_new = weight - learn_rate * (
        first_new / (jnp.sqrt(second_new) + adam_eps) + weight_decay * weight
    )
    teacher_new = teacher_keep * teacher + (1.0 - teacher_keep) * weight_new
    return (weight_new, first_new, second_new, teacher_new)


def norm_totals(edge, attn_zero, attn_one, mlp_zero, mlp_one, loss_row, width, tokens):
    stop = 4 * width

    def kernel(edge_ref, first_ref, second_ref, zero_ref, one_ref, loss_ref, out_ref):
        def square(value):
            return jnp.sum(value * value)

        small = edge_ref[:, width:]
        lane = lax.broadcasted_iota(jnp.int32, small.shape, 1)
        posit = jnp.where(lane < tokens, small, 0.0)
        vecs = jnp.where(lane >= tokens, small, 0.0)
        parts = [
            jnp.sum(loss_ref[...]),
            square(edge_ref[:, :width]) + square(second_ref[:, stop:]),
            square(first_ref[...]) + square(second_ref[:, :stop]),
            square(zero_ref[...]) + square(one_ref[...]),
            square(posit),
            square(vecs),
        ]
        row = lax.broadcasted_iota(jnp.int32, (8, LANES), 0)
        out = jnp.zeros((8, LANES), full_type)
        for place, part in enumerate(parts):
            out = jnp.where(row == place, part, out)
        out_ref[...] = out

    args = (edge, attn_zero, attn_one, mlp_zero, mlp_one, loss_row)
    return pl.pallas_call(
        kernel,
        grid=(1,),
        in_specs=[whole_block(arg.shape) for arg in args],
        out_specs=whole_block((8, LANES)),
        out_shape=shape_of((8, LANES), full_type),
        compiler_params=grant(16),
        name="norm_totals",
    )(*args)


def update(totals, edge, attn_zero, attn_one, mlp_zero, mlp_one, groups, sizes, width, tokens):
    stop = mlp_zero.shape[1]

    def kernel(total_ref, edge_ref, first_ref, second_ref, zero_ref, one_ref, *refs):
        ins, outs = refs[:20], refs[20:]

        def step(group, gradient, cols=slice(None)):
            limit = entry_clip * sizes[group] ** 0.5
            norm_value = jnp.sqrt(total_ref[group + 1 : group + 2, 0:1])
            gradient = gradient * (limit / jnp.maximum(norm_value, limit))
            weight, first, second, teacher = (
                ref[:, cols] for ref in ins[4 * group : 4 * group + 4]
            )
            news = adam_step(weight, first, second, teacher, gradient)
            for ref, new in zip(outs[4 * group : 4 * group + 4], news):
                ref[:, cols] = new

        step(0, edge_ref[:, :width], slice(0, width))
        step(0, second_ref[:, 4 * width :], slice(width, 2 * width))
        step(1, first_ref[...], slice(0, 4 * width))
        step(1, second_ref[:, : 4 * width], slice(4 * width, 8 * width))
        step(2, zero_ref[...], slice(0, stop))
        step(2, one_ref[...], slice(stop, 2 * stop))
        step(3, edge_ref[:, width : width + tokens])
        start = tokens // LANES * LANES
        turned = edge_ref[:, width + start : width + start + LANES].T
        count = ins[16].shape[0]
        step(4, turned[tokens - start : tokens - start + count])

    args = [totals, edge, attn_zero, attn_one, mlp_zero, mlp_one] + [part for group in groups for part in group]
    outs = [shape_of(part.shape, full_type) for group in groups for part in group]
    return pl.pallas_call(
        kernel,
        grid=(1,),
        in_specs=[whole_block(arg.shape) for arg in args],
        out_specs=[whole_block(out.shape) for out in outs],
        out_shape=outs,
        compiler_params=grant(40),
        name="update",
    )(*args)


def pad_lanes(value):
    extra = -value.shape[1] % LANES
    return jnp.pad(value, ((0, 0), (0, extra)))


def local(
    patches,
    masked_at,
    edge_w,
    attn_w,
    mlp_w,
    posit_w,
    vecs_w,
    edge_m,
    attn_m,
    mlp_m,
    posit_m,
    vecs_m,
    edge_v,
    attn_v,
    mlp_v,
    posit_v,
    vecs_v,
    edge_t,
    attn_t,
    mlp_t,
    posit_t,
    vecs_t,
):
    seqs, tokens, width = patches.shape
    plan = Plan()
    total_masked = seqs * plan.count * tokens // 2
    ff_width = mlp_w.shape[1] // (2 * LAYERS)
    small_cols = tokens + vecs_w.shape[1]
    flat_patch = patches.reshape(-1, width)
    mask_flat = masked_at.astype(full_type).reshape(-1, 1)
    mover = plan.mover(width)

    def shards(edge, attn, mlp, posit, vecs):
        small = pad_lanes(jnp.concatenate([posit, vecs], axis=1))
        return [edge[:, :width], edge[:, width:], small] + [
            [
                part[:, layer * part.shape[1] // LAYERS : (layer + 1) * part.shape[1] // LAYERS]
                for part in (attn, mlp)
            ]
            for layer in range(LAYERS)
        ]

    def joined(parts):
        return jnp.concatenate([half(part) for part in parts], axis=1)

    t_patch, _, t_small, t_one, t_two = shards(edge_t, attn_t, mlp_t, posit_t, vecs_t)
    s_patch, s_head, s_small, s_one, s_two = shards(edge_w, attn_w, mlp_w, posit_w, vecs_w)
    chunks = [
        [t_patch, t_one[0], t_small],
        [t_one[1]],
        t_two,
        [s_patch, s_one[0], s_small],
        [s_one[1]],
        [s_two[0], s_head],
        [s_two[1]],
    ]
    groups = [[0], [1], [2], [3], [4, 5, 6]]
    group_start = [0, 1, 2, 3, 4]

    def attn_weights(blocks, start):
        return Weight(blocks, start, 3 * width), Weight(blocks, start + 3 * width, width)

    def mlp_weights(blocks, start):
        return Weight(blocks, start, ff_width), Weight(blocks, start + ff_width, ff_width)

    def small_of(blocks):
        return Weight(blocks, 5 * width, t_small.shape[1])

    def finish(blocks):
        return list(blocks) + [plan.swap(blocks[1], plan.core_stage)]

    def attend_forward(states, table, layer, w_qkv, w_out, keep, outs=None):
        if outs is None:
            outs = norm_project(states, table, layer, w_qkv, keep)
        projected = outs[0].reshape(seqs, tokens, w_qkv.cols)
        mixed = attend(projected).reshape(-1, width)
        results = mix_out(mixed, states, mover, table, LAYERS + layer, w_out, keep)
        if keep:
            return results[0], results[1], (states, outs[1], projected) + tuple(results[2:])
        return results[0], results[1], ()

    saved_attn = [None] * LAYERS
    saved_mlp = [None] * LAYERS

    def segment_t0(_, blocks):
        patch = Weight(blocks, 0, width)
        states, table, patch_rel = embed(
            flat_patch, None, mover, patch, small_of(blocks), True
        )
        weights = attn_weights(blocks, width)
        return states, table, patch_rel, norm_project(states, table, 0, weights[0], False)

    def segment_t0_rest(values, blocks):
        states, table, patch_rel, outs = values
        weights = attn_weights(blocks, width)
        middle, normed, _ = attend_forward(states, table, 0, *weights, False, outs)
        return middle, normed, table, patch_rel

    def segment_t1(values, blocks):
        middle, normed, table, patch_rel = values
        (states,) = feed_forward(normed, middle, *mlp_weights(blocks, 0), False)
        return states, table, patch_rel

    def segment_t2(values, blocks):
        first, table, patch_rel = values
        middle, normed, _ = attend_forward(first, table, 1, *attn_weights(blocks, 0), False)
        (second,) = feed_forward(normed, middle, *mlp_weights(blocks, 4 * width), False)
        return make_target(first, second, seqs), patch_rel

    def segment_s0(values, blocks):
        target, patch_rel = values
        patch = Weight(blocks, 0, width)
        states, table = embed(flat_patch, mask_flat, mover, patch, small_of(blocks), False)
        weights = attn_weights(blocks, width)
        middle, normed, saved = attend_forward(states, table, 0, *weights, True)
        saved_attn[0] = (weights[0], saved)
        return target, patch_rel, table, middle, normed

    def segment_s1(values, blocks):
        target, patch_rel, table, middle, normed = values
        weights = mlp_weights(blocks, 0)
        states, active, slope = feed_forward(normed, middle, *weights, True)
        saved_mlp[0] = (weights, middle, normed, active, slope)
        return target, patch_rel, table, states

    def segment_s2(values, blocks):
        target, patch_rel, table, states = values
        weights = attn_weights(blocks, 0)
        middle, normed, saved = attend_forward(states, table, 1, *weights, True)
        saved_attn[1] = (weights[0], saved)
        return target, patch_rel, table, middle, normed, blocks

    segments = [segment_t0_rest, segment_t1, segment_t2, segment_s0, segment_s1, segment_s2]
    early = len(plan.early)
    group_values = [joined([part for c in group for part in chunks[c]]) for group in groups]
    own = [None] * len(chunks)
    blocks = [None] * len(chunks)
    values = ()
    ahead = {}
    for tick in range(len(chunks) + early + 1):
        sends = {}
        for group, start in enumerate(group_start):
            if 0 <= tick - start < early:
                sends["early", group] = (group_values[group], plan.stages[tick - start])
        for chunk in range(len(chunks)):
            if tick == chunk + early:
                sends["first", chunk] = (own[chunk], plan.stages[early])
            if tick == chunk + early + 1 and ("second", chunk) not in ahead:
                sends["second", chunk] = (own[chunk], plan.stages[early + 1])
                sends["core", chunk] = (own[chunk], plan.core_stage)
        gots = {key: plan.swap(value, perm) for key, (value, perm) in sends.items()}
        if tick == early + 2:
            gots.update(ahead)
        place = tick - early - 2
        if 0 <= place < len(segments):
            values = segments[place](values, finish(blocks[place]))
        if tick == early + 1:
            lead = [gots.pop(key) for key in (("second", 0), ("core", 0), ("first", 1))]
            later = [g for g in range(len(groups)) if group_start[g] > tick]
            lead, held = lax.optimization_barrier((lead, [group_values[g] for g in later]))
            for g, value in zip(later, held):
                group_values[g] = value
            own[1] = jnp.concatenate([own[1], lead[2]], axis=0)
            ahead = {
                ("second", 1): plan.swap(own[1], plan.stages[early + 1]),
                ("core", 1): plan.swap(own[1], plan.core_stage),
            }
            blocks[0] = (own[0], lead[0], lead[1])
            values = segment_t0(values, finish(blocks[0]))
        apart = {key: got for key, got in gots.items() if FAST_LANE and key[1] == 0 and tick}
        gots = {key: got for key, got in gots.items() if key not in apart}
        later = [g for g in range(len(groups)) if group_start[g] > tick]
        idle = [c for c in range(1, len(chunks)) if own[c] is not None and c + early > tick]
        gots, values, held, held_own, _ = lax.optimization_barrier(
            (gots, values, [group_values[g] for g in later], [own[c] for c in idle], apart)
        )
        for g, value in zip(later, held):
            group_values[g] = value
        for c, value in zip(idle, held_own):
            own[c] = value
        gots.update(apart)
        for (kind, index), got in gots.items():
            if kind == "early":
                group_values[index] = jnp.concatenate([group_values[index], got], axis=0)
                if tick - group_start[index] == early - 1:
                    start = 0
                    for chunk in groups[index]:
                        stop = start + sum(part.shape[1] for part in chunks[chunk])
                        own[chunk] = group_values[index][:, start:stop]
                        start = stop
            elif kind == "first":
                own[index] = jnp.concatenate([own[index], got], axis=0)
        for chunk in range(len(chunks)):
            if ("second", chunk) in gots:
                blocks[chunk] = (own[chunk], gots["second", chunk], gots["core", chunk])
    pump = Pump(plan)
    target, patch_rel, table, middle, normed, head_blocks = values
    weights = mlp_weights(finish(blocks[-1]), 0)
    states, active, slope = feed_forward(normed, middle, *weights, True)
    saved_mlp[1] = (weights, middle, normed, active, slope)
    flow, final_normed, grad_pred, grad_gain_final, loss_row = head_step(
        states,
        table,
        mover,
        Weight(head_blocks, 4 * width, width),
        target,
        mask_flat,
        total_masked,
    )

    gain_ones = [None] * LAYERS
    gain_twos = [None] * LAYERS
    shards = {}
    last_stage = len(plan.stages)

    def send_off(name, pieces, narrow, ticks=()):
        pump.add(
            scatter_steps(plan, pieces, narrow), lambda out: shards.__setitem__(name, out), ticks
        )

    for layer in reversed(range(LAYERS)):
        w_qkv, (states, normed_one, projected, mixed_rel, w_out_rel) = saved_attn[layer]
        (w_up, w_down), middle, normed_two, active, slope = saved_mlp[layer]
        pump.begin()
        grad_hidden, grad_down, grad_middle, grad_branch, gain_twos[layer] = feed_back(
            flow, slope, middle, table, LAYERS + layer, w_up, w_down
        )
        grad_hidden, grad_down, grad_middle, grad_branch = pump.end(
            (grad_hidden, grad_down, grad_middle, grad_branch)
        )
        pump.begin()
        piece = weight_grads([(normed_two, [grad_hidden]), (grad_down, [active])])
        piece, grad_branch = pump.end((piece, grad_branch))
        send_off(
            ("mlp", layer), [piece], 3, {1: 2, last_stage: 2} if layer else {last_stage: 2}
        )
        pump.begin()
        grad_mixed, branch_whole = mix_back(grad_branch, w_out_rel, mover)
        grad_mixed = grad_mixed.reshape(seqs, tokens, width)
        grad_proj = ()
        for seq in range(seqs - 1):
            grad_proj = attend_back(projected, grad_mixed, seq, tuple(grad_proj))
        grad_proj, grad_mixed, branch_whole = pump.end((grad_proj, grad_mixed, branch_whole))
        pump.begin()
        grad_proj = attend_back(projected, grad_mixed, seqs - 1, tuple(grad_proj))
        grad_proj = [part.reshape(-1, width) for part in grad_proj]
        pairs = [(normed_one, grad_proj), (mixed_rel, [branch_whole])]
        if layer == 0:
            piece = weight_grads(pairs)
            piece, grad_proj = pump.end((piece, grad_proj))
            send_off(("attn", 0), [piece], 3)
            pump.begin()
        results = project_back(
            grad_proj,
            grad_middle,
            states,
            table,
            layer,
            w_qkv,
            mover,
            None if layer else mask_flat,
        )
        flow, gain_ones[layer] = results[:2]
        if layer:
            flow, grad_proj = pump.end((flow, grad_proj))
            pairs = [(normed_one, grad_proj), (mixed_rel, [branch_whole])]
            pairs.append((final_normed, [grad_pred]))
            pump.begin()
            piece = weight_grads(pairs)
            piece, flow = pump.end((piece, flow))
            send_off(("attn", layer), [piece], 2)
    grad_embed, grad_maskvec = results[2:]
    vectors = gain_ones + gain_twos + [grad_gain_final, grad_maskvec]
    pieces = pump.end(
        [weight_grads([(patch_rel, [grad_embed])]), small_grads(flow, vectors, seqs)]
    )
    send_off("edge", pieces, 2)
    pump.drain()
    pieces = (
        shards["edge"],
        shards["attn", 0],
        shards["attn", 1],
        shards["mlp", 0],
        shards["mlp", 1],
    )
    totals = norm_totals(*pieces, loss_row, width, tokens)
    for perm in [plan.core_stage] + plan.stages:
        totals = totals + plan.swap(totals, perm)
    groups = [
        (edge_w, edge_m, edge_v, edge_t),
        (attn_w, attn_m, attn_v, attn_t),
        (mlp_w, mlp_m, mlp_v, mlp_t),
        (posit_w, posit_m, posit_v, posit_t),
        (vecs_w.T, vecs_m.T, vecs_v.T, vecs_t.T),
    ]
    sizes = [group[0].size * plan.count for group in groups]
    news = update(totals, *pieces, groups, sizes, width, tokens)
    news = [
        [news[4 * group + part] for group in range(4)] + [news[16 + part].T] for part in range(4)
    ]
    return (totals[0, 0] / total_masked,) + tuple(new for part in news for new in part)


def solution(mesh):
    rows = P(AXES, None)
    in_specs = (P(AXES, None, None),) + (rows,) * 21
    out_specs = (P(),) + (rows,) * 20
    return jax.shard_map(local, mesh=mesh, in_specs=in_specs, out_specs=out_specs, check_vma=False)
```
